32 devices in a mesh: ctx: 8 (over z, x), fsdp: 4 (over y, core).
Axes of the slice: x: 2, y: 2, z: 4, core: 2. Of those that a mesh axis runs over, the one named last changes fastest.
Arguments:
- tokens: bfloat16 [3, 4, 1024, 768], P(None, 'fsdp', 'ctx'), may hold values from -6 to 6
- doc_starts: int32 [3, 4, 8], P(None, 'fsdp'), may hold values from 0 to 1023, as said below
- joint_weight: bfloat16 [768, 2304], P('fsdp'), may hold values from -0.21875 to 0.21875
- mixer_weight: bfloat16 [768, 768], P('fsdp'), may hold values from -2.5 to 2.5
- inner_weight: bfloat16 [768, 3072], P('fsdp'), may hold values from -0.21875 to 0.21875
- outer_weight: bfloat16 [3072, 768], P('fsdp'), may hold values from -0.109375 to 0.109375
- query_bias: bfloat16 [768], P('fsdp'), may hold values from -4 to 4
- value_bias: bfloat16 [768], P('fsdp'), may hold values from -0.4375 to 0.4375
- mixer_bias: bfloat16 [768], P('fsdp'), may hold values from -4 to 4
- first_gain: bfloat16 [768], P('fsdp'), may hold values from 0.5 to 1.5
- first_shift: bfloat16 [768], P('fsdp'), may hold values from -4 to 4
- inner_bias: bfloat16 [3072], P('fsdp'), may hold values from -4 to 4
- outer_bias: bfloat16 [768], P('fsdp'), may hold values from -4 to 4
- second_gain: bfloat16 [768], P('fsdp'), may hold values from 0.5 to 1.5
- second_shift: bfloat16 [768], P('fsdp'), may hold values from -4 to 4
- upstream: bfloat16 [3, 4, 1024, 768], P(None, 'fsdp', 'ctx'), may hold values from -6 to 6
Outputs:
- result: bfloat16 [3, 4, 1024, 768], P(None, 'fsdp', 'ctx')
- tokens_gradient: float32 [3, 4, 1024, 768], P(None, 'fsdp', 'ctx')
- joint_gradient: float32 [768, 2304], P('fsdp', 'ctx')
- mixer_gradient: float32 [768, 768], P('fsdp', 'ctx')
- inner_gradient: float32 [768, 3072], P('fsdp', 'ctx')
- outer_gradient: float32 [3072, 768], P('fsdp', 'ctx')
- query_gradient: float32 [768], P(('ctx', 'fsdp'))
- values_gradient: float32 [768], P(('ctx', 'fsdp'))
- mixing_gradient: float32 [768], P(('ctx', 'fsdp'))
- scale_gradient: float32 [768], P(('ctx', 'fsdp'))
- shift_gradient: float32 [768], P(('ctx', 'fsdp'))
- hidden_gradient: float32 [3072], P(('ctx', 'fsdp'))
- return_gradient: float32 [768], P(('ctx', 'fsdp'))
- rescale_gradient: float32 [768], P(('ctx', 'fsdp'))
- reshift_gradient: float32 [768], P(('ctx', 'fsdp'))
The draws below stay inside these ranges and needn't reach their ends.
Inputs may be any that keep to these rules, and one draw needn't show every extreme that they name: `doc_starts`: each row of 8 starts begins with 0 and rises strictly; documents may begin anywhere in a sequence.
All inputs are finite; a program needn't handle non-finite values.
Results may differ from the reference program's by a relative error of at most 0.017.
Values may be sent and summed in bfloat16 or wider, within the bound.
A program may use at most 320 MiB of HBM per device.

```python
import math
import jax
import jax.numpy as jnp
from jax import lax

D = 768
H = 12
HD = 64
FF = 3072
MB = 3
NDOC = 8
SEQ = 1024
STREAMS = 4


def draw_doc_starts(key, part):

    def one_row(row_key):
        cuts = jax.random.permutation(row_key, SEQ - 1)[0:NDOC - 1] + 1
        return jnp.concatenate([jnp.zeros((1,), jnp.int32), jnp.sort(cuts).astype(jnp.int32)])
    row_keys = jax.random.split(key, MB * STREAMS)
    rows_all = jax.vmap(one_row)(row_keys)
    rows_all = rows_all.at[0, NDOC - 1].set(SEQ - 1)
    return rows_all.reshape(MB, STREAMS, NDOC)


def levels(rng, extent, shards, low, top_value):
    level = 1.0
    for position, shards_of in shards:
        draws = jax.random.uniform(jax.random.fold_in(jax.random.fold_in(rng, 6), position), (shards_of,), jnp.float32, low / len(shards), top_value / len(shards))
        level = level * jnp.repeat(jnp.exp(draws), extent[position] // shards_of).reshape((-1,) + (1,) * (len(extent) - 1 - position))
    return level


def scatter_about(rng, dims, scale, bound, cuts=(), kind=jnp.bfloat16):
    loudness = levels(rng, dims, cuts, -0.22, 0.18) if cuts else 1.0
    values = jax.random.normal(rng, dims, jnp.float32) * scale * loudness
    return jnp.minimum(jnp.maximum(values, -bound), bound).astype(kind)


def setup_inputs(seed: int = 0) -> dict:
    key_of = jax.random.split(jax.random.key(seed), 17)
    return {
        "tokens": scatter_about(key_of[0], (MB, STREAMS, SEQ, D), 1.0, 6.0, ((1, 4), (2, 8))),
        "doc_starts": draw_doc_starts(jax.random.fold_in(key_of[16], 71), 0),
        "joint_weight": scatter_about(key_of[2], (D, 3 * D), D ** -0.5, 0.21875, ((0, 4),)),
        "mixer_weight": scatter_about(key_of[3], (D, D), (D // 128) ** -0.5, 2.5, ((0, 4),)),
        "inner_weight": scatter_about(key_of[4], (D, FF), D ** -0.5, 0.21875, ((0, 4),)),
        "outer_weight": scatter_about(key_of[5], (FF, D), FF ** -0.5, 0.109375, ((0, 4),)),
        "query_bias": scatter_about(key_of[6], (D,), 0.3, 4.0, ((0, 4),)),
        "value_bias": scatter_about(key_of[7], (D,), 0.03, 0.4375, ((0, 4),)),
        "mixer_bias": scatter_about(key_of[8], (D,), 0.3, 4.0, ((0, 4),)),
        "first_gain": jnp.clip(1.0 + 0.1 * jax.random.normal(key_of[9], (D,), jnp.float32), 0.5, 1.5).astype(jnp.bfloat16),
        "first_shift": scatter_about(key_of[10], (D,), 0.3, 4.0, ((0, 4),)),
        "inner_bias": scatter_about(key_of[11], (FF,), 0.3, 4.0, ((0, 4),)),
        "outer_bias": scatter_about(key_of[12], (D,), 0.3, 4.0, ((0, 4),)),
        "second_gain": jnp.clip(1.0 + 0.1 * jax.random.normal(key_of[13], (D,), jnp.float32), 0.5, 1.5).astype(jnp.bfloat16),
        "second_shift": scatter_about(key_of[14], (D,), 0.3, 4.0, ((0, 4),)),
        "upstream": scatter_about(key_of[15], (MB, STREAMS, SEQ, D), 1.0, 6.0, ((1, 4), (2, 8))),
    }


HIGHEST_PRECISION = lax.Precision.HIGHEST
SCALE = 0.125
EPSILON = 1e-12
MASKED = -1000000000.0
ROOT_HALF = 0.7071067811865476

@jax.custom_vjp
def low(v):
    return lax.optimization_barrier(v.astype(jnp.bfloat16)).astype(jnp.float32)

@jax.custom_vjp
def low_back(v):
    return v

def low_keep(v):
    return (low(v), None)

def low_pass(kept, grad):
    return (grad,)

def back_keep(v):
    return (v, None)

def back_low(kept, grad):
    return (low(grad),)
low.defvjp(low_keep, low_pass)
low_back.defvjp(back_keep, back_low)

def layer_norm(hidden, gain, shift):
    average = lax.optimization_barrier(jnp.mean(hidden, axis=-1, keepdims=True))
    centred = hidden - average
    reciprocal = lax.rsqrt(lax.optimization_barrier(jnp.mean(centred * centred, axis=-1, keepdims=True)) + EPSILON)
    return centred * reciprocal * gain + shift

def doc_index(positions, starts_row):
    return lax.optimization_barrier(jnp.sum((starts_row[None, :] <= positions[:, None]).astype(jnp.int32), axis=1)) - 1

def sequence_layer(params, inputs, starts_row):
    joint_weight, mixer_weight, inner_weight, outer_weight, query_bias, value_bias, mixer_bias, first_gain, first_shift, inner_bias, outer_bias, second_gain, second_shift = params
    length = inputs.shape[0]
    projected = jnp.dot(inputs, joint_weight, precision=HIGHEST_PRECISION)
    queries = low_back(low(projected[:, 0:D] + query_bias)).reshape(length, H, HD)
    key_rows = low_back(low(projected[:, D:2 * D])).reshape(length, H, HD)
    values = low_back(low(projected[:, 2 * D:3 * D] + value_bias)).reshape(length, H, HD)
    docs = doc_index(jnp.arange(length, dtype=jnp.int32), starts_row)
    block = math.gcd(length, 512)

    def attend(paired):
        query_block, query_docs = paired
        raw_scores = low_back(jnp.einsum('ihd,jhd->hij', query_block, key_rows, precision=HIGHEST_PRECISION))
        allowed = query_docs[:, None] == docs[None, :]
        scores = jnp.where(allowed[None], raw_scores * SCALE, MASKED)
        highest = lax.optimization_barrier(jnp.max(scores, axis=-1, keepdims=True))
        expo = jnp.exp(scores - highest)
        probs = expo / lax.optimization_barrier(jnp.sum(expo, axis=-1, keepdims=True))
        return jnp.einsum('hij,jhd->ihd', low(probs), values, precision=HIGHEST_PRECISION)
    mixed = lax.map(jax.checkpoint(attend), (queries.reshape(length // block, block, H, HD), docs.reshape(length // block, block)))
    attended = low_back(low(mixed.reshape(length, D)))
    branch = low_back(jnp.dot(attended, mixer_weight, precision=HIGHEST_PRECISION) + mixer_bias)
    first = layer_norm(inputs + branch, first_gain, first_shift)
    inner = low_back(jnp.dot(low(first), inner_weight, precision=HIGHEST_PRECISION) + inner_bias)
    activated = inner * (0.5 * (1.0 + lax.erf(inner * ROOT_HALF)))
    outer = low_back(jnp.dot(low(activated), outer_weight, precision=HIGHEST_PRECISION) + outer_bias)
    return layer_norm(first + outer, second_gain, second_shift)

def reference(tokens, doc_starts, joint_weight, mixer_weight, inner_weight, outer_weight, query_bias, value_bias, mixer_bias, first_gain, first_shift, inner_bias, outer_bias, second_gain, second_shift, upstream):
    params = (joint_weight.astype(jnp.float32), mixer_weight.astype(jnp.float32), inner_weight.astype(jnp.float32), outer_weight.astype(jnp.float32), query_bias.astype(jnp.float32), value_bias.astype(jnp.float32), mixer_bias.astype(jnp.float32), first_gain.astype(jnp.float32), first_shift.astype(jnp.float32), inner_bias.astype(jnp.float32), outer_bias.astype(jnp.float32), second_gain.astype(jnp.float32), second_shift.astype(jnp.float32))
    count = tokens.shape[0] * tokens.shape[1]
    flat_inputs = tokens.astype(jnp.float32).reshape(count, SEQ, D)
    flat_starts = doc_starts.reshape(count, NDOC)

    def forward(weights, inputs):

        def one_sequence(paired):
            return sequence_layer(weights, paired[0], paired[1])
        return lax.map(one_sequence, (inputs, flat_starts))
    outputs, pullback = jax.vjp(forward, params, flat_inputs)
    weight_grads, input_grads = pullback(upstream.astype(jnp.float32).reshape(count, SEQ, D))
    joint_gradient, mixer_gradient, inner_gradient, outer_gradient, query_gradient, values_gradient, mixing_gradient, scale_gradient, shift_gradient, hidden_gradient, return_gradient, rescale_gradient, reshift_gradient = weight_grads
    return (outputs.reshape(tokens.shape).astype(jnp.bfloat16), input_grads.reshape(tokens.shape), joint_gradient, mixer_gradient, inner_gradient, outer_gradient, query_gradient, values_gradient, mixing_gradient, scale_gradient, shift_gradient, hidden_gradient, return_gradient, rescale_gradient, reshift_gradient)
```

```python
import functools
import math

import jax
import jax.numpy as jnp
from jax import lax
from jax.experimental import pallas as pl
from jax.experimental.pallas import tpu as pltpu
from jax.sharding import PartitionSpec as P

D = 768
H = 12
HD = 64
FF = 3072
MB = 3

SCALE = 0.125
EPSILON = 1e-12
MASKED = -1000000000.0
ROOT_HALF = 0.7071067811865476
GAUSS_PEAK = 0.3989422804014327

F32 = jnp.float32
BF16 = jnp.bfloat16


def doc_index(positions, starts_row):
    return jnp.sum((starts_row[None, :] <= positions[:, None]).astype(jnp.int32), axis=1) - 1


def norm_forward(hidden, gain, shift):
    average = jnp.mean(hidden, axis=-1, keepdims=True)
    centred = hidden - average
    reciprocal = lax.rsqrt(jnp.mean(centred * centred, axis=-1, keepdims=True) + EPSILON)
    normed = centred * reciprocal
    return (normed * gain + shift, normed, reciprocal)


def norm_backward(incoming, normed, reciprocal, gain):
    scaled = incoming * gain
    return reciprocal * (
        scaled
        - jnp.mean(scaled, axis=-1, keepdims=True)
        - normed * jnp.mean(scaled * normed, axis=-1, keepdims=True)
    )


def gelu_parts(inner):
    cumulative = 0.5 * (1.0 + lax.erf(inner * ROOT_HALF))
    return (inner * cumulative, cumulative + inner * jnp.exp(-0.5 * inner * inner) * GAUSS_PEAK)


def exchange_kernel(count, x_ref, y_ref, held, send_sem, recv_sem, own_sem):
    me = lax.axis_index("ctx")
    barrier = pltpu.get_barrier_semaphore()

    def greet(step, carry):
        peer = lax.rem(me + step, count)
        pl.semaphore_signal(barrier, inc=1, device_id={"ctx": peer})
        return carry

    lax.fori_loop(1, count, greet, 0)
    own_in = pltpu.make_async_copy(x_ref.at[me], held, own_sem)
    own_in.start()
    pl.semaphore_wait(barrier, count - 1)

    def transfer(step):
        peer = lax.rem(me + step, count)
        return pltpu.make_async_remote_copy(
            src_ref=x_ref.at[peer],
            dst_ref=y_ref.at[me],
            send_sem=send_sem.at[step],
            recv_sem=recv_sem.at[step],
            device_id={"ctx": peer},
        )

    def begin(step, carry):
        transfer(step).start()
        return carry

    lax.fori_loop(1, count, begin, 0)
    own_in.wait()
    own_out = pltpu.make_async_copy(held, y_ref.at[me], own_sem)
    own_out.start()
    own_out.wait()

    def finish(step, carry):
        transfer(step).wait()
        return carry

    lax.fori_loop(1, count, finish, 0)


def exchange(x, number):
    count = x.shape[0]
    return pl.pallas_call(
        functools.partial(exchange_kernel, count),
        out_shape=jax.ShapeDtypeStruct(x.shape, x.dtype),
        in_specs=[pl.BlockSpec(memory_space=pl.ANY)],
        out_specs=pl.BlockSpec(memory_space=pl.ANY),
        scratch_shapes=[
            pltpu.VMEM(x.shape[1:], x.dtype),
            pltpu.SemaphoreType.DMA((count,)),
            pltpu.SemaphoreType.DMA((count,)),
            pltpu.SemaphoreType.DMA,
        ],
        compiler_params=pltpu.CompilerParams(collective_id=number, has_side_effects=True),
        name=f"exchange_{number}",
    )(x)


def across(ref, first, rows, width, lanes):
    parts = [ref[first + i, 0, rows, :] for i in range(width // lanes)]
    return parts[0] if len(parts) == 1 else jnp.concatenate(parts, axis=1)


def key_documents(starts_ref, unit, length, lanes, key_docs):
    position = lax.broadcasted_iota(jnp.int32, (length, lanes), 0)
    docs = jnp.zeros((length, lanes), jnp.int32) - 1
    for j in range(starts_ref.shape[1]):
        docs = docs + jnp.where(position >= starts_ref[unit, j], 1, 0)
    key_docs[...] = docs


def same_document(key_docs, first, width, query_docs):
    keys = key_docs[pl.ds(first, width), :]
    lanes = keys.shape[1]
    parts = [keys == query_docs[:, i : i + lanes] for i in range(0, query_docs.shape[1], lanes)]
    return parts[0] if len(parts) == 1 else jnp.concatenate(parts, axis=1)


def over_chunks(chunks, body, carry):
    if chunks == 1:
        return body(0, carry)
    return lax.fori_loop(0, chunks, body, carry)


def attend_kernel(
    width, starts_ref, x_ref, docs_ref, o_ref, wide_ref, lse_ref, key_rows, value_t, key_docs
):
    count, _, _, lanes = x_ref.shape
    length = count * lanes
    depth = min(length, 1024)
    unit = pl.program_id(0)
    for i in range(count):
        rows = slice(i * lanes, (i + 1) * lanes)
        key_rows[rows, :] = x_ref[i, 0, HD : 2 * HD, :].T
        value_t[:, rows] = x_ref[i, 0, 2 * HD : 3 * HD, :]
    key_documents(starts_ref, unit, length, lanes, key_docs)
    group = width // lanes

    def block(number, carry):
        begin = pl.multiple_of(number * width, width)
        queries = across(x_ref, number * group, slice(0, HD), width, lanes) * SCALE
        query_docs = docs_ref[0, :, pl.ds(begin, width)]

        def chunk(index, running):
            peak, total, mixed = running
            first = pl.multiple_of(index * depth, depth)
            scores = jnp.dot(
                key_rows[pl.ds(first, depth), :], queries, preferred_element_type=F32
            )
            same = same_document(key_docs, first, depth, query_docs)
            scores = jnp.where(same, scores, MASKED)
            new_peak = jnp.maximum(peak, jnp.max(scores, axis=0, keepdims=True))
            scaling = jnp.exp(peak - new_peak)
            weights = jnp.exp(scores - new_peak)
            return (
                new_peak,
                total * scaling + jnp.sum(weights, axis=0, keepdims=True),
                mixed * scaling
                + jnp.dot(
                    value_t[:, pl.ds(first, depth)],
                    weights.astype(BF16),
                    preferred_element_type=F32,
                ),
            )

        peak, total, mixed = over_chunks(
            length // depth,
            chunk,
            (
                jnp.full((1, width), -jnp.inf, F32),
                jnp.zeros((1, width), F32),
                jnp.zeros((HD, width), F32),
            ),
        )
        mixed = mixed / total
        wide_ref[0, :, pl.ds(begin, width)] = mixed
        lse_ref[0, :, pl.ds(begin, width)] = peak + jnp.log(total)
        low = mixed.astype(BF16)
        for i in range(group):
            o_ref[number * group + i, 0] = low[:, i * lanes : (i + 1) * lanes]
        return carry

    lax.fori_loop(0, length // width, block, 0)


def attend_back_kernel(
    width,
    starts_ref,
    x_ref,
    flow_ref,
    docs_ref,
    wide_ref,
    lse_ref,
    d_ref,
    key_rows,
    value_rows,
    key_t,
    key_docs,
    d_key,
    d_value,
):
    count, _, _, lanes = x_ref.shape
    length = count * lanes
    depth = min(length, 1024)
    unit = pl.program_id(0)
    for i in range(count):
        rows = slice(i * lanes, (i + 1) * lanes)
        key_rows[rows, :] = x_ref[i, 0, HD : 2 * HD, :].T
        value_rows[rows, :] = x_ref[i, 0, 2 * HD : 3 * HD, :].T
        key_t[:, rows] = x_ref[i, 0, HD : 2 * HD, :]
    key_documents(starts_ref, unit, length, lanes, key_docs)
    d_key[...] = jnp.zeros_like(d_key)
    d_value[...] = jnp.zeros_like(d_value)
    group = width // lanes

    def block(number, carry):
        begin = pl.multiple_of(number * width, width)
        queries = across(x_ref, number * group, slice(0, HD), width, lanes) * SCALE
        flow = across(flow_ref, number * group, slice(0, HD), width, lanes)
        query_rows = queries.T
        flow_rows = flow.T
        query_docs = docs_ref[0, :, pl.ds(begin, width)]
        log_total = lse_ref[0, :, pl.ds(begin, width)]
        spread = jnp.sum(
            flow.astype(F32) * wide_ref[0, :, pl.ds(begin, width)], axis=0, keepdims=True
        )

        def chunk(index, d_query):
            first = pl.multiple_of(index * depth, depth)
            rows = pl.ds(first, depth)
            scores = jnp.dot(key_rows[rows, :], queries, preferred_element_type=F32)
            same = same_document(key_docs, first, depth, query_docs)
            probs = jnp.exp(jnp.where(same, scores, MASKED) - log_total)
            pressure = jnp.dot(value_rows[rows, :], flow, preferred_element_type=F32)
            d_scores = (probs * (pressure - spread)).astype(BF16)
            d_value[rows, :] += jnp.dot(
                probs.astype(BF16), flow_rows, preferred_element_type=F32
            )
            d_key[rows, :] += jnp.dot(d_scores, query_rows, preferred_element_type=F32)
            return d_query + jnp.dot(key_t[:, rows], d_scores, preferred_element_type=F32)

        d_query = over_chunks(length // depth, chunk, jnp.zeros((HD, width), F32))
        low = (d_query * SCALE).astype(BF16)
        for i in range(group):
            d_ref[number * group + i, 0, 0:HD, :] = low[:, i * lanes : (i + 1) * lanes]
        return carry

    lax.fori_loop(0, length // width, block, 0)
    for i in range(count):
        rows = slice(i * lanes, (i + 1) * lanes)
        d_ref[i, 0, HD : 2 * HD, :] = d_key[rows, :].T.astype(BF16)
        d_ref[i, 0, 2 * HD : 3 * HD, :] = d_value[rows, :].T.astype(BF16)


def unit_block(*dims):
    return pl.BlockSpec(dims, lambda u, starts: (0, u) + (0,) * (len(dims) - 2))


def own_block(*dims):
    return pl.BlockSpec(dims, lambda u, starts: (u,) + (0,) * (len(dims) - 1))


def attend(x, starts, docs):
    count, units, _, lanes = x.shape
    length = count * lanes
    width = 2 * lanes if count % 2 == 0 else lanes
    return pl.pallas_call(
        functools.partial(attend_kernel, width),
        out_shape=(
            jax.ShapeDtypeStruct((count, units, HD, lanes), BF16),
            jax.ShapeDtypeStruct((units, HD, length), F32),
            jax.ShapeDtypeStruct((units, 1, length), F32),
        ),
        grid_spec=pltpu.PrefetchScalarGridSpec(
            num_scalar_prefetch=1,
            grid=(units,),
            in_specs=[unit_block(count, 1, 3 * HD, lanes), own_block(1, 1, length)],
            out_specs=[
                unit_block(count, 1, HD, lanes),
                own_block(1, HD, length),
                own_block(1, 1, length),
            ],
            scratch_shapes=[
                pltpu.VMEM((length, HD), BF16),
                pltpu.VMEM((HD, length), BF16),
                pltpu.VMEM((length, lanes), jnp.int32),
            ],
        ),
        compiler_params=pltpu.CompilerParams(dimension_semantics=("arbitrary",)),
        name="attend",
    )(starts, x, docs)


def attend_back(x, flow, starts, docs, wide, lse):
    count, units, _, lanes = x.shape
    length = count * lanes
    width = 2 * lanes if count % 2 == 0 else lanes
    return pl.pallas_call(
        functools.partial(attend_back_kernel, width),
        out_shape=jax.ShapeDtypeStruct(x.shape, BF16),
        grid_spec=pltpu.PrefetchScalarGridSpec(
            num_scalar_prefetch=1,
            grid=(units,),
            in_specs=[
                unit_block(count, 1, 3 * HD, lanes),
                unit_block(count, 1, HD, lanes),
                own_block(1, 1, length),
                own_block(1, HD, length),
                own_block(1, 1, length),
            ],
            out_specs=unit_block(count, 1, 3 * HD, lanes),
            scratch_shapes=[
                pltpu.VMEM((length, HD), BF16),
                pltpu.VMEM((length, HD), BF16),
                pltpu.VMEM((HD, length), BF16),
                pltpu.VMEM((length, lanes), jnp.int32),
                pltpu.VMEM((length, HD), F32),
                pltpu.VMEM((length, HD), F32),
            ],
        ),
        compiler_params=pltpu.CompilerParams(dimension_semantics=("arbitrary",)),
        name="attend_back",
    )(starts, x, flow, docs, wide, lse)


def to_units(columns, parts, count, units):
    rows = columns.shape[1] // MB
    x = columns.reshape(parts, H, HD, MB, rows).transpose(3, 1, 0, 2, 4)
    x = x.reshape(MB * H, parts * HD, rows)
    x = jnp.pad(x, ((0, units * count - MB * H), (0, 0), (0, 0)))
    return x.reshape(units, count, parts * HD, rows).transpose(1, 0, 2, 3)


def from_units(x, parts):
    count, units, _, rows = x.shape
    x = x.transpose(1, 0, 2, 3).reshape(units * count, parts * HD, rows)[: MB * H]
    x = x.reshape(MB, H, parts, HD, rows).transpose(2, 1, 3, 0, 4)
    return x.reshape(parts * D, MB * rows)


def mul_nn(a, b):
    return jnp.dot(a, b, preferred_element_type=F32)


def mul_tn(a, b):
    return lax.dot_general(a, b, (((0,), (0,)), ((), ())), preferred_element_type=F32)


def mul_nt(a, b):
    return lax.dot_general(a, b, (((1,), (1,)), ((), ())), preferred_element_type=F32)


def mul_tt(a, b):
    return lax.dot_general(a, b, (((0,), (1,)), ((), ())), preferred_element_type=F32)


def on_device(
    count,
    shards,
    tokens,
    doc_starts,
    joint_weight,
    mixer_weight,
    inner_weight,
    outer_weight,
    query_bias,
    value_bias,
    mixer_bias,
    first_gain,
    first_shift,
    inner_bias,
    outer_bias,
    second_gain,
    second_shift,
    upstream,
):
    rows = tokens.shape[2]
    length = rows * count
    units = -(-MB * H // count)
    me = lax.axis_index("ctx")

    joint = lax.all_gather(joint_weight, "fsdp", axis=0, tiled=True)
    vectors = jnp.concatenate(
        [
            query_bias,
            value_bias,
            mixer_bias,
            first_gain,
            first_shift,
            outer_bias,
            second_gain,
            second_shift,
            inner_bias,
        ]
    )
    vectors = lax.all_gather(vectors, "fsdp", axis=0)
    part = D // shards
    names = [vectors[:, i * part : (i + 1) * part].reshape(D).astype(F32) for i in range(8)]
    qbias, vbias, mbias, gain_one, shift_one, obias, gain_two, shift_two = names
    ibias = vectors[:, 8 * part :].reshape(FF).astype(F32)
    mixer = lax.all_gather(mixer_weight, "fsdp", axis=0, tiled=True)
    inner = lax.all_gather(inner_weight, "fsdp", axis=0, tiled=True)
    outer = lax.all_gather(outer_weight, "fsdp", axis=0, tiled=True)

    source = tokens.reshape(MB * rows, D)
    unit_ids = jnp.arange(units, dtype=jnp.int32) * count + me
    unit_starts = doc_starts[:, 0][jnp.minimum(unit_ids // H, MB - 1)]
    positions = jnp.arange(length, dtype=jnp.int32)
    unit_docs = jax.vmap(lambda s: doc_index(positions, s))(unit_starts)[:, None, :]

    joint_bias = jnp.concatenate([qbias, jnp.zeros((D,), F32), vbias])
    projected = (mul_tt(joint, source) + joint_bias[:, None]).astype(BF16)
    received = exchange(to_units(projected, 3, count, units), 0)
    mixed, wide, lse = attend(received, unit_starts, unit_docs)
    attended = from_units(exchange(mixed, 1), 1)

    branch = mul_tn(attended, mixer) + mbias
    first, first_normed, first_recip = norm_forward(
        source.astype(F32) + branch, gain_one, shift_one
    )
    first_low = first.astype(BF16)
    inner_pre = mul_nn(first_low, inner) + ibias
    activated, gelu_slope = gelu_parts(inner_pre)
    activated_low = activated.astype(BF16)
    outer_out = mul_nn(activated_low, outer) + obias
    final, second_normed, second_recip = norm_forward(first + outer_out, gain_two, shift_two)
    result = final.astype(BF16).reshape(MB, 1, rows, D)

    incoming = upstream.reshape(MB * rows, D).astype(F32)
    rescale_grad = jnp.sum(incoming * second_normed, axis=0)
    reshift_grad = jnp.sum(incoming, axis=0)
    d_second = norm_backward(incoming, second_normed, second_recip, gain_two)
    d_outer = d_second.astype(BF16)
    return_grad = jnp.sum(d_outer.astype(F32), axis=0)
    outer_grad = mul_tn(activated_low, d_outer)
    d_inner = (mul_nt(d_outer, outer) * gelu_slope).astype(BF16)
    hidden_grad = jnp.sum(d_inner.astype(F32), axis=0)
    inner_grad = mul_tn(first_low, d_inner)
    d_first = d_second + mul_nt(d_inner, inner)
    scale_grad = jnp.sum(d_first * first_normed, axis=0)
    shift_grad = jnp.sum(d_first, axis=0)
    d_residual = norm_backward(d_first, first_normed, first_recip, gain_one)
    d_branch = d_residual.astype(BF16)
    mixing_grad = jnp.sum(d_branch.astype(F32), axis=0)
    mixer_grad = mul_nn(attended, d_branch)
    flow = mul_nt(mixer, d_branch).astype(BF16)
    flow_units = exchange(to_units(flow, 1, count, units), 2)
    d_units = attend_back(received, flow_units, unit_starts, unit_docs, wide, lse)
    d_joint = from_units(exchange(d_units, 3), 3)
    bias_sums = jnp.sum(d_joint.astype(F32), axis=1)
    query_grad = bias_sums[0:D]
    values_grad = bias_sums[2 * D :]
    joint_grad = lax.dot_general(
        source, d_joint, (((0,), (1,)), ((), ())), preferred_element_type=F32
    )
    tokens_grad = d_residual + mul_tt(d_joint, joint)
    tokens_grad = tokens_grad.reshape(MB, 1, rows, D)

    def reduced(grad):
        over_rows = lax.psum_scatter(
            grad.astype(BF16), "fsdp", scatter_dimension=0, tiled=True
        )
        return lax.psum_scatter(over_rows, "ctx", scatter_dimension=1, tiled=True).astype(F32)

    outer_out_grad = reduced(outer_grad)
    inner_out = reduced(inner_grad)
    mixer_out = reduced(mixer_grad)
    joint_out = reduced(joint_grad)

    world = count * shards
    small = [
        query_grad,
        values_grad,
        mixing_grad,
        scale_grad,
        shift_grad,
        hidden_grad,
        return_grad,
        rescale_grad,
        reshift_grad,
    ]
    packed = jnp.concatenate([v.reshape(world, -1) for v in small], axis=1)
    packed = lax.psum(packed, ("ctx", "fsdp"))
    index = me * shards + lax.axis_index("fsdp")
    own = lax.dynamic_slice_in_dim(packed, index, 1, 0)[0]
    sums = []
    begin = 0
    for v in small:
        size = v.shape[0] // world
        sums.append(own[begin : begin + size])
        begin += size
    return (result, tokens_grad, joint_out, mixer_out, inner_out, outer_out_grad, *sums)


def solution(mesh):
    in_specs = (
        P(None, "fsdp", "ctx", None),
        P(None, "fsdp", None),
        P("fsdp", None),
        P("fsdp", None),
        P("fsdp", None),
        P("fsdp", None),
        P("fsdp"),
        P("fsdp"),
        P("fsdp"),
        P("fsdp"),
        P("fsdp"),
        P("fsdp"),
        P("fsdp"),
        P("fsdp"),
        P("fsdp"),
        P(None, "fsdp", "ctx", None),
    )
    out_specs = (
        P(None, "fsdp", "ctx", None),
        P(None, "fsdp", "ctx", None),
        P("fsdp", "ctx"),
        P("fsdp", "ctx"),
        P("fsdp", "ctx"),
        P("fsdp", "ctx"),
        P(("ctx", "fsdp")),
        P(("ctx", "fsdp")),
        P(("ctx", "fsdp")),
        P(("ctx", "fsdp")),
        P(("ctx", "fsdp")),
        P(("ctx", "fsdp")),
        P(("ctx", "fsdp")),
        P(("ctx", "fsdp")),
        P(("ctx", "fsdp")),
    )
    return jax.shard_map(
        functools.partial(on_device, mesh.shape["ctx"], mesh.shape["fsdp"]),
        mesh=mesh,
        in_specs=in_specs,
        out_specs=out_specs,
        check_vma=False,
    )
```

```python
import functools
import math

import jax
import jax.numpy as jnp
from jax import lax
from jax.experimental import pallas as pl
from jax.experimental.pallas import tpu as pltpu
from jax.sharding import PartitionSpec as P

D = 768
H = 12
HD = 64
FF = 3072
MB = 3

SCALE = 0.125
EPSILON = 1e-12
MASKED = -1000000000.0
ROOT_HALF = 0.7071067811865476
GAUSS_PEAK = 0.3989422804014327

F32 = jnp.float32
BF16 = jnp.bfloat16


def doc_index(positions, starts_row):
    return jnp.sum((starts_row[None, :] <= positions[:, None]).astype(jnp.int32), axis=1) - 1


def norm_forward(hidden, gain, shift):
    average = jnp.mean(hidden, axis=-1, keepdims=True)
    centred = hidden - average
    reciprocal = lax.rsqrt(jnp.mean(centred * centred, axis=-1, keepdims=True) + EPSILON)
    normed = centred * reciprocal
    return (normed * gain + shift, normed, reciprocal)


def norm_backward(incoming, normed, reciprocal, gain):
    scaled = incoming * gain
    return reciprocal * (
        scaled
        - jnp.mean(scaled, axis=-1, keepdims=True)
        - normed * jnp.mean(scaled * normed, axis=-1, keepdims=True)
    )


def gelu_parts(inner):
    cumulative = 0.5 * (1.0 + lax.erf(inner * ROOT_HALF))
    return (inner * cumulative, cumulative + inner * jnp.exp(-0.5 * inner * inner) * GAUSS_PEAK)


def exchange_kernel(count, x_ref, y_ref, held, send_sem, recv_sem, own_sem):
    me = lax.axis_index("ctx")
    barrier = pltpu.get_barrier_semaphore()

    def greet(step, carry):
        peer = lax.rem(me + step, count)
        pl.semaphore_signal(barrier, inc=1, device_id={"ctx": peer})
        return carry

    lax.fori_loop(1, count, greet, 0)
    own_in = pltpu.make_async_copy(x_ref.at[me], held, own_sem)
    own_in.start()
    pl.semaphore_wait(barrier, count - 1)

    def transfer(step):
        peer = lax.rem(me + step, count)
        return pltpu.make_async_remote_copy(
            src_ref=x_ref.at[peer],
            dst_ref=y_ref.at[me],
            send_sem=send_sem.at[step],
            recv_sem=recv_sem.at[step],
            device_id={"ctx": peer},
        )

    def begin(step, carry):
        transfer(step).start()
        return carry

    lax.fori_loop(1, count, begin, 0)
    own_in.wait()
    own_out = pltpu.make_async_copy(held, y_ref.at[me], own_sem)
    own_out.start()
    own_out.wait()

    def finish(step, carry):
        transfer(step).wait()
        return carry

    lax.fori_loop(1, count, finish, 0)


def exchange(x, number):
    count = x.shape[0]
    return pl.pallas_call(
        functools.partial(exchange_kernel, count),
        out_shape=jax.ShapeDtypeStruct(x.shape, x.dtype),
        in_specs=[pl.BlockSpec(memory_space=pl.ANY)],
        out_specs=pl.BlockSpec(memory_space=pl.ANY),
        scratch_shapes=[
            pltpu.VMEM(x.shape[1:], x.dtype),
            pltpu.SemaphoreType.DMA((count,)),
            pltpu.SemaphoreType.DMA((count,)),
            pltpu.SemaphoreType.DMA,
        ],
        compiler_params=pltpu.CompilerParams(collective_id=number, has_side_effects=True),
        name=f"exchange_{number}",
    )(x)


def across(ref, first, rows, width, lanes):
    parts = [ref[first + i, 0, rows, :] for i in range(width // lanes)]
    return parts[0] if len(parts) == 1 else jnp.concatenate(parts, axis=1)


def key_documents(starts_ref, unit, length, lanes, key_docs):
    position = lax.broadcasted_iota(jnp.int32, (length, lanes), 0)
    docs = jnp.zeros((length, lanes), jnp.int32) - 1
    for j in range(starts_ref.shape[1]):
        docs = docs + jnp.where(position >= starts_ref[unit, j], 1, 0)
    key_docs[...] = docs


def same_document(key_docs, first, width, query_docs):
    keys = key_docs[pl.ds(first, width), :]
    lanes = keys.shape[1]
    parts = [keys == query_docs[:, i : i + lanes] for i in range(0, query_docs.shape[1], lanes)]
    return parts[0] if len(parts) == 1 else jnp.concatenate(parts, axis=1)


def over_chunks(chunks, body, carry):
    if chunks == 1:
        return body(0, carry)
    return lax.fori_loop(0, chunks, body, carry)


def attend_kernel(
    width, starts_ref, x_ref, docs_ref, o_ref, wide_ref, lse_ref, key_rows, value_t, key_docs
):
    count, _, _, lanes = x_ref.shape
    length = count * lanes
    depth = min(length, 1024)
    unit = pl.program_id(0)
    for i in range(count):
        rows = slice(i * lanes, (i + 1) * lanes)
        key_rows[rows, :] = x_ref[i, 0, HD : 2 * HD, :].T
        value_t[:, rows] = x_ref[i, 0, 2 * HD : 3 * HD, :]
    key_documents(starts_ref, unit, length, lanes, key_docs)
    group = width // lanes

    def block(number, carry):
        begin = pl.multiple_of(number * width, width)
        queries = across(x_ref, number * group, slice(0, HD), width, lanes) * SCALE
        query_docs = docs_ref[0, :, pl.ds(begin, width)]

        def chunk(index, running):
            peak, total, mixed = running
            first = pl.multiple_of(index * depth, depth)
            scores = jnp.dot(
                key_rows[pl.ds(first, depth), :], queries, preferred_element_type=F32
            )
            same = same_document(key_docs, first, depth, query_docs)
            scores = jnp.where(same, scores, MASKED)
            new_peak = jnp.maximum(peak, jnp.max(scores, axis=0, keepdims=True))
            scaling = jnp.exp(peak - new_peak)
            weights = jnp.exp(scores - new_peak)
            return (
                new_peak,
                total * scaling + jnp.sum(weights, axis=0, keepdims=True),
                mixed * scaling
                + jnp.dot(
                    value_t[:, pl.ds(first, depth)],
                    weights.astype(BF16),
                    preferred_element_type=F32,
                ),
            )

        peak, total, mixed = over_chunks(
            length // depth,
            chunk,
            (
                jnp.full((1, width), -jnp.inf, F32),
                jnp.zeros((1, width), F32),
                jnp.zeros((HD, width), F32),
            ),
        )
        mixed = mixed / total
        wide_ref[0, :, pl.ds(begin, width)] = mixed
        lse_ref[0, :, pl.ds(begin, width)] = peak + jnp.log(total)
        low = mixed.astype(BF16)
        for i in range(group):
            o_ref[number * group + i, 0] = low[:, i * lanes : (i + 1) * lanes]
        return carry

    lax.fori_loop(0, length // width, block, 0)


def attend_back_kernel(
    width,
    starts_ref,
    x_ref,
    flow_ref,
    docs_ref,
    wide_ref,
    lse_ref,
    d_ref,
    key_rows,
    value_rows,
    key_t,
    key_docs,
    d_key,
    d_value,
):
    count, _, _, lanes = x_ref.shape
    length = count * lanes
    depth = min(length, 1024)
    unit = pl.program_id(0)
    for i in range(count):
        rows = slice(i * lanes, (i + 1) * lanes)
        key_rows[rows, :] = x_ref[i, 0, HD : 2 * HD, :].T
        value_rows[rows, :] = x_ref[i, 0, 2 * HD : 3 * HD, :].T
        key_t[:, rows] = x_ref[i, 0, HD : 2 * HD, :]
    key_documents(starts_ref, unit, length, lanes, key_docs)
    d_key[...] = jnp.zeros_like(d_key)
    d_value[...] = jnp.zeros_like(d_value)
    group = width // lanes

    def block(number, carry):
        begin = pl.multiple_of(number * width, width)
        queries = across(x_ref, number * group, slice(0, HD), width, lanes) * SCALE
        flow = across(flow_ref, number * group, slice(0, HD), width, lanes)
        query_rows = queries.T
        flow_rows = flow.T
        query_docs = docs_ref[0, :, pl.ds(begin, width)]
        log_total = lse_ref[0, :, pl.ds(begin, width)]
        spread = jnp.sum(
            flow.astype(F32) * wide_ref[0, :, pl.ds(begin, width)], axis=0, keepdims=True
        )

        def chunk(index, d_query):
            first = pl.multiple_of(index * depth, depth)
            rows = pl.ds(first, depth)
            scores = jnp.dot(key_rows[rows, :], queries, preferred_element_type=F32)
            same = same_document(key_docs, first, depth, query_docs)
            probs = jnp.exp(jnp.where(same, scores, MASKED) - log_total)
            pressure = jnp.dot(value_rows[rows, :], flow, preferred_element_type=F32)
            d_scores = (probs * (pressure - spread)).astype(BF16)
            d_value[rows, :] += jnp.dot(
                probs.astype(BF16), flow_rows, preferred_element_type=F32
            )
            d_key[rows, :] += jnp.dot(d_scores, query_rows, preferred_element_type=F32)
            return d_query + jnp.dot(key_t[:, rows], d_scores, preferred_element_type=F32)

        d_query = over_chunks(length // depth, chunk, jnp.zeros((HD, width), F32))
        low = (d_query * SCALE).astype(BF16)
        for i in range(group):
            d_ref[number * group + i, 0, 0:HD, :] = low[:, i * lanes : (i + 1) * lanes]
        return carry

    lax.fori_loop(0, length // width, block, 0)
    for i in range(count):
        rows = slice(i * lanes, (i + 1) * lanes)
        d_ref[i, 0, HD : 2 * HD, :] = d_key[rows, :].T.astype(BF16)
        d_ref[i, 0, 2 * HD : 3 * HD, :] = d_value[rows, :].T.astype(BF16)


def unit_block(*dims):
    return pl.BlockSpec(dims, lambda u, starts: (0, u) + (0,) * (len(dims) - 2))


def own_block(*dims):
    return pl.BlockSpec(dims, lambda u, starts: (u,) + (0,) * (len(dims) - 1))


def attend(x, starts, docs):
    count, units, _, lanes = x.shape
    length = count * lanes
    width = 2 * lanes if count % 2 == 0 else lanes
    return pl.pallas_call(
        functools.partial(attend_kernel, width),
        out_shape=(
            jax.ShapeDtypeStruct((count, units, HD, lanes), BF16),
            jax.ShapeDtypeStruct((units, HD, length), F32),
            jax.ShapeDtypeStruct((units, 1, length), F32),
        ),
        grid_spec=pltpu.PrefetchScalarGridSpec(
            num_scalar_prefetch=1,
            grid=(units,),
            in_specs=[unit_block(count, 1, 3 * HD, lanes), own_block(1, 1, length)],
            out_specs=[
                unit_block(count, 1, HD, lanes),
                own_block(1, HD, length),
                own_block(1, 1, length),
            ],
            scratch_shapes=[
                pltpu.VMEM((length, HD), BF16),
                pltpu.VMEM((HD, length), BF16),
                pltpu.VMEM((length, lanes), jnp.int32),
            ],
        ),
        compiler_params=pltpu.CompilerParams(dimension_semantics=("arbitrary",)),
        name="attend",
    )(starts, x, docs)


def attend_back(x, flow, starts, docs, wide, lse):
    count, units, _, lanes = x.shape
    length = count * lanes
    width = 2 * lanes if count % 2 == 0 else lanes
    return pl.pallas_call(
        functools.partial(attend_back_kernel, width),
        out_shape=jax.ShapeDtypeStruct(x.shape, BF16),
        grid_spec=pltpu.PrefetchScalarGridSpec(
            num_scalar_prefetch=1,
            grid=(units,),
            in_specs=[
                unit_block(count, 1, 3 * HD, lanes),
                unit_block(count, 1, HD, lanes),
                own_block(1, 1, length),
                own_block(1, HD, length),
                own_block(1, 1, length),
            ],
            out_specs=unit_block(count, 1, 3 * HD, lanes),
            scratch_shapes=[
                pltpu.VMEM((length, HD), BF16),
                pltpu.VMEM((length, HD), BF16),
                pltpu.VMEM((HD, length), BF16),
                pltpu.VMEM((length, lanes), jnp.int32),
                pltpu.VMEM((length, HD), F32),
                pltpu.VMEM((length, HD), F32),
            ],
        ),
        compiler_params=pltpu.CompilerParams(dimension_semantics=("arbitrary",)),
        name="attend_back",
    )(starts, x, flow, docs, wide, lse)


def to_units(columns, parts, count, units):
    rows = columns.shape[1] // MB
    x = columns.reshape(parts, H, HD, MB, rows).transpose(3, 1, 0, 2, 4)
    x = x.reshape(MB * H, parts * HD, rows)
    x = jnp.pad(x, ((0, units * count - MB * H), (0, 0), (0, 0)))
    return x.reshape(units, count, parts * HD, rows).transpose(1, 0, 2, 3)


def from_units(x, parts):
    count, units, _, rows = x.shape
    x = x.transpose(1, 0, 2, 3).reshape(units * count, parts * HD, rows)[: MB * H]
    x = x.reshape(MB, H, parts, HD, rows).transpose(2, 1, 3, 0, 4)
    return x.reshape(parts * D, MB * rows)


def mul_nn(a, b):
    return jnp.dot(a, b, preferred_element_type=F32)


def mul_tn(a, b):
    return lax.dot_general(a, b, (((0,), (0,)), ((), ())), preferred_element_type=F32)


def mul_nt(a, b):
    return lax.dot_general(a, b, (((1,), (1,)), ((), ())), preferred_element_type=F32)


def mul_tt(a, b):
    return lax.dot_general(a, b, (((0,), (1,)), ((), ())), preferred_element_type=F32)


def first_rows(half, tile):
    return half if half <= tile else (half // tile + 1) // 2 * tile


def reduce_kernel(count, heads, *refs):
    jobs = len(heads)
    grads, outs, scratch = refs[:jobs], refs[jobs : 2 * jobs], refs[2 * jobs :]
    sets = [scratch[7 * j : 7 * j + 7] for j in range(jobs)]
    load_sem, send_sem, recv_sem, z_send, z_recv = scratch[7 * jobs :]
    me, shard = lax.axis_index("ctx"), lax.axis_index("fsdp")
    depth = count // 2
    y, core = shard // 2, lax.rem(shard, 2)
    z, x = me // 2, lax.rem(me, 2)
    other_core = {"fsdp": 2 * y + 1 - core}
    other_y = {"fsdp": 2 * (1 - y) + core}
    other_x = {"ctx": 2 * z + 1 - x}

    def along_z(step):
        return lax.rem(z + step, depth)

    barrier = pltpu.get_barrier_semaphore()
    for peer in (other_core, other_y, other_x):
        pl.semaphore_signal(barrier, inc=1, device_id=peer)
    for step in range(1, depth):
        pl.semaphore_signal(barrier, inc=1, device_id={"ctx": 2 * along_z(step) + x})

    def remote(src, dst, j, slot, peer):
        return pltpu.make_async_remote_copy(
            src_ref=src,
            dst_ref=dst,
            send_sem=send_sem.at[j, slot],
            recv_sem=recv_sem.at[j, slot],
            device_id=peer,
        )

    def plan(j):
        own, got, y_one, x_one, x_two, y_two, z_got = sets[j]
        half, lanes = own.shape[3], own.shape[4]
        head = heads[j]
        tail = head < half
        loads, firsts = [], []
        for side in range(2):
            columns = pl.ds(side * lanes, lanes)
            for low in range(2):
                loads.append(
                    pltpu.make_async_copy(
                        grads[j].at[:, low, core, :, columns],
                        own.at[side, :, low],
                        load_sem.at[j, 2 * side + low],
                    )
                )
            for low in range(2):
                firsts.append(
                    remote(
                        grads[j].at[:, low, 1 - core, :, columns],
                        got.at[side, :, low],
                        j,
                        2 * side + low,
                        other_core,
                    )
                )
        second = [remote(own.at[1 - y, :, :, 0:head, :], y_one, j, 4, other_y)]
        third = [remote(own.at[y, :, 1 - x, 0:head, :], x_two, j, 5, other_x)]
        if tail:
            second.append(remote(own.at[:, :, 1 - x, head:half, :], x_one, j, 6, other_x))
            third.append(remote(own.at[1 - y, :, x, head:half, :], y_two, j, 7, other_y))
        fourth = [
            pltpu.make_async_remote_copy(
                src_ref=own.at[y, along_z(step), x],
                dst_ref=z_got.at[z],
                send_sem=z_send.at[j, step],
                recv_sem=z_recv.at[j, step],
                device_id={"ctx": 2 * along_z(step) + x},
            )
            for step in range(1, depth)
        ]
        last = [remote(outs[j].at[core], outs[j].at[core], j, 8, other_core)]
        return (loads, firsts, second, third, fourth, last)

    plans = [plan(j) for j in range(jobs)]

    def add(a, b):
        return (a.astype(F32) + b.astype(F32)).astype(a.dtype)

    def start(copies):
        for copy in copies:
            copy.start()

    def stage_one(j):
        own, got = sets[j][0], sets[j][1]
        for copy in plans[j][0]:
            copy.wait()
        for copy in plans[j][1]:
            copy.wait_recv()

        def body(block, carry):
            for side in range(2):
                for low in range(2):
                    own[side, block, low] = add(own[side, block, low], got[side, block, low])
            return carry

        lax.fori_loop(0, depth, body, 0)
        start(plans[j][2])

    def stage_two(j):
        own, _, y_one, x_one, _, _, _ = sets[j]
        half, head = own.shape[3], heads[j]
        for copy in plans[j][2]:
            copy.wait()

        def body(block, carry):
            for low in range(2):
                own[y, block, low, 0:head, :] = add(
                    own[y, block, low, 0:head, :], y_one[block, low]
                )
            if head < half:
                for side in range(2):
                    own[side, block, x, head:half, :] = add(
                        own[side, block, x, head:half, :], x_one[side, block]
                    )
            return carry

        lax.fori_loop(0, depth, body, 0)
        start(plans[j][3])

    def stage_three(j):
        own, _, _, _, x_two, y_two, _ = sets[j]
        half, head = own.shape[3], heads[j]
        for copy in plans[j][3]:
            copy.wait()

        def body(block, carry):
            own[y, block, x, 0:head, :] = add(own[y, block, x, 0:head, :], x_two[block])
            if head < half:
                own[y, block, x, head:half, :] = add(
                    own[y, block, x, head:half, :], y_two[block]
                )
            return carry

        lax.fori_loop(0, depth, body, 0)
        start(plans[j][4])

    def stage_four(j):
        own, z_got = sets[j][0], sets[j][6]
        for copy in plans[j][4]:
            copy.wait()
        total = own[y, z, x].astype(F32)
        for step in range(1, depth):
            total = total + z_got[along_z(step)].astype(F32)
        outs[j][core] = total.astype(outs[j].dtype)
        start(plans[j][5])

    def stage_five(j):
        for copy in plans[j][5]:
            copy.wait()
        for copy in plans[j][1]:
            copy.wait_send()

    for j in range(jobs):
        start(plans[j][0])
    pl.semaphore_wait(barrier, 2 + depth)
    for j in range(jobs):
        start(plans[j][1])
    stages = (stage_one, stage_two, stage_three, stage_four, stage_five)
    for tick in range(jobs + len(stages) - 1):
        for k in reversed(range(len(stages))):
            if 0 <= tick - k < jobs:
                stages[k](tick - k)


def reduce_all(grads, number):
    count = grads[0].shape[0]
    depth = count // 2
    heads, scratch, outs = [], [], []
    for g in grads:
        half, lanes = g.shape[2], g.shape[3] // 2
        head = first_rows(half, 16 if g.dtype == BF16 else 8)
        tail = max(half - head, 16 if g.dtype == BF16 else 8)
        heads.append(head)
        for shape in (
            (2, depth, 2, half, lanes),
            (2, depth, 2, half, lanes),
            (depth, 2, head, lanes),
            (2, depth, tail, lanes),
            (depth, head, lanes),
            (depth, tail, lanes),
            (depth, half, lanes),
        ):
            scratch.append(pltpu.VMEM(shape, g.dtype))
        outs.append(jax.ShapeDtypeStruct((2, half, lanes), g.dtype))
    jobs = len(grads)
    scratch += [
        pltpu.SemaphoreType.DMA((jobs, 4)),
        pltpu.SemaphoreType.DMA((jobs, 9)),
        pltpu.SemaphoreType.DMA((jobs, 9)),
        pltpu.SemaphoreType.DMA((jobs, depth)),
        pltpu.SemaphoreType.DMA((jobs, depth)),
    ]
    return pl.pallas_call(
        functools.partial(reduce_kernel, count, tuple(heads)),
        out_shape=tuple(outs),
        in_specs=[pl.BlockSpec(memory_space=pl.ANY)] * jobs,
        out_specs=[pl.BlockSpec(memory_space=pltpu.VMEM)] * jobs,
        scratch_shapes=scratch,
        compiler_params=pltpu.CompilerParams(
            collective_id=number, has_side_effects=True, vmem_limit_bytes=56 * 1024 * 1024
        ),
        name="reduce_all",
    )(*[g.reshape(depth, 2, *g.shape[1:]) for g in grads])


def on_device(
    count,
    shards,
    tokens,
    doc_starts,
    joint_weight,
    mixer_weight,
    inner_weight,
    outer_weight,
    query_bias,
    value_bias,
    mixer_bias,
    first_gain,
    first_shift,
    inner_bias,
    outer_bias,
    second_gain,
    second_shift,
    upstream,
):
    rows = tokens.shape[2]
    length = rows * count
    units = -(-MB * H // count)
    me = lax.axis_index("ctx")

    joint = lax.all_gather(joint_weight, "fsdp", axis=0, tiled=True)
    vectors = jnp.concatenate(
        [
            query_bias,
            value_bias,
            mixer_bias,
            first_gain,
            first_shift,
            outer_bias,
            second_gain,
            second_shift,
            inner_bias,
        ]
    )
    vectors = lax.all_gather(vectors, "fsdp", axis=0)
    part = D // shards
    names = [vectors[:, i * part : (i + 1) * part].reshape(D).astype(F32) for i in range(8)]
    qbias, vbias, mbias, gain_one, shift_one, obias, gain_two, shift_two = names
    ibias = vectors[:, 8 * part :].reshape(FF).astype(F32)
    mixer = lax.all_gather(mixer_weight, "fsdp", axis=0, tiled=True)
    inner = lax.all_gather(inner_weight, "fsdp", axis=0, tiled=True)
    outer = lax.all_gather(outer_weight, "fsdp", axis=0, tiled=True)

    source = tokens.reshape(MB * rows, D)
    unit_ids = jnp.arange(units, dtype=jnp.int32) * count + me
    unit_starts = doc_starts[:, 0][jnp.minimum(unit_ids // H, MB - 1)]
    positions = jnp.arange(length, dtype=jnp.int32)
    unit_docs = jax.vmap(lambda s: doc_index(positions, s))(unit_starts)[:, None, :]

    joint_bias = jnp.concatenate([qbias, jnp.zeros((D,), F32), vbias])
    projected = (mul_tt(joint, source) + joint_bias[:, None]).astype(BF16)
    received = exchange(to_units(projected, 3, count, units), 0)
    mixed, wide, lse = attend(received, unit_starts, unit_docs)
    attended = from_units(exchange(mixed, 1), 1)

    branch = mul_tn(attended, mixer) + mbias
    first, first_normed, first_recip = norm_forward(
        source.astype(F32) + branch, gain_one, shift_one
    )
    first_low = first.astype(BF16)
    inner_pre = mul_nn(first_low, inner) + ibias
    activated, gelu_slope = gelu_parts(inner_pre)
    activated_low = activated.astype(BF16)
    outer_out = mul_nn(activated_low, outer) + obias
    final, second_normed, second_recip = norm_forward(first + outer_out, gain_two, shift_two)
    result = final.astype(BF16).reshape(MB, 1, rows, D)

    incoming = upstream.reshape(MB * rows, D).astype(F32)
    rescale_grad = jnp.sum(incoming * second_normed, axis=0)
    reshift_grad = jnp.sum(incoming, axis=0)
    d_second = norm_backward(incoming, second_normed, second_recip, gain_two)
    d_outer = d_second.astype(BF16)
    return_grad = jnp.sum(d_outer.astype(F32), axis=0)
    outer_grad = mul_tn(d_outer, activated_low)
    d_inner = (mul_nt(d_outer, outer) * gelu_slope).astype(BF16)
    hidden_grad = jnp.sum(d_inner.astype(F32), axis=0)
    inner_grad = mul_tn(d_inner, first_low)
    d_first = d_second + mul_nt(d_inner, inner)
    scale_grad = jnp.sum(d_first * first_normed, axis=0)
    shift_grad = jnp.sum(d_first, axis=0)
    d_residual = norm_backward(d_first, first_normed, first_recip, gain_one)
    d_branch = d_residual.astype(BF16)
    mixing_grad = jnp.sum(d_branch.astype(F32), axis=0)
    mixer_grad = mul_tt(d_branch, attended)
    flow = mul_nt(mixer, d_branch).astype(BF16)
    flow_units = exchange(to_units(flow, 1, count, units), 2)
    d_units = attend_back(received, flow_units, unit_starts, unit_docs, wide, lse)
    d_joint = from_units(exchange(d_units, 3), 3)
    bias_sums = jnp.sum(d_joint.astype(F32), axis=1)
    query_grad = bias_sums[0:D]
    values_grad = bias_sums[2 * D :]
    joint_grad = mul_nn(d_joint, source)
    tokens_grad = d_residual + mul_tt(d_joint, joint)
    tokens_grad = tokens_grad.reshape(MB, 1, rows, D)

    small = [
        query_grad,
        values_grad,
        mixing_grad,
        scale_grad,
        shift_grad,
        hidden_grad,
        return_grad,
        rescale_grad,
        reshift_grad,
    ]
    world = count * shards
    packed = jnp.concatenate([v.reshape(world, -1) for v in small], axis=1)
    turned = [outer_grad, inner_grad, mixer_grad, joint_grad]
    if shards == 4 and count % 2 == 0 and D % (32 * count) == 0:
        core = lax.rem(lax.axis_index("fsdp"), 2)
        bias_job = packed.reshape(count, 2, 2, -1).transpose(0, 2, 1, 3)
        spare = -packed.shape[1] % 128
        bias_job = jnp.pad(bias_job, ((0, 0), (0, 0), (0, 0), (0, spare)))
        bias_job = jnp.pad(bias_job.reshape(count, 2, 1, -1), ((0, 0), (0, 0), (0, 7), (0, 0)))
        jobs = [g.astype(BF16).reshape(count, 2, -1, g.shape[1]) for g in turned] + [bias_job]
        *sums, own = reduce_all(jobs, 4)
        blocks = []
        for g in sums:
            width = g.shape[2] // 2
            g = g.reshape(-1, 2 * width)
            blocks.append(lax.dynamic_slice_in_dim(g, core * width, width, 1).T.astype(F32))
        own = lax.dynamic_index_in_dim(own, core, 0, False)[0, : packed.shape[1]]
    else:

        def reduced(grad):
            over_lanes = lax.psum_scatter(
                grad.astype(BF16), "fsdp", scatter_dimension=1, tiled=True
            )
            over_rows = lax.psum_scatter(over_lanes, "ctx", scatter_dimension=0, tiled=True)
            return over_rows.T.astype(F32)

        blocks = [reduced(g) for g in turned]
        packed = lax.psum(packed, ("ctx", "fsdp"))
        index = me * shards + lax.axis_index("fsdp")
        own = lax.dynamic_slice_in_dim(packed, index, 1, 0)[0]
    outer_out_grad, inner_out, mixer_out, joint_out = blocks
    sums = []
    begin = 0
    for v in small:
        size = v.shape[0] // world
        sums.append(own[begin : begin + size])
        begin += size
    return (result, tokens_grad, joint_out, mixer_out, inner_out, outer_out_grad, *sums)


def solution(mesh):
    in_specs = (
        P(None, "fsdp", "ctx", None),
        P(None, "fsdp", None),
        P("fsdp", None),
        P("fsdp", None),
        P("fsdp", None),
        P("fsdp", None),
        P("fsdp"),
        P("fsdp"),
        P("fsdp"),
        P("fsdp"),
        P("fsdp"),
        P("fsdp"),
        P("fsdp"),
        P("fsdp"),
        P("fsdp"),
        P(None, "fsdp", "ctx", None),
    )
    out_specs = (
        P(None, "fsdp", "ctx", None),
        P(None, "fsdp", "ctx", None),
        P("fsdp", "ctx"),
        P("fsdp", "ctx"),
        P("fsdp", "ctx"),
        P("fsdp", "ctx"),
        P(("ctx", "fsdp")),
        P(("ctx", "fsdp")),
        P(("ctx", "fsdp")),
        P(("ctx", "fsdp")),
        P(("ctx", "fsdp")),
        P(("ctx", "fsdp")),
        P(("ctx", "fsdp")),
        P(("ctx", "fsdp")),
        P(("ctx", "fsdp")),
    )
    return jax.shard_map(
        functools.partial(on_device, mesh.shape["ctx"], mesh.shape["fsdp"]),
        mesh=mesh,
        in_specs=in_specs,
        out_specs=out_specs,
        check_vma=False,
    )
```

```python
import functools
import math

import jax
import jax.numpy as jnp
from jax import lax
from jax.experimental import pallas as pl
from jax.experimental.pallas import tpu as pltpu
from jax.sharding import PartitionSpec as P

D = 768
H = 12
HD = 64
FF = 3072
MB = 3

SCALE = 0.125
EPSILON = 1e-12
MASKED = -1000000000.0
ROOT_HALF = 0.7071067811865476
GAUSS_PEAK = 0.3989422804014327

F32 = jnp.float32
BF16 = jnp.bfloat16


def doc_index(positions, starts_row):
    return jnp.sum((starts_row[None, :] <= positions[:, None]).astype(jnp.int32), axis=1) - 1


def norm_forward(hidden, gain, shift):
    average = jnp.mean(hidden, axis=-1, keepdims=True)
    centred = hidden - average
    reciprocal = lax.rsqrt(jnp.mean(centred * centred, axis=-1, keepdims=True) + EPSILON)
    normed = centred * reciprocal
    return (normed * gain + shift, normed, reciprocal)


def norm_backward(incoming, normed, reciprocal, gain):
    scaled = incoming * gain
    return reciprocal * (
        scaled
        - jnp.mean(scaled, axis=-1, keepdims=True)
        - normed * jnp.mean(scaled * normed, axis=-1, keepdims=True)
    )


def gelu_parts(inner):
    cumulative = 0.5 * (1.0 + lax.erf(inner * ROOT_HALF))
    return (inner * cumulative, cumulative + inner * jnp.exp(-0.5 * inner * inner) * GAUSS_PEAK)


def exchange_kernel(count, x_ref, y_ref, held, send_sem, recv_sem, own_sem):
    me = lax.axis_index("ctx")
    barrier = pltpu.get_barrier_semaphore()

    def greet(step, carry):
        peer = lax.rem(me + step, count)
        pl.semaphore_signal(barrier, inc=1, device_id={"ctx": peer})
        return carry

    lax.fori_loop(1, count, greet, 0)
    own_in = pltpu.make_async_copy(x_ref.at[me], held, own_sem)
    own_in.start()
    pl.semaphore_wait(barrier, count - 1)

    def transfer(step):
        peer = lax.rem(me + step, count)
        return pltpu.make_async_remote_copy(
            src_ref=x_ref.at[peer],
            dst_ref=y_ref.at[me],
            send_sem=send_sem.at[step],
            recv_sem=recv_sem.at[step],
            device_id={"ctx": peer},
        )

    def begin(step, carry):
        transfer(step).start()
        return carry

    lax.fori_loop(1, count, begin, 0)
    own_in.wait()
    own_out = pltpu.make_async_copy(held, y_ref.at[me], own_sem)
    own_out.start()
    own_out.wait()

    def finish(step, carry):
        transfer(step).wait()
        return carry

    lax.fori_loop(1, count, finish, 0)


def exchange(x, number):
    count = x.shape[0]
    return pl.pallas_call(
        functools.partial(exchange_kernel, count),
        out_shape=jax.ShapeDtypeStruct(x.shape, x.dtype),
        in_specs=[pl.BlockSpec(memory_space=pl.ANY)],
        out_specs=pl.BlockSpec(memory_space=pl.ANY),
        scratch_shapes=[
            pltpu.VMEM(x.shape[1:], x.dtype),
            pltpu.SemaphoreType.DMA((count,)),
            pltpu.SemaphoreType.DMA((count,)),
            pltpu.SemaphoreType.DMA,
        ],
        compiler_params=pltpu.CompilerParams(collective_id=number, has_side_effects=True),
        name=f"exchange_{number}",
    )(x)


def across(ref, first, rows, width, lanes):
    parts = [ref[first + i, 0, rows, :] for i in range(width // lanes)]
    return parts[0] if len(parts) == 1 else jnp.concatenate(parts, axis=1)


def key_documents(starts_ref, unit, length, lanes, key_docs):
    position = lax.broadcasted_iota(jnp.int32, (length, lanes), 0)
    docs = jnp.zeros((length, lanes), jnp.int32) - 1
    for j in range(starts_ref.shape[1]):
        docs = docs + jnp.where(position >= starts_ref[unit, j], 1, 0)
    key_docs[...] = docs


def same_document(key_docs, first, width, query_docs):
    keys = key_docs[pl.ds(first, width), :]
    lanes = keys.shape[1]
    parts = [keys == query_docs[:, i : i + lanes] for i in range(0, query_docs.shape[1], lanes)]
    return parts[0] if len(parts) == 1 else jnp.concatenate(parts, axis=1)


def over_chunks(chunks, body, carry):
    if chunks == 1:
        return body(0, carry)
    return lax.fori_loop(0, chunks, body, carry)


def attend_back_kernel(
    width,
    starts_ref,
    x_ref,
    flow_ref,
    docs_ref,
    wide_ref,
    lse_ref,
    d_ref,
    key_rows,
    value_rows,
    key_t,
    key_docs,
    d_key,
    d_value,
):
    count, _, _, lanes = x_ref.shape
    length = count * lanes
    depth = min(length, 1024)
    unit = pl.program_id(0)
    for i in range(count):
        rows = slice(i * lanes, (i + 1) * lanes)
        key_rows[rows, :] = x_ref[i, 0, HD : 2 * HD, :].T
        value_rows[rows, :] = x_ref[i, 0, 2 * HD : 3 * HD, :].T
        key_t[:, rows] = x_ref[i, 0, HD : 2 * HD, :]
    key_documents(starts_ref, unit, length, lanes, key_docs)
    d_key[...] = jnp.zeros_like(d_key)
    d_value[...] = jnp.zeros_like(d_value)
    group = width // lanes

    def block(number, carry):
        begin = pl.multiple_of(number * width, width)
        queries = across(x_ref, number * group, slice(0, HD), width, lanes)
        flow = across(flow_ref, number * group, slice(0, HD), width, lanes)
        query_rows = queries.T
        flow_rows = flow.T
        query_docs = docs_ref[0, :, pl.ds(begin, width)]
        log_total = lse_ref[0, :, pl.ds(begin, width)]
        spread = jnp.sum(
            flow.astype(F32) * wide_ref[0, :, pl.ds(begin, width)], axis=0, keepdims=True
        )

        def chunk(index, d_query):
            first = pl.multiple_of(index * depth, depth)
            rows = pl.ds(first, depth)
            scores = jnp.dot(key_rows[rows, :], queries, preferred_element_type=F32)
            same = same_document(key_docs, first, depth, query_docs)
            probs = jnp.exp(jnp.where(same, scores, MASKED) - log_total)
            pressure = jnp.dot(value_rows[rows, :], flow, preferred_element_type=F32)
            d_scores = (probs * (pressure - spread)).astype(BF16)
            d_value[rows, :] += jnp.dot(
                probs.astype(BF16), flow_rows, preferred_element_type=F32
            )
            d_key[rows, :] += jnp.dot(d_scores, query_rows, preferred_element_type=F32)
            return d_query + jnp.dot(key_t[:, rows], d_scores, preferred_element_type=F32)

        d_query = over_chunks(length // depth, chunk, jnp.zeros((HD, width), F32))
        low = (d_query * SCALE).astype(BF16)
        for i in range(group):
            d_ref[number * group + i, 0, 0:HD, :] = low[:, i * lanes : (i + 1) * lanes]
        return carry

    lax.fori_loop(0, length // width, block, 0)
    for i in range(count):
        rows = slice(i * lanes, (i + 1) * lanes)
        d_ref[i, 0, HD : 2 * HD, :] = d_key[rows, :].T.astype(BF16)
        d_ref[i, 0, 2 * HD : 3 * HD, :] = d_value[rows, :].T.astype(BF16)


def unit_block(*dims):
    return pl.BlockSpec(dims, lambda u, starts: (0, u) + (0,) * (len(dims) - 2))


def own_block(*dims):
    return pl.BlockSpec(dims, lambda u, starts: (u,) + (0,) * (len(dims) - 1))


def attend_back(x, flow, starts, docs, wide, lse):
    count, units, _, lanes = x.shape
    length = count * lanes
    width = 2 * lanes if count % 2 == 0 else lanes
    return pl.pallas_call(
        functools.partial(attend_back_kernel, width),
        out_shape=jax.ShapeDtypeStruct(x.shape, BF16),
        grid_spec=pltpu.PrefetchScalarGridSpec(
            num_scalar_prefetch=1,
            grid=(units,),
            in_specs=[
                unit_block(count, 1, 3 * HD, lanes),
                unit_block(count, 1, HD, lanes),
                own_block(1, 1, length),
                own_block(1, HD, length),
                own_block(1, 1, length),
            ],
            out_specs=unit_block(count, 1, 3 * HD, lanes),
            scratch_shapes=[
                pltpu.VMEM((length, HD), BF16),
                pltpu.VMEM((length, HD), BF16),
                pltpu.VMEM((HD, length), BF16),
                pltpu.VMEM((length, lanes), jnp.int32),
                pltpu.VMEM((length, HD), F32),
                pltpu.VMEM((length, HD), F32),
            ],
        ),
        compiler_params=pltpu.CompilerParams(dimension_semantics=("arbitrary",)),
        name="attend_back",
    )(starts, x, flow, docs, wide, lse)


def to_units(columns, parts, count, units):
    rows = columns.shape[1] // MB
    x = columns.reshape(parts, H, HD, MB, rows).transpose(1, 3, 0, 2, 4)
    x = x.reshape(MB * H, parts * HD, rows)
    x = jnp.pad(x, ((0, units * count - MB * H), (0, 0), (0, 0)))
    return x.reshape(units, count, parts * HD, rows).transpose(1, 0, 2, 3)


def from_units(x, parts):
    count, units, _, rows = x.shape
    x = x.transpose(1, 0, 2, 3).reshape(units * count, parts * HD, rows)[: MB * H]
    x = x.reshape(H, MB, parts, HD, rows).transpose(2, 0, 3, 1, 4)
    return x.reshape(parts * D, MB * rows)


def mul_nn(a, b):
    return jnp.dot(a, b, preferred_element_type=F32)


def mul_tn(a, b):
    return lax.dot_general(a, b, (((0,), (0,)), ((), ())), preferred_element_type=F32)


def mul_nt(a, b):
    return lax.dot_general(a, b, (((1,), (1,)), ((), ())), preferred_element_type=F32)


def mul_tt(a, b):
    return lax.dot_general(a, b, (((0,), (1,)), ((), ())), preferred_element_type=F32)


def forward_kernel(
    width,
    starts_ref,
    tok_ref,
    docs_ref,
    joint_ref,
    vec_ref,
    mixer_ref,
    inner_ref,
    outer_ref,
    att_ref,
    got_ref,
    wide_ref,
    lse_ref,
    joint_out,
    vec_out,
    mixer_out,
    inner_out,
    outer_out,
    joint_all,
    bias_rows,
    put,
    back_put,
    back_got,
    key_rows,
    value_t,
    key_docs,
    mixer_own,
    inner_own,
    outer_own,
    put_sem,
    got_sem,
    back_put_sem,
    back_got_sem,
    joint_sems,
    weight_sems,
    own_sems,
):
    count, units, _, lanes = got_ref.shape
    length = count * lanes
    depth = min(length, 1024)
    group = width // lanes
    pairs = H // 2
    total_units = MB * H
    part = joint_ref.shape[0]
    me, shard = lax.axis_index("ctx"), lax.axis_index("fsdp")
    y, core = shard // 2, lax.rem(shard, 2)
    x = lax.rem(me, 2)
    far = 2 * (1 - y) + core
    other_core = {"fsdp": 2 * y + 1 - core}
    other_y = {"fsdp": far}
    other_x = {"ctx": me + 1 - 2 * x}
    mine = (total_units - me + count - 1) // count

    barrier = pltpu.get_barrier_semaphore()

    def greet(step, carry):
        pl.semaphore_signal(barrier, inc=1, device_id={"ctx": lax.rem(me + step, count)})
        return carry

    lax.fori_loop(1, count, greet, 0)
    pl.semaphore_signal(barrier, inc=1, device_id=other_core)
    pl.semaphore_signal(barrier, inc=1, device_id=other_y)

    def remote(src, dst, sems, index, peer):
        return pltpu.make_async_remote_copy(
            src_ref=src,
            dst_ref=dst,
            send_sem=sems.at[(0, *index)],
            recv_sem=sems.at[(1, *index)],
            device_id=peer,
        )

    def own_joint(pair, third):
        columns = pl.ds(pl.multiple_of(third * D + pair * 128, 128), 128)
        return pltpu.make_async_copy(
            joint_ref.at[:, columns],
            joint_all.at[pair, shard, :, pl.ds(third * 128, 128)],
            own_sems.at[0, pair, third],
        )

    def joint_copy(kind, pair, third, which, peer, source=None):
        here = joint_all.at[pair, which, :, pl.ds(third * 128, 128)]
        if source is None:
            source = here
        else:
            source = source.at[:, pl.ds(pl.multiple_of(third * D + pair * 128, 128), 128)]
        return remote(source, here, joint_sems, (kind, pair, third), peer)

    def joint_y(pair, third):
        return joint_copy(0, pair, third, shard, other_y, joint_ref)

    def joint_core(pair, third):
        return joint_copy(1, pair, third, shard, other_core, joint_ref)

    def joint_pass(pair, third):
        return joint_copy(2, pair, third, far, other_core)

    def joint_store(pair, third):
        columns = pl.ds(pl.multiple_of(third * D + pair * 128, 128), 128)
        return pltpu.make_async_copy(
            joint_all.at[pair, :, :, pl.ds(third * 128, 128)],
            joint_out.at[:, :, columns],
            own_sems.at[0, pair, third],
        )

    def each_third(pair, make, act):
        for third in range(3):
            getattr(make(pair, third), act)()

    def every_pair(make, act):
        def body(pair, carry):
            each_third(pair, make, act)
            return carry

        lax.fori_loop(0, pairs, body, 0)

    every_pair(own_joint, "start")
    wholes = ((mixer_ref, mixer_own, mixer_out), (inner_ref, inner_own, inner_out), (outer_ref, outer_own, outer_out))
    own_in = [
        pltpu.make_async_copy(ref, held, own_sems.at[1, i, 0])
        for i, (ref, held, _) in enumerate(wholes)
    ]
    own_out = [
        pltpu.make_async_copy(held, out.at[shard], own_sems.at[1, i, 1])
        for i, (_, held, out) in enumerate(wholes)
    ]
    for copy in own_in:
        copy.start()
    vec_own = pltpu.make_async_copy(vec_ref, vec_out.at[shard], own_sems.at[1, 3, 0])
    vec_own.start()
    pl.semaphore_wait(barrier, count + 1)

    vec_y = remote(vec_ref, vec_out.at[shard], weight_sems, (0, 0), other_y)
    vec_core = remote(vec_ref, vec_out.at[shard], weight_sems, (0, 1), other_core)
    vec_pass = remote(vec_out.at[far], vec_out.at[far], weight_sems, (0, 2), other_core)
    mixer_y = remote(mixer_ref, mixer_out.at[shard], weight_sems, (1, 0), other_y)
    mixer_core = remote(mixer_ref, mixer_out.at[shard], weight_sems, (1, 1), other_core)
    mixer_pass = remote(mixer_out.at[far], mixer_out.at[far], weight_sems, (1, 2), other_core)
    halves = []
    for i, (ref, out) in enumerate(((inner_ref, inner_out), (outer_ref, outer_out))):
        size = ref.shape[0] // 2
        rows = pl.ds(pl.multiple_of(x * size, size), size)
        halves.append(
            (
                remote(ref.at[rows, :], out.at[shard, rows, :], weight_sems, (2 + i, 0), other_y),
                remote(ref, out.at[shard], weight_sems, (2 + i, 1), other_core),
                remote(
                    out.at[far, rows, :], out.at[far, rows, :], weight_sems, (2 + i, 3), other_x
                ),
                remote(out.at[far], out.at[far], weight_sems, (2 + i, 2), other_core),
            )
        )
    vec_y.start()
    vec_core.start()
    every_pair(joint_y, "start")
    every_pair(joint_core, "start")
    mixer_y.start()
    mixer_core.start()
    for copies in halves:
        copies[0].start()
        copies[1].start()
    for first, second in zip(own_in, own_out):
        first.wait()
        second.start()

    vec_own.wait()
    vec_y.wait_recv()
    vec_pass.start()
    vec_core.wait_recv()
    vec_pass.wait_recv()

    def bias_of(slot):
        pieces = [
            vec_out[f, slot : slot + 1, 0:part].astype(F32) for f in range(4)
        ]
        return jnp.concatenate(pieces, axis=1)

    query_bias, value_bias = bias_of(0), bias_of(1)
    for pair in range(pairs):
        columns = slice(pair * 128, (pair + 1) * 128)
        bias_rows[pair, :, 0:128] = jnp.broadcast_to(query_bias[:, columns], (8, 128))
        bias_rows[pair, :, 128:256] = jnp.zeros((8, 128), F32)
        bias_rows[pair, :, 256:384] = jnp.broadcast_to(value_bias[:, columns], (8, 128))

    def sent_sem(unit):
        return lax.rem(unit, count), unit // count

    def send_copy(unit):
        owner, slot = sent_sem(unit)
        return pltpu.make_async_remote_copy(
            src_ref=put.at[owner, slot],
            dst_ref=got_ref.at[me, slot],
            send_sem=put_sem.at[owner, slot],
            recv_sem=got_sem.at[me, slot],
            device_id={"ctx": owner},
        )

    def keep_copy(unit):
        owner, slot = sent_sem(unit)
        return pltpu.make_async_copy(
            put.at[owner, slot], got_ref.at[me, slot], own_sems.at[2, slot, 0]
        )

    def project(pair, carry):
        each_third(pair, own_joint, "wait")
        each_third(pair, joint_y, "wait_recv")
        each_third(pair, joint_pass, "start")
        each_third(pair, joint_core, "wait_recv")
        each_third(pair, joint_pass, "wait_recv")
        each_third(pair, joint_store, "start")
        weight = joint_all[pair].reshape(4 * part, 384)
        rows = jnp.dot(tok_ref[...], weight, preferred_element_type=F32)
        rows = (rows + bias_rows[pair, 0:1, :]).astype(BF16)
        for third in range(3):
            for batch in range(MB):
                block = rows[batch * lanes : (batch + 1) * lanes, third * 128 : (third + 1) * 128]
                turned = block.T
                if third == 0:
                    turned = turned * SCALE
                for j in range(2):
                    unit = (2 * pair + j) * MB + batch
                    put[lax.rem(unit, count), unit // count, third * HD : (third + 1) * HD, :] = (
                        turned[j * HD : (j + 1) * HD]
                    )
        for i in range(2 * MB):
            unit = 2 * pair * MB + i

            @pl.when(lax.rem(unit, count) != me)
            def _():
                send_copy(unit).start()

            @pl.when(lax.rem(unit, count) == me)
            def _():
                keep_copy(unit).start()

        return carry

    lax.fori_loop(0, pairs, project, 0)

    mixer_y.wait_recv()
    mixer_pass.start()

    def arrival(sender, slot):
        return pltpu.make_async_remote_copy(
            src_ref=put.at[sender, slot],
            dst_ref=got_ref.at[sender, slot],
            send_sem=put_sem.at[sender, slot],
            recv_sem=got_sem.at[sender, slot],
            device_id={"ctx": sender},
        )

    def back_copy(peer, slot):
        return pltpu.make_async_remote_copy(
            src_ref=back_put.at[peer, slot],
            dst_ref=back_got.at[me, slot],
            send_sem=back_put_sem.at[peer, slot],
            recv_sem=back_got_sem.at[me, slot],
            device_id={"ctx": peer},
        )

    def back_keep(slot):
        return pltpu.make_async_copy(
            back_put.at[me, slot], back_got.at[me, slot], own_sems.at[2, slot, 1]
        )

    def relay(i):
        halves[i][0].wait_recv()
        halves[i][2].start()

    def hand_on(i):
        halves[i][2].wait_recv()
        halves[i][3].start()

    early = total_units // count > 2

    def unit_step(slot, carry):
        def wait_one(step, inner):
            arrival(lax.rem(me + step, count), slot).wait_recv()
            return inner

        lax.fori_loop(1, count, wait_one, 0)
        keep_copy(slot * count + me).wait()
        for i in range(count):
            rows = slice(i * lanes, (i + 1) * lanes)
            key_rows[rows, :] = got_ref[i, slot, HD : 2 * HD, :].T
            value_t[:, rows] = got_ref[i, slot, 2 * HD : 3 * HD, :]
        key_documents(starts_ref, slot, length, lanes, key_docs)

        def block(number, inner):
            begin = pl.multiple_of(number * width, width)
            parts = [got_ref[number * group + i, slot, 0:HD, :] for i in range(group)]
            queries = parts[0] if group == 1 else jnp.concatenate(parts, axis=1)
            query_docs = docs_ref[slot, :, pl.ds(begin, width)]

            def chunk(index, running):
                peak, total, mixed = running
                first = pl.multiple_of(index * depth, depth)
                scores = jnp.dot(
                    key_rows[pl.ds(first, depth), :], queries, preferred_element_type=F32
                )
                same = same_document(key_docs, first, depth, query_docs)
                scores = jnp.where(same, scores, MASKED)
                new_peak = jnp.maximum(peak, jnp.max(scores, axis=0, keepdims=True))
                scaling = jnp.exp(peak - new_peak)
                weights = jnp.exp(scores - new_peak)
                return (
                    new_peak,
                    total * scaling + jnp.sum(weights, axis=0, keepdims=True),
                    mixed * scaling
                    + jnp.dot(
                        value_t[:, pl.ds(first, depth)],
                        weights.astype(BF16),
                        preferred_element_type=F32,
                    ),
                )

            peak, total, mixed = over_chunks(
                length // depth,
                chunk,
                (
                    jnp.full((1, width), -jnp.inf, F32),
                    jnp.zeros((1, width), F32),
                    jnp.zeros((HD, width), F32),
                ),
            )
            mixed = mixed / total
            wide_ref[slot, :, pl.ds(begin, width)] = mixed
            lse_ref[slot, :, pl.ds(begin, width)] = peak + jnp.log(total)
            low = mixed.astype(BF16)
            for i in range(group):
                back_put[number * group + i, slot] = low[:, i * lanes : (i + 1) * lanes]
            return inner

        lax.fori_loop(0, length // width, block, 0)

        def send_one(step, inner):
            back_copy(lax.rem(me + step, count), slot).start()
            return inner

        lax.fori_loop(1, count, send_one, 0)
        back_keep(slot).start()
        if early:

            @pl.when(slot == 2)
            def _():
                relay(0)

        return carry

    lax.fori_loop(0, mine, unit_step, 0)

    if not early:
        relay(0)
    relay(1)
    hand_on(0)

    def home(unit, carry):
        owner, slot = lax.rem(unit, count), unit // count

        @pl.when(owner != me)
        def _():
            pltpu.make_async_remote_copy(
                src_ref=back_put.at[owner, slot],
                dst_ref=back_got.at[owner, slot],
                send_sem=back_put_sem.at[owner, slot],
                recv_sem=back_got_sem.at[owner, slot],
                device_id={"ctx": owner},
            ).wait_recv()

        @pl.when(owner == me)
        def _():
            back_keep(slot).wait()

        return carry

    lax.fori_loop(0, total_units, home, 0)
    for pair in range(pairs):
        for batch in range(MB):
            tops = []
            for j in range(2):
                unit = (2 * pair + j) * MB + batch
                tops.append(back_got[unit % count, unit // count])
            block = jnp.concatenate(tops, axis=0).T
            att_ref[batch * lanes : (batch + 1) * lanes, pair * 128 : (pair + 1) * 128] = block

    hand_on(1)
    for copies in halves:
        copies[0].wait_send()
        copies[1].wait()
        copies[2].wait_send()
        copies[3].wait()
    vec_y.wait_send()
    vec_core.wait_send()
    vec_pass.wait_send()
    mixer_y.wait_send()
    mixer_core.wait()
    mixer_pass.wait()
    every_pair(joint_y, "wait_send")
    every_pair(joint_core, "wait_send")
    every_pair(joint_pass, "wait_send")
    for copy in own_out:
        copy.wait()

    def sent(unit, carry):
        @pl.when(lax.rem(unit, count) != me)
        def _():
            send_copy(unit).wait_send()

        return carry

    lax.fori_loop(0, total_units, sent, 0)

    def returned(slot, carry):
        def one(step, inner):
            back_copy(lax.rem(me + step, count), slot).wait_send()
            return inner

        lax.fori_loop(1, count, one, 0)
        return carry

    lax.fori_loop(0, mine, returned, 0)
    every_pair(joint_store, "wait")


def forward(count, starts, tokens, docs, joint, vectors, mixer, inner, outer, number):
    units = starts.shape[0]
    lanes = tokens.shape[0] // MB
    length = count * lanes
    width = 2 * lanes
    part = joint.shape[0]
    pairs = H // 2
    vm = pl.BlockSpec(memory_space=pltpu.VMEM)
    hbm = pl.BlockSpec(memory_space=pl.ANY)
    dma = pltpu.SemaphoreType.DMA
    return pl.pallas_call(
        functools.partial(forward_kernel, width),
        out_shape=(
            jax.ShapeDtypeStruct(tokens.shape, BF16),
            jax.ShapeDtypeStruct((count, units, 3 * HD, lanes), BF16),
            jax.ShapeDtypeStruct((units, HD, length), F32),
            jax.ShapeDtypeStruct((units, 1, length), F32),
            jax.ShapeDtypeStruct((4, *joint.shape), BF16),
            jax.ShapeDtypeStruct((4, *vectors.shape), BF16),
            jax.ShapeDtypeStruct((4, *mixer.shape), BF16),
            jax.ShapeDtypeStruct((4, *inner.shape), BF16),
            jax.ShapeDtypeStruct((4, *outer.shape), BF16),
        ),
        in_specs=[pl.BlockSpec(memory_space=pltpu.SMEM), vm, vm, hbm, vm, hbm, hbm, hbm],
        out_specs=(vm, vm, vm, vm, hbm, vm, hbm, hbm, hbm),
        scratch_shapes=[
            pltpu.VMEM((pairs, 4, part, 384), BF16),
            pltpu.VMEM((pairs, 8, 384), F32),
            pltpu.VMEM((count, units, 3 * HD, lanes), BF16),
            pltpu.VMEM((count, units, HD, lanes), BF16),
            pltpu.VMEM((count, units, HD, lanes), BF16),
            pltpu.VMEM((length, HD), BF16),
            pltpu.VMEM((HD, length), BF16),
            pltpu.VMEM((length, lanes), jnp.int32),
            pltpu.VMEM(mixer.shape, BF16),
            pltpu.VMEM(inner.shape, BF16),
            pltpu.VMEM(outer.shape, BF16),
            dma((count, units)),
            dma((count, units)),
            dma((count, units)),
            dma((count, units)),
            dma((2, 3, pairs, 3)),
            dma((2, 4, 4)),
            dma((3, max(pairs, units, 4), 3)),
        ],
        compiler_params=pltpu.CompilerParams(
            collective_id=number, has_side_effects=True, vmem_limit_bytes=56 * 1024 * 1024
        ),
        name="forward",
    )(starts, tokens, docs, joint, vectors, mixer, inner, outer)


def first_rows(half, tile):
    return half if half <= tile else (half // tile + 1) // 2 * tile


def reduce_kernel(count, heads, *refs):
    jobs = len(heads)
    grads, outs, scratch = refs[:jobs], refs[jobs : 2 * jobs], refs[2 * jobs :]
    sets = [scratch[7 * j : 7 * j + 7] for j in range(jobs)]
    load_sem, send_sem, recv_sem, z_send, z_recv = scratch[7 * jobs :]
    me, shard = lax.axis_index("ctx"), lax.axis_index("fsdp")
    depth = count // 2
    y, core = shard // 2, lax.rem(shard, 2)
    z, x = me // 2, lax.rem(me, 2)
    other_core = {"fsdp": 2 * y + 1 - core}
    other_y = {"fsdp": 2 * (1 - y) + core}
    other_x = {"ctx": 2 * z + 1 - x}

    def along_z(step):
        return lax.rem(z + step, depth)

    barrier = pltpu.get_barrier_semaphore()
    for peer in (other_core, other_y, other_x):
        pl.semaphore_signal(barrier, inc=1, device_id=peer)
    for step in range(1, depth):
        pl.semaphore_signal(barrier, inc=1, device_id={"ctx": 2 * along_z(step) + x})

    def remote(src, dst, j, slot, peer):
        return pltpu.make_async_remote_copy(
            src_ref=src,
            dst_ref=dst,
            send_sem=send_sem.at[j, slot],
            recv_sem=recv_sem.at[j, slot],
            device_id=peer,
        )

    def plan(j):
        own, got, y_one, x_one, x_two, y_two, z_got = sets[j]
        half, lanes = own.shape[3], own.shape[4]
        head = heads[j]
        tail = head < half
        loads, firsts = [], []
        for side in range(2):
            columns = pl.ds(side * lanes, lanes)
            for low in range(2):
                loads.append(
                    pltpu.make_async_copy(
                        grads[j].at[:, low, core, :, columns],
                        own.at[side, :, low],
                        load_sem.at[j, 2 * side + low],
                    )
                )
            for low in range(2):
                firsts.append(
                    remote(
                        grads[j].at[:, low, 1 - core, :, columns],
                        got.at[side, :, low],
                        j,
                        2 * side + low,
                        other_core,
                    )
                )
        second = [remote(own.at[1 - y, :, :, 0:head, :], y_one, j, 4, other_y)]
        third = [remote(own.at[y, :, 1 - x, 0:head, :], x_two, j, 5, other_x)]
        if tail:
            second.append(remote(own.at[:, :, 1 - x, head:half, :], x_one, j, 6, other_x))
            third.append(remote(own.at[1 - y, :, x, head:half, :], y_two, j, 7, other_y))
        fourth = [
            pltpu.make_async_remote_copy(
                src_ref=own.at[y, along_z(step), x],
                dst_ref=z_got.at[z],
                send_sem=z_send.at[j, step],
                recv_sem=z_recv.at[j, step],
                device_id={"ctx": 2 * along_z(step) + x},
            )
            for step in range(1, depth)
        ]
        last = [remote(outs[j].at[core], outs[j].at[core], j, 8, other_core)]
        return (loads, firsts, second, third, fourth, last)

    plans = [plan(j) for j in range(jobs)]

    def add(a, b):
        return (a.astype(F32) + b.astype(F32)).astype(a.dtype)

    def start(copies):
        for copy in copies:
            copy.start()

    def stage_one(j):
        own, got = sets[j][0], sets[j][1]
        for copy in plans[j][0]:
            copy.wait()
        for copy in plans[j][1]:
            copy.wait_recv()

        def body(block, carry):
            for side in range(2):
                for low in range(2):
                    own[side, block, low] = add(own[side, block, low], got[side, block, low])
            return carry

        lax.fori_loop(0, depth, body, 0)
        start(plans[j][2])

    def stage_two(j):
        own, _, y_one, x_one, _, _, _ = sets[j]
        half, head = own.shape[3], heads[j]
        for copy in plans[j][2]:
            copy.wait()

        def body(block, carry):
            for low in range(2):
                own[y, block, low, 0:head, :] = add(
                    own[y, block, low, 0:head, :], y_one[block, low]
                )
            if head < half:
                for side in range(2):
                    own[side, block, x, head:half, :] = add(
                        own[side, block, x, head:half, :], x_one[side, block]
                    )
            return carry

        lax.fori_loop(0, depth, body, 0)
        start(plans[j][3])

    def stage_three(j):
        own, _, _, _, x_two, y_two, _ = sets[j]
        half, head = own.shape[3], heads[j]
        for copy in plans[j][3]:
            copy.wait()

        def body(block, carry):
            own[y, block, x, 0:head, :] = add(own[y, block, x, 0:head, :], x_two[block])
            if head < half:
                own[y, block, x, head:half, :] = add(
                    own[y, block, x, head:half, :], y_two[block]
                )
            return carry

        lax.fori_loop(0, depth, body, 0)
        start(plans[j][4])

    def stage_four(j):
        own, z_got = sets[j][0], sets[j][6]
        for copy in plans[j][4]:
            copy.wait()
        total = own[y, z, x].astype(F32)
        for step in range(1, depth):
            total = total + z_got[along_z(step)].astype(F32)
        outs[j][core] = total.astype(outs[j].dtype)
        start(plans[j][5])

    def stage_five(j):
        for copy in plans[j][5]:
            copy.wait()
        for copy in plans[j][1]:
            copy.wait_send()

    for j in range(jobs):
        start(plans[j][0])
    pl.semaphore_wait(barrier, 2 + depth)
    for j in range(jobs):
        start(plans[j][1])
    stages = (stage_one, stage_two, stage_three, stage_four, stage_five)
    for tick in range(jobs + len(stages) - 1):
        for k in reversed(range(len(stages))):
            if 0 <= tick - k < jobs:
                stages[k](tick - k)


def reduce_all(grads, number):
    count = grads[0].shape[0]
    depth = count // 2
    heads, scratch, outs = [], [], []
    for g in grads:
        half, lanes = g.shape[2], g.shape[3] // 2
        head = first_rows(half, 16 if g.dtype == BF16 else 8)
        tail = max(half - head, 16 if g.dtype == BF16 else 8)
        heads.append(head)
        for shape in (
            (2, depth, 2, half, lanes),
            (2, depth, 2, half, lanes),
            (depth, 2, head, lanes),
            (2, depth, tail, lanes),
            (depth, head, lanes),
            (depth, tail, lanes),
            (depth, half, lanes),
        ):
            scratch.append(pltpu.VMEM(shape, g.dtype))
        outs.append(jax.ShapeDtypeStruct((2, half, lanes), g.dtype))
    jobs = len(grads)
    scratch += [
        pltpu.SemaphoreType.DMA((jobs, 4)),
        pltpu.SemaphoreType.DMA((jobs, 9)),
        pltpu.SemaphoreType.DMA((jobs, 9)),
        pltpu.SemaphoreType.DMA((jobs, depth)),
        pltpu.SemaphoreType.DMA((jobs, depth)),
    ]
    return pl.pallas_call(
        functools.partial(reduce_kernel, count, tuple(heads)),
        out_shape=tuple(outs),
        in_specs=[pl.BlockSpec(memory_space=pl.ANY)] * jobs,
        out_specs=[pl.BlockSpec(memory_space=pltpu.VMEM)] * jobs,
        scratch_shapes=scratch,
        compiler_params=pltpu.CompilerParams(
            collective_id=number, has_side_effects=True, vmem_limit_bytes=56 * 1024 * 1024
        ),
        name="reduce_all",
    )(*[g.reshape(depth, 2, *g.shape[1:]) for g in grads])


def on_device(
    count,
    shards,
    tokens,
    doc_starts,
    joint_weight,
    mixer_weight,
    inner_weight,
    outer_weight,
    query_bias,
    value_bias,
    mixer_bias,
    first_gain,
    first_shift,
    inner_bias,
    outer_bias,
    second_gain,
    second_shift,
    upstream,
):
    rows = tokens.shape[2]
    length = rows * count
    units = -(-MB * H // count)
    me = lax.axis_index("ctx")

    part = D // shards
    vectors = jnp.stack(
        [
            query_bias,
            value_bias,
            mixer_bias,
            first_gain,
            first_shift,
            outer_bias,
            second_gain,
            second_shift,
        ]
    )
    vectors = jnp.pad(vectors, ((0, 8), (0, D - part)))
    vectors = vectors.at[8].set(inner_bias)
    source = tokens.reshape(MB * rows, D)
    unit_ids = jnp.arange(units, dtype=jnp.int32) * count + me
    unit_starts = doc_starts[:, 0][lax.rem(unit_ids, MB)]
    positions = jnp.arange(length, dtype=jnp.int32)
    unit_docs = jax.vmap(lambda s: doc_index(positions, s))(unit_starts)[:, None, :]

    attended, received, wide, lse, joint, vectors, mixer, inner, outer = forward(
        count,
        unit_starts,
        source,
        unit_docs,
        joint_weight,
        vectors,
        mixer_weight,
        inner_weight,
        outer_weight,
        0,
    )
    joint = joint.reshape(D, 3 * D)
    mixer, inner, outer = mixer.reshape(D, D), inner.reshape(D, FF), outer.reshape(FF, D)
    heads_of = [
        vectors[:, i, :part].reshape(D).astype(F32)
        for i in range(8)
    ]
    _, _, mbias, gain_one, shift_one, obias, gain_two, shift_two = heads_of
    ibias = vectors[:, 8].reshape(FF).astype(F32)

    branch = mul_nn(attended, mixer) + mbias
    first, first_normed, first_recip = norm_forward(
        source.astype(F32) + branch, gain_one, shift_one
    )
    first_low = first.astype(BF16)
    inner_pre = mul_nn(first_low, inner) + ibias
    activated, gelu_slope = gelu_parts(inner_pre)
    activated_low = activated.astype(BF16)
    outer_out = mul_nn(activated_low, outer) + obias
    final, second_normed, second_recip = norm_forward(first + outer_out, gain_two, shift_two)
    result = final.astype(BF16).reshape(MB, 1, rows, D)

    incoming = upstream.reshape(MB * rows, D).astype(F32)
    rescale_grad = jnp.sum(incoming * second_normed, axis=0)
    reshift_grad = jnp.sum(incoming, axis=0)
    d_second = norm_backward(incoming, second_normed, second_recip, gain_two)
    d_outer = d_second.astype(BF16)
    return_grad = jnp.sum(d_outer.astype(F32), axis=0)
    outer_grad = mul_tn(d_outer, activated_low)
    d_inner = (mul_nt(d_outer, outer) * gelu_slope).astype(BF16)
    hidden_grad = jnp.sum(d_inner.astype(F32), axis=0)
    inner_grad = mul_tn(d_inner, first_low)
    d_first = d_second + mul_nt(d_inner, inner)
    scale_grad = jnp.sum(d_first * first_normed, axis=0)
    shift_grad = jnp.sum(d_first, axis=0)
    d_residual = norm_backward(d_first, first_normed, first_recip, gain_one)
    d_branch = d_residual.astype(BF16)
    mixing_grad = jnp.sum(d_branch.astype(F32), axis=0)
    mixer_grad = mul_tn(d_branch, attended)
    flow = mul_nt(mixer, d_branch).astype(BF16)
    flow_units = exchange(to_units(flow, 1, count, units), 2)
    d_units = attend_back(received, flow_units, unit_starts, unit_docs, wide, lse)
    d_joint = from_units(exchange(d_units, 3), 3)
    bias_sums = jnp.sum(d_joint.astype(F32), axis=1)
    query_grad = bias_sums[0:D]
    values_grad = bias_sums[2 * D :]
    joint_grad = mul_nn(d_joint, source)
    tokens_grad = d_residual + mul_tt(d_joint, joint)
    tokens_grad = tokens_grad.reshape(MB, 1, rows, D)

    small = [
        query_grad,
        values_grad,
        mixing_grad,
        scale_grad,
        shift_grad,
        hidden_grad,
        return_grad,
        rescale_grad,
        reshift_grad,
    ]
    world = count * shards
    packed = jnp.concatenate([v.reshape(world, -1) for v in small], axis=1)
    turned = [outer_grad, inner_grad, mixer_grad, joint_grad]
    if shards == 4 and count % 2 == 0 and D % (32 * count) == 0:
        core = lax.rem(lax.axis_index("fsdp"), 2)
        bias_job = packed.reshape(count, 2, 2, -1).transpose(0, 2, 1, 3)
        spare = -packed.shape[1] % 128
        bias_job = jnp.pad(bias_job, ((0, 0), (0, 0), (0, 0), (0, spare)))
        bias_job = jnp.pad(bias_job.reshape(count, 2, 1, -1), ((0, 0), (0, 0), (0, 7), (0, 0)))
        jobs = [g.astype(BF16).reshape(count, 2, -1, g.shape[1]) for g in turned] + [bias_job]
        *sums, own = reduce_all(jobs, 4)
        blocks = []
        for g in sums:
            width = g.shape[2] // 2
            g = g.reshape(-1, 2 * width)
            blocks.append(lax.dynamic_slice_in_dim(g, core * width, width, 1).T.astype(F32))
        own = lax.dynamic_index_in_dim(own, core, 0, False)[0, : packed.shape[1]]
    else:

        def reduced(grad):
            over_lanes = lax.psum_scatter(
                grad.astype(BF16), "fsdp", scatter_dimension=1, tiled=True
            )
            over_rows = lax.psum_scatter(over_lanes, "ctx", scatter_dimension=0, tiled=True)
            return over_rows.T.astype(F32)

        blocks = [reduced(g) for g in turned]
        packed = lax.psum(packed, ("ctx", "fsdp"))
        index = me * shards + lax.axis_index("fsdp")
        own = lax.dynamic_slice_in_dim(packed, index, 1, 0)[0]
    outer_out_grad, inner_out, mixer_out, joint_out = blocks
    sums = []
    begin = 0
    for v in small:
        size = v.shape[0] // world
        sums.append(own[begin : begin + size])
        begin += size
    return (result, tokens_grad, joint_out, mixer_out, inner_out, outer_out_grad, *sums)


def solution(mesh):
    in_specs = (
        P(None, "fsdp", "ctx", None),
        P(None, "fsdp", None),
        P("fsdp", None),
        P("fsdp", None),
        P("fsdp", None),
        P("fsdp", None),
        P("fsdp"),
        P("fsdp"),
        P("fsdp"),
        P("fsdp"),
        P("fsdp"),
        P("fsdp"),
        P("fsdp"),
        P("fsdp"),
        P("fsdp"),
        P(None, "fsdp", "ctx", None),
    )
    out_specs = (
        P(None, "fsdp", "ctx", None),
        P(None, "fsdp", "ctx", None),
        P("fsdp", "ctx"),
        P("fsdp", "ctx"),
        P("fsdp", "ctx"),
        P("fsdp", "ctx"),
        P(("ctx", "fsdp")),
        P(("ctx", "fsdp")),
        P(("ctx", "fsdp")),
        P(("ctx", "fsdp")),
        P(("ctx", "fsdp")),
        P(("ctx", "fsdp")),
        P(("ctx", "fsdp")),
        P(("ctx", "fsdp")),
        P(("ctx", "fsdp")),
    )
    return jax.shard_map(
        functools.partial(on_device, mesh.shape["ctx"], mesh.shape["fsdp"]),
        mesh=mesh,
        in_specs=in_specs,
        out_specs=out_specs,
        check_vma=False,
    )
```

```python
import functools
import math

import jax
import jax.numpy as jnp
from jax import lax
from jax.experimental import pallas as pl
from jax.experimental.pallas import tpu as pltpu
from jax.sharding import PartitionSpec as P

D = 768
H = 12
HD = 64
FF = 3072
MB = 3

SCALE = 0.125
EPSILON = 1e-12
MASKED = -1000000000.0
ROOT_HALF = 0.7071067811865476
GAUSS_PEAK = 0.3989422804014327

F32 = jnp.float32
BF16 = jnp.bfloat16


def doc_index(positions, starts_row):
    return jnp.sum((starts_row[None, :] <= positions[:, None]).astype(jnp.int32), axis=1) - 1


def norm_forward(hidden, gain, shift):
    average = jnp.mean(hidden, axis=-1, keepdims=True)
    centred = hidden - average
    reciprocal = lax.rsqrt(jnp.mean(centred * centred, axis=-1, keepdims=True) + EPSILON)
    normed = centred * reciprocal
    return (normed * gain + shift, normed, reciprocal)


def norm_backward(incoming, normed, reciprocal, gain):
    scaled = incoming * gain
    return reciprocal * (
        scaled
        - jnp.mean(scaled, axis=-1, keepdims=True)
        - normed * jnp.mean(scaled * normed, axis=-1, keepdims=True)
    )


def gelu_parts(inner):
    cumulative = 0.5 * (1.0 + lax.erf(inner * ROOT_HALF))
    return (inner * cumulative, cumulative + inner * jnp.exp(-0.5 * inner * inner) * GAUSS_PEAK)


def exchange_kernel(count, x_ref, y_ref, held, send_sem, recv_sem, own_sem):
    me = lax.axis_index("ctx")
    barrier = pltpu.get_barrier_semaphore()

    def greet(step, carry):
        peer = lax.rem(me + step, count)
        pl.semaphore_signal(barrier, inc=1, device_id={"ctx": peer})
        return carry

    lax.fori_loop(1, count, greet, 0)
    own_in = pltpu.make_async_copy(x_ref.at[me], held, own_sem)
    own_in.start()
    pl.semaphore_wait(barrier, count - 1)

    def transfer(step):
        peer = lax.rem(me + step, count)
        return pltpu.make_async_remote_copy(
            src_ref=x_ref.at[peer],
            dst_ref=y_ref.at[me],
            send_sem=send_sem.at[step],
            recv_sem=recv_sem.at[step],
            device_id={"ctx": peer},
        )

    def begin(step, carry):
        transfer(step).start()
        return carry

    lax.fori_loop(1, count, begin, 0)
    own_in.wait()
    own_out = pltpu.make_async_copy(held, y_ref.at[me], own_sem)
    own_out.start()
    own_out.wait()

    def finish(step, carry):
        transfer(step).wait()
        return carry

    lax.fori_loop(1, count, finish, 0)


def exchange(x, number):
    count = x.shape[0]
    return pl.pallas_call(
        functools.partial(exchange_kernel, count),
        out_shape=jax.ShapeDtypeStruct(x.shape, x.dtype),
        in_specs=[pl.BlockSpec(memory_space=pl.ANY)],
        out_specs=pl.BlockSpec(memory_space=pl.ANY),
        scratch_shapes=[
            pltpu.VMEM(x.shape[1:], x.dtype),
            pltpu.SemaphoreType.DMA((count,)),
            pltpu.SemaphoreType.DMA((count,)),
            pltpu.SemaphoreType.DMA,
        ],
        compiler_params=pltpu.CompilerParams(collective_id=number, has_side_effects=True),
        name=f"exchange_{number}",
    )(x)


def across(ref, first, rows, width, lanes):
    parts = [ref[first + i, 0, rows, :] for i in range(width // lanes)]
    return parts[0] if len(parts) == 1 else jnp.concatenate(parts, axis=1)


def key_documents(starts_ref, unit, length, lanes, key_docs):
    position = lax.broadcasted_iota(jnp.int32, (length, lanes), 0)
    docs = jnp.zeros((length, lanes), jnp.int32) - 1
    for j in range(starts_ref.shape[1]):
        docs = docs + jnp.where(position >= starts_ref[unit, j], 1, 0)
    key_docs[...] = docs


def same_document(key_docs, first, width, query_docs):
    keys = key_docs[pl.ds(first, width), :]
    lanes = keys.shape[1]
    parts = [keys == query_docs[:, i : i + lanes] for i in range(0, query_docs.shape[1], lanes)]
    return parts[0] if len(parts) == 1 else jnp.concatenate(parts, axis=1)


def over_chunks(chunks, body, carry):
    if chunks == 1:
        return body(0, carry)
    return lax.fori_loop(0, chunks, body, carry)


def attend_back_kernel(
    width,
    starts_ref,
    x_ref,
    flow_ref,
    docs_ref,
    wide_ref,
    lse_ref,
    d_ref,
    key_rows,
    value_rows,
    key_t,
    key_docs,
    d_key,
    d_value,
):
    count, _, _, lanes = x_ref.shape
    length = count * lanes
    depth = min(length, 1024)
    unit = pl.program_id(0)
    for i in range(count):
        rows = slice(i * lanes, (i + 1) * lanes)
        key_rows[rows, :] = x_ref[i, 0, HD : 2 * HD, :].T
        value_rows[rows, :] = x_ref[i, 0, 2 * HD : 3 * HD, :].T
        key_t[:, rows] = x_ref[i, 0, HD : 2 * HD, :]
    key_documents(starts_ref, unit, length, lanes, key_docs)
    d_key[...] = jnp.zeros_like(d_key)
    d_value[...] = jnp.zeros_like(d_value)
    group = width // lanes

    def block(number, carry):
        begin = pl.multiple_of(number * width, width)
        queries = across(x_ref, number * group, slice(0, HD), width, lanes)
        flow = across(flow_ref, number * group, slice(0, HD), width, lanes)
        query_rows = queries.T
        flow_rows = flow.T
        query_docs = docs_ref[0, :, pl.ds(begin, width)]
        log_total = lse_ref[0, :, pl.ds(begin, width)]
        spread = jnp.sum(
            flow.astype(F32) * wide_ref[0, :, pl.ds(begin, width)], axis=0, keepdims=True
        )

        def chunk(index, d_query):
            first = pl.multiple_of(index * depth, depth)
            rows = pl.ds(first, depth)
            scores = jnp.dot(key_rows[rows, :], queries, preferred_element_type=F32)
            same = same_document(key_docs, first, depth, query_docs)
            probs = jnp.exp(jnp.where(same, scores, MASKED) - log_total)
            pressure = jnp.dot(value_rows[rows, :], flow, preferred_element_type=F32)
            d_scores = (probs * (pressure - spread)).astype(BF16)
            d_value[rows, :] += jnp.dot(
                probs.astype(BF16), flow_rows, preferred_element_type=F32
            )
            d_key[rows, :] += jnp.dot(d_scores, query_rows, preferred_element_type=F32)
            return d_query + jnp.dot(key_t[:, rows], d_scores, preferred_element_type=F32)

        d_query = over_chunks(length // depth, chunk, jnp.zeros((HD, width), F32))
        low = (d_query * SCALE).astype(BF16)
        for i in range(group):
            d_ref[number * group + i, 0, 0:HD, :] = low[:, i * lanes : (i + 1) * lanes]
        return carry

    lax.fori_loop(0, length // width, block, 0)
    for i in range(count):
        rows = slice(i * lanes, (i + 1) * lanes)
        d_ref[i, 0, HD : 2 * HD, :] = d_key[rows, :].T.astype(BF16)
        d_ref[i, 0, 2 * HD : 3 * HD, :] = d_value[rows, :].T.astype(BF16)


def unit_block(*dims):
    return pl.BlockSpec(dims, lambda u, starts: (0, u) + (0,) * (len(dims) - 2))


def own_block(*dims):
    return pl.BlockSpec(dims, lambda u, starts: (u,) + (0,) * (len(dims) - 1))


def attend_back(x, flow, starts, docs, wide, lse):
    count, units, _, lanes = x.shape
    length = count * lanes
    width = 2 * lanes if count % 2 == 0 else lanes
    return pl.pallas_call(
        functools.partial(attend_back_kernel, width),
        out_shape=jax.ShapeDtypeStruct(x.shape, BF16),
        grid_spec=pltpu.PrefetchScalarGridSpec(
            num_scalar_prefetch=1,
            grid=(units,),
            in_specs=[
                unit_block(count, 1, 3 * HD, lanes),
                unit_block(count, 1, HD, lanes),
                own_block(1, 1, length),
                own_block(1, HD, length),
                own_block(1, 1, length),
            ],
            out_specs=unit_block(count, 1, 3 * HD, lanes),
            scratch_shapes=[
                pltpu.VMEM((length, HD), BF16),
                pltpu.VMEM((length, HD), BF16),
                pltpu.VMEM((HD, length), BF16),
                pltpu.VMEM((length, lanes), jnp.int32),
                pltpu.VMEM((length, HD), F32),
                pltpu.VMEM((length, HD), F32),
            ],
        ),
        compiler_params=pltpu.CompilerParams(dimension_semantics=("arbitrary",)),
        name="attend_back",
    )(starts, x, flow, docs, wide, lse)


def to_units(columns, parts, count, units):
    rows = columns.shape[1] // MB
    x = columns.reshape(parts, H, HD, MB, rows).transpose(1, 3, 0, 2, 4)
    x = x.reshape(MB * H, parts * HD, rows)
    x = jnp.pad(x, ((0, units * count - MB * H), (0, 0), (0, 0)))
    return x.reshape(units, count, parts * HD, rows).transpose(1, 0, 2, 3)


def from_units(x, parts):
    count, units, _, rows = x.shape
    x = x.transpose(1, 0, 2, 3).reshape(units * count, parts * HD, rows)[: MB * H]
    x = x.reshape(H, MB, parts, HD, rows).transpose(2, 0, 3, 1, 4)
    return x.reshape(parts * D, MB * rows)


def mul_nn(a, b):
    return jnp.dot(a, b, preferred_element_type=F32)


def mul_tn(a, b):
    return lax.dot_general(a, b, (((0,), (0,)), ((), ())), preferred_element_type=F32)


def mul_nt(a, b):
    return lax.dot_general(a, b, (((1,), (1,)), ((), ())), preferred_element_type=F32)


def mul_tt(a, b):
    return lax.dot_general(a, b, (((0,), (1,)), ((), ())), preferred_element_type=F32)


def forward_kernel(
    width,
    starts_ref,
    tok_ref,
    docs_ref,
    joint_ref,
    vec_ref,
    mixer_ref,
    inner_ref,
    outer_ref,
    att_ref,
    got_ref,
    wide_ref,
    lse_ref,
    joint_out,
    vec_out,
    mixer_out,
    inner_out,
    outer_out,
    joint_all,
    bias_rows,
    put,
    back_put,
    back_got,
    key_rows,
    value_t,
    key_docs,
    mixer_own,
    inner_own,
    outer_own,
    put_sem,
    got_sem,
    back_put_sem,
    back_got_sem,
    joint_sems,
    weight_sems,
    own_sems,
):
    count, units, _, lanes = got_ref.shape
    length = count * lanes
    depth = min(length, 1024)
    group = width // lanes
    pairs = H // 2
    total_units = MB * H
    part = joint_ref.shape[0]
    me, shard = lax.axis_index("ctx"), lax.axis_index("fsdp")
    y, core = shard // 2, lax.rem(shard, 2)
    x = lax.rem(me, 2)
    far = 2 * (1 - y) + core
    other_core = {"fsdp": 2 * y + 1 - core}
    other_y = {"fsdp": far}
    other_x = {"ctx": me + 1 - 2 * x}
    mine = (total_units - me + count - 1) // count

    barrier = pltpu.get_barrier_semaphore()

    def greet(step, carry):
        pl.semaphore_signal(barrier, inc=1, device_id={"ctx": lax.rem(me + step, count)})
        return carry

    lax.fori_loop(1, count, greet, 0)
    pl.semaphore_signal(barrier, inc=1, device_id=other_core)
    pl.semaphore_signal(barrier, inc=1, device_id=other_y)

    def remote(src, dst, sems, index, peer):
        return pltpu.make_async_remote_copy(
            src_ref=src,
            dst_ref=dst,
            send_sem=sems.at[(0, *index)],
            recv_sem=sems.at[(1, *index)],
            device_id=peer,
        )

    def own_joint(pair, third):
        columns = pl.ds(pl.multiple_of(third * D + pair * 128, 128), 128)
        return pltpu.make_async_copy(
            joint_ref.at[:, columns],
            joint_all.at[pair, shard, :, pl.ds(third * 128, 128)],
            own_sems.at[0, pair, third],
        )

    def joint_copy(kind, pair, third, which, peer, source=None):
        here = joint_all.at[pair, which, :, pl.ds(third * 128, 128)]
        if source is None:
            source = here
        else:
            source = source.at[:, pl.ds(pl.multiple_of(third * D + pair * 128, 128), 128)]
        return remote(source, here, joint_sems, (kind, pair, third), peer)

    def joint_y(pair, third):
        return joint_copy(0, pair, third, shard, other_y, joint_ref)

    def joint_core(pair, third):
        return joint_copy(1, pair, third, shard, other_core, joint_ref)

    def joint_pass(pair, third):
        return joint_copy(2, pair, third, far, other_core)

    def joint_store(pair):
        return pltpu.make_async_copy(
            joint_all.at[pair], joint_out.at[pair], own_sems.at[0, pair, 0]
        )

    def each_third(pair, make, act):
        for third in range(3):
            getattr(make(pair, third), act)()

    def every_pair(make, act):
        def body(pair, carry):
            each_third(pair, make, act)
            return carry

        lax.fori_loop(0, pairs, body, 0)

    every_pair(own_joint, "start")
    wholes = ((mixer_ref, mixer_own, mixer_out), (inner_ref, inner_own, inner_out), (outer_ref, outer_own, outer_out))
    own_in = [
        pltpu.make_async_copy(ref, held, own_sems.at[1, i, 0])
        for i, (ref, held, _) in enumerate(wholes)
    ]
    own_out = [
        pltpu.make_async_copy(held, out.at[shard], own_sems.at[1, i, 1])
        for i, (_, held, out) in enumerate(wholes)
    ]
    for copy in own_in:
        copy.start()
    vec_own = pltpu.make_async_copy(vec_ref, vec_out.at[shard], own_sems.at[1, 3, 0])
    vec_own.start()
    pl.semaphore_wait(barrier, count + 1)

    vec_y = remote(vec_ref, vec_out.at[shard], weight_sems, (0, 0), other_y)
    vec_core = remote(vec_ref, vec_out.at[shard], weight_sems, (0, 1), other_core)
    vec_pass = remote(vec_out.at[far], vec_out.at[far], weight_sems, (0, 2), other_core)
    mixer_y = remote(mixer_ref, mixer_out.at[shard], weight_sems, (1, 0), other_y)
    mixer_core = remote(mixer_ref, mixer_out.at[shard], weight_sems, (1, 1), other_core)
    mixer_pass = remote(mixer_out.at[far], mixer_out.at[far], weight_sems, (1, 2), other_core)
    halves = []
    for i, (ref, out) in enumerate(((inner_ref, inner_out), (outer_ref, outer_out))):
        size = ref.shape[0] // 2
        rows = pl.ds(pl.multiple_of(x * size, size), size)
        halves.append(
            (
                remote(ref.at[rows, :], out.at[shard, rows, :], weight_sems, (2 + i, 0), other_y),
                remote(ref, out.at[shard], weight_sems, (2 + i, 1), other_core),
                remote(
                    out.at[far, rows, :], out.at[far, rows, :], weight_sems, (2 + i, 3), other_x
                ),
                remote(out.at[far], out.at[far], weight_sems, (2 + i, 2), other_core),
            )
        )
    vec_y.start()
    vec_core.start()
    every_pair(joint_y, "start")
    every_pair(joint_core, "start")
    mixer_y.start()
    mixer_core.start()
    for copies in halves:
        copies[0].start()
        copies[1].start()
    for first, second in zip(own_in, own_out):
        first.wait()
        second.start()

    vec_own.wait()
    vec_y.wait_recv()
    vec_pass.start()
    vec_core.wait_recv()
    vec_pass.wait_recv()

    def bias_of(slot):
        pieces = [
            vec_out[f, slot : slot + 1, 0:part].astype(F32) for f in range(4)
        ]
        return jnp.concatenate(pieces, axis=1)

    query_bias, value_bias = bias_of(0), bias_of(1)
    for pair in range(pairs):
        columns = slice(pair * 128, (pair + 1) * 128)
        bias_rows[pair, :, 0:128] = jnp.broadcast_to(query_bias[:, columns], (8, 128))
        bias_rows[pair, :, 128:256] = jnp.zeros((8, 128), F32)
        bias_rows[pair, :, 256:384] = jnp.broadcast_to(value_bias[:, columns], (8, 128))

    def sent_sem(unit):
        return lax.rem(unit, count), unit // count

    def send_copy(unit):
        owner, slot = sent_sem(unit)
        return pltpu.make_async_remote_copy(
            src_ref=put.at[owner, slot],
            dst_ref=got_ref.at[me, slot],
            send_sem=put_sem.at[owner, slot],
            recv_sem=got_sem.at[me, slot],
            device_id={"ctx": owner},
        )

    def keep_copy(unit):
        owner, slot = sent_sem(unit)
        return pltpu.make_async_copy(
            put.at[owner, slot], got_ref.at[me, slot], own_sems.at[2, slot, 0]
        )

    def project(pair, carry):
        each_third(pair, own_joint, "wait")
        each_third(pair, joint_y, "wait_recv")
        each_third(pair, joint_pass, "start")
        each_third(pair, joint_core, "wait_recv")
        each_third(pair, joint_pass, "wait_recv")
        joint_store(pair).start()
        weight = joint_all[pair].reshape(4 * part, 384)
        rows = jnp.dot(tok_ref[...], weight, preferred_element_type=F32)
        rows = (rows + bias_rows[pair, 0:1, :]).astype(BF16)
        for third in range(3):
            for batch in range(MB):
                block = rows[batch * lanes : (batch + 1) * lanes, third * 128 : (third + 1) * 128]
                turned = block.T
                if third == 0:
                    turned = turned * SCALE
                for j in range(2):
                    unit = (2 * pair + j) * MB + batch
                    put[lax.rem(unit, count), unit // count, third * HD : (third + 1) * HD, :] = (
                        turned[j * HD : (j + 1) * HD]
                    )
        for i in range(2 * MB):
            unit = 2 * pair * MB + i

            @pl.when(lax.rem(unit, count) != me)
            def _():
                send_copy(unit).start()

            @pl.when(lax.rem(unit, count) == me)
            def _():
                keep_copy(unit).start()

        return carry

    lax.fori_loop(0, pairs, project, 0)

    mixer_y.wait_recv()
    mixer_pass.start()

    def arrival(sender, slot):
        return pltpu.make_async_remote_copy(
            src_ref=put.at[sender, slot],
            dst_ref=got_ref.at[sender, slot],
            send_sem=put_sem.at[sender, slot],
            recv_sem=got_sem.at[sender, slot],
            device_id={"ctx": sender},
        )

    def back_copy(peer, slot):
        return pltpu.make_async_remote_copy(
            src_ref=back_put.at[peer, slot],
            dst_ref=back_got.at[me, slot],
            send_sem=back_put_sem.at[peer, slot],
            recv_sem=back_got_sem.at[me, slot],
            device_id={"ctx": peer},
        )

    def back_keep(slot):
        return pltpu.make_async_copy(
            back_put.at[me, slot], back_got.at[me, slot], own_sems.at[2, slot, 1]
        )

    def relay(i):
        halves[i][0].wait_recv()
        halves[i][2].start()

    def hand_on(i):
        halves[i][2].wait_recv()
        halves[i][3].start()

    early = total_units // count > 2

    def unit_step(slot, carry):
        def wait_one(step, inner):
            arrival(lax.rem(me + step, count), slot).wait_recv()
            return inner

        lax.fori_loop(1, count, wait_one, 0)
        keep_copy(slot * count + me).wait()
        for i in range(count):
            rows = slice(i * lanes, (i + 1) * lanes)
            key_rows[rows, :] = got_ref[i, slot, HD : 2 * HD, :].T
            value_t[:, rows] = got_ref[i, slot, 2 * HD : 3 * HD, :]
        key_documents(starts_ref, slot, length, lanes, key_docs)

        def block(number, inner):
            begin = pl.multiple_of(number * width, width)
            parts = [got_ref[number * group + i, slot, 0:HD, :] for i in range(group)]
            queries = parts[0] if group == 1 else jnp.concatenate(parts, axis=1)
            query_docs = docs_ref[slot, :, pl.ds(begin, width)]

            def chunk(index, running):
                peak, total, mixed = running
                first = pl.multiple_of(index * depth, depth)
                scores = jnp.dot(
                    key_rows[pl.ds(first, depth), :], queries, preferred_element_type=F32
                )
                same = same_document(key_docs, first, depth, query_docs)
                scores = jnp.where(same, scores, MASKED)
                new_peak = jnp.maximum(peak, jnp.max(scores, axis=0, keepdims=True))
                scaling = jnp.exp(peak - new_peak)
                weights = jnp.exp(scores - new_peak)
                return (
                    new_peak,
                    total * scaling + jnp.sum(weights, axis=0, keepdims=True),
                    mixed * scaling
                    + jnp.dot(
                        value_t[:, pl.ds(first, depth)],
                        weights.astype(BF16),
                        preferred_element_type=F32,
                    ),
                )

            peak, total, mixed = over_chunks(
                length // depth,
                chunk,
                (
                    jnp.full((1, width), -jnp.inf, F32),
                    jnp.zeros((1, width), F32),
                    jnp.zeros((HD, width), F32),
                ),
            )
            mixed = mixed / total
            wide_ref[slot, :, pl.ds(begin, width)] = mixed
            lse_ref[slot, :, pl.ds(begin, width)] = peak + jnp.log(total)
            low = mixed.astype(BF16)
            for i in range(group):
                back_put[number * group + i, slot] = low[:, i * lanes : (i + 1) * lanes]
            return inner

        lax.fori_loop(0, length // width, block, 0)

        def send_one(step, inner):
            back_copy(lax.rem(me + step, count), slot).start()
            return inner

        lax.fori_loop(1, count, send_one, 0)
        back_keep(slot).start()
        if early:

            @pl.when(slot == 2)
            def _():
                relay(0)

        return carry

    lax.fori_loop(0, mine, unit_step, 0)

    if not early:
        relay(0)
    relay(1)
    hand_on(0)

    def home(unit, carry):
        owner, slot = lax.rem(unit, count), unit // count

        @pl.when(owner != me)
        def _():
            pltpu.make_async_remote_copy(
                src_ref=back_put.at[owner, slot],
                dst_ref=back_got.at[owner, slot],
                send_sem=back_put_sem.at[owner, slot],
                recv_sem=back_got_sem.at[owner, slot],
                device_id={"ctx": owner},
            ).wait_recv()

        @pl.when(owner == me)
        def _():
            back_keep(slot).wait()

        return carry

    lax.fori_loop(0, total_units, home, 0)
    for pair in range(pairs):
        for batch in range(MB):
            tops = []
            for j in range(2):
                unit = (2 * pair + j) * MB + batch
                tops.append(back_got[unit % count, unit // count])
            block = jnp.concatenate(tops, axis=0).T
            att_ref[batch * lanes : (batch + 1) * lanes, pair * 128 : (pair + 1) * 128] = block

    hand_on(1)
    for copies in halves:
        copies[0].wait_send()
        copies[1].wait()
        copies[2].wait_send()
        copies[3].wait()
    vec_y.wait_send()
    vec_core.wait_send()
    vec_pass.wait_send()
    mixer_y.wait_send()
    mixer_core.wait()
    mixer_pass.wait()
    every_pair(joint_y, "wait_send")
    every_pair(joint_core, "wait_send")
    every_pair(joint_pass, "wait_send")
    for copy in own_out:
        copy.wait()

    def sent(unit, carry):
        @pl.when(lax.rem(unit, count) != me)
        def _():
            send_copy(unit).wait_send()

        return carry

    lax.fori_loop(0, total_units, sent, 0)

    def returned(slot, carry):
        def one(step, inner):
            back_copy(lax.rem(me + step, count), slot).wait_send()
            return inner

        lax.fori_loop(1, count, one, 0)
        return carry

    lax.fori_loop(0, mine, returned, 0)
    for pair in range(pairs):
        joint_store(pair).wait()


def forward(count, starts, tokens, docs, joint, vectors, mixer, inner, outer, number):
    units = starts.shape[0]
    lanes = tokens.shape[0] // MB
    length = count * lanes
    width = 2 * lanes
    part = joint.shape[0]
    pairs = H // 2
    vm = pl.BlockSpec(memory_space=pltpu.VMEM)
    hbm = pl.BlockSpec(memory_space=pl.ANY)
    dma = pltpu.SemaphoreType.DMA
    return pl.pallas_call(
        functools.partial(forward_kernel, width),
        out_shape=(
            jax.ShapeDtypeStruct(tokens.shape, BF16),
            jax.ShapeDtypeStruct((count, units, 3 * HD, lanes), BF16),
            jax.ShapeDtypeStruct((units, HD, length), F32),
            jax.ShapeDtypeStruct((units, 1, length), F32),
            jax.ShapeDtypeStruct((pairs, 4, part, 384), BF16),
            jax.ShapeDtypeStruct((4, *vectors.shape), BF16),
            jax.ShapeDtypeStruct((4, *mixer.shape), BF16),
            jax.ShapeDtypeStruct((4, *inner.shape), BF16),
            jax.ShapeDtypeStruct((4, *outer.shape), BF16),
        ),
        in_specs=[pl.BlockSpec(memory_space=pltpu.SMEM), vm, vm, hbm, vm, hbm, hbm, hbm],
        out_specs=(vm, vm, vm, vm, hbm, vm, hbm, hbm, hbm),
        scratch_shapes=[
            pltpu.VMEM((pairs, 4, part, 384), BF16),
            pltpu.VMEM((pairs, 8, 384), F32),
            pltpu.VMEM((count, units, 3 * HD, lanes), BF16),
            pltpu.VMEM((count, units, HD, lanes), BF16),
            pltpu.VMEM((count, units, HD, lanes), BF16),
            pltpu.VMEM((length, HD), BF16),
            pltpu.VMEM((HD, length), BF16),
            pltpu.VMEM((length, lanes), jnp.int32),
            pltpu.VMEM(mixer.shape, BF16),
            pltpu.VMEM(inner.shape, BF16),
            pltpu.VMEM(outer.shape, BF16),
            dma((count, units)),
            dma((count, units)),
            dma((count, units)),
            dma((count, units)),
            dma((2, 3, pairs, 3)),
            dma((2, 4, 4)),
            dma((3, max(pairs, units, 4), 3)),
        ],
        compiler_params=pltpu.CompilerParams(
            collective_id=number, has_side_effects=True, vmem_limit_bytes=56 * 1024 * 1024
        ),
        name="forward",
    )(starts, tokens, docs, joint, vectors, mixer, inner, outer)


JOINT_JOB = 3
BIAS_ROWS = 16


def first_rows(half, tile):
    return half if half <= tile else (half // tile + 1) // 2 * tile


class Place:
    def __init__(self, count):
        self.count = count
        self.depth = count // 2
        self.me, self.shard = lax.axis_index("ctx"), lax.axis_index("fsdp")
        self.y, self.core = self.shard // 2, lax.rem(self.shard, 2)
        self.z, self.x = self.me // 2, lax.rem(self.me, 2)
        self.other_core = {"fsdp": 2 * self.y + 1 - self.core}
        self.other_y = {"fsdp": 2 * (1 - self.y) + self.core}
        self.other_x = {"ctx": 2 * self.z + 1 - self.x}

    def along_z(self, step):
        return lax.rem(self.z + step, self.depth)

    def peer_z(self, step):
        return {"ctx": 2 * self.along_z(step) + self.x}


def start(copies):
    for copy in copies:
        copy.start()


def added(a, b):
    return (a.astype(F32) + b.astype(F32)).astype(a.dtype)


class Reduction:
    def __init__(self, place, j, grad, out, head, buffers, load_sem, sems, z_sems):
        own, got, y_one, x_one, x_two, y_two, z_got = buffers
        self.place, self.out, self.head, self.own, self.buffers = place, out, head, own, buffers
        half, lanes = own.shape[3], own.shape[4]
        self.half = half
        p = place

        def remote(src, dst, slot, peer):
            return pltpu.make_async_remote_copy(
                src_ref=src,
                dst_ref=dst,
                send_sem=sems.at[0, j, slot],
                recv_sem=sems.at[1, j, slot],
                device_id=peer,
            )

        self.loads, self.firsts = [], []
        for side in range(2):
            columns = pl.ds(side * lanes, lanes)
            for low in range(2):
                slot = 2 * side + low
                self.loads.append(
                    pltpu.make_async_copy(
                        grad.at[:, low, p.core, :, columns],
                        own.at[side, :, low],
                        load_sem.at[j, slot],
                    )
                )
                self.firsts.append(
                    remote(
                        grad.at[:, low, 1 - p.core, :, columns],
                        got.at[side, :, low],
                        slot,
                        p.other_core,
                    )
                )
        self.second = [remote(own.at[1 - p.y, :, :, 0:head, :], y_one, 4, p.other_y)]
        self.third = [remote(own.at[p.y, :, 1 - p.x, 0:head, :], x_two, 5, p.other_x)]
        if head < half:
            self.second.append(remote(own.at[:, :, 1 - p.x, head:half, :], x_one, 6, p.other_x))
            self.third.append(remote(own.at[1 - p.y, :, p.x, head:half, :], y_two, 7, p.other_y))
        self.fourth = [
            pltpu.make_async_remote_copy(
                src_ref=own.at[p.y, p.along_z(step), p.x],
                dst_ref=z_got.at[p.z],
                send_sem=z_sems.at[0, j, step],
                recv_sem=z_sems.at[1, j, step],
                device_id=p.peer_z(step),
            )
            for step in range(1, p.depth)
        ]
        self.last = [remote(out.at[p.core], out.at[p.core], 8, p.other_core)]

    def stage_zero(self):
        start(self.loads)
        start(self.firsts)

    def stage_one(self):
        own, got = self.own, self.buffers[1]
        for copy in self.loads:
            copy.wait()
        for copy in self.firsts:
            copy.wait_recv()

        def body(block, carry):
            for side in range(2):
                for low in range(2):
                    own[side, block, low] = added(own[side, block, low], got[side, block, low])
            return carry

        lax.fori_loop(0, self.place.depth, body, 0)
        start(self.second)

    def stage_two(self):
        p, own, head, half = self.place, self.own, self.head, self.half
        y_one, x_one = self.buffers[2], self.buffers[3]
        for copy in self.second:
            copy.wait()

        def body(block, carry):
            for low in range(2):
                own[p.y, block, low, 0:head, :] = added(
                    own[p.y, block, low, 0:head, :], y_one[block, low]
                )
            if head < half:
                for side in range(2):
                    own[side, block, p.x, head:half, :] = added(
                        own[side, block, p.x, head:half, :], x_one[side, block]
                    )
            return carry

        lax.fori_loop(0, p.depth, body, 0)
        start(self.third)

    def stage_three(self):
        p, own, head, half = self.place, self.own, self.head, self.half
        x_two, y_two = self.buffers[4], self.buffers[5]
        for copy in self.third:
            copy.wait()

        def body(block, carry):
            own[p.y, block, p.x, 0:head, :] = added(
                own[p.y, block, p.x, 0:head, :], x_two[block]
            )
            if head < half:
                own[p.y, block, p.x, head:half, :] = added(
                    own[p.y, block, p.x, head:half, :], y_two[block]
                )
            return carry

        lax.fori_loop(0, p.depth, body, 0)
        start(self.fourth)

    def stage_four(self):
        p, z_got = self.place, self.buffers[6]
        for copy in self.fourth:
            copy.wait()
        total = self.own[p.y, p.z, p.x].astype(F32)
        for step in range(1, p.depth):
            total = total + z_got[p.along_z(step)].astype(F32)
        self.out[p.core] = total.astype(self.out.dtype)
        start(self.last)

    def stage_five(self):
        for copy in self.last:
            copy.wait()
        for copy in self.firsts:
            copy.wait_send()


def reduction_buffers(count, half, lanes, dtype):
    depth = count // 2
    head = first_rows(half, 16)
    tail = max(half - head, 16)
    shapes = (
        (2, depth, 2, half, lanes),
        (2, depth, 2, half, lanes),
        (depth, 2, head, lanes),
        (2, depth, tail, lanes),
        (depth, head, lanes),
        (depth, tail, lanes),
        (depth, half, lanes),
        (2, half, lanes),
    )
    return head, [pltpu.VMEM(shape, dtype) for shape in shapes]


def backward_kernel(width, heads, *refs):
    (
        starts_ref,
        flow_ref,
        docs_ref,
        got_ref,
        wide_ref,
        lse_ref,
        tok_ref,
        residual_ref,
        bias_ref,
        joint_ref,
        outer_grad,
        inner_grad,
        mixer_grad,
        tokens_out,
        outer_out,
        inner_out,
        mixer_out,
        joint_out,
        bias_out,
        flow_put,
        flow_got,
        put,
        home_got,
        key_rows,
        value_rows,
        key_t,
        key_docs,
        d_key,
        d_value,
        joint_all,
        joint_grad,
        d_turned,
        bias_sum,
        bias_got,
        bias_z,
        flow_sems,
        home_sems,
        own_sems,
        load_sem,
        sems,
        z_sems,
        bias_sems,
        *buffers,
    ) = refs
    count, units, _, lanes = got_ref.shape
    length = count * lanes
    depth = min(length, 1024)
    group = width // lanes
    pairs = H // 2
    total_units = MB * H
    p = Place(count)
    me = p.me
    mine = (total_units - me + count - 1) // count

    barrier = pltpu.get_barrier_semaphore()

    def greet(step, carry):
        pl.semaphore_signal(barrier, inc=1, device_id={"ctx": lax.rem(me + step, count)})
        return carry

    lax.fori_loop(1, count, greet, 0)
    pl.semaphore_signal(barrier, inc=1, device_id=p.other_core)
    pl.semaphore_signal(barrier, inc=1, device_id=p.other_y)
    joint_load = pltpu.make_async_copy(joint_ref, joint_all, own_sems.at[2, 0])
    joint_load.start()

    grads = (outer_grad, inner_grad, mixer_grad, joint_grad)
    outs = (outer_out, inner_out, mixer_out, joint_out)
    jobs = [
        Reduction(
            p,
            j,
            grads[j],
            buffers[8 * j + 7],
            heads[j],
            buffers[8 * j : 8 * j + 7],
            load_sem,
            sems,
            z_sems,
        )
        for j in range(4)
    ]
    outer_job, inner_job, mixer_job, joint_job = jobs

    pl.semaphore_wait(barrier, count + 1)
    for job in (outer_job, inner_job, mixer_job):
        job.stage_zero()

    def unit_copy(source, target, sem, owner, slot):
        return pltpu.make_async_remote_copy(
            src_ref=source.at[owner, slot],
            dst_ref=target.at[me, slot],
            send_sem=sem.at[0, owner, slot],
            recv_sem=sem.at[1, me, slot],
            device_id={"ctx": owner},
        )

    def unit_arrival(source, target, sem, sender, slot):
        return pltpu.make_async_remote_copy(
            src_ref=source.at[sender, slot],
            dst_ref=target.at[sender, slot],
            send_sem=sem.at[0, sender, slot],
            recv_sem=sem.at[1, sender, slot],
            device_id={"ctx": sender},
        )

    def unit_keep(source, target, kind, slot):
        return pltpu.make_async_copy(
            source.at[me, slot], target.at[me, slot], own_sems.at[kind, slot]
        )

    for pair in range(pairs):
        for batch in range(MB):
            block = flow_ref[
                batch * lanes : (batch + 1) * lanes, pair * 128 : (pair + 1) * 128
            ].T
            for j in range(2):
                unit = (2 * pair + j) * MB + batch
                flow_put[unit % count, unit // count] = block[j * HD : (j + 1) * HD]

    def send_flow(unit, carry):
        owner, slot = lax.rem(unit, count), unit // count

        @pl.when(owner != me)
        def _():
            unit_copy(flow_put, flow_got, flow_sems, owner, slot).start()

        @pl.when(owner == me)
        def _():
            unit_keep(flow_put, flow_got, 0, slot).start()

        return carry

    lax.fori_loop(0, total_units, send_flow, 0)
    outer_job.stage_one()
    inner_job.stage_one()
    mixer_job.stage_one()

    def unit_step(slot, carry):
        def wait_one(step, inner):
            unit_arrival(flow_put, flow_got, flow_sems, lax.rem(me + step, count), slot).wait_recv()
            return inner

        lax.fori_loop(1, count, wait_one, 0)
        unit_keep(flow_put, flow_got, 0, slot).wait()
        for i in range(count):
            rows = slice(i * lanes, (i + 1) * lanes)
            key_rows[rows, :] = got_ref[i, slot, HD : 2 * HD, :].T
            value_rows[rows, :] = got_ref[i, slot, 2 * HD : 3 * HD, :].T
            key_t[:, rows] = got_ref[i, slot, HD : 2 * HD, :]
        key_documents(starts_ref, slot, length, lanes, key_docs)
        d_key[...] = jnp.zeros_like(d_key)
        d_value[...] = jnp.zeros_like(d_value)

        def block(number, inner):
            begin = pl.multiple_of(number * width, width)

            def beside(ref):
                parts = [ref[number * group + i, slot, 0:HD, :] for i in range(group)]
                return parts[0] if group == 1 else jnp.concatenate(parts, axis=1)

            queries, flow = beside(got_ref), beside(flow_got)
            query_rows, flow_rows = queries.T, flow.T
            query_docs = docs_ref[slot, :, pl.ds(begin, width)]
            log_total = lse_ref[slot, :, pl.ds(begin, width)]
            spread = jnp.sum(
                flow.astype(F32) * wide_ref[slot, :, pl.ds(begin, width)], axis=0, keepdims=True
            )

            def chunk(index, d_query):
                first = pl.multiple_of(index * depth, depth)
                rows = pl.ds(first, depth)
                scores = jnp.dot(key_rows[rows, :], queries, preferred_element_type=F32)
                same = same_document(key_docs, first, depth, query_docs)
                probs = jnp.exp(jnp.where(same, scores, MASKED) - log_total)
                pressure = jnp.dot(value_rows[rows, :], flow, preferred_element_type=F32)
                d_scores = (probs * (pressure - spread)).astype(BF16)
                d_value[rows, :] += jnp.dot(
                    probs.astype(BF16), flow_rows, preferred_element_type=F32
                )
                d_key[rows, :] += jnp.dot(d_scores, query_rows, preferred_element_type=F32)
                return d_query + jnp.dot(key_t[:, rows], d_scores, preferred_element_type=F32)

            d_query = over_chunks(length // depth, chunk, jnp.zeros((HD, width), F32))
            low = (d_query * SCALE).astype(BF16)
            for i in range(group):
                put[number * group + i, slot, 0:HD, :] = low[:, i * lanes : (i + 1) * lanes]
            return inner

        lax.fori_loop(0, length // width, block, 0)
        for i in range(count):
            rows = slice(i * lanes, (i + 1) * lanes)
            put[i, slot, HD : 2 * HD, :] = d_key[rows, :].T.astype(BF16)
            put[i, slot, 2 * HD : 3 * HD, :] = d_value[rows, :].T.astype(BF16)

        def send_one(step, inner):
            unit_copy(put, home_got, home_sems, lax.rem(me + step, count), slot).start()
            return inner

        lax.fori_loop(1, count, send_one, 0)
        unit_keep(put, home_got, 1, slot).start()

        @pl.when(slot == 1)
        def _():
            outer_job.stage_two()

        @pl.when(slot == 3)
        def _():
            inner_job.stage_two()

        return carry

    lax.fori_loop(0, mine, unit_step, 0)
    mixer_job.stage_two()
    outer_job.stage_three()

    bias_sum[0] = bias_ref[...]
    ones = jnp.ones((8, MB * lanes), BF16)
    for pair in range(pairs):
        columns = []
        for batch in range(MB):
            blocks = []
            for j in range(2):
                unit = (2 * pair + j) * MB + batch
                owner, slot = unit % count, unit // count

                @pl.when(owner != me)
                def _():
                    unit_arrival(put, home_got, home_sems, owner, slot).wait_recv()

                @pl.when(owner == me)
                def _():
                    unit_keep(put, home_got, 1, slot).wait()

                blocks.append(home_got[owner, slot])
            rows = [b[third * HD : (third + 1) * HD] for third in range(3) for b in blocks]
            columns.append(jnp.concatenate(rows, axis=0))
        d_pair = jnp.concatenate(columns, axis=1)
        d_turned[pair] = d_pair.T
        grad = jnp.dot(d_pair, tok_ref[...], preferred_element_type=F32).astype(BF16)
        half = joint_grad.shape[3]
        for third in range(3):
            row, end = third * D + pair * 128, third * D + (pair + 1) * 128
            while row < end:
                block, inside = row // half, row % half
                size = min(end - row, half - inside)
                taken = row - third * D - pair * 128 + third * 128
                joint_grad[block // 4, block // 2 % 2, block % 2, inside : inside + size, :] = (
                    grad[taken : taken + size]
                )
                row += size
        sums = lax.dot_general(
            ones, d_pair, (((1,), (1,)), ((), ())), preferred_element_type=F32
        )
        bias_sum[0, 0:1, pair * 128 : (pair + 1) * 128] = sums[0:1, 0:128]
        bias_sum[0, 1:2, pair * 128 : (pair + 1) * 128] = sums[0:1, 256:384]

    joint_job.stage_zero()

    def bias_copy(level, peer):
        return pltpu.make_async_remote_copy(
            src_ref=bias_sum.at[level],
            dst_ref=bias_got.at[level],
            send_sem=bias_sems.at[0, level],
            recv_sem=bias_sems.at[1, level],
            device_id=peer,
        )

    bias_steps = [
        bias_copy(0, p.other_core),
        bias_copy(1, p.other_y),
        bias_copy(2, p.other_x),
    ]
    bias_last = [
        pltpu.make_async_remote_copy(
            src_ref=bias_sum.at[3],
            dst_ref=bias_z.at[p.z],
            send_sem=bias_sems.at[0, 3 + step],
            recv_sem=bias_sems.at[1, 3 + step],
            device_id=p.peer_z(step),
        )
        for step in range(1, p.depth)
    ]

    def bias_level(level):
        bias_steps[level].wait()
        bias_sum[level + 1] = bias_sum[level] + bias_got[level]

    bias_steps[0].start()
    inner_job.stage_three()
    mixer_job.stage_three()
    joint_job.stage_one()
    bias_level(0)
    bias_steps[1].start()

    joint_load.wait()
    total = residual_ref[...]
    for pair in range(pairs):
        total = total + lax.dot_general(
            d_turned[pair],
            joint_all[pair],
            (((1,), (1,)), ((), ())),
            preferred_element_type=F32,
        )
    tokens_out[...] = total

    bias_level(1)
    bias_steps[2].start()
    joint_job.stage_two()
    bias_level(2)
    start(bias_last)
    outer_job.stage_four()
    inner_job.stage_four()
    joint_job.stage_three()
    mixer_job.stage_four()

    def finish(j):
        jobs[j].stage_five()
        whole = buffers[8 * j + 7]
        lanes_half = whole.shape[2] // 2
        rows = jnp.concatenate([whole[0], whole[1]], axis=0).astype(F32)
        rows = jnp.where(p.core == 0, rows[:, :lanes_half], rows[:, lanes_half:])
        outs[j][...] = rows.T

    finish(0)
    finish(1)
    finish(2)
    for copy in bias_last:
        copy.wait()
    bias_total = bias_sum[3]
    for step in range(1, p.depth):
        bias_total = bias_total + bias_z[p.along_z(step)]
    bias_out[...] = bias_total

    def sent(unit, carry):
        @pl.when(lax.rem(unit, count) != me)
        def _():
            unit_copy(flow_put, flow_got, flow_sems, lax.rem(unit, count), unit // count).wait_send()

        return carry

    lax.fori_loop(0, total_units, sent, 0)

    def returned(slot, carry):
        def one(step, inner):
            unit_copy(put, home_got, home_sems, lax.rem(me + step, count), slot).wait_send()
            return inner

        lax.fori_loop(1, count, one, 0)
        return carry

    lax.fori_loop(0, mine, returned, 0)
    joint_job.stage_four()
    finish(3)


def backward(
    starts, flow, docs, got, wide, lse, source, residual, biases, joint, outer, inner, mixer, number
):
    count, units, _, lanes = got.shape
    length = count * lanes
    width = 2 * lanes
    pairs = H // 2
    vm = pl.BlockSpec(memory_space=pltpu.VMEM)
    hbm = pl.BlockSpec(memory_space=pl.ANY)
    dma = pltpu.SemaphoreType.DMA
    half_joint = 3 * D // (2 * count)
    grads = [g.reshape(count // 2, 2, 2, -1, g.shape[1]) for g in (outer, inner, mixer)]
    shapes = [(g.shape[3], g.shape[4] // 2) for g in grads] + [(half_joint, D // 2)]
    heads, buffers = [], []
    for half, width_half in shapes:
        head, some = reduction_buffers(count, half, width_half, BF16)
        heads.append(head)
        buffers += some
    outs = [jax.ShapeDtypeStruct((w // 2, 2 * half), F32) for half, w in shapes]
    return pl.pallas_call(
        functools.partial(backward_kernel, width, tuple(heads)),
        out_shape=(
            jax.ShapeDtypeStruct(residual.shape, F32),
            *outs,
            jax.ShapeDtypeStruct((BIAS_ROWS, D), F32),
        ),
        in_specs=[pl.BlockSpec(memory_space=pltpu.SMEM)] + [vm] * 8 + [hbm] * 4,
        out_specs=(vm,) * 6,
        scratch_shapes=[
            pltpu.VMEM((count, units, HD, lanes), BF16),
            pltpu.VMEM((count, units, HD, lanes), BF16),
            pltpu.VMEM((count, units, 3 * HD, lanes), BF16),
            pltpu.VMEM((count, units, 3 * HD, lanes), BF16),
            pltpu.VMEM((length, HD), BF16),
            pltpu.VMEM((length, HD), BF16),
            pltpu.VMEM((HD, length), BF16),
            pltpu.VMEM((length, lanes), jnp.int32),
            pltpu.VMEM((length, HD), F32),
            pltpu.VMEM((length, HD), F32),
            pltpu.VMEM((pairs, D, 384), BF16),
            pltpu.VMEM((count // 2, 2, 2, half_joint, D), BF16),
            pltpu.VMEM((pairs, MB * lanes, 384), BF16),
            pltpu.VMEM((4, BIAS_ROWS, D), F32),
            pltpu.VMEM((3, BIAS_ROWS, D), F32),
            pltpu.VMEM((count // 2, BIAS_ROWS, D), F32),
            dma((2, count, units)),
            dma((2, count, units)),
            dma((3, units)),
            dma((4, 4)),
            dma((2, 4, 9)),
            dma((2, 4, count // 2)),
            dma((2, 3 + count // 2)),
            *buffers,
        ],
        compiler_params=pltpu.CompilerParams(
            collective_id=number, has_side_effects=True, vmem_limit_bytes=62 * 1024 * 1024
        ),
        name="backward",
    )(starts, flow, docs, got, wide, lse, source, residual, biases, joint, *grads)


def on_device(
    count,
    shards,
    tokens,
    doc_starts,
    joint_weight,
    mixer_weight,
    inner_weight,
    outer_weight,
    query_bias,
    value_bias,
    mixer_bias,
    first_gain,
    first_shift,
    inner_bias,
    outer_bias,
    second_gain,
    second_shift,
    upstream,
):
    rows = tokens.shape[2]
    length = rows * count
    units = -(-MB * H // count)
    me = lax.axis_index("ctx")

    part = D // shards
    vectors = jnp.stack(
        [
            query_bias,
            value_bias,
            mixer_bias,
            first_gain,
            first_shift,
            outer_bias,
            second_gain,
            second_shift,
        ]
    )
    vectors = jnp.pad(vectors, ((0, 8), (0, D - part)))
    vectors = vectors.at[8].set(inner_bias)
    source = tokens.reshape(MB * rows, D)
    unit_ids = jnp.arange(units, dtype=jnp.int32) * count + me
    unit_starts = doc_starts[:, 0][lax.rem(unit_ids, MB)]
    positions = jnp.arange(length, dtype=jnp.int32)
    unit_docs = jax.vmap(lambda s: doc_index(positions, s))(unit_starts)[:, None, :]

    attended, received, wide, lse, joint, vectors, mixer, inner, outer = forward(
        count,
        unit_starts,
        source,
        unit_docs,
        joint_weight,
        vectors,
        mixer_weight,
        inner_weight,
        outer_weight,
        0,
    )
    joint = joint.reshape(H // 2, D, 384)
    mixer, inner, outer = mixer.reshape(D, D), inner.reshape(D, FF), outer.reshape(FF, D)
    heads_of = [
        vectors[:, i, :part].reshape(D).astype(F32)
        for i in range(8)
    ]
    _, _, mbias, gain_one, shift_one, obias, gain_two, shift_two = heads_of
    ibias = vectors[:, 8].reshape(FF).astype(F32)

    branch = mul_nn(attended, mixer) + mbias
    first, first_normed, first_recip = norm_forward(
        source.astype(F32) + branch, gain_one, shift_one
    )
    first_low = first.astype(BF16)
    inner_pre = mul_nn(first_low, inner) + ibias
    activated, gelu_slope = gelu_parts(inner_pre)
    activated_low = activated.astype(BF16)
    outer_out = mul_nn(activated_low, outer) + obias
    final, second_normed, second_recip = norm_forward(first + outer_out, gain_two, shift_two)
    result = final.astype(BF16).reshape(MB, 1, rows, D)

    incoming = upstream.reshape(MB * rows, D).astype(F32)
    rescale_grad = jnp.sum(incoming * second_normed, axis=0)
    reshift_grad = jnp.sum(incoming, axis=0)
    d_second = norm_backward(incoming, second_normed, second_recip, gain_two)
    d_outer = d_second.astype(BF16)
    return_grad = jnp.sum(d_outer.astype(F32), axis=0)
    outer_grad = mul_tn(d_outer, activated_low)
    d_inner = (mul_nt(d_outer, outer) * gelu_slope).astype(BF16)
    hidden_grad = jnp.sum(d_inner.astype(F32), axis=0)
    inner_grad = mul_tn(d_inner, first_low)
    d_first = d_second + mul_nt(d_inner, inner)
    scale_grad = jnp.sum(d_first * first_normed, axis=0)
    shift_grad = jnp.sum(d_first, axis=0)
    d_residual = norm_backward(d_first, first_normed, first_recip, gain_one)
    d_branch = d_residual.astype(BF16)
    mixing_grad = jnp.sum(d_branch.astype(F32), axis=0)
    mixer_grad = mul_tn(d_branch, attended)
    world = count * shards
    index = me * shards + lax.axis_index("fsdp")
    sums = [
        mixing_grad,
        scale_grad,
        shift_grad,
        return_grad,
        rescale_grad,
        reshift_grad,
        *hidden_grad.reshape(FF // D, D),
    ]
    turned = [outer_grad, inner_grad, mixer_grad]
    if shards == 4 and count % 2 == 0 and D % (32 * count) == 0:
        flow = mul_nt(d_branch, mixer).astype(BF16)
        biases = jnp.pad(jnp.stack(sums), ((2, BIAS_ROWS - 2 - len(sums)), (0, 0)))
        tokens_grad, *blocks, biases = backward(
            unit_starts,
            flow,
            unit_docs,
            received,
            wide,
            lse,
            source,
            d_residual,
            biases,
            joint,
            *[g.astype(BF16) for g in turned],
            1,
        )
    else:
        natural = joint.reshape(H // 2, D, 3, 128).transpose(1, 2, 0, 3).reshape(D, 3 * D)
        flow = mul_nt(mixer, d_branch).astype(BF16)
        flow_units = exchange(to_units(flow, 1, count, units), 2)
        d_units = attend_back(received, flow_units, unit_starts, unit_docs, wide, lse)
        d_joint = from_units(exchange(d_units, 3), 3)
        bias_sums = jnp.sum(d_joint.astype(F32), axis=1)
        turned.append(mul_nn(d_joint, source))
        tokens_grad = d_residual + mul_tt(d_joint, natural)

        def reduced(grad):
            over_lanes = lax.psum_scatter(
                grad.astype(BF16), "fsdp", scatter_dimension=1, tiled=True
            )
            over_rows = lax.psum_scatter(over_lanes, "ctx", scatter_dimension=0, tiled=True)
            return over_rows.T.astype(F32)

        blocks = [reduced(g) for g in turned]
        biases = jnp.stack([bias_sums[:D], bias_sums[2 * D :], *sums])
        biases = lax.psum(biases, ("ctx", "fsdp"))
    tokens_grad = tokens_grad.reshape(MB, 1, rows, D)
    outer_out_grad, inner_out, mixer_out, joint_out = blocks
    own = lax.dynamic_slice_in_dim(biases[:8], index * (D // world), D // world, 1)
    hidden_rows = biases[8 : 8 + FF // D].reshape(FF)
    own_hidden = lax.dynamic_slice_in_dim(hidden_rows, index * (FF // world), FF // world, 0)
    sums = [*own[:5], own_hidden, *own[5:]]
    return (result, tokens_grad, joint_out, mixer_out, inner_out, outer_out_grad, *sums)


def solution(mesh):
    in_specs = (
        P(None, "fsdp", "ctx", None),
        P(None, "fsdp", None),
        P("fsdp", None),
        P("fsdp", None),
        P("fsdp", None),
        P("fsdp", None),
        P("fsdp"),
        P("fsdp"),
        P("fsdp"),
        P("fsdp"),
        P("fsdp"),
        P("fsdp"),
        P("fsdp"),
        P("fsdp"),
        P("fsdp"),
        P(None, "fsdp", "ctx", None),
    )
    out_specs = (
        P(None, "fsdp", "ctx", None),
        P(None, "fsdp", "ctx", None),
        P("fsdp", "ctx"),
        P("fsdp", "ctx"),
        P("fsdp", "ctx"),
        P("fsdp", "ctx"),
        P(("ctx", "fsdp")),
        P(("ctx", "fsdp")),
        P(("ctx", "fsdp")),
        P(("ctx", "fsdp")),
        P(("ctx", "fsdp")),
        P(("ctx", "fsdp")),
        P(("ctx", "fsdp")),
        P(("ctx", "fsdp")),
        P(("ctx", "fsdp")),
    )
    return jax.shard_map(
        functools.partial(on_device, mesh.shape["ctx"], mesh.shape["fsdp"]),
        mesh=mesh,
        in_specs=in_specs,
        out_specs=out_specs,
        check_vma=False,
    )
```

```python
import functools
import math

import jax
import jax.numpy as jnp
from jax import lax
from jax.experimental import pallas as pl
from jax.experimental.pallas import tpu as pltpu
from jax.sharding import PartitionSpec as P

D = 768
H = 12
HD = 64
FF = 3072
MB = 3

SCALE = 0.125
EPSILON = 1e-12
MASKED = -1000000000.0
ROOT_HALF = 0.7071067811865476
GAUSS_PEAK = 0.3989422804014327

F32 = jnp.float32
BF16 = jnp.bfloat16


def norm_forward(hidden, gain, shift):
    average = jnp.mean(hidden, axis=-1, keepdims=True)
    centred = hidden - average
    reciprocal = lax.rsqrt(jnp.mean(centred * centred, axis=-1, keepdims=True) + EPSILON)
    normed = centred * reciprocal
    return (normed * gain + shift, normed, reciprocal)


def norm_backward(incoming, normed, reciprocal, gain):
    scaled = incoming * gain
    return reciprocal * (
        scaled
        - jnp.mean(scaled, axis=-1, keepdims=True)
        - normed * jnp.mean(scaled * normed, axis=-1, keepdims=True)
    )


def gelu_parts(inner):
    cumulative = 0.5 * (1.0 + lax.erf(inner * ROOT_HALF))
    return (inner * cumulative, cumulative + inner * jnp.exp(-0.5 * inner * inner) * GAUSS_PEAK)


UNITS = MB * H
BIAS_ROWS = 16
RELAY_PIECES = 3


def spare_owner(count, j):
    stride = count // (UNITS % count)
    return j * stride + (j % 2 if stride > 1 else 0)


def owner_of(count, unit):
    full, rest = UNITS // count, UNITS % count
    if rest == 0:
        return unit % count
    if full == 0:
        return spare_owner(count, unit)
    late = unit // (full * count)
    return (1 - late) * (unit % count) + late * spare_owner(count, unit - full * count)


def spare_index(count, device):
    return device // (count // (UNITS % count))


def owned(count, device):
    full, rest = UNITS // count, UNITS % count
    if rest == 0:
        return full
    j = spare_index(count, device)
    extra = (spare_owner(count, j) == device) & (j < rest)
    return full + extra.astype(jnp.int32)


def batch_of(count, device, slot):
    full, rest = UNITS // count, UNITS % count
    if rest == 0:
        return (slot * count + device) % MB
    if full == 0:
        return jnp.minimum(spare_index(count, device), UNITS - 1) % MB
    late = slot // full
    unit = slot * count + (1 - late) * device + late * spare_index(count, device)
    return unit % MB


def exchange_kernel(count, x_ref, y_ref, held, send_sem, recv_sem, own_sem):
    me = lax.axis_index("ctx")
    barrier = pltpu.get_barrier_semaphore()

    def greet(step, carry):
        peer = lax.rem(me + step, count)
        pl.semaphore_signal(barrier, inc=1, device_id={"ctx": peer})
        return carry

    lax.fori_loop(1, count, greet, 0)
    own_in = pltpu.make_async_copy(x_ref.at[me], held, own_sem)
    own_in.start()
    pl.semaphore_wait(barrier, count - 1)

    def transfer(step):
        peer = lax.rem(me + step, count)
        return pltpu.make_async_remote_copy(
            src_ref=x_ref.at[peer],
            dst_ref=y_ref.at[me],
            send_sem=send_sem.at[step],
            recv_sem=recv_sem.at[step],
            device_id={"ctx": peer},
        )

    def begin(step, carry):
        transfer(step).start()
        return carry

    lax.fori_loop(1, count, begin, 0)
    own_in.wait()
    own_out = pltpu.make_async_copy(held, y_ref.at[me], own_sem)
    own_out.start()
    own_out.wait()

    def finish(step, carry):
        transfer(step).wait()
        return carry

    lax.fori_loop(1, count, finish, 0)


def exchange(x, number):
    count = x.shape[0]
    return pl.pallas_call(
        functools.partial(exchange_kernel, count),
        out_shape=jax.ShapeDtypeStruct(x.shape, x.dtype),
        in_specs=[pl.BlockSpec(memory_space=pl.ANY)],
        out_specs=pl.BlockSpec(memory_space=pl.ANY),
        scratch_shapes=[
            pltpu.VMEM(x.shape[1:], x.dtype),
            pltpu.SemaphoreType.DMA((count,)),
            pltpu.SemaphoreType.DMA((count,)),
            pltpu.SemaphoreType.DMA,
        ],
        compiler_params=pltpu.CompilerParams(collective_id=number, has_side_effects=True),
        name=f"exchange_{number}",
    )(x)


def across(ref, first, rows, width, lanes):
    parts = [ref[first + i, 0, rows, :] for i in range(width // lanes)]
    return parts[0] if len(parts) == 1 else jnp.concatenate(parts, axis=1)


def document(starts_ref, batch, position):
    docs = jnp.zeros(position.shape, jnp.int32) - 1
    for j in range(starts_ref.shape[1]):
        docs = docs + jnp.where(position >= starts_ref[batch, j], 1, 0)
    return docs


def key_documents(starts_ref, batch, key_docs):
    key_docs[...] = document(
        starts_ref, batch, lax.broadcasted_iota(jnp.int32, key_docs.shape, 0)
    )


def query_documents(starts_ref, batch, begin, width):
    return document(
        starts_ref, batch, lax.broadcasted_iota(jnp.int32, (1, width), 1) + begin
    )


def same_document(key_docs, first, width, query_docs):
    keys = key_docs[pl.ds(first, width), :]
    lanes = keys.shape[1]
    parts = [keys == query_docs[:, i : i + lanes] for i in range(0, query_docs.shape[1], lanes)]
    return parts[0] if len(parts) == 1 else jnp.concatenate(parts, axis=1)


def over_chunks(chunks, body, carry):
    if chunks == 1:
        return body(0, carry)
    return lax.fori_loop(0, chunks, body, carry)


def attend_back_kernel(
    width,
    starts_ref,
    x_ref,
    flow_ref,
    wide_ref,
    lse_ref,
    d_ref,
    key_rows,
    value_rows,
    key_t,
    key_docs,
    d_key,
    d_value,
):
    count, _, _, lanes = x_ref.shape
    length = count * lanes
    depth = min(length, 1024)
    unit = pl.program_id(0)
    for i in range(count):
        rows = slice(i * lanes, (i + 1) * lanes)
        key_rows[rows, :] = x_ref[i, 0, HD : 2 * HD, :].T
        value_rows[rows, :] = x_ref[i, 0, 2 * HD : 3 * HD, :].T
        key_t[:, rows] = x_ref[i, 0, HD : 2 * HD, :]
    batch = batch_of(count, lax.axis_index("ctx"), unit)
    key_documents(starts_ref, batch, key_docs)
    d_key[...] = jnp.zeros_like(d_key)
    d_value[...] = jnp.zeros_like(d_value)
    group = width // lanes

    def block(number, carry):
        begin = pl.multiple_of(number * width, width)
        queries = across(x_ref, number * group, slice(0, HD), width, lanes)
        flow = across(flow_ref, number * group, slice(0, HD), width, lanes)
        query_rows = queries.T
        flow_rows = flow.T
        query_docs = query_documents(starts_ref, batch, begin, width)
        log_total = lse_ref[0, :, pl.ds(begin, width)]
        spread = jnp.sum(
            flow.astype(F32) * wide_ref[0, :, pl.ds(begin, width)], axis=0, keepdims=True
        )

        def chunk(index, d_query):
            first = pl.multiple_of(index * depth, depth)
            rows = pl.ds(first, depth)
            scores = jnp.dot(key_rows[rows, :], queries, preferred_element_type=F32)
            same = same_document(key_docs, first, depth, query_docs)
            probs = jnp.exp(jnp.where(same, scores, MASKED) - log_total)
            pressure = jnp.dot(value_rows[rows, :], flow, preferred_element_type=F32)
            d_scores = (probs * (pressure - spread)).astype(BF16)
            d_value[rows, :] += jnp.dot(
                probs.astype(BF16), flow_rows, preferred_element_type=F32
            )
            d_key[rows, :] += jnp.dot(d_scores, query_rows, preferred_element_type=F32)
            return d_query + jnp.dot(key_t[:, rows], d_scores, preferred_element_type=F32)

        d_query = over_chunks(length // depth, chunk, jnp.zeros((HD, width), F32))
        low = (d_query * SCALE).astype(BF16)
        for i in range(group):
            d_ref[number * group + i, 0, 0:HD, :] = low[:, i * lanes : (i + 1) * lanes]
        return carry

    lax.fori_loop(0, length // width, block, 0)
    for i in range(count):
        rows = slice(i * lanes, (i + 1) * lanes)
        d_ref[i, 0, HD : 2 * HD, :] = d_key[rows, :].T.astype(BF16)
        d_ref[i, 0, 2 * HD : 3 * HD, :] = d_value[rows, :].T.astype(BF16)


def unit_block(*dims):
    return pl.BlockSpec(dims, lambda u, starts: (0, u) + (0,) * (len(dims) - 2))


def own_block(*dims):
    return pl.BlockSpec(dims, lambda u, starts: (u,) + (0,) * (len(dims) - 1))


def attend_back(x, flow, starts, wide, lse):
    count, units, _, lanes = x.shape
    length = count * lanes
    width = 2 * lanes if count % 2 == 0 else lanes
    return pl.pallas_call(
        functools.partial(attend_back_kernel, width),
        out_shape=jax.ShapeDtypeStruct(x.shape, BF16),
        grid_spec=pltpu.PrefetchScalarGridSpec(
            num_scalar_prefetch=1,
            grid=(units,),
            in_specs=[
                unit_block(count, 1, 3 * HD, lanes),
                unit_block(count, 1, HD, lanes),
                own_block(1, HD, length),
                own_block(1, 1, length),
            ],
            out_specs=unit_block(count, 1, 3 * HD, lanes),
            scratch_shapes=[
                pltpu.VMEM((length, HD), BF16),
                pltpu.VMEM((length, HD), BF16),
                pltpu.VMEM((HD, length), BF16),
                pltpu.VMEM((length, lanes), jnp.int32),
                pltpu.VMEM((length, HD), F32),
                pltpu.VMEM((length, HD), F32),
            ],
        ),
        compiler_params=pltpu.CompilerParams(dimension_semantics=("arbitrary",)),
        name="attend_back",
    )(starts, x, flow, wide, lse)


def to_units(columns, parts, count, units):
    rows = columns.shape[1] // MB
    x = columns.reshape(parts, H, HD, MB, rows).transpose(1, 3, 0, 2, 4)
    x = x.reshape(UNITS, parts * HD, rows)
    places = [owner_of(count, u) * units + u // count for u in range(UNITS)]
    y = jnp.zeros((count * units, parts * HD, rows), columns.dtype)
    return y.at[jnp.array(places)].set(x).reshape(count, units, parts * HD, rows)


def from_units(x, parts):
    count, units, _, rows = x.shape
    places = [owner_of(count, u) * units + u // count for u in range(UNITS)]
    x = x.reshape(count * units, parts * HD, rows)[jnp.array(places)]
    x = x.reshape(H, MB, parts, HD, rows).transpose(2, 0, 3, 1, 4)
    return x.reshape(parts * D, MB * rows)


def mul_nn(a, b):
    return jnp.dot(a, b, preferred_element_type=F32)


def mul_tn(a, b):
    return lax.dot_general(a, b, (((0,), (0,)), ((), ())), preferred_element_type=F32)


def mul_nt(a, b):
    return lax.dot_general(a, b, (((1,), (1,)), ((), ())), preferred_element_type=F32)


def mul_tt(a, b):
    return lax.dot_general(a, b, (((0,), (1,)), ((), ())), preferred_element_type=F32)


def forward_kernel(
    width,
    starts_ref,
    tok_ref,
    joint_ref,
    mixer_ref,
    inner_ref,
    outer_ref,
    *refs,
):
    vec_refs = refs[:9]
    (
    att_ref,
    got_ref,
    wide_ref,
    lse_ref,
    joint_out,
    vec_out,
    mixer_out,
    inner_out,
    outer_out,
    joint_all,
    vec_put,
    bias_rows,
    put,
    back_put,
    back_got,
    key_rows,
    value_t,
    key_docs,
    mixer_own,
    inner_own,
    outer_own,
    put_sem,
    got_sem,
    back_put_sem,
    back_got_sem,
    joint_sems,
    weight_sems,
    relay_sems,
    own_sems,
    ) = refs[9:]
    count, units, _, lanes = got_ref.shape
    length = count * lanes
    depth = min(length, 1024)
    group = width // lanes
    pairs = H // 2
    total_units = MB * H
    part = joint_ref.shape[0]
    me, shard = lax.axis_index("ctx"), lax.axis_index("fsdp")
    y, core = shard // 2, lax.rem(shard, 2)
    x = lax.rem(me, 2)
    far = 2 * (1 - y) + core
    other_core = {"fsdp": 2 * y + 1 - core}
    other_y = {"fsdp": far}
    other_x = {"ctx": me + 1 - 2 * x}
    mine = owned(count, me)

    barrier = pltpu.get_barrier_semaphore()

    def greet(step, carry):
        pl.semaphore_signal(barrier, inc=1, device_id={"ctx": lax.rem(me + step, count)})
        return carry

    lax.fori_loop(1, count, greet, 0)
    pl.semaphore_signal(barrier, inc=1, device_id=other_core)
    pl.semaphore_signal(barrier, inc=1, device_id=other_y)

    def remote(src, dst, sems, index, peer):
        return pltpu.make_async_remote_copy(
            src_ref=src,
            dst_ref=dst,
            send_sem=sems.at[(0, *index)],
            recv_sem=sems.at[(1, *index)],
            device_id=peer,
        )

    def own_joint(pair, third):
        columns = pl.ds(pl.multiple_of(third * D + pair * 128, 128), 128)
        return pltpu.make_async_copy(
            joint_ref.at[:, columns],
            joint_all.at[pair, shard, :, pl.ds(third * 128, 128)],
            own_sems.at[0, pair, third],
        )

    def joint_copy(kind, pair, third, which, peer, source=None):
        here = joint_all.at[pair, which, :, pl.ds(third * 128, 128)]
        if source is None:
            source = here
        else:
            source = source.at[:, pl.ds(pl.multiple_of(third * D + pair * 128, 128), 128)]
        return remote(source, here, joint_sems, (kind, pair, third), peer)

    def joint_y(pair, third):
        return joint_copy(0, pair, third, shard, other_y, joint_ref)

    def joint_core(pair, third):
        return joint_copy(1, pair, third, shard, other_core, joint_ref)

    def joint_pass(pair, third):
        return joint_copy(2, pair, third, far, other_core)

    def joint_store(pair):
        return pltpu.make_async_copy(
            joint_all.at[pair], joint_out.at[pair], own_sems.at[0, pair, 0]
        )

    def each_third(pair, make, act):
        for third in range(3):
            getattr(make(pair, third), act)()

    def every_pair(make, act):
        def body(pair, carry):
            each_third(pair, make, act)
            return carry

        lax.fori_loop(0, pairs, body, 0)

    every_pair(own_joint, "start")
    wholes = ((mixer_ref, mixer_own, mixer_out), (inner_ref, inner_own, inner_out), (outer_ref, outer_own, outer_out))
    own_in = [
        pltpu.make_async_copy(ref, held, own_sems.at[1, i, 0])
        for i, (ref, held, _) in enumerate(wholes)
    ]
    own_out = [
        pltpu.make_async_copy(held, out.at[shard], own_sems.at[1, i, 1])
        for i, (_, held, out) in enumerate(wholes)
    ]
    for copy in own_in:
        copy.start()
    for i, ref in enumerate(vec_refs):
        vec_put[i : i + 1, 0 : ref.shape[0]] = ref[...].astype(F32).reshape(1, ref.shape[0])
    vec_out[shard] = vec_put[...]
    pl.semaphore_wait(barrier, count + 1)

    vec_y = remote(vec_put, vec_out.at[shard], weight_sems, (0, 0), other_y)
    vec_core = remote(vec_put, vec_out.at[shard], weight_sems, (0, 1), other_core)
    vec_pass = remote(vec_out.at[far], vec_out.at[far], weight_sems, (0, 2), other_core)
    mixer_y = remote(mixer_ref, mixer_out.at[shard], weight_sems, (1, 0), other_y)
    mixer_core = remote(mixer_ref, mixer_out.at[shard], weight_sems, (1, 1), other_core)
    mixer_pass = remote(mixer_out.at[far], mixer_out.at[far], weight_sems, (1, 2), other_core)
    class Relayed:
        def __init__(self, ref, out, index):
            size = ref.shape[0] // 2
            piece = size // RELAY_PIECES
            self.over_y, self.over_x = [], []
            for k in range(RELAY_PIECES):
                rows = pl.ds(pl.multiple_of(x * size + k * piece, piece), piece)
                self.over_y.append(
                    remote(
                        ref.at[rows, :],
                        out.at[shard, rows, :],
                        relay_sems,
                        (index, 0, k),
                        other_y,
                    )
                )
                passed = out.at[far, rows, :]
                self.over_x.append(remote(passed, passed, relay_sems, (index, 1, k), other_x))
            self.core = remote(ref, out.at[shard], weight_sems, (2 + index, 0), other_core)
            self.all = remote(out.at[far], out.at[far], weight_sems, (2 + index, 1), other_core)

        def begin(self):
            for copy in self.over_y:
                copy.start()
            self.core.start()

        def relay(self, k):
            self.over_y[k].wait_recv()
            self.over_x[k].start()

        def hand_on(self):
            for copy in self.over_x:
                copy.wait_recv()
            self.all.start()

        def end(self):
            for copy in self.over_y + self.over_x:
                copy.wait_send()
            self.core.wait()
            self.all.wait()

    outer_way = Relayed(outer_ref, outer_out, 0)
    inner_way = Relayed(inner_ref, inner_out, 1)
    vec_y.start()
    vec_core.start()

    def send_joint(pair, carry):
        each_third(pair, joint_y, "start")
        each_third(pair, joint_core, "start")
        return carry

    lax.fori_loop(0, pairs, send_joint, 0)
    outer_way.begin()
    inner_way.begin()
    mixer_y.start()
    mixer_core.start()
    for first, second in zip(own_in, own_out):
        first.wait()
        second.start()

    vec_y.wait_recv()
    vec_pass.start()
    vec_core.wait_recv()
    vec_pass.wait_recv()

    def bias_of(slot):
        pieces = [
            vec_out[f, slot : slot + 1, 0:part] for f in range(4)
        ]
        return jnp.concatenate(pieces, axis=1)

    query_bias, value_bias = bias_of(0), bias_of(1)
    for pair in range(pairs):
        columns = slice(pair * 128, (pair + 1) * 128)
        bias_rows[pair, :, 0:128] = jnp.broadcast_to(query_bias[:, columns], (8, 128))
        bias_rows[pair, :, 128:256] = jnp.zeros((8, 128), F32)
        bias_rows[pair, :, 256:384] = jnp.broadcast_to(value_bias[:, columns], (8, 128))

    def sent_sem(unit):
        return owner_of(count, unit), unit // count

    def send_copy(unit):
        owner, slot = sent_sem(unit)
        return pltpu.make_async_remote_copy(
            src_ref=put.at[owner, slot],
            dst_ref=got_ref.at[me, slot],
            send_sem=put_sem.at[owner, slot],
            recv_sem=got_sem.at[me, slot],
            device_id={"ctx": owner},
        )

    def keep_copy(slot):
        return pltpu.make_async_copy(
            put.at[me, slot], got_ref.at[me, slot], own_sems.at[2, slot, 0]
        )

    def project(pair, carry):
        each_third(pair, own_joint, "wait")
        each_third(pair, joint_y, "wait_recv")
        each_third(pair, joint_pass, "start")
        each_third(pair, joint_core, "wait_recv")
        each_third(pair, joint_pass, "wait_recv")
        joint_store(pair).start()
        weight = joint_all[pair].reshape(4 * part, 384)
        rows = jnp.dot(tok_ref[...], weight, preferred_element_type=F32)
        rows = (rows + bias_rows[pair, 0:1, :]).astype(BF16)
        for third in range(3):
            for batch in range(MB):
                block = rows[batch * lanes : (batch + 1) * lanes, third * 128 : (third + 1) * 128]
                turned = block.T
                if third == 0:
                    turned = turned * SCALE
                for j in range(2):
                    unit = (2 * pair + j) * MB + batch
                    put[owner_of(count, unit), unit // count, third * HD : (third + 1) * HD, :] = (
                        turned[j * HD : (j + 1) * HD]
                    )
        for i in range(2 * MB):
            unit = 2 * pair * MB + lax.rem(i + me, 2 * MB)
            owner, slot = owner_of(count, unit), unit // count

            @pl.when(owner != me)
            def _():
                send_copy(unit).start()

            @pl.when(owner == me)
            def _():
                keep_copy(slot).start()

        return carry

    lax.fori_loop(0, pairs, project, 0)

    def arrival(sender, slot):
        return pltpu.make_async_remote_copy(
            src_ref=put.at[sender, slot],
            dst_ref=got_ref.at[sender, slot],
            send_sem=put_sem.at[sender, slot],
            recv_sem=got_sem.at[sender, slot],
            device_id={"ctx": sender},
        )

    def back_copy(peer, slot):
        return pltpu.make_async_remote_copy(
            src_ref=back_put.at[peer, slot],
            dst_ref=back_got.at[me, slot],
            send_sem=back_put_sem.at[peer, slot],
            recv_sem=back_got_sem.at[me, slot],
            device_id={"ctx": peer},
        )

    def back_keep(slot):
        return pltpu.make_async_copy(
            back_put.at[me, slot], back_got.at[me, slot], own_sems.at[2, slot, 1]
        )

    early = total_units // count > 2

    def unit_step(slot, carry):
        def wait_one(step, inner):
            arrival(lax.rem(me + step, count), slot).wait_recv()
            return inner

        lax.fori_loop(1, count, wait_one, 0)
        keep_copy(slot).wait()
        for i in range(count):
            rows = slice(i * lanes, (i + 1) * lanes)
            key_rows[rows, :] = got_ref[i, slot, HD : 2 * HD, :].T
            value_t[:, rows] = got_ref[i, slot, 2 * HD : 3 * HD, :]
        batch = batch_of(count, me, slot)
        key_documents(starts_ref, batch, key_docs)

        def block(number, inner):
            begin = pl.multiple_of(number * width, width)
            parts = [got_ref[number * group + i, slot, 0:HD, :] for i in range(group)]
            queries = parts[0] if group == 1 else jnp.concatenate(parts, axis=1)
            query_docs = query_documents(starts_ref, batch, begin, width)

            def chunk(index, running):
                peak, total, mixed = running
                first = pl.multiple_of(index * depth, depth)
                scores = jnp.dot(
                    key_rows[pl.ds(first, depth), :], queries, preferred_element_type=F32
                )
                same = same_document(key_docs, first, depth, query_docs)
                scores = jnp.where(same, scores, MASKED)
                new_peak = jnp.maximum(peak, jnp.max(scores, axis=0, keepdims=True))
                scaling = jnp.exp(peak - new_peak)
                weights = jnp.exp(scores - new_peak)
                return (
                    new_peak,
                    total * scaling + jnp.sum(weights, axis=0, keepdims=True),
                    mixed * scaling
                    + jnp.dot(
                        value_t[:, pl.ds(first, depth)],
                        weights.astype(BF16),
                        preferred_element_type=F32,
                    ),
                )

            peak, total, mixed = over_chunks(
                length // depth,
                chunk,
                (
                    jnp.full((1, width), -jnp.inf, F32),
                    jnp.zeros((1, width), F32),
                    jnp.zeros((HD, width), F32),
                ),
            )
            mixed = mixed / total
            wide_ref[slot, :, pl.ds(begin, width)] = mixed
            lse_ref[slot, :, pl.ds(begin, width)] = peak + jnp.log(total)
            low = mixed.astype(BF16)
            for i in range(group):
                back_put[number * group + i, slot] = low[:, i * lanes : (i + 1) * lanes]
            return inner

        lax.fori_loop(0, length // width, block, 0)

        def send_one(step, inner):
            back_copy(lax.rem(me + step, count), slot).start()
            return inner

        lax.fori_loop(1, count, send_one, 0)
        back_keep(slot).start()
        if early:

            @pl.when(slot == 0)
            def _():
                outer_way.relay(0)
                outer_way.relay(1)

            @pl.when(slot == 1)
            def _():
                outer_way.relay(2)
                inner_way.relay(0)

            @pl.when(slot == 2)
            def _():
                inner_way.relay(1)
                inner_way.relay(2)

        return carry

    lax.fori_loop(0, mine, unit_step, 0)

    if not early:
        for k in range(RELAY_PIECES):
            outer_way.relay(k)
        for k in range(RELAY_PIECES):
            inner_way.relay(k)
    mixer_y.wait_recv()
    mixer_pass.start()
    outer_way.hand_on()
    inner_way.hand_on()

    def home(unit, carry):
        owner, slot = owner_of(count, unit), unit // count

        @pl.when(owner != me)
        def _():
            pltpu.make_async_remote_copy(
                src_ref=back_put.at[owner, slot],
                dst_ref=back_got.at[owner, slot],
                send_sem=back_put_sem.at[owner, slot],
                recv_sem=back_got_sem.at[owner, slot],
                device_id={"ctx": owner},
            ).wait_recv()

        @pl.when(owner == me)
        def _():
            back_keep(slot).wait()

        return carry

    lax.fori_loop(0, total_units, home, 0)
    for pair in range(pairs):
        for batch in range(MB):
            tops = []
            for j in range(2):
                unit = (2 * pair + j) * MB + batch
                tops.append(back_got[owner_of(count, unit), unit // count])
            block = jnp.concatenate(tops, axis=0).T
            att_ref[batch * lanes : (batch + 1) * lanes, pair * 128 : (pair + 1) * 128] = block

    outer_way.end()
    inner_way.end()
    vec_y.wait_send()
    vec_core.wait_send()
    vec_pass.wait_send()
    mixer_y.wait_send()
    mixer_core.wait()
    mixer_pass.wait()
    every_pair(joint_y, "wait_send")
    every_pair(joint_core, "wait_send")
    every_pair(joint_pass, "wait_send")
    for copy in own_out:
        copy.wait()

    def sent(unit, carry):
        @pl.when(owner_of(count, unit) != me)
        def _():
            send_copy(unit).wait_send()

        return carry

    lax.fori_loop(0, total_units, sent, 0)

    def returned(slot, carry):
        def one(step, inner):
            back_copy(lax.rem(me + step, count), slot).wait_send()
            return inner

        lax.fori_loop(1, count, one, 0)
        return carry

    lax.fori_loop(0, mine, returned, 0)
    for pair in range(pairs):
        joint_store(pair).wait()


def forward(count, starts, tokens, joint, mixer, inner, outer, vectors, number):
    units = -(-UNITS // count)
    lanes = tokens.shape[0] // MB
    length = count * lanes
    width = 2 * lanes
    part = joint.shape[0]
    pairs = H // 2
    vm = pl.BlockSpec(memory_space=pltpu.VMEM)
    hbm = pl.BlockSpec(memory_space=pl.ANY)
    dma = pltpu.SemaphoreType.DMA
    return pl.pallas_call(
        functools.partial(forward_kernel, width),
        out_shape=(
            jax.ShapeDtypeStruct(tokens.shape, BF16),
            jax.ShapeDtypeStruct((count, units, 3 * HD, lanes), BF16),
            jax.ShapeDtypeStruct((units, HD, length), F32),
            jax.ShapeDtypeStruct((units, 1, length), F32),
            jax.ShapeDtypeStruct((pairs, 4, part, 384), BF16),
            jax.ShapeDtypeStruct((4, BIAS_ROWS, D), F32),
            jax.ShapeDtypeStruct((4, *mixer.shape), BF16),
            jax.ShapeDtypeStruct((4, *inner.shape), BF16),
            jax.ShapeDtypeStruct((4, *outer.shape), BF16),
        ),
        in_specs=[pl.BlockSpec(memory_space=pltpu.SMEM), vm] + [hbm] * 4 + [vm] * 9,
        out_specs=(vm, vm, vm, vm, hbm, vm, hbm, hbm, hbm),
        scratch_shapes=[
            pltpu.VMEM((pairs, 4, part, 384), BF16),
            pltpu.VMEM((BIAS_ROWS, D), F32),
            pltpu.VMEM((pairs, 8, 384), F32),
            pltpu.VMEM((count, units, 3 * HD, lanes), BF16),
            pltpu.VMEM((count, units, HD, lanes), BF16),
            pltpu.VMEM((count, units, HD, lanes), BF16),
            pltpu.VMEM((length, HD), BF16),
            pltpu.VMEM((HD, length), BF16),
            pltpu.VMEM((length, lanes), jnp.int32),
            pltpu.VMEM(mixer.shape, BF16),
            pltpu.VMEM(inner.shape, BF16),
            pltpu.VMEM(outer.shape, BF16),
            dma((count, units)),
            dma((count, units)),
            dma((count, units)),
            dma((count, units)),
            dma((2, 3, pairs, 3)),
            dma((2, 4, 4)),
            dma((2, 2, 2, RELAY_PIECES)),
            dma((3, max(pairs, units, 4), 3)),
        ],
        compiler_params=pltpu.CompilerParams(
            collective_id=number, has_side_effects=True, vmem_limit_bytes=56 * 1024 * 1024
        ),
        name="forward",
    )(starts, tokens, joint, mixer, inner, outer, *vectors)


def first_rows(half, tile):
    return half if half <= tile else (half // tile + 1) // 2 * tile


class Place:
    def __init__(self, count):
        self.count = count
        self.depth = count // 2
        self.me, self.shard = lax.axis_index("ctx"), lax.axis_index("fsdp")
        self.y, self.core = self.shard // 2, lax.rem(self.shard, 2)
        self.z, self.x = self.me // 2, lax.rem(self.me, 2)
        self.other_core = {"fsdp": 2 * self.y + 1 - self.core}
        self.other_y = {"fsdp": 2 * (1 - self.y) + self.core}
        self.other_x = {"ctx": 2 * self.z + 1 - self.x}

        self.hi, self.lo = self.z // 2, lax.rem(self.z, 2)

    def along_z(self, step):
        return lax.rem(self.z + step, self.depth)

    def peer_z(self, step):
        return {"ctx": 2 * self.along_z(step) + self.x}


def start(copies):
    for copy in copies:
        copy.start()


def added(a, b):
    return (a.astype(F32) + b.astype(F32)).astype(a.dtype)


class Reduction:
    def __init__(self, place, j, grad, out, head, paired, buffers, sems, z_sems):
        got, y_one, x_one, x_two, y_two, z_got = buffers
        self.place, self.grad, self.out, self.head, self.buffers = place, grad, out, head, buffers
        half, lanes = grad.shape[4], grad.shape[5] // 2
        self.half, self.lanes, self.paired = half, lanes, paired
        p = place
        here, there = self.side(p.y), self.side(1 - p.y)

        def remote(src, dst, slot, peer):
            return pltpu.make_async_remote_copy(
                src_ref=src,
                dst_ref=dst,
                send_sem=sems.at[0, j, slot],
                recv_sem=sems.at[1, j, slot],
                device_id=peer,
            )

        def z_copy(z, target, step):
            return pltpu.make_async_remote_copy(
                src_ref=grad.at[z // 2, lax.rem(z, 2), p.x, p.core, :, here],
                dst_ref=z_got.at[target],
                send_sem=z_sems.at[0, j, step],
                recv_sem=z_sems.at[1, j, step],
                device_id={"ctx": 2 * z + p.x},
            )

        self.first = [remote(grad.at[:, :, :, 1 - p.core], got, 0, p.other_core)]
        self.second = [remote(grad.at[:, :, :, p.core, 0:head, there], y_one, 1, p.other_y)]
        self.third = [
            remote(grad.at[:, :, 1 - p.x, p.core, 0:head, here], x_two, 2, p.other_x)
        ]
        if head < half:
            self.second.append(
                remote(grad.at[:, :, 1 - p.x, p.core, head:half, :], x_one, 3, p.other_x)
            )
            self.third.append(
                remote(grad.at[:, :, p.x, p.core, head:half, there], y_two, 4, p.other_y)
            )
        if paired:
            near = {"ctx": 2 * (2 * p.hi + 1 - p.lo) + p.x}
            self.fourth = [
                remote(
                    grad.at[:, 1 - p.lo, p.x, p.core, :, here], z_got.at[pl.ds(0, 2)], 6, near
                )
            ]
            self.fifth = [z_copy(2 * (1 - p.hi) + p.lo, 2, 1)]
        else:
            self.fourth = []
            self.fifth = [z_copy(lax.rem(p.z + step, 4), p.z, step) for step in range(1, 4)]
        self.last = [remote(out.at[p.core], out.at[p.core], 5, p.other_core)]

    def side(self, y):
        return pl.ds(pl.multiple_of(y * self.lanes, 128), self.lanes)

    def each(self, body):
        def step(block, carry):
            body(block // 2, lax.rem(block, 2))
            return carry

        lax.fori_loop(0, 4, step, 0)

    def stage_zero(self):
        start(self.first)

    def stage_one(self):
        p, grad, got = self.place, self.grad, self.buffers[0]
        for copy in self.first:
            copy.wait_recv()

        def body(hi, lo):
            for x in range(2):
                grad[hi, lo, x, p.core] = added(grad[hi, lo, x, p.core], got[hi, lo, x])

        self.each(body)
        start(self.second)

    def stage_two(self):
        p, grad, head, half = self.place, self.grad, self.head, self.half
        y_one, x_one = self.buffers[1], self.buffers[2]
        here = self.side(p.y)
        for copy in self.second:
            copy.wait()

        def body(hi, lo):
            for x in range(2):
                grad[hi, lo, x, p.core, 0:head, here] = added(
                    grad[hi, lo, x, p.core, 0:head, here], y_one[hi, lo, x]
                )
            if head < half:
                grad[hi, lo, p.x, p.core, head:half, :] = added(
                    grad[hi, lo, p.x, p.core, head:half, :], x_one[hi, lo]
                )

        self.each(body)
        start(self.third)

    def stage_three(self):
        p, grad, head, half = self.place, self.grad, self.head, self.half
        x_two, y_two = self.buffers[3], self.buffers[4]
        here = self.side(p.y)
        for copy in self.third:
            copy.wait()

        def body(hi, lo):
            grad[hi, lo, p.x, p.core, 0:head, here] = added(
                grad[hi, lo, p.x, p.core, 0:head, here], x_two[hi, lo]
            )
            if head < half:
                grad[hi, lo, p.x, p.core, head:half, here] = added(
                    grad[hi, lo, p.x, p.core, head:half, here], y_two[hi, lo]
                )

        self.each(body)
        start(self.fourth if self.paired else self.fifth)

    def stage_four(self):
        p, grad, z_got = self.place, self.grad, self.buffers[5]
        here = self.side(p.y)
        for copy in self.fourth:
            copy.wait()
        for hi in range(2):
            grad[hi, p.lo, p.x, p.core, :, here] = added(
                grad[hi, p.lo, p.x, p.core, :, here], z_got[hi]
            )
        start(self.fifth)

    def stage_five(self):
        p, z_got = self.place, self.buffers[5]
        for copy in self.fifth:
            copy.wait()
        total = self.grad[p.hi, p.lo, p.x, p.core, :, self.side(p.y)].astype(F32)
        if self.paired:
            total = total + z_got[2].astype(F32)
        else:
            for step in range(1, 4):
                total = total + z_got[lax.rem(p.z + step, 4)].astype(F32)
        self.out[p.core] = total.astype(self.out.dtype)
        start(self.last)

    def stage_six(self):
        for copy in self.last:
            copy.wait()
        for copy in self.first:
            copy.wait_send()


def reduction_buffers(half, lanes, head, dtype):
    tail = max(half - head, 16)
    shapes = (
        (2, 2, 2, half, 2 * lanes),
        (2, 2, 2, head, lanes),
        (2, 2, tail, 2 * lanes),
        (2, 2, head, lanes),
        (2, 2, tail, lanes),
        (4, half, lanes),
        (2, half, lanes),
    )
    return [pltpu.VMEM(shape, dtype) for shape in shapes]


def backward_kernel(width, plan, *refs):
    (
        starts_ref,
        flow_ref,
        got_ref,
        wide_ref,
        lse_ref,
        tok_ref,
        residual_ref,
        bias_ref,
        joint_ref,
        d_outer_ref,
        act_ref,
        d_inner_ref,
        first_ref,
        d_branch_ref,
        att_ref,
        tokens_out,
        outer_out,
        inner_out,
        mixer_out,
        joint_out,
        bias_out,
        flow_put,
        flow_got,
        put,
        home_got,
        key_rows,
        value_rows,
        key_t,
        key_docs,
        d_key,
        d_value,
        joint_all,
        outer_one,
        outer_two,
        inner_one,
        inner_two,
        mixer_grad,
        joint_one,
        joint_two,
        d_turned,
        bias_sum,
        bias_got,
        flow_sems,
        home_sems,
        own_sems,
        sems,
        z_sems,
        bias_sems,
        *buffers,
    ) = refs
    count, units, _, lanes = got_ref.shape
    length = count * lanes
    depth = min(length, 1024)
    group = width // lanes
    pairs = H // 2
    total_units = MB * H
    p = Place(count)
    me = p.me
    mine = owned(count, me)

    barrier = pltpu.get_barrier_semaphore()

    def greet(step, carry):
        pl.semaphore_signal(barrier, inc=1, device_id={"ctx": lax.rem(me + step, count)})
        return carry

    lax.fori_loop(1, count, greet, 0)
    pl.semaphore_signal(barrier, inc=1, device_id=p.other_core)
    pl.semaphore_signal(barrier, inc=1, device_id=p.other_y)
    pl.semaphore_signal(barrier, inc=1, device_id={**p.other_y, **p.other_x})
    joint_load = pltpu.make_async_copy(joint_ref, joint_all, own_sems.at[2, 0])
    joint_load.start()

    grads = (outer_one, outer_two, inner_one, inner_two, mixer_grad, joint_one, joint_two)
    jobs = [
        Reduction(
            p,
            j,
            grads[j],
            buffers[7 * j + 6],
            plan[j][2],
            plan[j][3],
            buffers[7 * j : 7 * j + 6],
            sems,
            z_sems,
        )
        for j in range(len(grads))
    ]
    o_one, o_two, i_one, i_two, m_one, j_one, j_two = jobs

    def store_rows(targets, row, values, columns):
        half = sum(t.shape[4] for t in targets)
        done = 0
        while done < values.shape[0]:
            block, inside = (row + done) // half, (row + done) % half
            k = 0
            while inside >= targets[k].shape[4]:
                inside -= targets[k].shape[4]
                k += 1
            size = min(values.shape[0] - done, targets[k].shape[4] - inside)
            targets[k][
                block // 8,
                block // 4 % 2,
                block // 2 % 2,
                block % 2,
                inside : inside + size,
                columns,
            ] = values[done : done + size]
            done += size

    d_outer_turned = d_outer_ref[...].T

    def outer_gradient(which):
        for side in range(2):
            begin = (2 * side + which) * D
            values = jnp.dot(
                d_outer_turned, act_ref[:, begin : begin + D], preferred_element_type=F32
            )
            columns = slice(side * D, (side + 1) * D)
            store_rows(((outer_one, outer_two)[which],), 0, values.astype(BF16), columns)

    def inner_gradient():
        for k in range(FF // D):
            turned = d_inner_ref[:, k * D : (k + 1) * D].T
            values = jnp.dot(turned, first_ref[...], preferred_element_type=F32)
            store_rows((inner_one, inner_two), k * D, values.astype(BF16), slice(0, D))

    def mixer_gradient():
        values = jnp.dot(d_branch_ref[...].T, att_ref[...], preferred_element_type=F32)
        store_rows((mixer_grad,), 0, values.astype(BF16), slice(0, D))

    def unit_copy(source, target, sem, owner, slot):
        return pltpu.make_async_remote_copy(
            src_ref=source.at[owner, slot],
            dst_ref=target.at[me, slot],
            send_sem=sem.at[0, owner, slot],
            recv_sem=sem.at[1, me, slot],
            device_id={"ctx": owner},
        )

    def unit_arrival(source, target, sem, sender, slot):
        return pltpu.make_async_remote_copy(
            src_ref=source.at[sender, slot],
            dst_ref=target.at[sender, slot],
            send_sem=sem.at[0, sender, slot],
            recv_sem=sem.at[1, sender, slot],
            device_id={"ctx": sender},
        )

    def unit_keep(source, target, kind, slot):
        return pltpu.make_async_copy(
            source.at[me, slot], target.at[me, slot], own_sems.at[kind, slot]
        )

    for pair in range(pairs):
        for batch in range(MB):
            block = flow_ref[
                batch * lanes : (batch + 1) * lanes, pair * 128 : (pair + 1) * 128
            ].T
            for j in range(2):
                unit = (2 * pair + j) * MB + batch
                flow_put[owner_of(count, unit), unit // count] = block[j * HD : (j + 1) * HD]

    pl.semaphore_wait(barrier, count + 2)

    def send_flow(turn, carry):
        slot, owner = turn // count, lax.rem(me + turn, count)

        @pl.when((owner != me) & (slot < owned(count, owner)))
        def _():
            unit_copy(flow_put, flow_got, flow_sems, owner, slot).start()

        @pl.when((owner == me) & (slot < mine))
        def _():
            unit_keep(flow_put, flow_got, 0, slot).start()

        return carry

    lax.fori_loop(0, units * count, send_flow, 0)
    bias_sum[0] = bias_ref[...]
    outer_gradient(0)
    o_one.stage_zero()
    outer_gradient(1)
    o_two.stage_zero()
    o_one.stage_one()
    inner_gradient()
    i_one.stage_zero()
    i_two.stage_zero()
    mixer_gradient()
    m_one.stage_zero()

    def unit_step(slot, carry):
        def wait_one(step, inner):
            unit_arrival(flow_put, flow_got, flow_sems, lax.rem(me + step, count), slot).wait_recv()
            return inner

        lax.fori_loop(1, count, wait_one, 0)
        unit_keep(flow_put, flow_got, 0, slot).wait()
        for i in range(count):
            rows = slice(i * lanes, (i + 1) * lanes)
            key_rows[rows, :] = got_ref[i, slot, HD : 2 * HD, :].T
            value_rows[rows, :] = got_ref[i, slot, 2 * HD : 3 * HD, :].T
            key_t[:, rows] = got_ref[i, slot, HD : 2 * HD, :]
        batch = batch_of(count, me, slot)
        key_documents(starts_ref, batch, key_docs)
        d_key[...] = jnp.zeros_like(d_key)
        d_value[...] = jnp.zeros_like(d_value)

        def block(number, inner):
            begin = pl.multiple_of(number * width, width)

            def beside(ref):
                parts = [ref[number * group + i, slot, 0:HD, :] for i in range(group)]
                return parts[0] if group == 1 else jnp.concatenate(parts, axis=1)

            queries, flow = beside(got_ref), beside(flow_got)
            query_rows, flow_rows = queries.T, flow.T
            query_docs = query_documents(starts_ref, batch, begin, width)
            log_total = lse_ref[slot, :, pl.ds(begin, width)]
            spread = jnp.sum(
                flow.astype(F32) * wide_ref[slot, :, pl.ds(begin, width)], axis=0, keepdims=True
            )

            def chunk(index, d_query):
                first = pl.multiple_of(index * depth, depth)
                rows = pl.ds(first, depth)
                scores = jnp.dot(key_rows[rows, :], queries, preferred_element_type=F32)
                same = same_document(key_docs, first, depth, query_docs)
                probs = jnp.exp(jnp.where(same, scores, MASKED) - log_total)
                pressure = jnp.dot(value_rows[rows, :], flow, preferred_element_type=F32)
                d_scores = (probs * (pressure - spread)).astype(BF16)
                d_value[rows, :] += jnp.dot(
                    probs.astype(BF16), flow_rows, preferred_element_type=F32
                )
                d_key[rows, :] += jnp.dot(d_scores, query_rows, preferred_element_type=F32)
                return d_query + jnp.dot(key_t[:, rows], d_scores, preferred_element_type=F32)

            d_query = over_chunks(length // depth, chunk, jnp.zeros((HD, width), F32))
            low = (d_query * SCALE).astype(BF16)
            for i in range(group):
                put[number * group + i, slot, 0:HD, :] = low[:, i * lanes : (i + 1) * lanes]
            return inner

        lax.fori_loop(0, length // width, block, 0)
        for i in range(count):
            rows = slice(i * lanes, (i + 1) * lanes)
            put[i, slot, HD : 2 * HD, :] = d_key[rows, :].T.astype(BF16)
            put[i, slot, 2 * HD : 3 * HD, :] = d_value[rows, :].T.astype(BF16)

        def send_one(step, inner):
            unit_copy(put, home_got, home_sems, lax.rem(me + step, count), slot).start()
            return inner

        lax.fori_loop(1, count, send_one, 0)
        unit_keep(put, home_got, 1, slot).start()

        @pl.when(slot == 0)
        def _():
            o_two.stage_one()

        @pl.when(slot == 2)
        def _():
            o_one.stage_two()
            i_one.stage_one()

        return carry

    lax.fori_loop(0, mine, unit_step, 0)
    o_two.stage_two()
    i_two.stage_one()
    o_one.stage_three()
    i_one.stage_two()
    m_one.stage_one()

    ones = jnp.ones((8, MB * lanes), BF16)
    for pair in range(pairs):
        columns = []
        for batch in range(MB):
            blocks = []
            for j in range(2):
                unit = (2 * pair + j) * MB + batch
                owner, slot = owner_of(count, unit), unit // count

                @pl.when(owner != me)
                def _():
                    unit_arrival(put, home_got, home_sems, owner, slot).wait_recv()

                @pl.when(owner == me)
                def _():
                    unit_keep(put, home_got, 1, slot).wait()

                blocks.append(home_got[owner, slot])
            rows = [b[third * HD : (third + 1) * HD] for third in range(3) for b in blocks]
            columns.append(jnp.concatenate(rows, axis=0))
        d_pair = jnp.concatenate(columns, axis=1)
        d_turned[pair] = d_pair.T
        grad = jnp.dot(d_pair, tok_ref[...], preferred_element_type=F32).astype(BF16)
        for third in range(3):
            store_rows(
                (joint_one, joint_two),
                third * D + pair * 128,
                grad[third * 128 : (third + 1) * 128],
                slice(0, D),
            )
        sums = lax.dot_general(
            ones, d_pair, (((1,), (1,)), ((), ())), preferred_element_type=F32
        )
        bias_sum[0, 0:1, pair * 128 : (pair + 1) * 128] = sums[0:1, 0:128]
        bias_sum[0, 1:2, pair * 128 : (pair + 1) * 128] = sums[0:1, 256:384]
        if pair == 2:
            o_two.stage_three()
            o_one.stage_four()
            i_two.stage_two()
            i_one.stage_three()

    m_one.stage_two()
    o_two.stage_four()

    plane = (p.other_y, p.other_x, {**p.other_y, **p.other_x})

    def bias_copy(level, number, slot, peer):
        return pltpu.make_async_remote_copy(
            src_ref=bias_sum.at[level],
            dst_ref=bias_got.at[slot],
            send_sem=bias_sems.at[0, number],
            recv_sem=bias_sems.at[1, number],
            device_id=peer,
        )

    bias_core = bias_copy(0, 0, 0, p.other_core)
    bias_plane = [bias_copy(1, 1 + i, 1 + i, peer) for i, peer in enumerate(plane)]
    bias_z = [
        bias_copy(2, 3 + step, 3 + step, {"ctx": 2 * lax.rem(p.z + step, 4) + p.x})
        for step in range(1, 4)
    ]
    bias_core.start()
    j_one.stage_zero()
    j_two.stage_zero()

    joint_load.wait()

    def token_terms(first, last, total):
        for pair in range(first, last):
            total = total + lax.dot_general(
                d_turned[pair],
                joint_all[pair],
                (((1,), (1,)), ((), ())),
                preferred_element_type=F32,
            )
        tokens_out[...] = total

    token_terms(0, pairs // 2, residual_ref[...])
    bias_core.wait()
    bias_sum[1] = bias_sum[0] + bias_got[0]
    start(bias_plane)
    j_one.stage_one()
    j_two.stage_one()
    i_two.stage_three()
    i_one.stage_four()
    token_terms(pairs // 2, pairs, tokens_out[...])
    m_one.stage_three()
    for copy in bias_plane:
        copy.wait()
    bias_sum[2] = bias_sum[1] + bias_got[1] + bias_got[2] + bias_got[3]
    start(bias_z)
    j_one.stage_two()
    i_two.stage_four()
    j_two.stage_two()
    m_one.stage_four()
    j_one.stage_three()
    j_two.stage_three()
    o_one.stage_five()
    o_two.stage_five()
    i_one.stage_five()

    def parts_of(j):
        jobs[j].stage_six()
        whole = buffers[7 * j + 6]
        return [whole[low].astype(F32) for low in range(2)]

    def own_lanes(rows):
        width_own = rows.shape[1] // 2
        return jnp.where(p.core == 0, rows[:, :width_own], rows[:, width_own:])

    def put_out(out, pieces):
        out[...] = jnp.concatenate(pieces, axis=0).T

    one, two = parts_of(0), parts_of(1)
    put_out(outer_out, [jnp.where(p.core == 0, a, b) for a, b in zip(one, two)])
    i_two.stage_five()
    m_one.stage_five()
    one, two = parts_of(2), parts_of(3)
    put_out(inner_out, [own_lanes(r) for r in (one[0], two[0], one[1], two[1])])
    put_out(mixer_out, [own_lanes(r) for r in parts_of(4)])
    for copy in bias_z:
        copy.wait()
    bias_out[...] = bias_sum[2] + bias_got[4] + bias_got[5] + bias_got[6]

    def sent(unit, carry):
        owner, slot = owner_of(count, unit), unit // count

        @pl.when(owner != me)
        def _():
            unit_copy(flow_put, flow_got, flow_sems, owner, slot).wait_send()

        return carry

    lax.fori_loop(0, total_units, sent, 0)

    def returned(slot, carry):
        def one(step, inner):
            unit_copy(put, home_got, home_sems, lax.rem(me + step, count), slot).wait_send()
            return inner

        lax.fori_loop(1, count, one, 0)
        return carry

    lax.fori_loop(0, mine, returned, 0)
    j_one.stage_five()
    j_two.stage_five()
    one, two = parts_of(5), parts_of(6)
    put_out(joint_out, [own_lanes(r) for r in (one[0], two[0], one[1], two[1])])


def backward(
    starts, flow, got, wide, lse, source, residual, biases, joint, activations, number
):
    count, units, _, lanes = got.shape
    length = count * lanes
    width = 2 * lanes
    pairs = H // 2
    vm = pl.BlockSpec(memory_space=pltpu.VMEM)
    hbm = pl.BlockSpec(memory_space=pl.ANY)
    dma = pltpu.SemaphoreType.DMA
    small = D // (2 * count)
    half_joint = 3 * D // (2 * count)
    early = first_rows(half_joint, 16)
    plan = (
        (small, FF // 2, small, True),
        (small, FF // 2, small, True),
        (2 * small, D, 4 * small // 3, True),
        (2 * small, D, 4 * small // 3, True),
        (small, D, small, True),
        (early, D, first_rows(early, 16), False),
        (half_joint - early, D, first_rows(half_joint - early, 16), False),
    )
    buffers = []
    for half, full, head, _ in plan:
        buffers += reduction_buffers(half, full // 2, head, BF16)
    outs = [
        jax.ShapeDtypeStruct((FF // 4, 2 * small), F32),
        jax.ShapeDtypeStruct((D // 4, FF // count), F32),
        jax.ShapeDtypeStruct((D // 4, 2 * small), F32),
        jax.ShapeDtypeStruct((D // 4, 2 * half_joint), F32),
    ]
    return pl.pallas_call(
        functools.partial(backward_kernel, width, plan),
        out_shape=(
            jax.ShapeDtypeStruct(residual.shape, F32),
            *outs,
            jax.ShapeDtypeStruct((BIAS_ROWS, D), F32),
        ),
        in_specs=[pl.BlockSpec(memory_space=pltpu.SMEM)] + [vm] * 7 + [hbm] + [vm] * 6,
        out_specs=(vm,) * 6,
        scratch_shapes=[
            pltpu.VMEM((count, units, HD, lanes), BF16),
            pltpu.VMEM((count, units, HD, lanes), BF16),
            pltpu.VMEM((count, units, 3 * HD, lanes), BF16),
            pltpu.VMEM((count, units, 3 * HD, lanes), BF16),
            pltpu.VMEM((length, HD), BF16),
            pltpu.VMEM((length, HD), BF16),
            pltpu.VMEM((HD, length), BF16),
            pltpu.VMEM((length, lanes), jnp.int32),
            pltpu.VMEM((length, HD), F32),
            pltpu.VMEM((length, HD), F32),
            pltpu.VMEM((pairs, D, 384), BF16),
            *[pltpu.VMEM((2, 2, 2, 2, half, full), BF16) for half, full, _, _ in plan],
            pltpu.VMEM((pairs, MB * lanes, 384), BF16),
            pltpu.VMEM((3, BIAS_ROWS, D), F32),
            pltpu.VMEM((7, BIAS_ROWS, D), F32),
            dma((2, count, units)),
            dma((2, count, units)),
            dma((3, units)),
            dma((2, len(plan), 7)),
            dma((2, len(plan), 4)),
            dma((2, 7)),
            *buffers,
        ],
        compiler_params=pltpu.CompilerParams(
            collective_id=number, has_side_effects=True, vmem_limit_bytes=67043328
        ),
        name="backward",
    )(starts, flow, got, wide, lse, source, residual, biases, joint, *activations)


def on_device(
    count,
    shards,
    tokens,
    doc_starts,
    joint_weight,
    mixer_weight,
    inner_weight,
    outer_weight,
    query_bias,
    value_bias,
    mixer_bias,
    first_gain,
    first_shift,
    inner_bias,
    outer_bias,
    second_gain,
    second_shift,
    upstream,
):
    rows = tokens.shape[2]
    length = rows * count
    units = -(-MB * H // count)
    me = lax.axis_index("ctx")

    part = D // shards
    vectors = [
        query_bias,
        value_bias,
        mixer_bias,
        first_gain,
        first_shift,
        outer_bias,
        second_gain,
        second_shift,
        inner_bias,
    ]
    source = tokens.reshape(MB * rows, D)
    batch_starts = doc_starts[:, 0]

    attended, received, wide, lse, joint, vectors, mixer, inner, outer = forward(
        count,
        batch_starts,
        source,
        joint_weight,
        mixer_weight,
        inner_weight,
        outer_weight,
        vectors,
        0,
    )
    joint = joint.reshape(H // 2, D, 384)
    mixer, inner, outer = mixer.reshape(D, D), inner.reshape(D, FF), outer.reshape(FF, D)
    heads_of = [
        vectors[:, i, :part].reshape(D)
        for i in range(8)
    ]
    _, _, mbias, gain_one, shift_one, obias, gain_two, shift_two = heads_of
    ibias = vectors[:, 8].reshape(FF)

    branch = mul_nn(attended, mixer) + mbias
    first, first_normed, first_recip = norm_forward(
        source.astype(F32) + branch, gain_one, shift_one
    )
    first_low = first.astype(BF16)
    inner_pre = mul_nn(first_low, inner) + ibias
    activated, gelu_slope = gelu_parts(inner_pre)
    activated_low = activated.astype(BF16)
    outer_out = mul_nn(activated_low, outer) + obias
    final, second_normed, second_recip = norm_forward(first + outer_out, gain_two, shift_two)
    result = final.astype(BF16).reshape(MB, 1, rows, D)

    incoming = upstream.reshape(MB * rows, D).astype(F32)
    rescale_grad = jnp.sum(incoming * second_normed, axis=0)
    reshift_grad = jnp.sum(incoming, axis=0)
    d_second = norm_backward(incoming, second_normed, second_recip, gain_two)
    d_outer = d_second.astype(BF16)
    return_grad = jnp.sum(d_outer.astype(F32), axis=0)
    d_inner = (mul_nt(d_outer, outer) * gelu_slope).astype(BF16)
    hidden_grad = jnp.sum(d_inner.astype(F32), axis=0)
    d_first = d_second + mul_nt(d_inner, inner)
    scale_grad = jnp.sum(d_first * first_normed, axis=0)
    shift_grad = jnp.sum(d_first, axis=0)
    d_residual = norm_backward(d_first, first_normed, first_recip, gain_one)
    d_branch = d_residual.astype(BF16)
    mixing_grad = jnp.sum(d_branch.astype(F32), axis=0)
    world = count * shards
    index = me * shards + lax.axis_index("fsdp")
    sums = [
        mixing_grad,
        scale_grad,
        shift_grad,
        return_grad,
        rescale_grad,
        reshift_grad,
        *hidden_grad.reshape(FF // D, D),
    ]
    if shards == 4 and count == 8:
        flow = mul_nt(d_branch, mixer).astype(BF16)
        biases = jnp.pad(jnp.stack(sums), ((2, BIAS_ROWS - 2 - len(sums)), (0, 0)))
        tokens_grad, *blocks, biases = backward(
            batch_starts,
            flow,
            received,
            wide,
            lse,
            source,
            d_residual,
            biases,
            joint,
            [d_outer, activated_low, d_inner, first_low, d_branch, attended],
            1,
        )
    else:
        natural = joint.reshape(H // 2, D, 3, 128).transpose(1, 2, 0, 3).reshape(D, 3 * D)
        flow = mul_nt(mixer, d_branch).astype(BF16)
        flow_units = exchange(to_units(flow, 1, count, units), 2)
        d_units = attend_back(received, flow_units, batch_starts, wide, lse)
        d_joint = from_units(exchange(d_units, 3), 3)
        bias_sums = jnp.sum(d_joint.astype(F32), axis=1)
        turned = [
            mul_tn(d_outer, activated_low),
            mul_tn(d_inner, first_low),
            mul_tn(d_branch, attended),
            mul_nn(d_joint, source),
        ]
        tokens_grad = d_residual + mul_tt(d_joint, natural)

        def reduced(grad):
            over_lanes = lax.psum_scatter(
                grad.astype(BF16), "fsdp", scatter_dimension=1, tiled=True
            )
            over_rows = lax.psum_scatter(over_lanes, "ctx", scatter_dimension=0, tiled=True)
            return over_rows.T.astype(F32)

        blocks = [reduced(g) for g in turned]
        biases = jnp.stack([bias_sums[:D], bias_sums[2 * D :], *sums])
        biases = lax.psum(biases, ("ctx", "fsdp"))
    tokens_grad = tokens_grad.reshape(MB, 1, rows, D)
    outer_out_grad, inner_out, mixer_out, joint_out = blocks
    own = lax.dynamic_slice_in_dim(biases[:8], index * (D // world), D // world, 1)
    hidden_rows = biases[8 : 8 + FF // D].reshape(FF)
    own_hidden = lax.dynamic_slice_in_dim(hidden_rows, index * (FF // world), FF // world, 0)
    sums = [*own[:5], own_hidden, *own[5:]]
    return (result, tokens_grad, joint_out, mixer_out, inner_out, outer_out_grad, *sums)


def solution(mesh):
    in_specs = (
        P(None, "fsdp", "ctx", None),
        P(None, "fsdp", None),
        P("fsdp", None),
        P("fsdp", None),
        P("fsdp", None),
        P("fsdp", None),
        P("fsdp"),
        P("fsdp"),
        P("fsdp"),
        P("fsdp"),
        P("fsdp"),
        P("fsdp"),
        P("fsdp"),
        P("fsdp"),
        P("fsdp"),
        P(None, "fsdp", "ctx", None),
    )
    out_specs = (
        P(None, "fsdp", "ctx", None),
        P(None, "fsdp", "ctx", None),
        P("fsdp", "ctx"),
        P("fsdp", "ctx"),
        P("fsdp", "ctx"),
        P("fsdp", "ctx"),
        P(("ctx", "fsdp")),
        P(("ctx", "fsdp")),
        P(("ctx", "fsdp")),
        P(("ctx", "fsdp")),
        P(("ctx", "fsdp")),
        P(("ctx", "fsdp")),
        P(("ctx", "fsdp")),
        P(("ctx", "fsdp")),
        P(("ctx", "fsdp")),
    )
    return jax.shard_map(
        functools.partial(on_device, mesh.shape["ctx"], mesh.shape["fsdp"]),
        mesh=mesh,
        in_specs=in_specs,
        out_specs=out_specs,
        check_vma=False,
    )
```

```python
import functools
import math

import jax
import jax.numpy as jnp
from jax import lax
from jax.experimental import pallas as pl
from jax.experimental.pallas import tpu as pltpu
from jax.sharding import PartitionSpec as P

D = 768
H = 12
HD = 64
FF = 3072
MB = 3

SCALE = 0.125
EPSILON = 1e-12
MASKED = -1000000000.0
ROOT_HALF = 0.7071067811865476
GAUSS_PEAK = 0.3989422804014327

F32 = jnp.float32
BF16 = jnp.bfloat16


def norm_forward(hidden, gain, shift):
    average = jnp.mean(hidden, axis=-1, keepdims=True)
    centred = hidden - average
    reciprocal = lax.rsqrt(jnp.mean(centred * centred, axis=-1, keepdims=True) + EPSILON)
    normed = centred * reciprocal
    return (normed * gain + shift, normed, reciprocal)


def norm_backward(incoming, normed, reciprocal, gain):
    scaled = incoming * gain
    return reciprocal * (
        scaled
        - jnp.mean(scaled, axis=-1, keepdims=True)
        - normed * jnp.mean(scaled * normed, axis=-1, keepdims=True)
    )


def gelu_parts(inner):
    cumulative = 0.5 * (1.0 + lax.erf(inner * ROOT_HALF))
    return (inner * cumulative, cumulative + inner * jnp.exp(-0.5 * inner * inner) * GAUSS_PEAK)


UNITS = MB * H
BIAS_ROWS = 16
RELAY_PIECES = 3


def spare_owner(count, j):
    stride = count // (UNITS % count)
    return j * stride + (j % 2 if stride > 1 else 0)


def owner_of(count, unit):
    full, rest = UNITS // count, UNITS % count
    if rest == 0:
        return unit % count
    if full == 0:
        return spare_owner(count, unit)
    late = unit // (full * count)
    return (1 - late) * (unit % count) + late * spare_owner(count, unit - full * count)


def spare_index(count, device):
    return device // (count // (UNITS % count))


def owned(count, device):
    full, rest = UNITS // count, UNITS % count
    if rest == 0:
        return full
    j = spare_index(count, device)
    extra = (spare_owner(count, j) == device) & (j < rest)
    return full + extra.astype(jnp.int32)


def batch_of(count, device, slot):
    full, rest = UNITS // count, UNITS % count
    if rest == 0:
        return (slot * count + device) % MB
    if full == 0:
        return jnp.minimum(spare_index(count, device), UNITS - 1) % MB
    late = slot // full
    unit = slot * count + (1 - late) * device + late * spare_index(count, device)
    return unit % MB


def exchange_kernel(count, x_ref, y_ref, held, send_sem, recv_sem, own_sem):
    me = lax.axis_index("ctx")
    barrier = pltpu.get_barrier_semaphore()

    def greet(step, carry):
        peer = lax.rem(me + step, count)
        pl.semaphore_signal(barrier, inc=1, device_id={"ctx": peer})
        return carry

    lax.fori_loop(1, count, greet, 0)
    own_in = pltpu.make_async_copy(x_ref.at[me], held, own_sem)
    own_in.start()
    pl.semaphore_wait(barrier, count - 1)

    def transfer(step):
        peer = lax.rem(me + step, count)
        return pltpu.make_async_remote_copy(
            src_ref=x_ref.at[peer],
            dst_ref=y_ref.at[me],
            send_sem=send_sem.at[step],
            recv_sem=recv_sem.at[step],
            device_id={"ctx": peer},
        )

    def begin(step, carry):
        transfer(step).start()
        return carry

    lax.fori_loop(1, count, begin, 0)
    own_in.wait()
    own_out = pltpu.make_async_copy(held, y_ref.at[me], own_sem)
    own_out.start()
    own_out.wait()

    def finish(step, carry):
        transfer(step).wait()
        return carry

    lax.fori_loop(1, count, finish, 0)


def exchange(x, number):
    count = x.shape[0]
    return pl.pallas_call(
        functools.partial(exchange_kernel, count),
        out_shape=jax.ShapeDtypeStruct(x.shape, x.dtype),
        in_specs=[pl.BlockSpec(memory_space=pl.ANY)],
        out_specs=pl.BlockSpec(memory_space=pl.ANY),
        scratch_shapes=[
            pltpu.VMEM(x.shape[1:], x.dtype),
            pltpu.SemaphoreType.DMA((count,)),
            pltpu.SemaphoreType.DMA((count,)),
            pltpu.SemaphoreType.DMA,
        ],
        compiler_params=pltpu.CompilerParams(collective_id=number, has_side_effects=True),
        name=f"exchange_{number}",
    )(x)


def across(ref, first, rows, width, lanes):
    parts = [ref[first + i, 0, rows, :] for i in range(width // lanes)]
    return parts[0] if len(parts) == 1 else jnp.concatenate(parts, axis=1)


def document(starts_ref, batch, position):
    docs = jnp.zeros(position.shape, jnp.int32) - 1
    for j in range(starts_ref.shape[2]):
        docs = docs + jnp.where(position >= starts_ref[batch, 0, j], 1, 0)
    return docs


def key_documents(starts_ref, batch, key_docs):
    key_docs[...] = document(
        starts_ref, batch, lax.broadcasted_iota(jnp.int32, key_docs.shape, 0)
    )


def query_documents(starts_ref, batch, begin, width):
    return document(
        starts_ref, batch, lax.broadcasted_iota(jnp.int32, (1, width), 1) + begin
    )


def same_document(key_docs, first, width, query_docs):
    keys = key_docs[pl.ds(first, width), :]
    lanes = keys.shape[1]
    parts = [keys == query_docs[:, i : i + lanes] for i in range(0, query_docs.shape[1], lanes)]
    return parts[0] if len(parts) == 1 else jnp.concatenate(parts, axis=1)


def over_chunks(chunks, body, carry):
    if chunks == 1:
        return body(0, carry)
    return lax.fori_loop(0, chunks, body, carry)


def attend_back_kernel(
    width,
    starts_ref,
    x_ref,
    flow_ref,
    wide_ref,
    lse_ref,
    d_ref,
    key_rows,
    value_rows,
    key_t,
    key_docs,
    d_key,
    d_value,
):
    count, _, _, lanes = x_ref.shape
    length = count * lanes
    depth = min(length, 1024)
    unit = pl.program_id(0)
    for i in range(count):
        rows = slice(i * lanes, (i + 1) * lanes)
        key_rows[rows, :] = x_ref[i, 0, HD : 2 * HD, :].T
        value_rows[rows, :] = x_ref[i, 0, 2 * HD : 3 * HD, :].T
        key_t[:, rows] = x_ref[i, 0, HD : 2 * HD, :]
    batch = batch_of(count, lax.axis_index("ctx"), unit)
    key_documents(starts_ref, batch, key_docs)
    d_key[...] = jnp.zeros_like(d_key)
    d_value[...] = jnp.zeros_like(d_value)
    group = width // lanes

    def block(number, carry):
        begin = pl.multiple_of(number * width, width)
        queries = across(x_ref, number * group, slice(0, HD), width, lanes)
        flow = across(flow_ref, number * group, slice(0, HD), width, lanes)
        query_rows = queries.T
        flow_rows = flow.T
        query_docs = query_documents(starts_ref, batch, begin, width)
        log_total = lse_ref[0, :, pl.ds(begin, width)]
        spread = jnp.sum(
            flow.astype(F32) * wide_ref[0, :, pl.ds(begin, width)], axis=0, keepdims=True
        )

        def chunk(index, d_query):
            first = pl.multiple_of(index * depth, depth)
            rows = pl.ds(first, depth)
            scores = jnp.dot(key_rows[rows, :], queries, preferred_element_type=F32)
            same = same_document(key_docs, first, depth, query_docs)
            probs = jnp.exp(jnp.where(same, scores, MASKED) - log_total)
            pressure = jnp.dot(value_rows[rows, :], flow, preferred_element_type=F32)
            d_scores = (probs * (pressure - spread)).astype(BF16)
            d_value[rows, :] += jnp.dot(
                probs.astype(BF16), flow_rows, preferred_element_type=F32
            )
            d_key[rows, :] += jnp.dot(d_scores, query_rows, preferred_element_type=F32)
            return d_query + jnp.dot(key_t[:, rows], d_scores, preferred_element_type=F32)

        d_query = over_chunks(length // depth, chunk, jnp.zeros((HD, width), F32))
        low = (d_query * SCALE).astype(BF16)
        for i in range(group):
            d_ref[number * group + i, 0, 0:HD, :] = low[:, i * lanes : (i + 1) * lanes]
        return carry

    lax.fori_loop(0, length // width, block, 0)
    for i in range(count):
        rows = slice(i * lanes, (i + 1) * lanes)
        d_ref[i, 0, HD : 2 * HD, :] = d_key[rows, :].T.astype(BF16)
        d_ref[i, 0, 2 * HD : 3 * HD, :] = d_value[rows, :].T.astype(BF16)


def unit_block(*dims):
    return pl.BlockSpec(dims, lambda u, starts: (0, u) + (0,) * (len(dims) - 2))


def own_block(*dims):
    return pl.BlockSpec(dims, lambda u, starts: (u,) + (0,) * (len(dims) - 1))


def attend_back(x, flow, starts, wide, lse):
    count, units, _, lanes = x.shape
    length = count * lanes
    width = 2 * lanes if count % 2 == 0 else lanes
    return pl.pallas_call(
        functools.partial(attend_back_kernel, width),
        out_shape=jax.ShapeDtypeStruct(x.shape, BF16),
        grid_spec=pltpu.PrefetchScalarGridSpec(
            num_scalar_prefetch=1,
            grid=(units,),
            in_specs=[
                unit_block(count, 1, 3 * HD, lanes),
                unit_block(count, 1, HD, lanes),
                own_block(1, HD, length),
                own_block(1, 1, length),
            ],
            out_specs=unit_block(count, 1, 3 * HD, lanes),
            scratch_shapes=[
                pltpu.VMEM((length, HD), BF16),
                pltpu.VMEM((length, HD), BF16),
                pltpu.VMEM((HD, length), BF16),
                pltpu.VMEM((length, lanes), jnp.int32),
                pltpu.VMEM((length, HD), F32),
                pltpu.VMEM((length, HD), F32),
            ],
        ),
        compiler_params=pltpu.CompilerParams(dimension_semantics=("arbitrary",)),
        name="attend_back",
    )(starts, x, flow, wide, lse)


def to_units(columns, parts, count, units):
    rows = columns.shape[1] // MB
    x = columns.reshape(parts, H, HD, MB, rows).transpose(1, 3, 0, 2, 4)
    x = x.reshape(UNITS, parts * HD, rows)
    places = [owner_of(count, u) * units + u // count for u in range(UNITS)]
    y = jnp.zeros((count * units, parts * HD, rows), columns.dtype)
    return y.at[jnp.array(places)].set(x).reshape(count, units, parts * HD, rows)


def from_units(x, parts):
    count, units, _, rows = x.shape
    places = [owner_of(count, u) * units + u // count for u in range(UNITS)]
    x = x.reshape(count * units, parts * HD, rows)[jnp.array(places)]
    x = x.reshape(H, MB, parts, HD, rows).transpose(2, 0, 3, 1, 4)
    return x.reshape(parts * D, MB * rows)


def mul_nn(a, b):
    return jnp.dot(a, b, preferred_element_type=F32)


def mul_tn(a, b):
    return lax.dot_general(a, b, (((0,), (0,)), ((), ())), preferred_element_type=F32)


def mul_nt(a, b):
    return lax.dot_general(a, b, (((1,), (1,)), ((), ())), preferred_element_type=F32)


def mul_tt(a, b):
    return lax.dot_general(a, b, (((0,), (1,)), ((), ())), preferred_element_type=F32)


def forward_kernel(
    width,
    starts_ref,
    tok_ref,
    joint_ref,
    mixer_ref,
    inner_ref,
    outer_ref,
    *refs,
):
    vec_refs = refs[:9]
    (
    att_ref,
    got_ref,
    wide_ref,
    lse_ref,
    joint_out,
    vec_full,
    inner_bias_full,
    mixer_out,
    inner_out,
    outer_out,
    joint_all,
    vec_put,
    vec_out,
    bias_rows,
    put,
    back_put,
    back_got,
    key_rows,
    value_t,
    key_docs,
    mixer_own,
    inner_own,
    outer_own,
    put_sem,
    got_sem,
    back_put_sem,
    back_got_sem,
    joint_sems,
    weight_sems,
    relay_sems,
    own_sems,
    ) = refs[9:]
    count, units, _, lanes = got_ref.shape
    length = count * lanes
    depth = min(length, 1024)
    group = width // lanes
    pairs = H // 2
    total_units = MB * H
    part = joint_ref.shape[0]
    me, shard = lax.axis_index("ctx"), lax.axis_index("fsdp")
    y, core = shard // 2, lax.rem(shard, 2)
    x = lax.rem(me, 2)
    far = 2 * (1 - y) + core
    other_core = {"fsdp": 2 * y + 1 - core}
    other_y = {"fsdp": far}
    other_x = {"ctx": me + 1 - 2 * x}
    mine = owned(count, me)

    barrier = pltpu.get_barrier_semaphore()

    def greet(step, carry):
        pl.semaphore_signal(barrier, inc=1, device_id={"ctx": lax.rem(me + step, count)})
        return carry

    lax.fori_loop(1, count, greet, 0)
    pl.semaphore_signal(barrier, inc=1, device_id=other_core)
    pl.semaphore_signal(barrier, inc=1, device_id=other_y)

    def remote(src, dst, sems, index, peer):
        return pltpu.make_async_remote_copy(
            src_ref=src,
            dst_ref=dst,
            send_sem=sems.at[(0, *index)],
            recv_sem=sems.at[(1, *index)],
            device_id=peer,
        )

    def own_joint(pair, third):
        columns = pl.ds(pl.multiple_of(third * D + pair * 128, 128), 128)
        return pltpu.make_async_copy(
            joint_ref.at[:, columns],
            joint_all.at[pair, shard, :, pl.ds(third * 128, 128)],
            own_sems.at[0, pair, third],
        )

    def joint_copy(kind, pair, third, which, peer, source=None):
        here = joint_all.at[pair, which, :, pl.ds(third * 128, 128)]
        if source is None:
            source = here
        else:
            source = source.at[:, pl.ds(pl.multiple_of(third * D + pair * 128, 128), 128)]
        return remote(source, here, joint_sems, (kind, pair, third), peer)

    def joint_y(pair, third):
        return joint_copy(0, pair, third, shard, other_y, joint_ref)

    def joint_core(pair, third):
        return joint_copy(1, pair, third, shard, other_core, joint_ref)

    def joint_pass(pair, third):
        return joint_copy(2, pair, third, far, other_core)

    def joint_store(pair):
        return pltpu.make_async_copy(
            joint_all.at[pair], joint_out.at[pair], own_sems.at[0, pair, 0]
        )

    def each_third(pair, make, act):
        for third in range(3):
            getattr(make(pair, third), act)()

    def every_pair(make, act):
        def body(pair, carry):
            each_third(pair, make, act)
            return carry

        lax.fori_loop(0, pairs, body, 0)

    every_pair(own_joint, "start")
    wholes = ((mixer_ref, mixer_own, mixer_out), (inner_ref, inner_own, inner_out), (outer_ref, outer_own, outer_out))
    own_in = [
        pltpu.make_async_copy(ref, held, own_sems.at[1, i, 0])
        for i, (ref, held, _) in enumerate(wholes)
    ]
    own_out = [
        pltpu.make_async_copy(held, out.at[shard], own_sems.at[1, i, 1])
        for i, (_, held, out) in enumerate(wholes)
    ]
    for copy in own_in:
        copy.start()
    for i, ref in enumerate(vec_refs):
        vec_put[i : i + 1, 0 : ref.shape[0]] = ref[...].astype(F32).reshape(1, ref.shape[0])
    vec_out[shard] = vec_put[...]
    pl.semaphore_wait(barrier, count + 1)

    class Vectors:
        def __init__(self, rows, columns, keys):
            mine, theirs = vec_out.at[shard, rows, columns], vec_out.at[far, rows, columns]
            source = vec_put.at[rows, columns]
            self.over_y = remote(source, mine, weight_sems, keys[0], other_y)
            self.core = remote(source, mine, weight_sems, keys[1], other_core)
            self.all = remote(theirs, theirs, weight_sems, keys[2], other_core)

        def begin(self):
            self.over_y.start()
            self.core.start()

        def hand_on(self):
            self.over_y.wait_recv()
            self.all.start()

        def arrive(self):
            self.core.wait_recv()
            self.all.wait_recv()

        def end(self):
            for copy in (self.over_y, self.core, self.all):
                copy.wait_send()

    narrow = Vectors(pl.ds(0, 8), pl.ds(0, -(-part // 128) * 128), ((0, 0), (0, 1), (0, 2)))
    broad = Vectors(pl.ds(8, 8), pl.ds(0, D), ((0, 3), (1, 3), (2, 3)))
    mixer_y = remote(mixer_ref, mixer_out.at[shard], weight_sems, (1, 0), other_y)
    mixer_core = remote(mixer_ref, mixer_out.at[shard], weight_sems, (1, 1), other_core)
    mixer_pass = remote(mixer_out.at[far], mixer_out.at[far], weight_sems, (1, 2), other_core)
    class Relayed:
        def __init__(self, ref, out, index, pieces):
            size = ref.shape[0] // 2
            piece = size // RELAY_PIECES
            self.over_y, self.over_x, self.rest = [], [], []
            for k in range(pieces):
                rows = pl.ds(pl.multiple_of(x * size + k * piece, piece), piece)
                self.over_y.append(
                    remote(
                        ref.at[rows, :],
                        out.at[shard, rows, :],
                        relay_sems,
                        (index, 0, k),
                        other_y,
                    )
                )
                passed = out.at[far, rows, :]
                self.over_x.append(remote(passed, passed, relay_sems, (index, 1, k), other_x))
            for k in range(2):
                if pieces < RELAY_PIECES:
                    rows = pl.ds(k * size + pieces * piece, size - pieces * piece)
                    self.rest.append(
                        remote(
                            ref.at[rows, :],
                            out.at[shard, rows, :],
                            relay_sems,
                            (index, 2, k),
                            other_y,
                        )
                    )
            self.core = remote(ref, out.at[shard], weight_sems, (2 + index, 0), other_core)
            self.all = remote(out.at[far], out.at[far], weight_sems, (2 + index, 1), other_core)

        def begin(self):
            for copy in self.over_y:
                copy.start()
            self.core.start()

        def begin_rest(self):
            for copy in self.rest:
                copy.start()

        def relay(self, k):
            self.over_y[k].wait_recv()
            self.over_x[k].start()

        def hand_on(self):
            for copy in self.over_x + self.rest:
                copy.wait_recv()
            self.all.start()

        def end(self):
            for copy in self.over_y + self.over_x + self.rest:
                copy.wait_send()
            self.core.wait()
            self.all.wait()

    outer_way = Relayed(outer_ref, outer_out, 0, RELAY_PIECES)
    inner_way = Relayed(inner_ref, inner_out, 1, 1)
    narrow.begin()

    def send_joint(pair, carry):
        each_third(pair, joint_y, "start")
        each_third(pair, joint_core, "start")
        return carry

    lax.fori_loop(0, pairs, send_joint, 0)
    outer_way.begin()
    inner_way.begin()
    mixer_y.start()
    mixer_core.start()
    inner_way.begin_rest()
    broad.begin()
    for first, second in zip(own_in, own_out):
        first.wait()
        second.start()

    narrow.hand_on()
    narrow.arrive()

    def bias_of(slot):
        pieces = [
            vec_out[f, slot : slot + 1, 0:part] for f in range(4)
        ]
        return jnp.concatenate(pieces, axis=1)

    query_bias, value_bias = bias_of(0), bias_of(1)
    for pair in range(pairs):
        columns = slice(pair * 128, (pair + 1) * 128)
        bias_rows[pair, :, 0:128] = jnp.broadcast_to(query_bias[:, columns], (8, 128))
        bias_rows[pair, :, 128:256] = jnp.zeros((8, 128), F32)
        bias_rows[pair, :, 256:384] = jnp.broadcast_to(value_bias[:, columns], (8, 128))

    def sent_sem(unit):
        return owner_of(count, unit), unit // count

    def send_copy(unit):
        owner, slot = sent_sem(unit)
        return pltpu.make_async_remote_copy(
            src_ref=put.at[owner, slot],
            dst_ref=got_ref.at[me, slot],
            send_sem=put_sem.at[owner, slot],
            recv_sem=got_sem.at[me, slot],
            device_id={"ctx": owner},
        )

    def keep_copy(slot):
        return pltpu.make_async_copy(
            put.at[me, slot], got_ref.at[me, slot], own_sems.at[2, slot, 0]
        )

    def project(pair, carry):
        each_third(pair, own_joint, "wait")
        each_third(pair, joint_y, "wait_recv")
        each_third(pair, joint_pass, "start")
        each_third(pair, joint_core, "wait_recv")
        each_third(pair, joint_pass, "wait_recv")
        joint_store(pair).start()
        weight = joint_all[pair].reshape(4 * part, 384)
        rows = jnp.dot(tok_ref[...], weight, preferred_element_type=F32)
        rows = (rows + bias_rows[pair, 0:1, :]).astype(BF16)
        for third in range(3):
            for batch in range(MB):
                block = rows[batch * lanes : (batch + 1) * lanes, third * 128 : (third + 1) * 128]
                turned = block.T
                if third == 0:
                    turned = turned * SCALE
                for j in range(2):
                    unit = (2 * pair + j) * MB + batch
                    put[owner_of(count, unit), unit // count, third * HD : (third + 1) * HD, :] = (
                        turned[j * HD : (j + 1) * HD]
                    )
        for i in range(2 * MB):
            unit = 2 * pair * MB + lax.rem(i + me, 2 * MB)
            owner, slot = owner_of(count, unit), unit // count

            @pl.when(owner != me)
            def _():
                send_copy(unit).start()

            @pl.when(owner == me)
            def _():
                keep_copy(slot).start()

        return carry

    lax.fori_loop(0, pairs, project, 0)

    def arrival(sender, slot):
        return pltpu.make_async_remote_copy(
            src_ref=put.at[sender, slot],
            dst_ref=got_ref.at[sender, slot],
            send_sem=put_sem.at[sender, slot],
            recv_sem=got_sem.at[sender, slot],
            device_id={"ctx": sender},
        )

    def back_copy(peer, slot):
        return pltpu.make_async_remote_copy(
            src_ref=back_put.at[peer, slot],
            dst_ref=back_got.at[me, slot],
            send_sem=back_put_sem.at[peer, slot],
            recv_sem=back_got_sem.at[me, slot],
            device_id={"ctx": peer},
        )

    def back_keep(slot):
        return pltpu.make_async_copy(
            back_put.at[me, slot], back_got.at[me, slot], own_sems.at[2, slot, 1]
        )

    early = total_units // count > 2

    def unit_step(slot, carry):
        def wait_one(step, inner):
            arrival(lax.rem(me + step, count), slot).wait_recv()
            return inner

        lax.fori_loop(1, count, wait_one, 0)
        keep_copy(slot).wait()
        for i in range(count):
            rows = slice(i * lanes, (i + 1) * lanes)
            key_rows[rows, :] = got_ref[i, slot, HD : 2 * HD, :].T
            value_t[:, rows] = got_ref[i, slot, 2 * HD : 3 * HD, :]
        batch = batch_of(count, me, slot)
        key_documents(starts_ref, batch, key_docs)

        def block(number, inner):
            begin = pl.multiple_of(number * width, width)
            parts = [got_ref[number * group + i, slot, 0:HD, :] for i in range(group)]
            queries = parts[0] if group == 1 else jnp.concatenate(parts, axis=1)
            query_docs = query_documents(starts_ref, batch, begin, width)

            def chunk(index, running):
                peak, total, mixed = running
                first = pl.multiple_of(index * depth, depth)
                scores = jnp.dot(
                    key_rows[pl.ds(first, depth), :], queries, preferred_element_type=F32
                )
                same = same_document(key_docs, first, depth, query_docs)
                scores = jnp.where(same, scores, MASKED)
                new_peak = jnp.maximum(peak, jnp.max(scores, axis=0, keepdims=True))
                scaling = jnp.exp(peak - new_peak)
                weights = jnp.exp(scores - new_peak)
                return (
                    new_peak,
                    total * scaling + jnp.sum(weights, axis=0, keepdims=True),
                    mixed * scaling
                    + jnp.dot(
                        value_t[:, pl.ds(first, depth)],
                        weights.astype(BF16),
                        preferred_element_type=F32,
                    ),
                )

            peak, total, mixed = over_chunks(
                length // depth,
                chunk,
                (
                    jnp.full((1, width), -jnp.inf, F32),
                    jnp.zeros((1, width), F32),
                    jnp.zeros((HD, width), F32),
                ),
            )
            mixed = mixed / total
            wide_ref[slot, :, pl.ds(begin, width)] = mixed
            lse_ref[slot, :, pl.ds(begin, width)] = peak + jnp.log(total)
            low = mixed.astype(BF16)
            for i in range(group):
                back_put[number * group + i, slot] = low[:, i * lanes : (i + 1) * lanes]
            return inner

        lax.fori_loop(0, length // width, block, 0)

        def send_one(step, inner):
            back_copy(lax.rem(me + step, count), slot).start()
            return inner

        lax.fori_loop(1, count, send_one, 0)
        back_keep(slot).start()
        if early:

            @pl.when(slot == 0)
            def _():
                outer_way.relay(0)
                outer_way.relay(1)

            @pl.when(slot == 1)
            def _():
                outer_way.relay(2)

            @pl.when(slot == 2)
            def _():
                inner_way.relay(0)

        return carry

    lax.fori_loop(0, mine, unit_step, 0)

    if not early:
        outer_way.relay(0)
        outer_way.relay(1)
        outer_way.relay(2)
        inner_way.relay(0)
    mixer_y.wait_recv()
    mixer_pass.start()
    outer_way.hand_on()

    def sent(unit, carry):
        @pl.when(owner_of(count, unit) != me)
        def _():
            send_copy(unit).wait_send()

        return carry

    lax.fori_loop(0, total_units, sent, 0)

    def returned(slot, carry):
        def one(step, inner):
            back_copy(lax.rem(me + step, count), slot).wait_send()
            return inner

        lax.fori_loop(1, count, one, 0)
        return carry

    lax.fori_loop(0, mine, returned, 0)
    inner_way.hand_on()
    broad.hand_on()

    def home(unit, carry):
        owner, slot = owner_of(count, unit), unit // count

        @pl.when(owner != me)
        def _():
            pltpu.make_async_remote_copy(
                src_ref=back_put.at[owner, slot],
                dst_ref=back_got.at[owner, slot],
                send_sem=back_put_sem.at[owner, slot],
                recv_sem=back_got_sem.at[owner, slot],
                device_id={"ctx": owner},
            ).wait_recv()

        @pl.when(owner == me)
        def _():
            back_keep(slot).wait()

        return carry

    lax.fori_loop(0, total_units, home, 0)
    for pair in range(pairs):
        for batch in range(MB):
            tops = []
            for j in range(2):
                unit = (2 * pair + j) * MB + batch
                tops.append(back_got[owner_of(count, unit), unit // count])
            block = jnp.concatenate(tops, axis=0).T
            att_ref[batch * lanes : (batch + 1) * lanes, pair * 128 : (pair + 1) * 128] = block

    outer_way.end()
    inner_way.end()
    broad.arrive()
    narrow.end()
    broad.end()
    for i in range(8):
        vec_full[i : i + 1, :] = bias_of(i)
    vec_full[8:16, :] = jnp.zeros((8, D), F32)
    for k in range(4):
        inner_bias_full[:, k * D : (k + 1) * D] = vec_out[k, 8:9, :]
    mixer_y.wait_send()
    mixer_core.wait()
    mixer_pass.wait()
    every_pair(joint_y, "wait_send")
    every_pair(joint_core, "wait_send")
    every_pair(joint_pass, "wait_send")
    for copy in own_out:
        copy.wait()

    for pair in range(pairs):
        joint_store(pair).wait()


def forward(count, starts, tokens, joint, mixer, inner, outer, vectors, number):
    units = -(-UNITS // count)
    lanes = tokens.shape[0] // MB
    length = count * lanes
    width = 2 * lanes
    part = joint.shape[0]
    pairs = H // 2
    vm = pl.BlockSpec(memory_space=pltpu.VMEM)
    hbm = pl.BlockSpec(memory_space=pl.ANY)
    dma = pltpu.SemaphoreType.DMA
    return pl.pallas_call(
        functools.partial(forward_kernel, width),
        out_shape=(
            jax.ShapeDtypeStruct(tokens.shape, BF16),
            jax.ShapeDtypeStruct((count, units, 3 * HD, lanes), BF16),
            jax.ShapeDtypeStruct((units, HD, length), F32),
            jax.ShapeDtypeStruct((units, 1, length), F32),
            jax.ShapeDtypeStruct((pairs, 4, part, 384), BF16),
            jax.ShapeDtypeStruct((BIAS_ROWS, D), F32),
            jax.ShapeDtypeStruct((1, FF), F32),
            jax.ShapeDtypeStruct((4, *mixer.shape), BF16),
            jax.ShapeDtypeStruct((4, *inner.shape), BF16),
            jax.ShapeDtypeStruct((4, *outer.shape), BF16),
        ),
        in_specs=[pl.BlockSpec(memory_space=pltpu.SMEM), vm] + [hbm] * 4 + [vm] * 9,
        out_specs=(vm, vm, vm, vm, hbm, vm, vm, hbm, hbm, hbm),
        scratch_shapes=[
            pltpu.VMEM((pairs, 4, part, 384), BF16),
            pltpu.VMEM((BIAS_ROWS, D), F32),
            pltpu.VMEM((4, BIAS_ROWS, D), F32),
            pltpu.VMEM((pairs, 8, 384), F32),
            pltpu.VMEM((count, units, 3 * HD, lanes), BF16),
            pltpu.VMEM((count, units, HD, lanes), BF16),
            pltpu.VMEM((count, units, HD, lanes), BF16),
            pltpu.VMEM((length, HD), BF16),
            pltpu.VMEM((HD, length), BF16),
            pltpu.VMEM((length, lanes), jnp.int32),
            pltpu.VMEM(mixer.shape, BF16),
            pltpu.VMEM(inner.shape, BF16),
            pltpu.VMEM(outer.shape, BF16),
            dma((count, units)),
            dma((count, units)),
            dma((count, units)),
            dma((count, units)),
            dma((2, 3, pairs, 3)),
            dma((2, 4, 4)),
            dma((2, 2, 3, RELAY_PIECES)),
            dma((3, max(pairs, units, 4), 3)),
        ],
        compiler_params=pltpu.CompilerParams(
            collective_id=number, has_side_effects=True, vmem_limit_bytes=56 * 1024 * 1024
        ),
        name="forward",
    )(starts, tokens, joint, mixer, inner, outer, *vectors)


def first_rows(half, tile):
    return half if half <= tile else (half // tile + 1) // 2 * tile


class Place:
    def __init__(self, count):
        self.count = count
        self.depth = count // 2
        self.me, self.shard = lax.axis_index("ctx"), lax.axis_index("fsdp")
        self.y, self.core = self.shard // 2, lax.rem(self.shard, 2)
        self.z, self.x = self.me // 2, lax.rem(self.me, 2)
        self.other_core = {"fsdp": 2 * self.y + 1 - self.core}
        self.other_y = {"fsdp": 2 * (1 - self.y) + self.core}
        self.other_x = {"ctx": 2 * self.z + 1 - self.x}

        self.hi, self.lo = self.z // 2, lax.rem(self.z, 2)

    def along_z(self, step):
        return lax.rem(self.z + step, self.depth)

    def peer_z(self, step):
        return {"ctx": 2 * self.along_z(step) + self.x}


def start(copies):
    for copy in copies:
        copy.start()


def added(a, b):
    return (a.astype(F32) + b.astype(F32)).astype(a.dtype)


class Reduction:
    def __init__(self, place, j, grad, out, head, paired, buffers, sems, z_sems):
        got, y_one, x_one, x_two, y_two, z_got = buffers
        self.place, self.grad, self.out, self.head, self.buffers = place, grad, out, head, buffers
        half, lanes = grad.shape[4], grad.shape[5] // 2
        self.half, self.lanes, self.paired = half, lanes, paired
        p = place
        here, there = self.side(p.y), self.side(1 - p.y)

        def remote(src, dst, slot, peer):
            return pltpu.make_async_remote_copy(
                src_ref=src,
                dst_ref=dst,
                send_sem=sems.at[0, j, slot],
                recv_sem=sems.at[1, j, slot],
                device_id=peer,
            )

        def z_copy(z, target, step):
            return pltpu.make_async_remote_copy(
                src_ref=grad.at[z // 2, lax.rem(z, 2), p.x, p.core, :, here],
                dst_ref=z_got.at[target],
                send_sem=z_sems.at[0, j, step],
                recv_sem=z_sems.at[1, j, step],
                device_id={"ctx": 2 * z + p.x},
            )

        self.first = [remote(grad.at[:, :, :, 1 - p.core], got, 0, p.other_core)]
        self.second = [remote(grad.at[:, :, :, p.core, 0:head, there], y_one, 1, p.other_y)]
        self.third = [
            remote(grad.at[:, :, 1 - p.x, p.core, 0:head, here], x_two, 2, p.other_x)
        ]
        if head < half:
            self.second.append(
                remote(grad.at[:, :, 1 - p.x, p.core, head:half, :], x_one, 3, p.other_x)
            )
            self.third.append(
                remote(grad.at[:, :, p.x, p.core, head:half, there], y_two, 4, p.other_y)
            )
        if paired:
            near = {"ctx": 2 * (2 * p.hi + 1 - p.lo) + p.x}
            self.fourth = [
                remote(
                    grad.at[:, 1 - p.lo, p.x, p.core, :, here], z_got.at[pl.ds(0, 2)], 6, near
                )
            ]
            self.fifth = [z_copy(2 * (1 - p.hi) + p.lo, 2, 1)]
        else:
            self.fourth = []
            self.fifth = [z_copy(lax.rem(p.z + step, 4), p.z, step) for step in range(1, 4)]
        self.last = [remote(out.at[p.core], out.at[p.core], 5, p.other_core)]

    def side(self, y):
        return pl.ds(pl.multiple_of(y * self.lanes, 128), self.lanes)

    def each(self, body):
        def step(block, carry):
            body(block // 2, lax.rem(block, 2))
            return carry

        lax.fori_loop(0, 4, step, 0)

    def stage_zero(self):
        start(self.first)

    def stage_one(self):
        p, grad, got = self.place, self.grad, self.buffers[0]
        for copy in self.first:
            copy.wait_recv()

        def body(hi, lo):
            for x in range(2):
                grad[hi, lo, x, p.core] = added(grad[hi, lo, x, p.core], got[hi, lo, x])

        self.each(body)
        start(self.second)

    def stage_two(self):
        p, grad, head, half = self.place, self.grad, self.head, self.half
        y_one, x_one = self.buffers[1], self.buffers[2]
        here = self.side(p.y)
        for copy in self.second:
            copy.wait()

        def body(hi, lo):
            for x in range(2):
                grad[hi, lo, x, p.core, 0:head, here] = added(
                    grad[hi, lo, x, p.core, 0:head, here], y_one[hi, lo, x]
                )
            if head < half:
                grad[hi, lo, p.x, p.core, head:half, :] = added(
                    grad[hi, lo, p.x, p.core, head:half, :], x_one[hi, lo]
                )

        self.each(body)
        start(self.third)

    def stage_three(self):
        p, grad, head, half = self.place, self.grad, self.head, self.half
        x_two, y_two = self.buffers[3], self.buffers[4]
        here = self.side(p.y)
        for copy in self.third:
            copy.wait()

        def body(hi, lo):
            grad[hi, lo, p.x, p.core, 0:head, here] = added(
                grad[hi, lo, p.x, p.core, 0:head, here], x_two[hi, lo]
            )
            if head < half:
                grad[hi, lo, p.x, p.core, head:half, here] = added(
                    grad[hi, lo, p.x, p.core, head:half, here], y_two[hi, lo]
                )

        self.each(body)
        start(self.fourth if self.paired else self.fifth)

    def stage_four(self):
        p, grad, z_got = self.place, self.grad, self.buffers[5]
        here = self.side(p.y)
        for copy in self.fourth:
            copy.wait()
        for hi in range(2):
            grad[hi, p.lo, p.x, p.core, :, here] = added(
                grad[hi, p.lo, p.x, p.core, :, here], z_got[hi]
            )
        start(self.fifth)

    def stage_five(self):
        p, z_got = self.place, self.buffers[5]
        for copy in self.fifth:
            copy.wait()
        total = self.grad[p.hi, p.lo, p.x, p.core, :, self.side(p.y)].astype(F32)
        if self.paired:
            total = total + z_got[2].astype(F32)
        else:
            for step in range(1, 4):
                total = total + z_got[lax.rem(p.z + step, 4)].astype(F32)
        self.out[p.core] = total.astype(self.out.dtype)
        start(self.last)

    def stage_six(self):
        for copy in self.last:
            copy.wait()
        for copy in self.first:
            copy.wait_send()


def reduction_buffers(half, lanes, head, dtype):
    tail = max(half - head, 16)
    shapes = (
        (2, 2, 2, half, 2 * lanes),
        (2, 2, 2, head, lanes),
        (2, 2, tail, 2 * lanes),
        (2, 2, head, lanes),
        (2, 2, tail, lanes),
        (4, half, lanes),
        (2, half, lanes),
    )
    return [pltpu.VMEM(shape, dtype) for shape in shapes]


def backward_kernel(width, plan, *refs):
    (
        starts_ref,
        flow_ref,
        got_ref,
        wide_ref,
        lse_ref,
        tok_ref,
        residual_ref,
        bias_ref,
        joint_ref,
        d_outer_ref,
        act_ref,
        d_inner_ref,
        first_ref,
        d_branch_ref,
        att_ref,
        tokens_out,
        outer_out,
        inner_out,
        mixer_out,
        joint_out,
        bias_out,
        flow_put,
        flow_got,
        put,
        home_got,
        key_rows,
        value_rows,
        key_t,
        key_docs,
        d_key,
        d_value,
        joint_all,
        outer_one,
        outer_two,
        inner_one,
        inner_two,
        mixer_grad,
        joint_one,
        joint_two,
        d_turned,
        bias_sum,
        bias_got,
        flow_sems,
        home_sems,
        own_sems,
        sems,
        z_sems,
        bias_sems,
        *buffers,
    ) = refs
    count, units, _, lanes = got_ref.shape
    length = count * lanes
    depth = min(length, 1024)
    group = width // lanes
    pairs = H // 2
    total_units = MB * H
    p = Place(count)
    me = p.me
    mine = owned(count, me)

    barrier = pltpu.get_barrier_semaphore()

    def greet(step, carry):
        pl.semaphore_signal(barrier, inc=1, device_id={"ctx": lax.rem(me + step, count)})
        return carry

    lax.fori_loop(1, count, greet, 0)
    pl.semaphore_signal(barrier, inc=1, device_id=p.other_core)
    pl.semaphore_signal(barrier, inc=1, device_id=p.other_y)
    pl.semaphore_signal(barrier, inc=1, device_id={**p.other_y, **p.other_x})
    joint_load = pltpu.make_async_copy(joint_ref, joint_all, own_sems.at[2, 0])
    joint_load.start()

    grads = (outer_one, outer_two, inner_one, inner_two, mixer_grad, joint_one, joint_two)
    jobs = [
        Reduction(
            p,
            j,
            grads[j],
            buffers[7 * j + 6],
            plan[j][2],
            plan[j][3],
            buffers[7 * j : 7 * j + 6],
            sems,
            z_sems,
        )
        for j in range(len(grads))
    ]
    o_one, o_two, i_one, i_two, m_one, j_one, j_two = jobs

    def store_rows(targets, row, values, columns):
        half = sum(t.shape[4] for t in targets)
        done = 0
        while done < values.shape[0]:
            block, inside = (row + done) // half, (row + done) % half
            k = 0
            while inside >= targets[k].shape[4]:
                inside -= targets[k].shape[4]
                k += 1
            size = min(values.shape[0] - done, targets[k].shape[4] - inside)
            targets[k][
                block // 8,
                block // 4 % 2,
                block // 2 % 2,
                block % 2,
                inside : inside + size,
                columns,
            ] = values[done : done + size]
            done += size

    d_outer_turned = d_outer_ref[...].T

    def outer_gradient(which):
        for side in range(2):
            begin = (2 * side + which) * D
            values = jnp.dot(
                d_outer_turned, act_ref[:, begin : begin + D], preferred_element_type=F32
            )
            columns = slice(side * D, (side + 1) * D)
            store_rows(((outer_one, outer_two)[which],), 0, values.astype(BF16), columns)

    def inner_gradient():
        for k in range(FF // D):
            turned = d_inner_ref[:, k * D : (k + 1) * D].T
            values = jnp.dot(turned, first_ref[...], preferred_element_type=F32)
            store_rows((inner_one, inner_two), k * D, values.astype(BF16), slice(0, D))

    def mixer_gradient():
        values = jnp.dot(d_branch_ref[...].T, att_ref[...], preferred_element_type=F32)
        store_rows((mixer_grad,), 0, values.astype(BF16), slice(0, D))

    def unit_copy(source, target, sem, owner, slot):
        return pltpu.make_async_remote_copy(
            src_ref=source.at[owner, slot],
            dst_ref=target.at[me, slot],
            send_sem=sem.at[0, owner, slot],
            recv_sem=sem.at[1, me, slot],
            device_id={"ctx": owner},
        )

    def unit_arrival(source, target, sem, sender, slot):
        return pltpu.make_async_remote_copy(
            src_ref=source.at[sender, slot],
            dst_ref=target.at[sender, slot],
            send_sem=sem.at[0, sender, slot],
            recv_sem=sem.at[1, sender, slot],
            device_id={"ctx": sender},
        )

    def unit_keep(source, target, kind, slot):
        return pltpu.make_async_copy(
            source.at[me, slot], target.at[me, slot], own_sems.at[kind, slot]
        )

    for pair in range(pairs):
        for batch in range(MB):
            block = flow_ref[
                batch * lanes : (batch + 1) * lanes, pair * 128 : (pair + 1) * 128
            ].T
            for j in range(2):
                unit = (2 * pair + j) * MB + batch
                flow_put[owner_of(count, unit), unit // count] = block[j * HD : (j + 1) * HD]

    pl.semaphore_wait(barrier, count + 2)

    def send_flow(turn, carry):
        slot, owner = turn // count, lax.rem(me + turn, count)

        @pl.when((owner != me) & (slot < owned(count, owner)))
        def _():
            unit_copy(flow_put, flow_got, flow_sems, owner, slot).start()

        @pl.when((owner == me) & (slot < mine))
        def _():
            unit_keep(flow_put, flow_got, 0, slot).start()

        return carry

    lax.fori_loop(0, units * count, send_flow, 0)
    bias_sum[0] = bias_ref[...]
    outer_gradient(0)
    o_one.stage_zero()
    outer_gradient(1)
    o_two.stage_zero()
    o_one.stage_one()
    inner_gradient()
    i_one.stage_zero()
    i_two.stage_zero()
    mixer_gradient()
    m_one.stage_zero()

    def unit_step(slot, carry):
        def wait_one(step, inner):
            unit_arrival(flow_put, flow_got, flow_sems, lax.rem(me + step, count), slot).wait_recv()
            return inner

        lax.fori_loop(1, count, wait_one, 0)
        unit_keep(flow_put, flow_got, 0, slot).wait()
        for i in range(count):
            rows = slice(i * lanes, (i + 1) * lanes)
            key_rows[rows, :] = got_ref[i, slot, HD : 2 * HD, :].T
            value_rows[rows, :] = got_ref[i, slot, 2 * HD : 3 * HD, :].T
            key_t[:, rows] = got_ref[i, slot, HD : 2 * HD, :]
        batch = batch_of(count, me, slot)
        key_documents(starts_ref, batch, key_docs)
        d_key[...] = jnp.zeros_like(d_key)
        d_value[...] = jnp.zeros_like(d_value)

        def block(number, inner):
            begin = pl.multiple_of(number * width, width)

            def beside(ref):
                parts = [ref[number * group + i, slot, 0:HD, :] for i in range(group)]
                return parts[0] if group == 1 else jnp.concatenate(parts, axis=1)

            queries, flow = beside(got_ref), beside(flow_got)
            query_rows, flow_rows = queries.T, flow.T
            query_docs = query_documents(starts_ref, batch, begin, width)
            log_total = lse_ref[slot, :, pl.ds(begin, width)]
            spread = jnp.sum(
                flow.astype(F32) * wide_ref[slot, :, pl.ds(begin, width)], axis=0, keepdims=True
            )

            def chunk(index, d_query):
                first = pl.multiple_of(index * depth, depth)
                rows = pl.ds(first, depth)
                scores = jnp.dot(key_rows[rows, :], queries, preferred_element_type=F32)
                same = same_document(key_docs, first, depth, query_docs)
                probs = jnp.exp(jnp.where(same, scores, MASKED) - log_total)
                pressure = jnp.dot(value_rows[rows, :], flow, preferred_element_type=F32)
                d_scores = (probs * (pressure - spread)).astype(BF16)
                d_value[rows, :] += jnp.dot(
                    probs.astype(BF16), flow_rows, preferred_element_type=F32
                )
                d_key[rows, :] += jnp.dot(d_scores, query_rows, preferred_element_type=F32)
                return d_query + jnp.dot(key_t[:, rows], d_scores, preferred_element_type=F32)

            d_query = over_chunks(length // depth, chunk, jnp.zeros((HD, width), F32))
            low = (d_query * SCALE).astype(BF16)
            for i in range(group):
                put[number * group + i, slot, 0:HD, :] = low[:, i * lanes : (i + 1) * lanes]
            return inner

        lax.fori_loop(0, length // width, block, 0)
        for i in range(count):
            rows = slice(i * lanes, (i + 1) * lanes)
            put[i, slot, HD : 2 * HD, :] = d_key[rows, :].T.astype(BF16)
            put[i, slot, 2 * HD : 3 * HD, :] = d_value[rows, :].T.astype(BF16)

        def send_one(step, inner):
            unit_copy(put, home_got, home_sems, lax.rem(me + step, count), slot).start()
            return inner

        lax.fori_loop(1, count, send_one, 0)
        unit_keep(put, home_got, 1, slot).start()

        @pl.when(slot == 0)
        def _():
            o_two.stage_one()

        @pl.when(slot == 2)
        def _():
            o_one.stage_two()
            i_one.stage_one()

        return carry

    lax.fori_loop(0, mine, unit_step, 0)
    o_two.stage_two()
    i_two.stage_one()
    o_one.stage_three()
    i_one.stage_two()
    m_one.stage_one()

    ones = jnp.ones((8, MB * lanes), BF16)
    for pair in range(pairs):
        columns = []
        for batch in range(MB):
            blocks = []
            for j in range(2):
                unit = (2 * pair + j) * MB + batch
                owner, slot = owner_of(count, unit), unit // count

                @pl.when(owner != me)
                def _():
                    unit_arrival(put, home_got, home_sems, owner, slot).wait_recv()

                @pl.when(owner == me)
                def _():
                    unit_keep(put, home_got, 1, slot).wait()

                blocks.append(home_got[owner, slot])
            rows = [b[third * HD : (third + 1) * HD] for third in range(3) for b in blocks]
            columns.append(jnp.concatenate(rows, axis=0))
        d_pair = jnp.concatenate(columns, axis=1)
        d_turned[pair] = d_pair.T
        grad = jnp.dot(d_pair, tok_ref[...], preferred_element_type=F32).astype(BF16)
        for third in range(3):
            store_rows(
                (joint_one, joint_two),
                third * D + pair * 128,
                grad[third * 128 : (third + 1) * 128],
                slice(0, D),
            )
        sums = lax.dot_general(
            ones, d_pair, (((1,), (1,)), ((), ())), preferred_element_type=F32
        )
        bias_sum[0, 0:1, pair * 128 : (pair + 1) * 128] = sums[0:1, 0:128]
        bias_sum[0, 1:2, pair * 128 : (pair + 1) * 128] = sums[0:1, 256:384]
        if pair == 2:
            o_two.stage_three()
            o_one.stage_four()
            i_two.stage_two()
            i_one.stage_three()

    m_one.stage_two()
    o_two.stage_four()

    plane = (p.other_y, p.other_x, {**p.other_y, **p.other_x})

    def bias_copy(level, number, slot, peer):
        return pltpu.make_async_remote_copy(
            src_ref=bias_sum.at[level],
            dst_ref=bias_got.at[slot],
            send_sem=bias_sems.at[0, number],
            recv_sem=bias_sems.at[1, number],
            device_id=peer,
        )

    bias_core = bias_copy(0, 0, 0, p.other_core)
    bias_plane = [bias_copy(1, 1 + i, 1 + i, peer) for i, peer in enumerate(plane)]
    bias_z = [
        bias_copy(2, 3 + step, 3 + step, {"ctx": 2 * lax.rem(p.z + step, 4) + p.x})
        for step in range(1, 4)
    ]
    bias_core.start()
    j_one.stage_zero()
    j_two.stage_zero()

    joint_load.wait()

    def token_terms(first, last, total):
        for pair in range(first, last):
            total = total + lax.dot_general(
                d_turned[pair],
                joint_all[pair],
                (((1,), (1,)), ((), ())),
                preferred_element_type=F32,
            )
        tokens_out[...] = total

    token_terms(0, pairs // 2, residual_ref[...])
    bias_core.wait()
    bias_sum[1] = bias_sum[0] + bias_got[0]
    start(bias_plane)
    j_one.stage_one()
    j_two.stage_one()
    i_two.stage_three()
    i_one.stage_four()
    token_terms(pairs // 2, pairs, tokens_out[...])
    m_one.stage_three()
    for copy in bias_plane:
        copy.wait()
    bias_sum[2] = bias_sum[1] + bias_got[1] + bias_got[2] + bias_got[3]
    start(bias_z)
    j_one.stage_two()
    i_two.stage_four()
    j_two.stage_two()
    m_one.stage_four()
    j_one.stage_three()
    j_two.stage_three()
    o_one.stage_five()
    o_two.stage_five()
    i_one.stage_five()

    def parts_of(j):
        jobs[j].stage_six()
        whole = buffers[7 * j + 6]
        return [whole[low].astype(F32) for low in range(2)]

    def own_lanes(rows):
        width_own = rows.shape[1] // 2
        return jnp.where(p.core == 0, rows[:, :width_own], rows[:, width_own:])

    def put_out(out, pieces):
        out[...] = jnp.concatenate(pieces, axis=0).T

    one, two = parts_of(0), parts_of(1)
    outer_out[...] = jnp.concatenate(
        [jnp.where(p.core == 0, a, b) for a, b in zip(one, two)], axis=0
    )
    i_two.stage_five()
    m_one.stage_five()
    one, two = parts_of(2), parts_of(3)
    put_out(inner_out, [own_lanes(r) for r in (one[0], two[0], one[1], two[1])])
    put_out(mixer_out, [own_lanes(r) for r in parts_of(4)])
    for copy in bias_z:
        copy.wait()
    bias_total = bias_sum[2] + bias_got[4] + bias_got[5] + bias_got[6]
    index = me * 4 + p.shard
    world = 4 * count
    lane = lax.broadcasted_iota(jnp.int32, (D, 128), 0)
    place = lax.broadcasted_iota(jnp.int32, (D, 128), 1)

    def picked(rows, first):
        ones_there = jnp.where(lane == place + first, 1.0, 0.0)
        return jnp.dot(
            rows, ones_there, precision=lax.Precision.HIGHEST, preferred_element_type=F32
        )

    own_hidden = FF // world
    in_row = D // own_hidden
    row = lax.broadcasted_iota(jnp.int32, (8, D), 0)
    hidden = jnp.where(row == index // in_row, bias_total[8:16], 0.0)
    hidden = jnp.broadcast_to(jnp.sum(hidden, axis=0, keepdims=True), (8, D))
    bias_out[0:8, :] = picked(bias_total[0:8], index * (D // world))
    bias_out[8:16, :] = picked(hidden, lax.rem(index, in_row) * own_hidden)

    def sent(unit, carry):
        owner, slot = owner_of(count, unit), unit // count

        @pl.when(owner != me)
        def _():
            unit_copy(flow_put, flow_got, flow_sems, owner, slot).wait_send()

        return carry

    lax.fori_loop(0, total_units, sent, 0)

    def returned(slot, carry):
        def one(step, inner):
            unit_copy(put, home_got, home_sems, lax.rem(me + step, count), slot).wait_send()
            return inner

        lax.fori_loop(1, count, one, 0)
        return carry

    lax.fori_loop(0, mine, returned, 0)
    j_one.stage_five()
    j_two.stage_five()
    one, two = parts_of(5), parts_of(6)
    put_out(joint_out, [own_lanes(r) for r in (one[0], two[0], one[1], two[1])])


def backward(
    starts, flow, got, wide, lse, source, residual, biases, joint, activations, number
):
    count, units, _, lanes = got.shape
    length = count * lanes
    width = 2 * lanes
    pairs = H // 2
    vm = pl.BlockSpec(memory_space=pltpu.VMEM)
    hbm = pl.BlockSpec(memory_space=pl.ANY)
    dma = pltpu.SemaphoreType.DMA
    small = D // (2 * count)
    half_joint = 3 * D // (2 * count)
    early = first_rows(half_joint, 16)
    plan = (
        (small, FF // 2, small, True),
        (small, FF // 2, small, True),
        (2 * small, D, 4 * small // 3, True),
        (2 * small, D, 4 * small // 3, True),
        (small, D, small, True),
        (early, D, first_rows(early, 16), False),
        (half_joint - early, D, first_rows(half_joint - early, 16), False),
    )
    buffers = []
    for half, full, head, _ in plan:
        buffers += reduction_buffers(half, full // 2, head, BF16)
    outs = [
        jax.ShapeDtypeStruct((2 * small, FF // 4), F32),
        jax.ShapeDtypeStruct((D // 4, FF // count), F32),
        jax.ShapeDtypeStruct((D // 4, 2 * small), F32),
        jax.ShapeDtypeStruct((D // 4, 2 * half_joint), F32),
    ]
    return pl.pallas_call(
        functools.partial(backward_kernel, width, plan),
        out_shape=(
            jax.ShapeDtypeStruct(residual.shape, F32),
            *outs,
            jax.ShapeDtypeStruct((BIAS_ROWS, 128), F32),
        ),
        in_specs=[pl.BlockSpec(memory_space=pltpu.SMEM)] + [vm] * 7 + [hbm] + [vm] * 6,
        out_specs=(vm,) * 6,
        scratch_shapes=[
            pltpu.VMEM((count, units, HD, lanes), BF16),
            pltpu.VMEM((count, units, HD, lanes), BF16),
            pltpu.VMEM((count, units, 3 * HD, lanes), BF16),
            pltpu.VMEM((count, units, 3 * HD, lanes), BF16),
            pltpu.VMEM((length, HD), BF16),
            pltpu.VMEM((length, HD), BF16),
            pltpu.VMEM((HD, length), BF16),
            pltpu.VMEM((length, lanes), jnp.int32),
            pltpu.VMEM((length, HD), F32),
            pltpu.VMEM((length, HD), F32),
            pltpu.VMEM((pairs, D, 384), BF16),
            *[pltpu.VMEM((2, 2, 2, 2, half, full), BF16) for half, full, _, _ in plan],
            pltpu.VMEM((pairs, MB * lanes, 384), BF16),
            pltpu.VMEM((3, BIAS_ROWS, D), F32),
            pltpu.VMEM((7, BIAS_ROWS, D), F32),
            dma((2, count, units)),
            dma((2, count, units)),
            dma((3, units)),
            dma((2, len(plan), 7)),
            dma((2, len(plan), 4)),
            dma((2, 7)),
            *buffers,
        ],
        compiler_params=pltpu.CompilerParams(
            collective_id=number, has_side_effects=True, vmem_limit_bytes=67043328
        ),
        name="backward",
    )(starts, flow, got, wide, lse, source, residual, biases, joint, *activations)


def settle_kernel(count, *refs):
    copies = [
        pltpu.make_async_copy(refs[i], refs[count + i], refs[2 * count].at[i])
        for i in range(count)
    ]
    start(copies)
    for copy in copies:
        copy.wait()


def settle(*arrays):
    count = len(arrays)
    return pl.pallas_call(
        functools.partial(settle_kernel, count),
        out_shape=[jax.ShapeDtypeStruct(a.shape, a.dtype) for a in arrays],
        in_specs=[pl.BlockSpec(memory_space=pltpu.VMEM)] * count,
        out_specs=[pl.BlockSpec(memory_space=pl.ANY)] * count,
        scratch_shapes=[pltpu.SemaphoreType.DMA((count,))],
        name="settle",
    )(*arrays)


def on_device(
    count,
    shards,
    tokens,
    doc_starts,
    joint_weight,
    mixer_weight,
    inner_weight,
    outer_weight,
    query_bias,
    value_bias,
    mixer_bias,
    first_gain,
    first_shift,
    inner_bias,
    outer_bias,
    second_gain,
    second_shift,
    upstream,
):
    rows = tokens.shape[2]
    length = rows * count
    units = -(-MB * H // count)
    me = lax.axis_index("ctx")

    part = D // shards
    vectors = [
        query_bias,
        value_bias,
        mixer_bias,
        first_gain,
        first_shift,
        outer_bias,
        second_gain,
        second_shift,
        inner_bias,
    ]
    source = tokens.reshape(MB * rows, D)
    attended, received, wide, lse, joint, vectors, ibias, mixer, inner, outer = forward(
        count,
        doc_starts,
        source,
        joint_weight,
        mixer_weight,
        inner_weight,
        outer_weight,
        vectors,
        0,
    )
    joint = joint.reshape(H // 2, D, 384)
    mixer, inner, outer = mixer.reshape(D, D), inner.reshape(D, FF), outer.reshape(FF, D)
    _, _, mbias, gain_one, shift_one, obias, gain_two, shift_two = [
        vectors[i : i + 1] for i in range(8)
    ]

    branch = mul_nn(attended, mixer) + mbias
    first, first_normed, first_recip = norm_forward(
        source.astype(F32) + branch, gain_one, shift_one
    )
    first_low = first.astype(BF16)
    inner_pre = mul_nn(first_low, inner) + ibias
    activated, gelu_slope = gelu_parts(inner_pre)
    activated_low = activated.astype(BF16)
    outer_out = mul_nn(activated_low, outer) + obias
    final, second_normed, second_recip = norm_forward(first + outer_out, gain_two, shift_two)
    result = final.astype(BF16).reshape(MB, 1, rows, D)

    incoming = upstream.reshape(MB * rows, D).astype(F32)
    rescale_grad = jnp.sum(incoming * second_normed, axis=0)
    reshift_grad = jnp.sum(incoming, axis=0)
    d_second = norm_backward(incoming, second_normed, second_recip, gain_two)
    d_outer = d_second.astype(BF16)
    return_grad = jnp.sum(d_outer.astype(F32), axis=0)
    d_inner = (mul_nt(d_outer, outer) * gelu_slope).astype(BF16)
    hidden_grad = jnp.sum(d_inner.astype(F32), axis=0)
    d_first = d_second + mul_nt(d_inner, inner)
    scale_grad = jnp.sum(d_first * first_normed, axis=0)
    shift_grad = jnp.sum(d_first, axis=0)
    d_residual = norm_backward(d_first, first_normed, first_recip, gain_one)
    d_branch = d_residual.astype(BF16)
    mixing_grad = jnp.sum(d_branch.astype(F32), axis=0)
    world = count * shards
    index = me * shards + lax.axis_index("fsdp")
    sums = [
        mixing_grad,
        scale_grad,
        shift_grad,
        return_grad,
        rescale_grad,
        reshift_grad,
        *hidden_grad.reshape(FF // D, D),
    ]
    if shards == 4 and count == 8:
        flow = mul_nt(d_branch, mixer).astype(BF16)
        biases = jnp.pad(jnp.stack(sums), ((2, BIAS_ROWS - 2 - len(sums)), (0, 0)))
        tokens_grad, *blocks, biases = backward(
            doc_starts,
            flow,
            received,
            wide,
            lse,
            source,
            d_residual,
            biases,
            joint,
            [d_outer, activated_low, d_inner, first_low, d_branch, attended],
            1,
        )
        tokens_grad, *blocks = settle(tokens_grad, *blocks)
        blocks[0] = blocks[0].T
        own, own_hidden = biases[:8, : D // world], biases[8, : FF // world]
    else:
        natural = joint.reshape(H // 2, D, 3, 128).transpose(1, 2, 0, 3).reshape(D, 3 * D)
        flow = mul_nt(mixer, d_branch).astype(BF16)
        flow_units = exchange(to_units(flow, 1, count, units), 2)
        d_units = attend_back(received, flow_units, doc_starts, wide, lse)
        d_joint = from_units(exchange(d_units, 3), 3)
        bias_sums = jnp.sum(d_joint.astype(F32), axis=1)
        turned = [
            mul_tn(d_outer, activated_low),
            mul_tn(d_inner, first_low),
            mul_tn(d_branch, attended),
            mul_nn(d_joint, source),
        ]
        tokens_grad = d_residual + mul_tt(d_joint, natural)

        def reduced(grad):
            over_lanes = lax.psum_scatter(
                grad.astype(BF16), "fsdp", scatter_dimension=1, tiled=True
            )
            over_rows = lax.psum_scatter(over_lanes, "ctx", scatter_dimension=0, tiled=True)
            return over_rows.T.astype(F32)

        blocks = [reduced(g) for g in turned]
        biases = jnp.stack([bias_sums[:D], bias_sums[2 * D :], *sums])
        biases = lax.psum(biases, ("ctx", "fsdp"))
        own = lax.dynamic_slice_in_dim(biases[:8], index * (D // world), D // world, 1)
        hidden_rows = biases[8 : 8 + FF // D].reshape(FF)
        own_hidden = lax.dynamic_slice_in_dim(hidden_rows, index * (FF // world), FF // world, 0)
    tokens_grad = tokens_grad.reshape(MB, 1, rows, D)
    outer_out_grad, inner_out, mixer_out, joint_out = blocks
    sums = [*own[:5], own_hidden, *own[5:]]
    return (result, tokens_grad, joint_out, mixer_out, inner_out, outer_out_grad, *sums)


def solution(mesh):
    in_specs = (
        P(None, "fsdp", "ctx", None),
        P(None, "fsdp", None),
        P("fsdp", None),
        P("fsdp", None),
        P("fsdp", None),
        P("fsdp", None),
        P("fsdp"),
        P("fsdp"),
        P("fsdp"),
        P("fsdp"),
        P("fsdp"),
        P("fsdp"),
        P("fsdp"),
        P("fsdp"),
        P("fsdp"),
        P(None, "fsdp", "ctx", None),
    )
    out_specs = (
        P(None, "fsdp", "ctx", None),
        P(None, "fsdp", "ctx", None),
        P("fsdp", "ctx"),
        P("fsdp", "ctx"),
        P("fsdp", "ctx"),
        P("fsdp", "ctx"),
        P(("ctx", "fsdp")),
        P(("ctx", "fsdp")),
        P(("ctx", "fsdp")),
        P(("ctx", "fsdp")),
        P(("ctx", "fsdp")),
        P(("ctx", "fsdp")),
        P(("ctx", "fsdp")),
        P(("ctx", "fsdp")),
        P(("ctx", "fsdp")),
    )
    return jax.shard_map(
        functools.partial(on_device, mesh.shape["ctx"], mesh.shape["fsdp"]),
        mesh=mesh,
        in_specs=in_specs,
        out_specs=out_specs,
        check_vma=False,
    )
```

```python
import functools
import math

import jax
import jax.numpy as jnp
from jax import lax
from jax.experimental import pallas as pl
from jax.experimental.pallas import tpu as pltpu
from jax.sharding import PartitionSpec as P

D = 768
H = 12
HD = 64
FF = 3072
MB = 3

SCALE = 0.125
EPSILON = 1e-12
MASKED = -1000000000.0
ROOT_HALF = 0.7071067811865476
GAUSS_PEAK = 0.3989422804014327

F32 = jnp.float32
BF16 = jnp.bfloat16


def norm_forward(hidden, gain, shift):
    average = jnp.mean(hidden, axis=-1, keepdims=True)
    centred = hidden - average
    reciprocal = lax.rsqrt(jnp.mean(centred * centred, axis=-1, keepdims=True) + EPSILON)
    normed = centred * reciprocal
    return (normed * gain + shift, normed, reciprocal)


def norm_backward(incoming, normed, reciprocal, gain):
    scaled = incoming * gain
    return reciprocal * (
        scaled
        - jnp.mean(scaled, axis=-1, keepdims=True)
        - normed * jnp.mean(scaled * normed, axis=-1, keepdims=True)
    )


def gelu_parts(inner):
    cumulative = 0.5 * (1.0 + lax.erf(inner * ROOT_HALF))
    return (inner * cumulative, cumulative + inner * jnp.exp(-0.5 * inner * inner) * GAUSS_PEAK)


UNITS = MB * H
BIAS_ROWS = 16
RELAY_PIECES = 3


def spare_owner(count, j):
    stride = count // (UNITS % count)
    return j * stride + (j % 2 if stride > 1 else 0)


def owner_of(count, unit):
    full, rest = UNITS // count, UNITS % count
    if rest == 0:
        return unit % count
    if full == 0:
        return spare_owner(count, unit)
    late = unit // (full * count)
    return (1 - late) * (unit % count) + late * spare_owner(count, unit - full * count)


def spare_index(count, device):
    return device // (count // (UNITS % count))


def owned(count, device):
    full, rest = UNITS // count, UNITS % count
    if rest == 0:
        return full
    j = spare_index(count, device)
    extra = (spare_owner(count, j) == device) & (j < rest)
    return full + extra.astype(jnp.int32)


def batch_of(count, device, slot):
    full, rest = UNITS // count, UNITS % count
    if rest == 0:
        return (slot * count + device) % MB
    if full == 0:
        return jnp.minimum(spare_index(count, device), UNITS - 1) % MB
    late = slot // full
    unit = slot * count + (1 - late) * device + late * spare_index(count, device)
    return unit % MB


def exchange_kernel(count, x_ref, y_ref, held, send_sem, recv_sem, own_sem):
    me = lax.axis_index("ctx")
    barrier = pltpu.get_barrier_semaphore()

    def greet(step, carry):
        peer = lax.rem(me + step, count)
        pl.semaphore_signal(barrier, inc=1, device_id={"ctx": peer})
        return carry

    lax.fori_loop(1, count, greet, 0)
    own_in = pltpu.make_async_copy(x_ref.at[me], held, own_sem)
    own_in.start()
    pl.semaphore_wait(barrier, count - 1)

    def transfer(step):
        peer = lax.rem(me + step, count)
        return pltpu.make_async_remote_copy(
            src_ref=x_ref.at[peer],
            dst_ref=y_ref.at[me],
            send_sem=send_sem.at[step],
            recv_sem=recv_sem.at[step],
            device_id={"ctx": peer},
        )

    def begin(step, carry):
        transfer(step).start()
        return carry

    lax.fori_loop(1, count, begin, 0)
    own_in.wait()
    own_out = pltpu.make_async_copy(held, y_ref.at[me], own_sem)
    own_out.start()
    own_out.wait()

    def finish(step, carry):
        transfer(step).wait()
        return carry

    lax.fori_loop(1, count, finish, 0)


def exchange(x, number):
    count = x.shape[0]
    return pl.pallas_call(
        functools.partial(exchange_kernel, count),
        out_shape=jax.ShapeDtypeStruct(x.shape, x.dtype),
        in_specs=[pl.BlockSpec(memory_space=pl.ANY)],
        out_specs=pl.BlockSpec(memory_space=pl.ANY),
        scratch_shapes=[
            pltpu.VMEM(x.shape[1:], x.dtype),
            pltpu.SemaphoreType.DMA((count,)),
            pltpu.SemaphoreType.DMA((count,)),
            pltpu.SemaphoreType.DMA,
        ],
        compiler_params=pltpu.CompilerParams(collective_id=number, has_side_effects=True),
        name=f"exchange_{number}",
    )(x)


def across(ref, first, rows, width, lanes):
    parts = [ref[first + i, 0, rows, :] for i in range(width // lanes)]
    return parts[0] if len(parts) == 1 else jnp.concatenate(parts, axis=1)


def document(starts_ref, batch, position):
    docs = jnp.zeros(position.shape, jnp.int32) - 1
    for j in range(starts_ref.shape[2]):
        docs = docs + jnp.where(position >= starts_ref[batch, 0, j], 1, 0)
    return docs


def key_documents(starts_ref, batch, key_docs):
    key_docs[...] = document(
        starts_ref, batch, lax.broadcasted_iota(jnp.int32, key_docs.shape, 0)
    )


def query_documents(starts_ref, batch, begin, width):
    return document(
        starts_ref, batch, lax.broadcasted_iota(jnp.int32, (1, width), 1) + begin
    )


def same_document(key_docs, first, width, query_docs):
    keys = key_docs[pl.ds(first, width), :]
    lanes = keys.shape[1]
    parts = [keys == query_docs[:, i : i + lanes] for i in range(0, query_docs.shape[1], lanes)]
    return parts[0] if len(parts) == 1 else jnp.concatenate(parts, axis=1)


def over_chunks(chunks, body, carry):
    if chunks == 1:
        return body(0, carry)
    return lax.fori_loop(0, chunks, body, carry)


def attend_back_kernel(
    width,
    starts_ref,
    x_ref,
    flow_ref,
    wide_ref,
    lse_ref,
    d_ref,
    key_rows,
    value_rows,
    key_t,
    key_docs,
    d_key,
    d_value,
):
    count, _, _, lanes = x_ref.shape
    length = count * lanes
    depth = min(length, 1024)
    unit = pl.program_id(0)
    for i in range(count):
        rows = slice(i * lanes, (i + 1) * lanes)
        key_rows[rows, :] = x_ref[i, 0, HD : 2 * HD, :].T
        value_rows[rows, :] = x_ref[i, 0, 2 * HD : 3 * HD, :].T
        key_t[:, rows] = x_ref[i, 0, HD : 2 * HD, :]
    batch = batch_of(count, lax.axis_index("ctx"), unit)
    key_documents(starts_ref, batch, key_docs)
    d_key[...] = jnp.zeros_like(d_key)
    d_value[...] = jnp.zeros_like(d_value)
    group = width // lanes

    def block(number, carry):
        begin = pl.multiple_of(number * width, width)
        queries = across(x_ref, number * group, slice(0, HD), width, lanes)
        flow = across(flow_ref, number * group, slice(0, HD), width, lanes)
        query_rows = queries.T
        flow_rows = flow.T
        query_docs = query_documents(starts_ref, batch, begin, width)
        log_total = lse_ref[0, :, pl.ds(begin, width)]
        spread = jnp.sum(
            flow.astype(F32) * wide_ref[0, :, pl.ds(begin, width)], axis=0, keepdims=True
        )

        def chunk(index, d_query):
            first = pl.multiple_of(index * depth, depth)
            rows = pl.ds(first, depth)
            scores = jnp.dot(key_rows[rows, :], queries, preferred_element_type=F32)
            same = same_document(key_docs, first, depth, query_docs)
            probs = jnp.exp(jnp.where(same, scores, MASKED) - log_total)
            pressure = jnp.dot(value_rows[rows, :], flow, preferred_element_type=F32)
            d_scores = (probs * (pressure - spread)).astype(BF16)
            d_value[rows, :] += jnp.dot(
                probs.astype(BF16), flow_rows, preferred_element_type=F32
            )
            d_key[rows, :] += jnp.dot(d_scores, query_rows, preferred_element_type=F32)
            return d_query + jnp.dot(key_t[:, rows], d_scores, preferred_element_type=F32)

        d_query = over_chunks(length // depth, chunk, jnp.zeros((HD, width), F32))
        low = (d_query * SCALE).astype(BF16)
        for i in range(group):
            d_ref[number * group + i, 0, 0:HD, :] = low[:, i * lanes : (i + 1) * lanes]
        return carry

    lax.fori_loop(0, length // width, block, 0)
    for i in range(count):
        rows = slice(i * lanes, (i + 1) * lanes)
        d_ref[i, 0, HD : 2 * HD, :] = d_key[rows, :].T.astype(BF16)
        d_ref[i, 0, 2 * HD : 3 * HD, :] = d_value[rows, :].T.astype(BF16)


def unit_block(*dims):
    return pl.BlockSpec(dims, lambda u, starts: (0, u) + (0,) * (len(dims) - 2))


def own_block(*dims):
    return pl.BlockSpec(dims, lambda u, starts: (u,) + (0,) * (len(dims) - 1))


def attend_back(x, flow, starts, wide, lse):
    count, units, _, lanes = x.shape
    length = count * lanes
    width = 2 * lanes if count % 2 == 0 else lanes
    return pl.pallas_call(
        functools.partial(attend_back_kernel, width),
        out_shape=jax.ShapeDtypeStruct(x.shape, BF16),
        grid_spec=pltpu.PrefetchScalarGridSpec(
            num_scalar_prefetch=1,
            grid=(units,),
            in_specs=[
                unit_block(count, 1, 3 * HD, lanes),
                unit_block(count, 1, HD, lanes),
                own_block(1, HD, length),
                own_block(1, 1, length),
            ],
            out_specs=unit_block(count, 1, 3 * HD, lanes),
            scratch_shapes=[
                pltpu.VMEM((length, HD), BF16),
                pltpu.VMEM((length, HD), BF16),
                pltpu.VMEM((HD, length), BF16),
                pltpu.VMEM((length, lanes), jnp.int32),
                pltpu.VMEM((length, HD), F32),
                pltpu.VMEM((length, HD), F32),
            ],
        ),
        compiler_params=pltpu.CompilerParams(dimension_semantics=("arbitrary",)),
        name="attend_back",
    )(starts, x, flow, wide, lse)


def to_units(columns, parts, count, units):
    rows = columns.shape[1] // MB
    x = columns.reshape(parts, H, HD, MB, rows).transpose(1, 3, 0, 2, 4)
    x = x.reshape(UNITS, parts * HD, rows)
    places = [owner_of(count, u) * units + u // count for u in range(UNITS)]
    y = jnp.zeros((count * units, parts * HD, rows), columns.dtype)
    return y.at[jnp.array(places)].set(x).reshape(count, units, parts * HD, rows)


def from_units(x, parts):
    count, units, _, rows = x.shape
    places = [owner_of(count, u) * units + u // count for u in range(UNITS)]
    x = x.reshape(count * units, parts * HD, rows)[jnp.array(places)]
    x = x.reshape(H, MB, parts, HD, rows).transpose(2, 0, 3, 1, 4)
    return x.reshape(parts * D, MB * rows)


def mul_nn(a, b):
    return jnp.dot(a, b, preferred_element_type=F32)


def mul_tn(a, b):
    return lax.dot_general(a, b, (((0,), (0,)), ((), ())), preferred_element_type=F32)


def mul_nt(a, b):
    return lax.dot_general(a, b, (((1,), (1,)), ((), ())), preferred_element_type=F32)


def mul_tt(a, b):
    return lax.dot_general(a, b, (((0,), (1,)), ((), ())), preferred_element_type=F32)


def forward_kernel(
    width,
    starts_ref,
    tok_ref,
    joint_ref,
    mixer_ref,
    inner_ref,
    outer_ref,
    *refs,
):
    vec_refs = refs[:9]
    (
    att_ref,
    got_out,
    wide_out,
    lse_out,
    joint_out,
    vec_full,
    inner_bias_full,
    mixer_out,
    inner_out,
    outer_out,
    got_ref,
    wide_ref,
    lse_ref,
    joint_all,
    vec_put,
    vec_out,
    bias_rows,
    put,
    back_put,
    back_got,
    key_rows,
    value_t,
    key_docs,
    mixer_own,
    inner_own,
    outer_own,
    put_sem,
    got_sem,
    back_put_sem,
    back_got_sem,
    joint_sems,
    weight_sems,
    relay_sems,
    own_sems,
    out_sems,
    ) = refs[9:]
    count, units, _, lanes = got_ref.shape
    length = count * lanes
    depth = min(length, 1024)
    group = width // lanes
    pairs = H // 2
    total_units = MB * H
    part = joint_ref.shape[0]
    me, shard = lax.axis_index("ctx"), lax.axis_index("fsdp")
    y, core = shard // 2, lax.rem(shard, 2)
    x = lax.rem(me, 2)
    far = 2 * (1 - y) + core
    other_core = {"fsdp": 2 * y + 1 - core}
    other_y = {"fsdp": far}
    other_x = {"ctx": me + 1 - 2 * x}
    mine = owned(count, me)

    barrier = pltpu.get_barrier_semaphore()

    def greet(step, carry):
        pl.semaphore_signal(barrier, inc=1, device_id={"ctx": lax.rem(me + step, count)})
        return carry

    lax.fori_loop(1, count, greet, 0)
    pl.semaphore_signal(barrier, inc=1, device_id=other_core)
    pl.semaphore_signal(barrier, inc=1, device_id=other_y)

    def remote(src, dst, sems, index, peer):
        return pltpu.make_async_remote_copy(
            src_ref=src,
            dst_ref=dst,
            send_sem=sems.at[(0, *index)],
            recv_sem=sems.at[(1, *index)],
            device_id=peer,
        )

    def own_joint(pair, third):
        columns = pl.ds(pl.multiple_of(third * D + pair * 128, 128), 128)
        return pltpu.make_async_copy(
            joint_ref.at[:, columns],
            joint_all.at[pair, shard, :, pl.ds(third * 128, 128)],
            own_sems.at[0, pair, third],
        )

    def joint_copy(kind, pair, third, which, peer, source=None):
        here = joint_all.at[pair, which, :, pl.ds(third * 128, 128)]
        if source is None:
            source = here
        else:
            source = source.at[:, pl.ds(pl.multiple_of(third * D + pair * 128, 128), 128)]
        return remote(source, here, joint_sems, (kind, pair, third), peer)

    def joint_y(pair, third):
        return joint_copy(0, pair, third, shard, other_y, joint_ref)

    def joint_core(pair, third):
        return joint_copy(1, pair, third, shard, other_core, joint_ref)

    def joint_pass(pair, third):
        return joint_copy(2, pair, third, far, other_core)

    def joint_store(pair):
        return pltpu.make_async_copy(
            joint_all.at[pair], joint_out.at[pair], own_sems.at[0, pair, 0]
        )

    def each_third(pair, make, act):
        for third in range(3):
            getattr(make(pair, third), act)()

    def every_pair(make, act):
        def body(pair, carry):
            each_third(pair, make, act)
            return carry

        lax.fori_loop(0, pairs, body, 0)

    every_pair(own_joint, "start")
    wholes = ((mixer_ref, mixer_own, mixer_out), (inner_ref, inner_own, inner_out), (outer_ref, outer_own, outer_out))
    own_in = [
        pltpu.make_async_copy(ref, held, own_sems.at[1, i, 0])
        for i, (ref, held, _) in enumerate(wholes)
    ]
    own_out = [
        pltpu.make_async_copy(held, out.at[shard], own_sems.at[1, i, 1])
        for i, (_, held, out) in enumerate(wholes)
    ]
    for copy in own_in:
        copy.start()
    for i, ref in enumerate(vec_refs):
        vec_put[i : i + 1, 0 : ref.shape[0]] = ref[...].astype(F32).reshape(1, ref.shape[0])
    vec_out[shard] = vec_put[...]
    pl.semaphore_wait(barrier, count + 1)

    class Vectors:
        def __init__(self, rows, columns, keys):
            mine, theirs = vec_out.at[shard, rows, columns], vec_out.at[far, rows, columns]
            source = vec_put.at[rows, columns]
            self.over_y = remote(source, mine, weight_sems, keys[0], other_y)
            self.core = remote(source, mine, weight_sems, keys[1], other_core)
            self.all = remote(theirs, theirs, weight_sems, keys[2], other_core)

        def begin(self):
            self.over_y.start()
            self.core.start()

        def hand_on(self):
            self.over_y.wait_recv()
            self.all.start()

        def arrive(self):
            self.core.wait_recv()
            self.all.wait_recv()

        def end(self):
            for copy in (self.over_y, self.core, self.all):
                copy.wait_send()

    narrow = Vectors(pl.ds(0, 8), pl.ds(0, -(-part // 128) * 128), ((0, 0), (0, 1), (0, 2)))
    broad = Vectors(pl.ds(8, 8), pl.ds(0, D), ((0, 3), (1, 3), (2, 3)))
    mixer_y = remote(mixer_ref, mixer_out.at[shard], weight_sems, (1, 0), other_y)
    mixer_core = remote(mixer_ref, mixer_out.at[shard], weight_sems, (1, 1), other_core)
    mixer_pass = remote(mixer_out.at[far], mixer_out.at[far], weight_sems, (1, 2), other_core)
    class Relayed:
        def __init__(self, ref, out, index, pieces):
            size = ref.shape[0] // 2
            piece = size // RELAY_PIECES
            self.over_y, self.over_x, self.rest = [], [], []
            for k in range(pieces):
                rows = pl.ds(pl.multiple_of(x * size + k * piece, piece), piece)
                self.over_y.append(
                    remote(
                        ref.at[rows, :],
                        out.at[shard, rows, :],
                        relay_sems,
                        (index, 0, k),
                        other_y,
                    )
                )
                passed = out.at[far, rows, :]
                self.over_x.append(remote(passed, passed, relay_sems, (index, 1, k), other_x))
            for k in range(2):
                if pieces < RELAY_PIECES:
                    rows = pl.ds(k * size + pieces * piece, size - pieces * piece)
                    self.rest.append(
                        remote(
                            ref.at[rows, :],
                            out.at[shard, rows, :],
                            relay_sems,
                            (index, 2, k),
                            other_y,
                        )
                    )
            self.core = remote(ref, out.at[shard], weight_sems, (2 + index, 0), other_core)
            self.all = remote(out.at[far], out.at[far], weight_sems, (2 + index, 1), other_core)

        def begin(self):
            for copy in self.over_y:
                copy.start()
            self.core.start()

        def begin_rest(self):
            for copy in self.rest:
                copy.start()

        def relay(self, k):
            self.over_y[k].wait_recv()
            self.over_x[k].start()

        def hand_on(self):
            for copy in self.over_x + self.rest:
                copy.wait_recv()
            self.all.start()

        def end(self):
            for copy in self.over_y + self.over_x + self.rest:
                copy.wait_send()
            self.core.wait()
            self.all.wait()

    outer_way = Relayed(outer_ref, outer_out, 0, RELAY_PIECES)
    inner_way = Relayed(inner_ref, inner_out, 1, 1)
    narrow.begin()

    def send_joint(pair, carry):
        each_third(pair, joint_y, "start")
        each_third(pair, joint_core, "start")
        return carry

    lax.fori_loop(0, pairs, send_joint, 0)
    outer_way.begin()
    inner_way.begin()
    mixer_y.start()
    mixer_core.start()
    inner_way.begin_rest()
    broad.begin()
    for first, second in zip(own_in, own_out):
        first.wait()
        second.start()

    narrow.hand_on()
    narrow.arrive()

    def bias_of(slot):
        pieces = [
            vec_out[f, slot : slot + 1, 0:part] for f in range(4)
        ]
        return jnp.concatenate(pieces, axis=1)

    query_bias, value_bias = bias_of(0), bias_of(1)
    for pair in range(pairs):
        columns = slice(pair * 128, (pair + 1) * 128)
        bias_rows[pair, :, 0:128] = jnp.broadcast_to(query_bias[:, columns], (8, 128))
        bias_rows[pair, :, 128:256] = jnp.zeros((8, 128), F32)
        bias_rows[pair, :, 256:384] = jnp.broadcast_to(value_bias[:, columns], (8, 128))

    def sent_sem(unit):
        return owner_of(count, unit), unit // count

    def send_copy(unit):
        owner, slot = sent_sem(unit)
        return pltpu.make_async_remote_copy(
            src_ref=put.at[owner, slot],
            dst_ref=got_ref.at[me, slot],
            send_sem=put_sem.at[owner, slot],
            recv_sem=got_sem.at[me, slot],
            device_id={"ctx": owner},
        )

    def keep_copy(slot):
        return pltpu.make_async_copy(
            put.at[me, slot], got_ref.at[me, slot], own_sems.at[2, slot, 0]
        )

    def project(pair, carry):
        each_third(pair, own_joint, "wait")
        each_third(pair, joint_y, "wait_recv")
        each_third(pair, joint_pass, "start")
        each_third(pair, joint_core, "wait_recv")
        each_third(pair, joint_pass, "wait_recv")
        joint_store(pair).start()
        weight = joint_all[pair].reshape(4 * part, 384)
        rows = jnp.dot(tok_ref[...], weight, preferred_element_type=F32)
        rows = (rows + bias_rows[pair, 0:1, :]).astype(BF16)
        for third in range(3):
            for batch in range(MB):
                block = rows[batch * lanes : (batch + 1) * lanes, third * 128 : (third + 1) * 128]
                turned = block.T
                if third == 0:
                    turned = turned * SCALE
                for j in range(2):
                    unit = (2 * pair + j) * MB + batch
                    put[owner_of(count, unit), unit // count, third * HD : (third + 1) * HD, :] = (
                        turned[j * HD : (j + 1) * HD]
                    )
        for i in range(2 * MB):
            unit = 2 * pair * MB + i
            owner, slot = owner_of(count, unit), unit // count

            @pl.when(owner != me)
            def _():
                send_copy(unit).start()

            @pl.when(owner == me)
            def _():
                keep_copy(slot).start()

        return carry

    lax.fori_loop(0, pairs, project, 0)

    def arrival(sender, slot):
        return pltpu.make_async_remote_copy(
            src_ref=put.at[sender, slot],
            dst_ref=got_ref.at[sender, slot],
            send_sem=put_sem.at[sender, slot],
            recv_sem=got_sem.at[sender, slot],
            device_id={"ctx": sender},
        )

    def back_copy(peer, slot):
        return pltpu.make_async_remote_copy(
            src_ref=back_put.at[peer, slot],
            dst_ref=back_got.at[me, slot],
            send_sem=back_put_sem.at[peer, slot],
            recv_sem=back_got_sem.at[me, slot],
            device_id={"ctx": peer},
        )

    def back_keep(slot):
        return pltpu.make_async_copy(
            back_put.at[me, slot], back_got.at[me, slot], own_sems.at[2, slot, 1]
        )

    early = total_units // count > 2

    def outputs(slot):
        return (
            pltpu.make_async_copy(got_ref.at[:, slot], got_out.at[:, slot], out_sems.at[slot, 0]),
            pltpu.make_async_copy(wide_ref.at[slot], wide_out.at[slot], out_sems.at[slot, 1]),
            pltpu.make_async_copy(lse_ref.at[slot], lse_out.at[slot], out_sems.at[slot, 2]),
        )

    def unit_step(slot, carry):
        def wait_one(step, inner):
            arrival(lax.rem(me + step, count), slot).wait_recv()
            return inner

        lax.fori_loop(1, count, wait_one, 0)
        keep_copy(slot).wait()
        outputs(slot)[0].start()
        for i in range(count):
            rows = slice(i * lanes, (i + 1) * lanes)
            key_rows[rows, :] = got_ref[i, slot, HD : 2 * HD, :].T
            value_t[:, rows] = got_ref[i, slot, 2 * HD : 3 * HD, :]
        batch = batch_of(count, me, slot)
        key_documents(starts_ref, batch, key_docs)

        def block(number, inner):
            begin = pl.multiple_of(number * width, width)
            parts = [got_ref[number * group + i, slot, 0:HD, :] for i in range(group)]
            queries = parts[0] if group == 1 else jnp.concatenate(parts, axis=1)
            query_docs = query_documents(starts_ref, batch, begin, width)

            def chunk(index, running):
                peak, total, mixed = running
                first = pl.multiple_of(index * depth, depth)
                scores = jnp.dot(
                    key_rows[pl.ds(first, depth), :], queries, preferred_element_type=F32
                )
                same = same_document(key_docs, first, depth, query_docs)
                scores = jnp.where(same, scores, MASKED)
                new_peak = jnp.maximum(peak, jnp.max(scores, axis=0, keepdims=True))
                scaling = jnp.exp(peak - new_peak)
                weights = jnp.exp(scores - new_peak)
                return (
                    new_peak,
                    total * scaling + jnp.sum(weights, axis=0, keepdims=True),
                    mixed * scaling
                    + jnp.dot(
                        value_t[:, pl.ds(first, depth)],
                        weights.astype(BF16),
                        preferred_element_type=F32,
                    ),
                )

            peak, total, mixed = over_chunks(
                length // depth,
                chunk,
                (
                    jnp.full((1, width), -jnp.inf, F32),
                    jnp.zeros((1, width), F32),
                    jnp.zeros((HD, width), F32),
                ),
            )
            mixed = mixed / total
            wide_ref[slot, :, pl.ds(begin, width)] = mixed
            lse_ref[slot, :, pl.ds(begin, width)] = jnp.broadcast_to(
                peak + jnp.log(total), (8, width)
            )
            low = mixed.astype(BF16)
            for i in range(group):
                back_put[number * group + i, slot] = low[:, i * lanes : (i + 1) * lanes]
            return inner

        lax.fori_loop(0, length // width, block, 0)

        def send_one(step, inner):
            back_copy(lax.rem(me + step, count), slot).start()
            return inner

        lax.fori_loop(1, count, send_one, 0)
        back_keep(slot).start()
        start(outputs(slot)[1:])
        if early:

            @pl.when(slot == 0)
            def _():
                outer_way.relay(0)
                outer_way.relay(1)

            @pl.when(slot == 1)
            def _():
                outer_way.relay(2)

            @pl.when(slot == 2)
            def _():
                inner_way.relay(0)

        return carry

    lax.fori_loop(0, mine, unit_step, 0)

    if not early:
        outer_way.relay(0)
        outer_way.relay(1)
        outer_way.relay(2)
        inner_way.relay(0)
    mixer_y.wait_recv()
    mixer_pass.start()
    outer_way.hand_on()

    def sent(unit, carry):
        @pl.when(owner_of(count, unit) != me)
        def _():
            send_copy(unit).wait_send()

        return carry

    lax.fori_loop(0, total_units, sent, 0)

    def returned(slot, carry):
        def one(step, inner):
            back_copy(lax.rem(me + step, count), slot).wait_send()
            return inner

        lax.fori_loop(1, count, one, 0)
        for copy in outputs(slot):
            copy.wait()
        return carry

    lax.fori_loop(0, mine, returned, 0)
    inner_way.hand_on()
    broad.hand_on()

    def home(unit, carry):
        owner, slot = owner_of(count, unit), unit // count

        @pl.when(owner != me)
        def _():
            pltpu.make_async_remote_copy(
                src_ref=back_put.at[owner, slot],
                dst_ref=back_got.at[owner, slot],
                send_sem=back_put_sem.at[owner, slot],
                recv_sem=back_got_sem.at[owner, slot],
                device_id={"ctx": owner},
            ).wait_recv()

        @pl.when(owner == me)
        def _():
            back_keep(slot).wait()

        return carry

    lax.fori_loop(0, total_units, home, 0)
    for pair in range(pairs):
        for batch in range(MB):
            tops = []
            for j in range(2):
                unit = (2 * pair + j) * MB + batch
                tops.append(back_got[owner_of(count, unit), unit // count])
            block = jnp.concatenate(tops, axis=0).T
            att_ref[batch * lanes : (batch + 1) * lanes, pair * 128 : (pair + 1) * 128] = block

    outer_way.end()
    inner_way.end()
    broad.arrive()
    narrow.end()
    broad.end()
    for i in range(8):
        vec_full[i : i + 1, :] = bias_of(i)
    vec_full[8:16, :] = jnp.zeros((8, D), F32)
    for k in range(4):
        inner_bias_full[:, k * D : (k + 1) * D] = vec_out[k, 8:9, :]
    mixer_y.wait_send()
    mixer_core.wait()
    mixer_pass.wait()
    every_pair(joint_y, "wait_send")
    every_pair(joint_core, "wait_send")
    every_pair(joint_pass, "wait_send")
    for copy in own_out:
        copy.wait()

    for pair in range(pairs):
        joint_store(pair).wait()


def forward(count, starts, tokens, joint, mixer, inner, outer, vectors, number):
    units = -(-UNITS // count)
    lanes = tokens.shape[0] // MB
    length = count * lanes
    width = 2 * lanes
    part = joint.shape[0]
    pairs = H // 2
    vm = pl.BlockSpec(memory_space=pltpu.VMEM)
    hbm = pl.BlockSpec(memory_space=pl.ANY)
    dma = pltpu.SemaphoreType.DMA
    return pl.pallas_call(
        functools.partial(forward_kernel, width),
        out_shape=(
            jax.ShapeDtypeStruct(tokens.shape, BF16),
            jax.ShapeDtypeStruct((count, units, 3 * HD, lanes), BF16),
            jax.ShapeDtypeStruct((units, HD, length), F32),
            jax.ShapeDtypeStruct((units, 8, length), F32),
            jax.ShapeDtypeStruct((pairs, 4, part, 384), BF16),
            jax.ShapeDtypeStruct((BIAS_ROWS, D), F32),
            jax.ShapeDtypeStruct((1, FF), F32),
            jax.ShapeDtypeStruct((4, *mixer.shape), BF16),
            jax.ShapeDtypeStruct((4, *inner.shape), BF16),
            jax.ShapeDtypeStruct((4, *outer.shape), BF16),
        ),
        in_specs=[pl.BlockSpec(memory_space=pltpu.SMEM), vm] + [hbm] * 4 + [vm] * 9,
        out_specs=(vm, hbm, hbm, hbm, hbm, vm, vm, hbm, hbm, hbm),
        scratch_shapes=[
            pltpu.VMEM((count, units, 3 * HD, lanes), BF16),
            pltpu.VMEM((units, HD, length), F32),
            pltpu.VMEM((units, 8, length), F32),
            pltpu.VMEM((pairs, 4, part, 384), BF16),
            pltpu.VMEM((BIAS_ROWS, D), F32),
            pltpu.VMEM((4, BIAS_ROWS, D), F32),
            pltpu.VMEM((pairs, 8, 384), F32),
            pltpu.VMEM((count, units, 3 * HD, lanes), BF16),
            pltpu.VMEM((count, units, HD, lanes), BF16),
            pltpu.VMEM((count, units, HD, lanes), BF16),
            pltpu.VMEM((length, HD), BF16),
            pltpu.VMEM((HD, length), BF16),
            pltpu.VMEM((length, lanes), jnp.int32),
            pltpu.VMEM(mixer.shape, BF16),
            pltpu.VMEM(inner.shape, BF16),
            pltpu.VMEM(outer.shape, BF16),
            dma((count, units)),
            dma((count, units)),
            dma((count, units)),
            dma((count, units)),
            dma((2, 3, pairs, 3)),
            dma((2, 4, 4)),
            dma((2, 2, 3, RELAY_PIECES)),
            dma((3, max(pairs, units, 4), 3)),
            dma((units, 3)),
        ],
        compiler_params=pltpu.CompilerParams(
            collective_id=number, has_side_effects=True, vmem_limit_bytes=56 * 1024 * 1024
        ),
        name="forward",
    )(starts, tokens, joint, mixer, inner, outer, *vectors)


def first_rows(half, tile):
    return half if half <= tile else (half // tile + 1) // 2 * tile


class Place:
    def __init__(self, count):
        self.count = count
        self.depth = count // 2
        self.me, self.shard = lax.axis_index("ctx"), lax.axis_index("fsdp")
        self.y, self.core = self.shard // 2, lax.rem(self.shard, 2)
        self.z, self.x = self.me // 2, lax.rem(self.me, 2)
        self.other_core = {"fsdp": 2 * self.y + 1 - self.core}
        self.other_y = {"fsdp": 2 * (1 - self.y) + self.core}
        self.other_x = {"ctx": 2 * self.z + 1 - self.x}

        self.hi, self.lo = self.z // 2, lax.rem(self.z, 2)

    def along_z(self, step):
        return lax.rem(self.z + step, self.depth)

    def peer_z(self, step):
        return {"ctx": 2 * self.along_z(step) + self.x}


def start(copies):
    for copy in copies:
        copy.start()


def added(a, b):
    return (a.astype(F32) + b.astype(F32)).astype(a.dtype)


class Reduction:
    def __init__(self, place, j, grad, out, head, paired, buffers, sems, z_sems):
        got, y_one, x_one, x_two, y_two, z_got = buffers
        self.place, self.grad, self.out, self.head, self.buffers = place, grad, out, head, buffers
        half, lanes = grad.shape[4], grad.shape[5] // 2
        self.half, self.lanes, self.paired = half, lanes, paired
        p = place
        here, there = self.side(p.y), self.side(1 - p.y)

        def remote(src, dst, slot, peer):
            return pltpu.make_async_remote_copy(
                src_ref=src,
                dst_ref=dst,
                send_sem=sems.at[0, j, slot],
                recv_sem=sems.at[1, j, slot],
                device_id=peer,
            )

        def z_copy(z, target, step):
            return pltpu.make_async_remote_copy(
                src_ref=grad.at[z // 2, lax.rem(z, 2), p.x, p.core, :, here],
                dst_ref=z_got.at[target],
                send_sem=z_sems.at[0, j, step],
                recv_sem=z_sems.at[1, j, step],
                device_id={"ctx": 2 * z + p.x},
            )

        self.first = [remote(grad.at[:, :, :, 1 - p.core], got, 0, p.other_core)]
        self.second = [remote(grad.at[:, :, :, p.core, 0:head, there], y_one, 1, p.other_y)]
        self.third = [
            remote(grad.at[:, :, 1 - p.x, p.core, 0:head, here], x_two, 2, p.other_x)
        ]
        if head < half:
            self.second.append(
                remote(grad.at[:, :, 1 - p.x, p.core, head:half, :], x_one, 3, p.other_x)
            )
            self.third.append(
                remote(grad.at[:, :, p.x, p.core, head:half, there], y_two, 4, p.other_y)
            )
        if paired:
            near = {"ctx": 2 * (2 * p.hi + 1 - p.lo) + p.x}
            self.fourth = [
                remote(
                    grad.at[:, 1 - p.lo, p.x, p.core, :, here], z_got.at[pl.ds(0, 2)], 6, near
                )
            ]
            self.fifth = [z_copy(2 * (1 - p.hi) + p.lo, 2, 1)]
        else:
            self.fourth = []
            self.fifth = [z_copy(lax.rem(p.z + step, 4), p.z, step) for step in range(1, 4)]
        self.last = [remote(out.at[p.core], out.at[p.core], 5, p.other_core)]

    def side(self, y):
        return pl.ds(pl.multiple_of(y * self.lanes, 128), self.lanes)

    def each(self, body):
        def step(block, carry):
            body(block // 2, lax.rem(block, 2))
            return carry

        lax.fori_loop(0, 4, step, 0)

    def stage_zero(self):
        start(self.first)

    def stage_one(self):
        p, grad, got = self.place, self.grad, self.buffers[0]
        for copy in self.first:
            copy.wait_recv()

        def body(hi, lo):
            for x in range(2):
                grad[hi, lo, x, p.core] = added(grad[hi, lo, x, p.core], got[hi, lo, x])

        self.each(body)
        start(self.second)

    def stage_two(self):
        p, grad, head, half = self.place, self.grad, self.head, self.half
        y_one, x_one = self.buffers[1], self.buffers[2]
        here = self.side(p.y)
        for copy in self.second:
            copy.wait()

        def body(hi, lo):
            for x in range(2):
                grad[hi, lo, x, p.core, 0:head, here] = added(
                    grad[hi, lo, x, p.core, 0:head, here], y_one[hi, lo, x]
                )
            if head < half:
                grad[hi, lo, p.x, p.core, head:half, :] = added(
                    grad[hi, lo, p.x, p.core, head:half, :], x_one[hi, lo]
                )

        self.each(body)
        start(self.third)

    def stage_three(self):
        p, grad, head, half = self.place, self.grad, self.head, self.half
        x_two, y_two = self.buffers[3], self.buffers[4]
        here = self.side(p.y)
        for copy in self.third:
            copy.wait()

        def body(hi, lo):
            grad[hi, lo, p.x, p.core, 0:head, here] = added(
                grad[hi, lo, p.x, p.core, 0:head, here], x_two[hi, lo]
            )
            if head < half:
                grad[hi, lo, p.x, p.core, head:half, here] = added(
                    grad[hi, lo, p.x, p.core, head:half, here], y_two[hi, lo]
                )

        self.each(body)
        start(self.fourth if self.paired else self.fifth)

    def stage_four(self):
        p, grad, z_got = self.place, self.grad, self.buffers[5]
        here = self.side(p.y)
        for copy in self.fourth:
            copy.wait()
        for hi in range(2):
            grad[hi, p.lo, p.x, p.core, :, here] = added(
                grad[hi, p.lo, p.x, p.core, :, here], z_got[hi]
            )
        start(self.fifth)

    def stage_five(self):
        p, z_got = self.place, self.buffers[5]
        for copy in self.fifth:
            copy.wait()
        total = self.grad[p.hi, p.lo, p.x, p.core, :, self.side(p.y)].astype(F32)
        if self.paired:
            total = total + z_got[2].astype(F32)
        else:
            for step in range(1, 4):
                total = total + z_got[lax.rem(p.z + step, 4)].astype(F32)
        self.out[p.core] = total.astype(self.out.dtype)
        start(self.last)

    def stage_six(self):
        for copy in self.last:
            copy.wait()
        for copy in self.first:
            copy.wait_send()


def reduction_buffers(half, lanes, head, dtype):
    tail = max(half - head, 16)
    shapes = (
        (2, 2, 2, half, 2 * lanes),
        (2, 2, 2, head, lanes),
        (2, 2, tail, 2 * lanes),
        (2, 2, head, lanes),
        (2, 2, tail, lanes),
        (4, half, lanes),
        (2, half, lanes),
    )
    return [pltpu.VMEM(shape, dtype) for shape in shapes]


def backward_kernel(width, plan, *refs):
    (
        starts_ref,
        flow_in,
        got_in,
        wide_in,
        lse_in,
        tok_in,
        residual_in,
        bias_in,
        joint_in,
        d_outer_in,
        act_in,
        d_inner_in,
        first_in,
        d_branch_in,
        att_in,
        tokens_out,
        outer_out,
        inner_out,
        mixer_out,
        joint_out,
        bias_out,
        flow_ref,
        got_ref,
        wide_ref,
        lse_ref,
        tok_ref,
        residual_ref,
        bias_ref,
        d_outer_ref,
        act_ref,
        d_inner_ref,
        first_ref,
        d_branch_ref,
        att_ref,
        flow_put,
        flow_got,
        put,
        home_got,
        key_rows,
        value_rows,
        key_t,
        key_docs,
        d_key,
        d_value,
        joint_all,
        outer_one,
        outer_two,
        inner_one,
        inner_two,
        mixer_grad,
        joint_one,
        joint_two,
        d_turned,
        bias_sum,
        bias_got,
        flow_sems,
        home_sems,
        own_sems,
        sems,
        z_sems,
        bias_sems,
        in_sems,
        *buffers,
    ) = refs
    count, units, _, lanes = got_ref.shape
    length = count * lanes
    depth = min(length, 1024)
    group = width // lanes
    pairs = H // 2
    total_units = MB * H
    p = Place(count)
    me = p.me
    mine = owned(count, me)

    sources = (
        (flow_in, flow_ref),
        (d_outer_in, d_outer_ref),
        (act_in, act_ref),
        (d_inner_in, d_inner_ref),
        (first_in, first_ref),
        (d_branch_in, d_branch_ref),
        (att_in, att_ref),
        (bias_in, bias_ref),
        (got_in, got_ref),
        (wide_in, wide_ref),
        (lse_in, lse_ref),
        (tok_in, tok_ref),
        (residual_in, residual_ref),
    )
    loads = [
        pltpu.make_async_copy(source, held, in_sems.at[k])
        for k, (source, held) in enumerate(sources)
    ]
    start(loads)

    def loaded(first, last):
        for copy in loads[first:last]:
            copy.wait()

    barrier = pltpu.get_barrier_semaphore()

    def greet(step, carry):
        pl.semaphore_signal(barrier, inc=1, device_id={"ctx": lax.rem(me + step, count)})
        return carry

    lax.fori_loop(1, count, greet, 0)
    pl.semaphore_signal(barrier, inc=1, device_id=p.other_core)
    pl.semaphore_signal(barrier, inc=1, device_id=p.other_y)
    pl.semaphore_signal(barrier, inc=1, device_id={**p.other_y, **p.other_x})
    joint_load = pltpu.make_async_copy(joint_in, joint_all, own_sems.at[2, 0])
    joint_load.start()

    grads = (outer_one, outer_two, inner_one, inner_two, mixer_grad, joint_one, joint_two)
    jobs = [
        Reduction(
            p,
            j,
            grads[j],
            buffers[7 * j + 6],
            plan[j][2],
            plan[j][3],
            buffers[7 * j : 7 * j + 6],
            sems,
            z_sems,
        )
        for j in range(len(grads))
    ]
    o_one, o_two, i_one, i_two, m_one, j_one, j_two = jobs

    def store_rows(targets, row, values, columns):
        half = sum(t.shape[4] for t in targets)
        done = 0
        while done < values.shape[0]:
            block, inside = (row + done) // half, (row + done) % half
            k = 0
            while inside >= targets[k].shape[4]:
                inside -= targets[k].shape[4]
                k += 1
            size = min(values.shape[0] - done, targets[k].shape[4] - inside)
            targets[k][
                block // 8,
                block // 4 % 2,
                block // 2 % 2,
                block % 2,
                inside : inside + size,
                columns,
            ] = values[done : done + size]
            done += size

    loaded(0, 3)
    d_outer_turned = d_outer_ref[...].T

    def outer_gradient(which):
        for side in range(2):
            begin = (2 * side + which) * D
            values = jnp.dot(
                d_outer_turned, act_ref[:, begin : begin + D], preferred_element_type=F32
            )
            columns = slice(side * D, (side + 1) * D)
            store_rows(((outer_one, outer_two)[which],), 0, values.astype(BF16), columns)

    def inner_gradient():
        for k in range(FF // D):
            turned = d_inner_ref[:, k * D : (k + 1) * D].T
            values = jnp.dot(turned, first_ref[...], preferred_element_type=F32)
            store_rows((inner_one, inner_two), k * D, values.astype(BF16), slice(0, D))

    def mixer_gradient():
        values = jnp.dot(d_branch_ref[...].T, att_ref[...], preferred_element_type=F32)
        store_rows((mixer_grad,), 0, values.astype(BF16), slice(0, D))

    def unit_copy(source, target, sem, owner, slot):
        return pltpu.make_async_remote_copy(
            src_ref=source.at[owner, slot],
            dst_ref=target.at[me, slot],
            send_sem=sem.at[0, owner, slot],
            recv_sem=sem.at[1, me, slot],
            device_id={"ctx": owner},
        )

    def unit_arrival(source, target, sem, sender, slot):
        return pltpu.make_async_remote_copy(
            src_ref=source.at[sender, slot],
            dst_ref=target.at[sender, slot],
            send_sem=sem.at[0, sender, slot],
            recv_sem=sem.at[1, sender, slot],
            device_id={"ctx": sender},
        )

    def unit_keep(source, target, kind, slot):
        return pltpu.make_async_copy(
            source.at[me, slot], target.at[me, slot], own_sems.at[kind, slot]
        )

    for pair in range(pairs):
        for batch in range(MB):
            block = flow_ref[
                batch * lanes : (batch + 1) * lanes, pair * 128 : (pair + 1) * 128
            ].T
            for j in range(2):
                unit = (2 * pair + j) * MB + batch
                flow_put[owner_of(count, unit), unit // count] = block[j * HD : (j + 1) * HD]

    outer_gradient(0)
    pl.semaphore_wait(barrier, count + 2)
    o_one.stage_zero()

    def send_flow(turn, carry):
        slot, owner = turn // count, lax.rem(me + turn, count)

        @pl.when((owner != me) & (slot < owned(count, owner)))
        def _():
            unit_copy(flow_put, flow_got, flow_sems, owner, slot).start()

        @pl.when((owner == me) & (slot < mine))
        def _():
            unit_keep(flow_put, flow_got, 0, slot).start()

        return carry

    lax.fori_loop(0, units * count, send_flow, 0)
    loaded(3, 8)
    bias_sum[0] = bias_ref[...]
    outer_gradient(1)
    o_two.stage_zero()
    o_one.stage_one()
    inner_gradient()
    i_one.stage_zero()
    i_two.stage_zero()
    mixer_gradient()
    m_one.stage_zero()

    loaded(8, len(loads))

    def unit_step(slot, carry):
        def wait_one(step, inner):
            unit_arrival(flow_put, flow_got, flow_sems, lax.rem(me + step, count), slot).wait_recv()
            return inner

        lax.fori_loop(1, count, wait_one, 0)
        unit_keep(flow_put, flow_got, 0, slot).wait()
        for i in range(count):
            rows = slice(i * lanes, (i + 1) * lanes)
            key_rows[rows, :] = got_ref[i, slot, HD : 2 * HD, :].T
            value_rows[rows, :] = got_ref[i, slot, 2 * HD : 3 * HD, :].T
            key_t[:, rows] = got_ref[i, slot, HD : 2 * HD, :]
        batch = batch_of(count, me, slot)
        key_documents(starts_ref, batch, key_docs)
        d_key[...] = jnp.zeros_like(d_key)
        d_value[...] = jnp.zeros_like(d_value)

        def block(number, inner):
            begin = pl.multiple_of(number * width, width)

            def beside(ref):
                parts = [ref[number * group + i, slot, 0:HD, :] for i in range(group)]
                return parts[0] if group == 1 else jnp.concatenate(parts, axis=1)

            queries, flow = beside(got_ref), beside(flow_got)
            query_rows, flow_rows = queries.T, flow.T
            query_docs = query_documents(starts_ref, batch, begin, width)
            log_total = lse_ref[slot, 0:1, pl.ds(begin, width)]
            spread = jnp.sum(
                flow.astype(F32) * wide_ref[slot, :, pl.ds(begin, width)], axis=0, keepdims=True
            )

            def chunk(index, d_query):
                first = pl.multiple_of(index * depth, depth)
                rows = pl.ds(first, depth)
                scores = jnp.dot(key_rows[rows, :], queries, preferred_element_type=F32)
                same = same_document(key_docs, first, depth, query_docs)
                probs = jnp.exp(jnp.where(same, scores, MASKED) - log_total)
                pressure = jnp.dot(value_rows[rows, :], flow, preferred_element_type=F32)
                d_scores = (probs * (pressure - spread)).astype(BF16)
                d_value[rows, :] += jnp.dot(
                    probs.astype(BF16), flow_rows, preferred_element_type=F32
                )
                d_key[rows, :] += jnp.dot(d_scores, query_rows, preferred_element_type=F32)
                return d_query + jnp.dot(key_t[:, rows], d_scores, preferred_element_type=F32)

            d_query = over_chunks(length // depth, chunk, jnp.zeros((HD, width), F32))
            low = (d_query * SCALE).astype(BF16)
            for i in range(group):
                put[number * group + i, slot, 0:HD, :] = low[:, i * lanes : (i + 1) * lanes]
            return inner

        lax.fori_loop(0, length // width, block, 0)
        for i in range(count):
            rows = slice(i * lanes, (i + 1) * lanes)
            put[i, slot, HD : 2 * HD, :] = d_key[rows, :].T.astype(BF16)
            put[i, slot, 2 * HD : 3 * HD, :] = d_value[rows, :].T.astype(BF16)

        def send_one(step, inner):
            unit_copy(put, home_got, home_sems, lax.rem(me + step, count), slot).start()
            return inner

        lax.fori_loop(1, count, send_one, 0)
        unit_keep(put, home_got, 1, slot).start()

        @pl.when(slot == 0)
        def _():
            o_two.stage_one()

        @pl.when(slot == 1)
        def _():
            i_one.stage_one()

        @pl.when(slot == 2)
        def _():
            o_one.stage_two()

        return carry

    lax.fori_loop(0, mine, unit_step, 0)
    o_two.stage_two()
    i_two.stage_one()
    o_one.stage_three()
    i_one.stage_two()
    m_one.stage_one()

    ones = jnp.ones((8, MB * lanes), BF16)
    for pair in range(pairs):
        columns = []
        for batch in range(MB):
            blocks = []
            for j in range(2):
                unit = (2 * pair + j) * MB + batch
                owner, slot = owner_of(count, unit), unit // count

                @pl.when(owner != me)
                def _():
                    unit_arrival(put, home_got, home_sems, owner, slot).wait_recv()

                @pl.when(owner == me)
                def _():
                    unit_keep(put, home_got, 1, slot).wait()

                blocks.append(home_got[owner, slot])
            rows = [b[third * HD : (third + 1) * HD] for third in range(3) for b in blocks]
            columns.append(jnp.concatenate(rows, axis=0))
        d_pair = jnp.concatenate(columns, axis=1)
        d_turned[pair] = d_pair.T
        grad = jnp.dot(d_pair, tok_ref[...], preferred_element_type=F32).astype(BF16)
        for third in range(3):
            store_rows(
                (joint_one, joint_two),
                third * D + pair * 128,
                grad[third * 128 : (third + 1) * 128],
                slice(0, D),
            )
        sums = lax.dot_general(
            ones, d_pair, (((1,), (1,)), ((), ())), preferred_element_type=F32
        )
        bias_sum[0, 0:1, pair * 128 : (pair + 1) * 128] = sums[0:1, 0:128]
        bias_sum[0, 1:2, pair * 128 : (pair + 1) * 128] = sums[0:1, 256:384]
        if pair == 2:
            o_two.stage_three()
            o_one.stage_four()
            i_two.stage_two()
            i_one.stage_three()

    m_one.stage_two()
    o_two.stage_four()

    plane = (p.other_y, p.other_x, {**p.other_y, **p.other_x})

    def bias_copy(level, number, slot, peer):
        return pltpu.make_async_remote_copy(
            src_ref=bias_sum.at[level],
            dst_ref=bias_got.at[slot],
            send_sem=bias_sems.at[0, number],
            recv_sem=bias_sems.at[1, number],
            device_id=peer,
        )

    bias_core = bias_copy(0, 0, 0, p.other_core)
    bias_plane = [bias_copy(1, 1 + i, 1 + i, peer) for i, peer in enumerate(plane)]
    bias_z = [
        bias_copy(2, 3 + step, 3 + step, {"ctx": 2 * lax.rem(p.z + step, 4) + p.x})
        for step in range(1, 4)
    ]
    bias_core.start()
    j_one.stage_zero()
    j_two.stage_zero()

    joint_load.wait()

    def token_terms(first, last, total):
        for pair in range(first, last):
            total = total + lax.dot_general(
                d_turned[pair],
                joint_all[pair],
                (((1,), (1,)), ((), ())),
                preferred_element_type=F32,
            )
        tokens_out[...] = total

    token_terms(0, pairs // 2, residual_ref[...])
    bias_core.wait()
    bias_sum[1] = bias_sum[0] + bias_got[0]
    start(bias_plane)
    j_one.stage_one()
    j_two.stage_one()
    i_two.stage_three()
    i_one.stage_four()
    token_terms(pairs // 2, pairs, tokens_out[...])
    m_one.stage_three()
    for copy in bias_plane:
        copy.wait()
    bias_sum[2] = bias_sum[1] + bias_got[1] + bias_got[2] + bias_got[3]
    start(bias_z)
    j_one.stage_two()
    i_two.stage_four()
    j_two.stage_two()
    m_one.stage_four()
    j_one.stage_three()
    j_two.stage_three()
    o_one.stage_five()
    o_two.stage_five()
    i_one.stage_five()

    def parts_of(j):
        jobs[j].stage_six()
        whole = buffers[7 * j + 6]
        return [whole[low].astype(F32) for low in range(2)]

    def own_lanes(rows):
        width_own = rows.shape[1] // 2
        return jnp.where(p.core == 0, rows[:, :width_own], rows[:, width_own:])

    def put_out(out, pieces):
        out[...] = jnp.concatenate(pieces, axis=0).T

    one, two = parts_of(0), parts_of(1)
    outer_out[...] = jnp.concatenate(
        [jnp.where(p.core == 0, a, b) for a, b in zip(one, two)], axis=0
    )
    i_two.stage_five()
    m_one.stage_five()
    one, two = parts_of(2), parts_of(3)
    put_out(inner_out, [own_lanes(r) for r in (one[0], two[0], one[1], two[1])])
    put_out(mixer_out, [own_lanes(r) for r in parts_of(4)])
    for copy in bias_z:
        copy.wait()
    bias_total = bias_sum[2] + bias_got[4] + bias_got[5] + bias_got[6]
    index = me * 4 + p.shard
    world = 4 * count
    lane = lax.broadcasted_iota(jnp.int32, (D, 128), 0)
    place = lax.broadcasted_iota(jnp.int32, (D, 128), 1)

    def picked(rows, first):
        ones_there = jnp.where(lane == place + first, 1.0, 0.0)
        return jnp.dot(
            rows, ones_there, precision=lax.Precision.HIGHEST, preferred_element_type=F32
        )

    own_hidden = FF // world
    in_row = D // own_hidden
    row = lax.broadcasted_iota(jnp.int32, (8, D), 0)
    hidden = jnp.where(row == index // in_row, bias_total[8:16], 0.0)
    hidden = jnp.broadcast_to(jnp.sum(hidden, axis=0, keepdims=True), (8, D))
    bias_out[0:8, :] = picked(bias_total[0:8], index * (D // world))
    bias_out[8:16, :] = picked(hidden, lax.rem(index, in_row) * own_hidden)

    def sent(unit, carry):
        owner, slot = owner_of(count, unit), unit // count

        @pl.when(owner != me)
        def _():
            unit_copy(flow_put, flow_got, flow_sems, owner, slot).wait_send()

        return carry

    lax.fori_loop(0, total_units, sent, 0)

    def returned(slot, carry):
        def one(step, inner):
            unit_copy(put, home_got, home_sems, lax.rem(me + step, count), slot).wait_send()
            return inner

        lax.fori_loop(1, count, one, 0)
        return carry

    lax.fori_loop(0, mine, returned, 0)
    j_one.stage_five()
    j_two.stage_five()
    one, two = parts_of(5), parts_of(6)
    put_out(joint_out, [own_lanes(r) for r in (one[0], two[0], one[1], two[1])])


def backward(
    starts, flow, got, wide, lse, source, residual, biases, joint, activations, number
):
    count, units, _, lanes = got.shape
    length = count * lanes
    width = 2 * lanes
    pairs = H // 2
    vm = pl.BlockSpec(memory_space=pltpu.VMEM)
    hbm = pl.BlockSpec(memory_space=pl.ANY)
    dma = pltpu.SemaphoreType.DMA
    small = D // (2 * count)
    half_joint = 3 * D // (2 * count)
    early = first_rows(half_joint, 16)
    plan = (
        (small, FF // 2, small, True),
        (small, FF // 2, small, True),
        (2 * small, D, 2 * small - 16, True),
        (2 * small, D, 2 * small - 16, True),
        (small, D, small, True),
        (early, D, first_rows(early, 16), False),
        (half_joint - early, D, first_rows(half_joint - early, 16), False),
    )
    buffers = []
    for half, full, head, _ in plan:
        buffers += reduction_buffers(half, full // 2, head, BF16)
    outs = [
        jax.ShapeDtypeStruct((2 * small, FF // 4), F32),
        jax.ShapeDtypeStruct((D // 4, FF // count), F32),
        jax.ShapeDtypeStruct((D // 4, 2 * small), F32),
        jax.ShapeDtypeStruct((D // 4, 2 * half_joint), F32),
    ]
    return pl.pallas_call(
        functools.partial(backward_kernel, width, plan),
        out_shape=(
            jax.ShapeDtypeStruct(residual.shape, F32),
            *outs,
            jax.ShapeDtypeStruct((BIAS_ROWS, 128), F32),
        ),
        in_specs=[pl.BlockSpec(memory_space=pltpu.SMEM)] + [hbm] * 14,
        out_specs=(vm,) * 6,
        scratch_shapes=[
            *[
                pltpu.VMEM(a.shape, a.dtype)
                for a in (flow, got, wide, lse, source, residual, biases, *activations)
            ],
            pltpu.VMEM((count, units, HD, lanes), BF16),
            pltpu.VMEM((count, units, HD, lanes), BF16),
            pltpu.VMEM((count, units, 3 * HD, lanes), BF16),
            pltpu.VMEM((count, units, 3 * HD, lanes), BF16),
            pltpu.VMEM((length, HD), BF16),
            pltpu.VMEM((length, HD), BF16),
            pltpu.VMEM((HD, length), BF16),
            pltpu.VMEM((length, lanes), jnp.int32),
            pltpu.VMEM((length, HD), F32),
            pltpu.VMEM((length, HD), F32),
            pltpu.VMEM((pairs, D, 384), BF16),
            *[pltpu.VMEM((2, 2, 2, 2, half, full), BF16) for half, full, _, _ in plan],
            pltpu.VMEM((pairs, MB * lanes, 384), BF16),
            pltpu.VMEM((3, BIAS_ROWS, D), F32),
            pltpu.VMEM((7, BIAS_ROWS, D), F32),
            dma((2, count, units)),
            dma((2, count, units)),
            dma((3, units)),
            dma((2, len(plan), 7)),
            dma((2, len(plan), 4)),
            dma((2, 7)),
            dma((13,)),
            *buffers,
        ],
        compiler_params=pltpu.CompilerParams(
            collective_id=number, has_side_effects=True, vmem_limit_bytes=67043328
        ),
        name="backward",
    )(starts, flow, got, wide, lse, source, residual, biases, joint, *activations)


def settle_kernel(count, *refs):
    copies = [
        pltpu.make_async_copy(refs[i], refs[count + i], refs[2 * count].at[i])
        for i in range(count)
    ]
    start(copies)
    for copy in copies:
        copy.wait()


def settle(*arrays):
    count = len(arrays)
    return pl.pallas_call(
        functools.partial(settle_kernel, count),
        out_shape=[jax.ShapeDtypeStruct(a.shape, a.dtype) for a in arrays],
        in_specs=[pl.BlockSpec(memory_space=pltpu.VMEM)] * count,
        out_specs=[pl.BlockSpec(memory_space=pl.ANY)] * count,
        scratch_shapes=[pltpu.SemaphoreType.DMA((count,))],
        name="settle",
    )(*arrays)


def on_device(
    count,
    shards,
    tokens,
    doc_starts,
    joint_weight,
    mixer_weight,
    inner_weight,
    outer_weight,
    query_bias,
    value_bias,
    mixer_bias,
    first_gain,
    first_shift,
    inner_bias,
    outer_bias,
    second_gain,
    second_shift,
    upstream,
):
    rows = tokens.shape[2]
    length = rows * count
    units = -(-MB * H // count)
    me = lax.axis_index("ctx")

    part = D // shards
    vectors = [
        query_bias,
        value_bias,
        mixer_bias,
        first_gain,
        first_shift,
        outer_bias,
        second_gain,
        second_shift,
        inner_bias,
    ]
    source = tokens.reshape(MB * rows, D)
    attended, received, wide, lse, joint, vectors, ibias, mixer, inner, outer = forward(
        count,
        doc_starts,
        source,
        joint_weight,
        mixer_weight,
        inner_weight,
        outer_weight,
        vectors,
        0,
    )
    joint = joint.reshape(H // 2, D, 384)
    mixer, inner, outer = mixer.reshape(D, D), inner.reshape(D, FF), outer.reshape(FF, D)
    _, _, mbias, gain_one, shift_one, obias, gain_two, shift_two = [
        vectors[i : i + 1] for i in range(8)
    ]

    branch = mul_nn(attended, mixer) + mbias
    first, first_normed, first_recip = norm_forward(
        source.astype(F32) + branch, gain_one, shift_one
    )
    first_low = first.astype(BF16)
    inner_pre = mul_nn(first_low, inner) + ibias
    activated, gelu_slope = gelu_parts(inner_pre)
    activated_low = activated.astype(BF16)
    outer_out = mul_nn(activated_low, outer) + obias
    final, second_normed, second_recip = norm_forward(first + outer_out, gain_two, shift_two)
    result = final.astype(BF16).reshape(MB, 1, rows, D)

    incoming = upstream.reshape(MB * rows, D).astype(F32)
    rescale_grad = jnp.sum(incoming * second_normed, axis=0)
    reshift_grad = jnp.sum(incoming, axis=0)
    d_second = norm_backward(incoming, second_normed, second_recip, gain_two)
    d_outer = d_second.astype(BF16)
    return_grad = jnp.sum(d_outer.astype(F32), axis=0)
    d_inner = (mul_nt(d_outer, outer) * gelu_slope).astype(BF16)
    hidden_grad = jnp.sum(d_inner.astype(F32), axis=0)
    d_first = d_second + mul_nt(d_inner, inner)
    scale_grad = jnp.sum(d_first * first_normed, axis=0)
    shift_grad = jnp.sum(d_first, axis=0)
    d_residual = norm_backward(d_first, first_normed, first_recip, gain_one)
    d_branch = d_residual.astype(BF16)
    mixing_grad = jnp.sum(d_branch.astype(F32), axis=0)
    world = count * shards
    index = me * shards + lax.axis_index("fsdp")
    sums = [
        mixing_grad,
        scale_grad,
        shift_grad,
        return_grad,
        rescale_grad,
        reshift_grad,
        *hidden_grad.reshape(FF // D, D),
    ]
    if shards == 4 and count == 8:
        flow = mul_nt(d_branch, mixer).astype(BF16)
        biases = jnp.pad(jnp.stack(sums), ((2, BIAS_ROWS - 2 - len(sums)), (0, 0)))
        tokens_grad, *blocks, biases = backward(
            doc_starts,
            flow,
            received,
            wide,
            lse,
            source,
            d_residual,
            biases,
            joint,
            [d_outer, activated_low, d_inner, first_low, d_branch, attended],
            1,
        )
        tokens_grad, *blocks = settle(tokens_grad, *blocks)
        blocks[0] = blocks[0].T
        own, own_hidden = biases[:8, : D // world], biases[8, : FF // world]
    else:
        natural = joint.reshape(H // 2, D, 3, 128).transpose(1, 2, 0, 3).reshape(D, 3 * D)
        flow = mul_nt(mixer, d_branch).astype(BF16)
        flow_units = exchange(to_units(flow, 1, count, units), 2)
        d_units = attend_back(received, flow_units, doc_starts, wide, lse[:, :1])
        d_joint = from_units(exchange(d_units, 3), 3)
        bias_sums = jnp.sum(d_joint.astype(F32), axis=1)
        turned = [
            mul_tn(d_outer, activated_low),
            mul_tn(d_inner, first_low),
            mul_tn(d_branch, attended),
            mul_nn(d_joint, source),
        ]
        tokens_grad = d_residual + mul_tt(d_joint, natural)

        def reduced(grad):
            over_lanes = lax.psum_scatter(
                grad.astype(BF16), "fsdp", scatter_dimension=1, tiled=True
            )
            over_rows = lax.psum_scatter(over_lanes, "ctx", scatter_dimension=0, tiled=True)
            return over_rows.T.astype(F32)

        blocks = [reduced(g) for g in turned]
        biases = jnp.stack([bias_sums[:D], bias_sums[2 * D :], *sums])
        biases = lax.psum(biases, ("ctx", "fsdp"))
        own = lax.dynamic_slice_in_dim(biases[:8], index * (D // world), D // world, 1)
        hidden_rows = biases[8 : 8 + FF // D].reshape(FF)
        own_hidden = lax.dynamic_slice_in_dim(hidden_rows, index * (FF // world), FF // world, 0)
    tokens_grad = tokens_grad.reshape(MB, 1, rows, D)
    outer_out_grad, inner_out, mixer_out, joint_out = blocks
    sums = [*own[:5], own_hidden, *own[5:]]
    return (result, tokens_grad, joint_out, mixer_out, inner_out, outer_out_grad, *sums)


def solution(mesh):
    in_specs = (
        P(None, "fsdp", "ctx", None),
        P(None, "fsdp", None),
        P("fsdp", None),
        P("fsdp", None),
        P("fsdp", None),
        P("fsdp", None),
        P("fsdp"),
        P("fsdp"),
        P("fsdp"),
        P("fsdp"),
        P("fsdp"),
        P("fsdp"),
        P("fsdp"),
        P("fsdp"),
        P("fsdp"),
        P(None, "fsdp", "ctx", None),
    )
    out_specs = (
        P(None, "fsdp", "ctx", None),
        P(None, "fsdp", "ctx", None),
        P("fsdp", "ctx"),
        P("fsdp", "ctx"),
        P("fsdp", "ctx"),
        P("fsdp", "ctx"),
        P(("ctx", "fsdp")),
        P(("ctx", "fsdp")),
        P(("ctx", "fsdp")),
        P(("ctx", "fsdp")),
        P(("ctx", "fsdp")),
        P(("ctx", "fsdp")),
        P(("ctx", "fsdp")),
        P(("ctx", "fsdp")),
        P(("ctx", "fsdp")),
    )
    return jax.shard_map(
        functools.partial(on_device, mesh.shape["ctx"], mesh.shape["fsdp"]),
        mesh=mesh,
        in_specs=in_specs,
        out_specs=out_specs,
        check_vma=False,
    )
```

```python
import functools
import math

import jax
import jax.numpy as jnp
from jax import lax
from jax.experimental import pallas as pl
from jax.experimental.pallas import tpu as pltpu
from jax.sharding import PartitionSpec as P

D = 768
H = 12
HD = 64
FF = 3072
MB = 3

SCALE = 0.125
EPSILON = 1e-12
MASKED = -1000000000.0
ROOT_HALF = 0.7071067811865476
GAUSS_PEAK = 0.3989422804014327

F32 = jnp.float32
BF16 = jnp.bfloat16


def norm_forward(hidden, gain, shift):
    average = jnp.mean(hidden, axis=-1, keepdims=True)
    centred = hidden - average
    reciprocal = lax.rsqrt(jnp.mean(centred * centred, axis=-1, keepdims=True) + EPSILON)
    normed = centred * reciprocal
    return (normed * gain + shift, normed, reciprocal)


def norm_backward(incoming, normed, reciprocal, gain):
    scaled = incoming * gain
    return reciprocal * (
        scaled
        - jnp.mean(scaled, axis=-1, keepdims=True)
        - normed * jnp.mean(scaled * normed, axis=-1, keepdims=True)
    )


def gelu_parts(inner):
    cumulative = 0.5 * (1.0 + lax.erf(inner * ROOT_HALF))
    return (inner * cumulative, cumulative + inner * jnp.exp(-0.5 * inner * inner) * GAUSS_PEAK)


UNITS = MB * H
BIAS_ROWS = 16
RELAY_PIECES = 3


def spare_owner(count, j):
    stride = count // (UNITS % count)
    return j * stride + (j % 2 if stride > 1 else 0)


def owner_of(count, unit):
    full, rest = UNITS // count, UNITS % count
    if rest == 0:
        return unit % count
    if full == 0:
        return spare_owner(count, unit)
    late = unit // (full * count)
    return (1 - late) * (unit % count) + late * spare_owner(count, unit - full * count)


def spare_index(count, device):
    return device // (count // (UNITS % count))


def owned(count, device):
    full, rest = UNITS // count, UNITS % count
    if rest == 0:
        return full
    j = spare_index(count, device)
    extra = (spare_owner(count, j) == device) & (j < rest)
    return full + extra.astype(jnp.int32)


def batch_of(count, device, slot):
    full, rest = UNITS // count, UNITS % count
    if rest == 0:
        return (slot * count + device) % MB
    if full == 0:
        return jnp.minimum(spare_index(count, device), UNITS - 1) % MB
    late = slot // full
    unit = slot * count + (1 - late) * device + late * spare_index(count, device)
    return unit % MB


def exchange_kernel(count, x_ref, y_ref, held, send_sem, recv_sem, own_sem):
    me = lax.axis_index("ctx")
    barrier = pltpu.get_barrier_semaphore()

    def greet(step, carry):
        peer = lax.rem(me + step, count)
        pl.semaphore_signal(barrier, inc=1, device_id={"ctx": peer})
        return carry

    lax.fori_loop(1, count, greet, 0)
    own_in = pltpu.make_async_copy(x_ref.at[me], held, own_sem)
    own_in.start()
    pl.semaphore_wait(barrier, count - 1)

    def transfer(step):
        peer = lax.rem(me + step, count)
        return pltpu.make_async_remote_copy(
            src_ref=x_ref.at[peer],
            dst_ref=y_ref.at[me],
            send_sem=send_sem.at[step],
            recv_sem=recv_sem.at[step],
            device_id={"ctx": peer},
        )

    def begin(step, carry):
        transfer(step).start()
        return carry

    lax.fori_loop(1, count, begin, 0)
    own_in.wait()
    own_out = pltpu.make_async_copy(held, y_ref.at[me], own_sem)
    own_out.start()
    own_out.wait()

    def finish(step, carry):
        transfer(step).wait()
        return carry

    lax.fori_loop(1, count, finish, 0)


def exchange(x, number):
    count = x.shape[0]
    return pl.pallas_call(
        functools.partial(exchange_kernel, count),
        out_shape=jax.ShapeDtypeStruct(x.shape, x.dtype),
        in_specs=[pl.BlockSpec(memory_space=pl.ANY)],
        out_specs=pl.BlockSpec(memory_space=pl.ANY),
        scratch_shapes=[
            pltpu.VMEM(x.shape[1:], x.dtype),
            pltpu.SemaphoreType.DMA((count,)),
            pltpu.SemaphoreType.DMA((count,)),
            pltpu.SemaphoreType.DMA,
        ],
        compiler_params=pltpu.CompilerParams(collective_id=number, has_side_effects=True),
        name=f"exchange_{number}",
    )(x)


def across(ref, first, rows, width, lanes):
    parts = [ref[first + i, 0, rows, :] for i in range(width // lanes)]
    return parts[0] if len(parts) == 1 else jnp.concatenate(parts, axis=1)


def document(starts_ref, batch, position):
    docs = jnp.zeros(position.shape, jnp.int32) - 1
    for j in range(starts_ref.shape[2]):
        docs = docs + jnp.where(position >= starts_ref[batch, 0, j], 1, 0)
    return docs


def key_documents(starts_ref, batch, key_docs):
    key_docs[...] = document(
        starts_ref, batch, lax.broadcasted_iota(jnp.int32, key_docs.shape, 0)
    )


def query_documents(starts_ref, batch, begin, width):
    return document(
        starts_ref, batch, lax.broadcasted_iota(jnp.int32, (1, width), 1) + begin
    )


def same_document(key_docs, first, width, query_docs):
    keys = key_docs[pl.ds(first, width), :]
    lanes = keys.shape[1]
    parts = [keys == query_docs[:, i : i + lanes] for i in range(0, query_docs.shape[1], lanes)]
    return parts[0] if len(parts) == 1 else jnp.concatenate(parts, axis=1)


def over_chunks(chunks, body, carry):
    if chunks == 1:
        return body(0, carry)
    return lax.fori_loop(0, chunks, body, carry)


def attend_back_kernel(
    width,
    starts_ref,
    x_ref,
    flow_ref,
    wide_ref,
    lse_ref,
    d_ref,
    key_rows,
    value_rows,
    key_t,
    key_docs,
    d_key,
    d_value,
):
    count, _, _, lanes = x_ref.shape
    length = count * lanes
    depth = min(length, 1024)
    unit = pl.program_id(0)
    for i in range(count):
        rows = slice(i * lanes, (i + 1) * lanes)
        key_rows[rows, :] = x_ref[i, 0, HD : 2 * HD, :].T
        value_rows[rows, :] = x_ref[i, 0, 2 * HD : 3 * HD, :].T
        key_t[:, rows] = x_ref[i, 0, HD : 2 * HD, :]
    batch = batch_of(count, lax.axis_index("ctx"), unit)
    key_documents(starts_ref, batch, key_docs)
    d_key[...] = jnp.zeros_like(d_key)
    d_value[...] = jnp.zeros_like(d_value)
    group = width // lanes

    def block(number, carry):
        begin = pl.multiple_of(number * width, width)
        queries = across(x_ref, number * group, slice(0, HD), width, lanes)
        flow = across(flow_ref, number * group, slice(0, HD), width, lanes)
        query_rows = queries.T
        flow_rows = flow.T
        query_docs = query_documents(starts_ref, batch, begin, width)
        log_total = lse_ref[0, :, pl.ds(begin, width)]
        spread = jnp.sum(
            flow.astype(F32) * wide_ref[0, :, pl.ds(begin, width)], axis=0, keepdims=True
        )

        def chunk(index, d_query):
            first = pl.multiple_of(index * depth, depth)
            rows = pl.ds(first, depth)
            scores = jnp.dot(key_rows[rows, :], queries, preferred_element_type=F32)
            same = same_document(key_docs, first, depth, query_docs)
            probs = jnp.exp(jnp.where(same, scores, MASKED) - log_total)
            pressure = jnp.dot(value_rows[rows, :], flow, preferred_element_type=F32)
            d_scores = (probs * (pressure - spread)).astype(BF16)
            d_value[rows, :] += jnp.dot(
                probs.astype(BF16), flow_rows, preferred_element_type=F32
            )
            d_key[rows, :] += jnp.dot(d_scores, query_rows, preferred_element_type=F32)
            return d_query + jnp.dot(key_t[:, rows], d_scores, preferred_element_type=F32)

        d_query = over_chunks(length // depth, chunk, jnp.zeros((HD, width), F32))
        low = (d_query * SCALE).astype(BF16)
        for i in range(group):
            d_ref[number * group + i, 0, 0:HD, :] = low[:, i * lanes : (i + 1) * lanes]
        return carry

    lax.fori_loop(0, length // width, block, 0)
    for i in range(count):
        rows = slice(i * lanes, (i + 1) * lanes)
        d_ref[i, 0, HD : 2 * HD, :] = d_key[rows, :].T.astype(BF16)
        d_ref[i, 0, 2 * HD : 3 * HD, :] = d_value[rows, :].T.astype(BF16)


def unit_block(*dims):
    return pl.BlockSpec(dims, lambda u, starts: (0, u) + (0,) * (len(dims) - 2))


def own_block(*dims):
    return pl.BlockSpec(dims, lambda u, starts: (u,) + (0,) * (len(dims) - 1))


def attend_back(x, flow, starts, wide, lse):
    count, units, _, lanes = x.shape
    length = count * lanes
    width = 2 * lanes if count % 2 == 0 else lanes
    return pl.pallas_call(
        functools.partial(attend_back_kernel, width),
        out_shape=jax.ShapeDtypeStruct(x.shape, BF16),
        grid_spec=pltpu.PrefetchScalarGridSpec(
            num_scalar_prefetch=1,
            grid=(units,),
            in_specs=[
                unit_block(count, 1, 3 * HD, lanes),
                unit_block(count, 1, HD, lanes),
                own_block(1, HD, length),
                own_block(1, 1, length),
            ],
            out_specs=unit_block(count, 1, 3 * HD, lanes),
            scratch_shapes=[
                pltpu.VMEM((length, HD), BF16),
                pltpu.VMEM((length, HD), BF16),
                pltpu.VMEM((HD, length), BF16),
                pltpu.VMEM((length, lanes), jnp.int32),
                pltpu.VMEM((length, HD), F32),
                pltpu.VMEM((length, HD), F32),
            ],
        ),
        compiler_params=pltpu.CompilerParams(dimension_semantics=("arbitrary",)),
        name="attend_back",
    )(starts, x, flow, wide, lse)


def to_units(columns, parts, count, units):
    rows = columns.shape[1] // MB
    x = columns.reshape(parts, H, HD, MB, rows).transpose(1, 3, 0, 2, 4)
    x = x.reshape(UNITS, parts * HD, rows)
    places = [owner_of(count, u) * units + u // count for u in range(UNITS)]
    y = jnp.zeros((count * units, parts * HD, rows), columns.dtype)
    return y.at[jnp.array(places)].set(x).reshape(count, units, parts * HD, rows)


def from_units(x, parts):
    count, units, _, rows = x.shape
    places = [owner_of(count, u) * units + u // count for u in range(UNITS)]
    x = x.reshape(count * units, parts * HD, rows)[jnp.array(places)]
    x = x.reshape(H, MB, parts, HD, rows).transpose(2, 0, 3, 1, 4)
    return x.reshape(parts * D, MB * rows)


def mul_nn(a, b):
    return jnp.dot(a, b, preferred_element_type=F32)


def mul_tn(a, b):
    return lax.dot_general(a, b, (((0,), (0,)), ((), ())), preferred_element_type=F32)


def mul_nt(a, b):
    return lax.dot_general(a, b, (((1,), (1,)), ((), ())), preferred_element_type=F32)


def mul_tt(a, b):
    return lax.dot_general(a, b, (((0,), (1,)), ((), ())), preferred_element_type=F32)


def forward_kernel(
    width,
    starts_ref,
    tok_in,
    joint_ref,
    mixer_ref,
    inner_ref,
    outer_ref,
    *refs,
):
    vec_refs = refs[:9]
    (
    att_out,
    got_out,
    wide_out,
    lse_out,
    joint_out,
    vec_full,
    inner_bias_full,
    mixer_out,
    inner_out,
    outer_out,
    tok_ref,
    att_ref,
    got_ref,
    wide_ref,
    lse_ref,
    joint_all,
    vec_put,
    vec_out,
    bias_rows,
    put,
    back_put,
    back_got,
    key_rows,
    value_t,
    key_docs,
    mixer_own,
    inner_own,
    outer_own,
    put_sem,
    got_sem,
    back_put_sem,
    back_got_sem,
    joint_sems,
    weight_sems,
    relay_sems,
    own_sems,
    out_sems,
    row_sems,
    ) = refs[9:]
    count, units, _, lanes = got_ref.shape
    length = count * lanes
    depth = min(length, 1024)
    group = width // lanes
    pairs = H // 2
    total_units = MB * H
    part = joint_ref.shape[0]
    me, shard = lax.axis_index("ctx"), lax.axis_index("fsdp")
    y, core = shard // 2, lax.rem(shard, 2)
    x = lax.rem(me, 2)
    far = 2 * (1 - y) + core
    other_core = {"fsdp": 2 * y + 1 - core}
    other_y = {"fsdp": far}
    other_x = {"ctx": me + 1 - 2 * x}
    mine = owned(count, me)

    barrier = pltpu.get_barrier_semaphore()

    def greet(step, carry):
        pl.semaphore_signal(barrier, inc=1, device_id={"ctx": lax.rem(me + step, count)})
        return carry

    lax.fori_loop(1, count, greet, 0)
    pl.semaphore_signal(barrier, inc=1, device_id=other_core)
    pl.semaphore_signal(barrier, inc=1, device_id=other_y)

    def remote(src, dst, sems, index, peer):
        return pltpu.make_async_remote_copy(
            src_ref=src,
            dst_ref=dst,
            send_sem=sems.at[(0, *index)],
            recv_sem=sems.at[(1, *index)],
            device_id=peer,
        )

    def own_joint(pair, third):
        columns = pl.ds(pl.multiple_of(third * D + pair * 128, 128), 128)
        return pltpu.make_async_copy(
            joint_ref.at[:, columns],
            joint_all.at[pair, shard, :, pl.ds(third * 128, 128)],
            own_sems.at[0, pair, third],
        )

    def joint_copy(kind, pair, third, which, peer, source=None):
        here = joint_all.at[pair, which, :, pl.ds(third * 128, 128)]
        if source is None:
            source = here
        else:
            source = source.at[:, pl.ds(pl.multiple_of(third * D + pair * 128, 128), 128)]
        return remote(source, here, joint_sems, (kind, pair, third), peer)

    def joint_y(pair, third):
        return joint_copy(0, pair, third, shard, other_y, joint_ref)

    def joint_core(pair, third):
        return joint_copy(1, pair, third, shard, other_core, joint_ref)

    def joint_pass(pair, third):
        return joint_copy(2, pair, third, far, other_core)

    def joint_store(pair):
        return pltpu.make_async_copy(
            joint_all.at[pair], joint_out.at[pair], own_sems.at[0, pair, 0]
        )

    def each_third(pair, make, act):
        for third in range(3):
            getattr(make(pair, third), act)()

    def every_pair(make, act):
        def body(pair, carry):
            each_third(pair, make, act)
            return carry

        lax.fori_loop(0, pairs, body, 0)

    tok_load = pltpu.make_async_copy(tok_in, tok_ref, row_sems.at[MB])
    tok_load.start()
    every_pair(own_joint, "start")
    wholes = ((mixer_ref, mixer_own, mixer_out), (inner_ref, inner_own, inner_out), (outer_ref, outer_own, outer_out))
    own_in = [
        pltpu.make_async_copy(ref, held, own_sems.at[1, i, 0])
        for i, (ref, held, _) in enumerate(wholes)
    ]
    own_out = [
        pltpu.make_async_copy(held, out.at[shard], own_sems.at[1, i, 1])
        for i, (_, held, out) in enumerate(wholes)
    ]
    for copy in own_in:
        copy.start()
    for i, ref in enumerate(vec_refs):
        vec_put[i : i + 1, 0 : ref.shape[0]] = ref[...].astype(F32).reshape(1, ref.shape[0])
    vec_out[shard] = vec_put[...]
    pl.semaphore_wait(barrier, count + 1)

    class Vectors:
        def __init__(self, rows, columns, keys):
            mine, theirs = vec_out.at[shard, rows, columns], vec_out.at[far, rows, columns]
            source = vec_put.at[rows, columns]
            self.over_y = remote(source, mine, weight_sems, keys[0], other_y)
            self.core = remote(source, mine, weight_sems, keys[1], other_core)
            self.all = remote(theirs, theirs, weight_sems, keys[2], other_core)

        def begin(self):
            self.over_y.start()
            self.core.start()

        def hand_on(self):
            self.over_y.wait_recv()
            self.all.start()

        def arrive(self):
            self.core.wait_recv()
            self.all.wait_recv()

        def end(self):
            for copy in (self.over_y, self.core, self.all):
                copy.wait_send()

    narrow = Vectors(pl.ds(0, 8), pl.ds(0, -(-part // 128) * 128), ((0, 0), (0, 1), (0, 2)))
    broad = Vectors(pl.ds(8, 8), pl.ds(0, D), ((0, 3), (1, 3), (2, 3)))
    mixer_y = remote(mixer_ref, mixer_out.at[shard], weight_sems, (1, 0), other_y)
    mixer_core = remote(mixer_ref, mixer_out.at[shard], weight_sems, (1, 1), other_core)
    mixer_pass = remote(mixer_out.at[far], mixer_out.at[far], weight_sems, (1, 2), other_core)
    class Relayed:
        def __init__(self, ref, out, index, pieces):
            size = ref.shape[0] // 2
            piece = size // RELAY_PIECES
            self.over_y, self.over_x, self.rest = [], [], []
            for k in range(pieces):
                rows = pl.ds(pl.multiple_of(x * size + k * piece, piece), piece)
                self.over_y.append(
                    remote(
                        ref.at[rows, :],
                        out.at[shard, rows, :],
                        relay_sems,
                        (index, 0, k),
                        other_y,
                    )
                )
                passed = out.at[far, rows, :]
                self.over_x.append(remote(passed, passed, relay_sems, (index, 1, k), other_x))
            for k in range(2):
                if pieces < RELAY_PIECES:
                    rows = pl.ds(k * size + pieces * piece, size - pieces * piece)
                    self.rest.append(
                        remote(
                            ref.at[rows, :],
                            out.at[shard, rows, :],
                            relay_sems,
                            (index, 2, k),
                            other_y,
                        )
                    )
            self.core = remote(ref, out.at[shard], weight_sems, (2 + index, 0), other_core)
            self.all = remote(out.at[far], out.at[far], weight_sems, (2 + index, 1), other_core)

        def begin(self):
            for copy in self.over_y:
                copy.start()
            self.core.start()

        def begin_rest(self):
            for copy in self.rest:
                copy.start()

        def relay(self, k):
            self.over_y[k].wait_recv()
            self.over_x[k].start()

        def hand_on(self):
            for copy in self.over_x + self.rest:
                copy.wait_recv()
            self.all.start()

        def end(self):
            for copy in self.over_y + self.over_x + self.rest:
                copy.wait_send()
            self.core.wait()
            self.all.wait()

    outer_way = Relayed(outer_ref, outer_out, 0, RELAY_PIECES)
    inner_way = Relayed(inner_ref, inner_out, 1, 1)
    narrow.begin()

    def send_joint(pair, carry):
        each_third(pair, joint_y, "start")
        each_third(pair, joint_core, "start")
        return carry

    lax.fori_loop(0, pairs, send_joint, 0)
    outer_way.begin()
    inner_way.begin()
    mixer_y.start()
    mixer_core.start()
    inner_way.begin_rest()
    broad.begin()
    for first, second in zip(own_in, own_out):
        first.wait()
        second.start()

    narrow.hand_on()
    narrow.arrive()
    tok_load.wait()

    def bias_of(slot):
        pieces = [
            vec_out[f, slot : slot + 1, 0:part] for f in range(4)
        ]
        return jnp.concatenate(pieces, axis=1)

    query_bias, value_bias = bias_of(0), bias_of(1)
    for pair in range(pairs):
        columns = slice(pair * 128, (pair + 1) * 128)
        bias_rows[pair, :, 0:128] = jnp.broadcast_to(query_bias[:, columns], (8, 128))
        bias_rows[pair, :, 128:256] = jnp.zeros((8, 128), F32)
        bias_rows[pair, :, 256:384] = jnp.broadcast_to(value_bias[:, columns], (8, 128))

    def sent_sem(unit):
        return owner_of(count, unit), unit // count

    def send_copy(unit):
        owner, slot = sent_sem(unit)
        return pltpu.make_async_remote_copy(
            src_ref=put.at[owner, slot],
            dst_ref=got_ref.at[me, slot],
            send_sem=put_sem.at[owner, slot],
            recv_sem=got_sem.at[me, slot],
            device_id={"ctx": owner},
        )

    def keep_copy(slot):
        return pltpu.make_async_copy(
            put.at[me, slot], got_ref.at[me, slot], own_sems.at[2, slot, 0]
        )

    def project(pair, carry):
        each_third(pair, own_joint, "wait")
        each_third(pair, joint_y, "wait_recv")
        each_third(pair, joint_pass, "start")
        each_third(pair, joint_core, "wait_recv")
        each_third(pair, joint_pass, "wait_recv")
        joint_store(pair).start()
        weight = joint_all[pair].reshape(4 * part, 384)
        rows = jnp.dot(tok_ref[...], weight, preferred_element_type=F32)
        rows = (rows + bias_rows[pair, 0:1, :]).astype(BF16)
        for third in range(3):
            for batch in range(MB):
                block = rows[batch * lanes : (batch + 1) * lanes, third * 128 : (third + 1) * 128]
                turned = block.T
                if third == 0:
                    turned = turned * SCALE
                for j in range(2):
                    unit = (2 * pair + j) * MB + batch
                    put[owner_of(count, unit), unit // count, third * HD : (third + 1) * HD, :] = (
                        turned[j * HD : (j + 1) * HD]
                    )
        for i in range(2 * MB):
            unit = 2 * pair * MB + i
            owner, slot = owner_of(count, unit), unit // count

            @pl.when(owner != me)
            def _():
                send_copy(unit).start()

            @pl.when(owner == me)
            def _():
                keep_copy(slot).start()

        return carry

    lax.fori_loop(0, pairs, project, 0)

    def arrival(sender, slot):
        return pltpu.make_async_remote_copy(
            src_ref=put.at[sender, slot],
            dst_ref=got_ref.at[sender, slot],
            send_sem=put_sem.at[sender, slot],
            recv_sem=got_sem.at[sender, slot],
            device_id={"ctx": sender},
        )

    def back_copy(peer, slot):
        return pltpu.make_async_remote_copy(
            src_ref=back_put.at[peer, slot],
            dst_ref=back_got.at[me, slot],
            send_sem=back_put_sem.at[peer, slot],
            recv_sem=back_got_sem.at[me, slot],
            device_id={"ctx": peer},
        )

    def back_keep(slot):
        return pltpu.make_async_copy(
            back_put.at[me, slot], back_got.at[me, slot], own_sems.at[2, slot, 1]
        )

    early = total_units // count > 2

    def outputs(slot):
        return (
            pltpu.make_async_copy(got_ref.at[:, slot], got_out.at[:, slot], out_sems.at[slot, 0]),
            pltpu.make_async_copy(wide_ref.at[slot], wide_out.at[slot], out_sems.at[slot, 1]),
            pltpu.make_async_copy(lse_ref.at[slot], lse_out.at[slot], out_sems.at[slot, 2]),
        )

    def unit_step(slot, carry):
        def wait_one(step, inner):
            arrival(lax.rem(me + step, count), slot).wait_recv()
            return inner

        lax.fori_loop(1, count, wait_one, 0)
        keep_copy(slot).wait()
        outputs(slot)[0].start()
        for i in range(count):
            rows = slice(i * lanes, (i + 1) * lanes)
            key_rows[rows, :] = got_ref[i, slot, HD : 2 * HD, :].T
            value_t[:, rows] = got_ref[i, slot, 2 * HD : 3 * HD, :]
        batch = batch_of(count, me, slot)
        key_documents(starts_ref, batch, key_docs)

        def block(number, inner):
            begin = pl.multiple_of(number * width, width)
            parts = [got_ref[number * group + i, slot, 0:HD, :] for i in range(group)]
            queries = parts[0] if group == 1 else jnp.concatenate(parts, axis=1)
            query_docs = query_documents(starts_ref, batch, begin, width)

            def chunk(index, running):
                peak, total, mixed = running
                first = pl.multiple_of(index * depth, depth)
                scores = jnp.dot(
                    key_rows[pl.ds(first, depth), :], queries, preferred_element_type=F32
                )
                same = same_document(key_docs, first, depth, query_docs)
                scores = jnp.where(same, scores, MASKED)
                new_peak = jnp.maximum(peak, jnp.max(scores, axis=0, keepdims=True))
                scaling = jnp.exp(peak - new_peak)
                weights = jnp.exp(scores - new_peak)
                return (
                    new_peak,
                    total * scaling + jnp.sum(weights, axis=0, keepdims=True),
                    mixed * scaling
                    + jnp.dot(
                        value_t[:, pl.ds(first, depth)],
                        weights.astype(BF16),
                        preferred_element_type=F32,
                    ),
                )

            peak, total, mixed = over_chunks(
                length // depth,
                chunk,
                (
                    jnp.full((1, width), -jnp.inf, F32),
                    jnp.zeros((1, width), F32),
                    jnp.zeros((HD, width), F32),
                ),
            )
            mixed = mixed / total
            wide_ref[slot, :, pl.ds(begin, width)] = mixed
            lse_ref[slot, :, pl.ds(begin, width)] = jnp.broadcast_to(
                peak + jnp.log(total), (8, width)
            )
            low = mixed.astype(BF16)
            for i in range(group):
                back_put[number * group + i, slot] = low[:, i * lanes : (i + 1) * lanes]
            return inner

        lax.fori_loop(0, length // width, block, 0)

        def send_one(step, inner):
            back_copy(lax.rem(me + step, count), slot).start()
            return inner

        lax.fori_loop(1, count, send_one, 0)
        back_keep(slot).start()
        start(outputs(slot)[1:])
        if early:

            @pl.when(slot == 0)
            def _():
                outer_way.relay(0)
                outer_way.relay(1)

            @pl.when(slot == 1)
            def _():
                outer_way.relay(2)

            @pl.when(slot == 2)
            def _():
                inner_way.relay(0)

        return carry

    lax.fori_loop(0, mine, unit_step, 0)

    if not early:
        outer_way.relay(0)
        outer_way.relay(1)
        outer_way.relay(2)
        inner_way.relay(0)
    mixer_y.wait_recv()
    mixer_pass.start()
    outer_way.hand_on()

    def sent(unit, carry):
        @pl.when(owner_of(count, unit) != me)
        def _():
            send_copy(unit).wait_send()

        return carry

    lax.fori_loop(0, total_units, sent, 0)

    def returned(slot, carry):
        def one(step, inner):
            back_copy(lax.rem(me + step, count), slot).wait_send()
            return inner

        lax.fori_loop(1, count, one, 0)
        for copy in outputs(slot):
            copy.wait()
        return carry

    lax.fori_loop(0, mine, returned, 0)
    inner_way.hand_on()
    broad.hand_on()

    def home(unit, carry):
        owner, slot = owner_of(count, unit), unit // count

        @pl.when(owner != me)
        def _():
            pltpu.make_async_remote_copy(
                src_ref=back_put.at[owner, slot],
                dst_ref=back_got.at[owner, slot],
                send_sem=back_put_sem.at[owner, slot],
                recv_sem=back_got_sem.at[owner, slot],
                device_id={"ctx": owner},
            ).wait_recv()

        @pl.when(owner == me)
        def _():
            back_keep(slot).wait()

        return carry

    lax.fori_loop(0, total_units, home, 0)
    att_stores = []
    for batch in range(MB):
        rows = slice(batch * lanes, (batch + 1) * lanes)
        for pair in range(pairs):
            tops = []
            for j in range(2):
                unit = (2 * pair + j) * MB + batch
                tops.append(back_got[owner_of(count, unit), unit // count])
            att_ref[rows, pair * 128 : (pair + 1) * 128] = jnp.concatenate(tops, axis=0).T
        att_stores.append(
            pltpu.make_async_copy(att_ref.at[rows, :], att_out.at[rows, :], row_sems.at[batch])
        )
        att_stores[-1].start()

    outer_way.end()
    inner_way.end()
    broad.arrive()
    narrow.end()
    broad.end()
    for i in range(8):
        vec_full[i : i + 1, :] = bias_of(i)
    vec_full[8:16, :] = jnp.zeros((8, D), F32)
    for k in range(4):
        inner_bias_full[:, k * D : (k + 1) * D] = vec_out[k, 8:9, :]
    mixer_y.wait_send()
    mixer_core.wait()
    mixer_pass.wait()
    every_pair(joint_y, "wait_send")
    every_pair(joint_core, "wait_send")
    every_pair(joint_pass, "wait_send")
    for copy in own_out:
        copy.wait()

    for copy in att_stores:
        copy.wait()
    for pair in range(pairs):
        joint_store(pair).wait()


def forward(count, starts, tokens, joint, mixer, inner, outer, vectors, number):
    units = -(-UNITS // count)
    lanes = tokens.shape[0] // MB
    length = count * lanes
    width = 2 * lanes
    part = joint.shape[0]
    pairs = H // 2
    vm = pl.BlockSpec(memory_space=pltpu.VMEM)
    hbm = pl.BlockSpec(memory_space=pl.ANY)
    dma = pltpu.SemaphoreType.DMA
    return pl.pallas_call(
        functools.partial(forward_kernel, width),
        out_shape=(
            jax.ShapeDtypeStruct(tokens.shape, BF16),
            jax.ShapeDtypeStruct((count, units, 3 * HD, lanes), BF16),
            jax.ShapeDtypeStruct((units, HD, length), F32),
            jax.ShapeDtypeStruct((units, 8, length), F32),
            jax.ShapeDtypeStruct((pairs, 4, part, 384), BF16),
            jax.ShapeDtypeStruct((BIAS_ROWS, D), F32),
            jax.ShapeDtypeStruct((1, FF), F32),
            jax.ShapeDtypeStruct((4, *mixer.shape), BF16),
            jax.ShapeDtypeStruct((4, *inner.shape), BF16),
            jax.ShapeDtypeStruct((4, *outer.shape), BF16),
        ),
        in_specs=[pl.BlockSpec(memory_space=pltpu.SMEM)] + [hbm] * 5 + [vm] * 9,
        out_specs=(hbm, hbm, hbm, hbm, hbm, vm, vm, hbm, hbm, hbm),
        scratch_shapes=[
            pltpu.VMEM(tokens.shape, BF16),
            pltpu.VMEM(tokens.shape, BF16),
            pltpu.VMEM((count, units, 3 * HD, lanes), BF16),
            pltpu.VMEM((units, HD, length), F32),
            pltpu.VMEM((units, 8, length), F32),
            pltpu.VMEM((pairs, 4, part, 384), BF16),
            pltpu.VMEM((BIAS_ROWS, D), F32),
            pltpu.VMEM((4, BIAS_ROWS, D), F32),
            pltpu.VMEM((pairs, 8, 384), F32),
            pltpu.VMEM((count, units, 3 * HD, lanes), BF16),
            pltpu.VMEM((count, units, HD, lanes), BF16),
            pltpu.VMEM((count, units, HD, lanes), BF16),
            pltpu.VMEM((length, HD), BF16),
            pltpu.VMEM((HD, length), BF16),
            pltpu.VMEM((length, lanes), jnp.int32),
            pltpu.VMEM(mixer.shape, BF16),
            pltpu.VMEM(inner.shape, BF16),
            pltpu.VMEM(outer.shape, BF16),
            dma((count, units)),
            dma((count, units)),
            dma((count, units)),
            dma((count, units)),
            dma((2, 3, pairs, 3)),
            dma((2, 4, 4)),
            dma((2, 2, 3, RELAY_PIECES)),
            dma((3, max(pairs, units, 4), 3)),
            dma((units, 3)),
            dma((MB + 1,)),
        ],
        compiler_params=pltpu.CompilerParams(
            collective_id=number, has_side_effects=True, vmem_limit_bytes=56 * 1024 * 1024
        ),
        name="forward",
    )(starts, tokens, joint, mixer, inner, outer, *vectors)


def first_rows(half, tile):
    return half if half <= tile else (half // tile + 1) // 2 * tile


class Place:
    def __init__(self, count):
        self.count = count
        self.depth = count // 2
        self.me, self.shard = lax.axis_index("ctx"), lax.axis_index("fsdp")
        self.y, self.core = self.shard // 2, lax.rem(self.shard, 2)
        self.z, self.x = self.me // 2, lax.rem(self.me, 2)
        self.other_core = {"fsdp": 2 * self.y + 1 - self.core}
        self.other_y = {"fsdp": 2 * (1 - self.y) + self.core}
        self.other_x = {"ctx": 2 * self.z + 1 - self.x}

        self.hi, self.lo = self.z // 2, lax.rem(self.z, 2)

    def along_z(self, step):
        return lax.rem(self.z + step, self.depth)

    def peer_z(self, step):
        return {"ctx": 2 * self.along_z(step) + self.x}


def start(copies):
    for copy in copies:
        copy.start()


def added(a, b):
    return (a.astype(F32) + b.astype(F32)).astype(a.dtype)


class Reduction:
    def __init__(self, place, j, grad, out, head, paired, buffers, sems, z_sems):
        got, y_one, x_one, x_two, y_two, z_got = buffers
        self.place, self.grad, self.out, self.head, self.buffers = place, grad, out, head, buffers
        half, lanes = grad.shape[4], grad.shape[5] // 2
        self.half, self.lanes, self.paired = half, lanes, paired
        p = place
        here, there = self.side(p.y), self.side(1 - p.y)

        def remote(src, dst, slot, peer):
            return pltpu.make_async_remote_copy(
                src_ref=src,
                dst_ref=dst,
                send_sem=sems.at[0, j, slot],
                recv_sem=sems.at[1, j, slot],
                device_id=peer,
            )

        def z_copy(z, target, step):
            return pltpu.make_async_remote_copy(
                src_ref=grad.at[z // 2, lax.rem(z, 2), p.x, p.core, :, here],
                dst_ref=z_got.at[target],
                send_sem=z_sems.at[0, j, step],
                recv_sem=z_sems.at[1, j, step],
                device_id={"ctx": 2 * z + p.x},
            )

        self.first = [remote(grad.at[:, :, :, 1 - p.core], got, 0, p.other_core)]
        self.second = [remote(grad.at[:, :, :, p.core, 0:head, there], y_one, 1, p.other_y)]
        self.third = [
            remote(grad.at[:, :, 1 - p.x, p.core, 0:head, here], x_two, 2, p.other_x)
        ]
        if head < half:
            self.second.append(
                remote(grad.at[:, :, 1 - p.x, p.core, head:half, :], x_one, 3, p.other_x)
            )
            self.third.append(
                remote(grad.at[:, :, p.x, p.core, head:half, there], y_two, 4, p.other_y)
            )
        if paired:
            near = {"ctx": 2 * (2 * p.hi + 1 - p.lo) + p.x}
            self.fourth = [
                remote(
                    grad.at[:, 1 - p.lo, p.x, p.core, :, here], z_got.at[pl.ds(0, 2)], 6, near
                )
            ]
            self.fifth = [z_copy(2 * (1 - p.hi) + p.lo, 2, 1)]
        else:
            self.fourth = []
            self.fifth = [z_copy(lax.rem(p.z + step, 4), p.z, step) for step in range(1, 4)]
        self.last = [remote(out.at[p.core], out.at[p.core], 5, p.other_core)]

    def side(self, y):
        return pl.ds(pl.multiple_of(y * self.lanes, 128), self.lanes)

    def each(self, body):
        def step(block, carry):
            body(block // 2, lax.rem(block, 2))
            return carry

        lax.fori_loop(0, 4, step, 0)

    def stage_zero(self):
        start(self.first)

    def stage_one(self):
        p, grad, got = self.place, self.grad, self.buffers[0]
        for copy in self.first:
            copy.wait_recv()

        def body(hi, lo):
            for x in range(2):
                grad[hi, lo, x, p.core] = added(grad[hi, lo, x, p.core], got[hi, lo, x])

        self.each(body)
        start(self.second)

    def stage_two(self):
        p, grad, head, half = self.place, self.grad, self.head, self.half
        y_one, x_one = self.buffers[1], self.buffers[2]
        here = self.side(p.y)
        for copy in self.second:
            copy.wait()

        def body(hi, lo):
            for x in range(2):
                grad[hi, lo, x, p.core, 0:head, here] = added(
                    grad[hi, lo, x, p.core, 0:head, here], y_one[hi, lo, x]
                )
            if head < half:
                grad[hi, lo, p.x, p.core, head:half, :] = added(
                    grad[hi, lo, p.x, p.core, head:half, :], x_one[hi, lo]
                )

        self.each(body)
        start(self.third)

    def stage_three(self):
        p, grad, head, half = self.place, self.grad, self.head, self.half
        x_two, y_two = self.buffers[3], self.buffers[4]
        here = self.side(p.y)
        for copy in self.third:
            copy.wait()

        def body(hi, lo):
            grad[hi, lo, p.x, p.core, 0:head, here] = added(
                grad[hi, lo, p.x, p.core, 0:head, here], x_two[hi, lo]
            )
            if head < half:
                grad[hi, lo, p.x, p.core, head:half, here] = added(
                    grad[hi, lo, p.x, p.core, head:half, here], y_two[hi, lo]
                )

        self.each(body)
        start(self.fourth if self.paired else self.fifth)

    def stage_four(self):
        p, grad, z_got = self.place, self.grad, self.buffers[5]
        here = self.side(p.y)
        for copy in self.fourth:
            copy.wait()
        for hi in range(2):
            grad[hi, p.lo, p.x, p.core, :, here] = added(
                grad[hi, p.lo, p.x, p.core, :, here], z_got[hi]
            )
        start(self.fifth)

    def stage_five(self):
        p, z_got = self.place, self.buffers[5]
        for copy in self.fifth:
            copy.wait()
        total = self.grad[p.hi, p.lo, p.x, p.core, :, self.side(p.y)].astype(F32)
        if self.paired:
            total = total + z_got[2].astype(F32)
        else:
            for step in range(1, 4):
                total = total + z_got[lax.rem(p.z + step, 4)].astype(F32)
        self.out[p.core] = total.astype(self.out.dtype)
        start(self.last)

    def stage_six(self):
        for copy in self.last:
            copy.wait()
        for copy in self.first:
            copy.wait_send()


def reduction_buffers(half, lanes, head, dtype):
    tail = max(half - head, 16)
    shapes = (
        (2, 2, 2, half, 2 * lanes),
        (2, 2, 2, head, lanes),
        (2, 2, tail, 2 * lanes),
        (2, 2, head, lanes),
        (2, 2, tail, lanes),
        (4, half, lanes),
        (2, half, lanes),
    )
    return [pltpu.VMEM(shape, dtype) for shape in shapes]


def backward_kernel(width, plan, *refs):
    (
        starts_ref,
        flow_in,
        got_in,
        wide_in,
        lse_in,
        tok_in,
        residual_in,
        bias_in,
        joint_in,
        d_outer_in,
        act_in,
        d_inner_in,
        first_in,
        d_branch_in,
        att_in,
        tokens_hbm,
        outer_hbm,
        inner_hbm,
        mixer_hbm,
        joint_out,
        bias_out,
        tokens_out,
        outer_out,
        inner_out,
        mixer_out,
        flow_ref,
        got_ref,
        wide_ref,
        lse_ref,
        tok_ref,
        residual_ref,
        bias_ref,
        d_outer_ref,
        act_ref,
        d_inner_ref,
        first_ref,
        d_branch_ref,
        att_ref,
        flow_put,
        flow_got,
        put,
        home_got,
        key_rows,
        value_rows,
        key_t,
        key_docs,
        d_key,
        d_value,
        joint_all,
        outer_one,
        outer_two,
        inner_one,
        inner_two,
        mixer_grad,
        joint_one,
        joint_two,
        d_turned,
        bias_sum,
        bias_got,
        flow_sems,
        home_sems,
        own_sems,
        sems,
        z_sems,
        bias_sems,
        in_sems,
        result_sems,
        *buffers,
    ) = refs
    count, units, _, lanes = got_ref.shape
    length = count * lanes
    depth = min(length, 1024)
    group = width // lanes
    pairs = H // 2
    total_units = MB * H
    p = Place(count)
    me = p.me
    mine = owned(count, me)

    sources = (
        (flow_in, flow_ref),
        (d_outer_in, d_outer_ref),
        (act_in, act_ref),
        (d_inner_in, d_inner_ref),
        (first_in, first_ref),
        (d_branch_in, d_branch_ref),
        (att_in, att_ref),
        (bias_in, bias_ref),
        (got_in, got_ref),
        (wide_in, wide_ref),
        (lse_in, lse_ref),
        (tok_in, tok_ref),
        (residual_in, residual_ref),
    )
    loads = [
        pltpu.make_async_copy(source, held, in_sems.at[k])
        for k, (source, held) in enumerate(sources)
    ]
    start(loads)

    def loaded(first, last):
        for copy in loads[first:last]:
            copy.wait()

    barrier = pltpu.get_barrier_semaphore()

    def greet(step, carry):
        pl.semaphore_signal(barrier, inc=1, device_id={"ctx": lax.rem(me + step, count)})
        return carry

    lax.fori_loop(1, count, greet, 0)
    pl.semaphore_signal(barrier, inc=1, device_id=p.other_core)
    pl.semaphore_signal(barrier, inc=1, device_id=p.other_y)
    pl.semaphore_signal(barrier, inc=1, device_id={**p.other_y, **p.other_x})
    joint_load = pltpu.make_async_copy(joint_in, joint_all, own_sems.at[2, 0])
    joint_load.start()

    grads = (outer_one, outer_two, inner_one, inner_two, mixer_grad, joint_one, joint_two)
    jobs = [
        Reduction(
            p,
            j,
            grads[j],
            buffers[7 * j + 6],
            plan[j][2],
            plan[j][3],
            buffers[7 * j : 7 * j + 6],
            sems,
            z_sems,
        )
        for j in range(len(grads))
    ]
    o_one, o_two, i_one, i_two, m_one, j_one, j_two = jobs

    def store_rows(targets, row, values, columns):
        half = sum(t.shape[4] for t in targets)
        done = 0
        while done < values.shape[0]:
            block, inside = (row + done) // half, (row + done) % half
            k = 0
            while inside >= targets[k].shape[4]:
                inside -= targets[k].shape[4]
                k += 1
            size = min(values.shape[0] - done, targets[k].shape[4] - inside)
            targets[k][
                block // 8,
                block // 4 % 2,
                block // 2 % 2,
                block % 2,
                inside : inside + size,
                columns,
            ] = values[done : done + size]
            done += size

    loaded(0, 3)
    d_outer_turned = d_outer_ref[...].T

    def outer_gradient(which):
        for side in range(2):
            begin = (2 * side + which) * D
            values = jnp.dot(
                d_outer_turned, act_ref[:, begin : begin + D], preferred_element_type=F32
            )
            columns = slice(side * D, (side + 1) * D)
            store_rows(((outer_one, outer_two)[which],), 0, values.astype(BF16), columns)

    def inner_gradient():
        for k in range(FF // D):
            turned = d_inner_ref[:, k * D : (k + 1) * D].T
            values = jnp.dot(turned, first_ref[...], preferred_element_type=F32)
            store_rows((inner_one, inner_two), k * D, values.astype(BF16), slice(0, D))

    def mixer_gradient():
        values = jnp.dot(d_branch_ref[...].T, att_ref[...], preferred_element_type=F32)
        store_rows((mixer_grad,), 0, values.astype(BF16), slice(0, D))

    def unit_copy(source, target, sem, owner, slot):
        return pltpu.make_async_remote_copy(
            src_ref=source.at[owner, slot],
            dst_ref=target.at[me, slot],
            send_sem=sem.at[0, owner, slot],
            recv_sem=sem.at[1, me, slot],
            device_id={"ctx": owner},
        )

    def unit_arrival(source, target, sem, sender, slot):
        return pltpu.make_async_remote_copy(
            src_ref=source.at[sender, slot],
            dst_ref=target.at[sender, slot],
            send_sem=sem.at[0, sender, slot],
            recv_sem=sem.at[1, sender, slot],
            device_id={"ctx": sender},
        )

    def unit_keep(source, target, kind, slot):
        return pltpu.make_async_copy(
            source.at[me, slot], target.at[me, slot], own_sems.at[kind, slot]
        )

    for pair in range(pairs):
        for batch in range(MB):
            block = flow_ref[
                batch * lanes : (batch + 1) * lanes, pair * 128 : (pair + 1) * 128
            ].T
            for j in range(2):
                unit = (2 * pair + j) * MB + batch
                flow_put[owner_of(count, unit), unit // count] = block[j * HD : (j + 1) * HD]

    outer_gradient(0)
    pl.semaphore_wait(barrier, count + 2)
    o_one.stage_zero()

    def send_flow(turn, carry):
        slot, owner = turn // count, lax.rem(me + turn, count)

        @pl.when((owner != me) & (slot < owned(count, owner)))
        def _():
            unit_copy(flow_put, flow_got, flow_sems, owner, slot).start()

        @pl.when((owner == me) & (slot < mine))
        def _():
            unit_keep(flow_put, flow_got, 0, slot).start()

        return carry

    lax.fori_loop(0, units * count, send_flow, 0)
    loaded(3, 8)
    bias_sum[0] = bias_ref[...]
    outer_gradient(1)
    o_two.stage_zero()
    o_one.stage_one()
    inner_gradient()
    i_one.stage_zero()
    i_two.stage_zero()
    mixer_gradient()
    m_one.stage_zero()

    loaded(8, len(loads))

    def unit_step(slot, carry):
        def wait_one(step, inner):
            unit_arrival(flow_put, flow_got, flow_sems, lax.rem(me + step, count), slot).wait_recv()
            return inner

        lax.fori_loop(1, count, wait_one, 0)
        unit_keep(flow_put, flow_got, 0, slot).wait()
        for i in range(count):
            rows = slice(i * lanes, (i + 1) * lanes)
            key_rows[rows, :] = got_ref[i, slot, HD : 2 * HD, :].T
            value_rows[rows, :] = got_ref[i, slot, 2 * HD : 3 * HD, :].T
            key_t[:, rows] = got_ref[i, slot, HD : 2 * HD, :]
        batch = batch_of(count, me, slot)
        key_documents(starts_ref, batch, key_docs)
        d_key[...] = jnp.zeros_like(d_key)
        d_value[...] = jnp.zeros_like(d_value)

        def block(number, inner):
            begin = pl.multiple_of(number * width, width)

            def beside(ref):
                parts = [ref[number * group + i, slot, 0:HD, :] for i in range(group)]
                return parts[0] if group == 1 else jnp.concatenate(parts, axis=1)

            queries, flow = beside(got_ref), beside(flow_got)
            query_rows, flow_rows = queries.T, flow.T
            query_docs = query_documents(starts_ref, batch, begin, width)
            log_total = lse_ref[slot, 0:1, pl.ds(begin, width)]
            spread = jnp.sum(
                flow.astype(F32) * wide_ref[slot, :, pl.ds(begin, width)], axis=0, keepdims=True
            )

            def chunk(index, d_query):
                first = pl.multiple_of(index * depth, depth)
                rows = pl.ds(first, depth)
                scores = jnp.dot(key_rows[rows, :], queries, preferred_element_type=F32)
                same = same_document(key_docs, first, depth, query_docs)
                probs = jnp.exp(jnp.where(same, scores, MASKED) - log_total)
                pressure = jnp.dot(value_rows[rows, :], flow, preferred_element_type=F32)
                d_scores = (probs * (pressure - spread)).astype(BF16)
                d_value[rows, :] += jnp.dot(
                    probs.astype(BF16), flow_rows, preferred_element_type=F32
                )
                d_key[rows, :] += jnp.dot(d_scores, query_rows, preferred_element_type=F32)
                return d_query + jnp.dot(key_t[:, rows], d_scores, preferred_element_type=F32)

            d_query = over_chunks(length // depth, chunk, jnp.zeros((HD, width), F32))
            low = (d_query * SCALE).astype(BF16)
            for i in range(group):
                put[number * group + i, slot, 0:HD, :] = low[:, i * lanes : (i + 1) * lanes]
            return inner

        lax.fori_loop(0, length // width, block, 0)
        for i in range(count):
            rows = slice(i * lanes, (i + 1) * lanes)
            put[i, slot, HD : 2 * HD, :] = d_key[rows, :].T.astype(BF16)
            put[i, slot, 2 * HD : 3 * HD, :] = d_value[rows, :].T.astype(BF16)

        def send_one(step, inner):
            unit_copy(put, home_got, home_sems, lax.rem(me + step, count), slot).start()
            return inner

        lax.fori_loop(1, count, send_one, 0)
        unit_keep(put, home_got, 1, slot).start()

        @pl.when(slot == 0)
        def _():
            o_two.stage_one()

        @pl.when(slot == 1)
        def _():
            i_one.stage_one()

        @pl.when(slot == 2)
        def _():
            o_one.stage_two()

        return carry

    lax.fori_loop(0, mine, unit_step, 0)
    o_two.stage_two()
    i_two.stage_one()
    o_one.stage_three()
    i_one.stage_two()
    m_one.stage_one()

    ones = jnp.ones((8, MB * lanes), BF16)
    for pair in range(pairs):
        columns = []
        for batch in range(MB):
            blocks = []
            for j in range(2):
                unit = (2 * pair + j) * MB + batch
                owner, slot = owner_of(count, unit), unit // count

                @pl.when(owner != me)
                def _():
                    unit_arrival(put, home_got, home_sems, owner, slot).wait_recv()

                @pl.when(owner == me)
                def _():
                    unit_keep(put, home_got, 1, slot).wait()

                blocks.append(home_got[owner, slot])
            rows = [b[third * HD : (third + 1) * HD] for third in range(3) for b in blocks]
            columns.append(jnp.concatenate(rows, axis=0))
        d_pair = jnp.concatenate(columns, axis=1)
        d_turned[pair] = d_pair.T
        grad = jnp.dot(d_pair, tok_ref[...], preferred_element_type=F32).astype(BF16)
        for third in range(3):
            store_rows(
                (joint_one, joint_two),
                third * D + pair * 128,
                grad[third * 128 : (third + 1) * 128],
                slice(0, D),
            )
        sums = lax.dot_general(
            ones, d_pair, (((1,), (1,)), ((), ())), preferred_element_type=F32
        )
        bias_sum[0, 0:1, pair * 128 : (pair + 1) * 128] = sums[0:1, 0:128]
        bias_sum[0, 1:2, pair * 128 : (pair + 1) * 128] = sums[0:1, 256:384]
        if pair == 2:
            o_two.stage_three()
            o_one.stage_four()
            i_two.stage_two()
            i_one.stage_three()

    m_one.stage_two()
    o_two.stage_four()

    plane = (p.other_y, p.other_x, {**p.other_y, **p.other_x})

    def bias_copy(level, number, slot, peer):
        return pltpu.make_async_remote_copy(
            src_ref=bias_sum.at[level],
            dst_ref=bias_got.at[slot],
            send_sem=bias_sems.at[0, number],
            recv_sem=bias_sems.at[1, number],
            device_id=peer,
        )

    bias_core = bias_copy(0, 0, 0, p.other_core)
    bias_plane = [bias_copy(1, 1 + i, 1 + i, peer) for i, peer in enumerate(plane)]
    bias_z = [
        bias_copy(2, 3 + step, 3 + step, {"ctx": 2 * lax.rem(p.z + step, 4) + p.x})
        for step in range(1, 4)
    ]
    bias_core.start()
    j_one.stage_zero()
    j_two.stage_zero()

    joint_load.wait()

    def token_terms(first, last, total):
        for pair in range(first, last):
            total = total + lax.dot_general(
                d_turned[pair],
                joint_all[pair],
                (((1,), (1,)), ((), ())),
                preferred_element_type=F32,
            )
        tokens_out[...] = total

    token_terms(0, pairs // 2, residual_ref[...])
    bias_core.wait()
    bias_sum[1] = bias_sum[0] + bias_got[0]
    start(bias_plane)
    j_one.stage_one()
    j_two.stage_one()
    i_two.stage_three()
    i_one.stage_four()
    token_terms(pairs // 2, pairs, tokens_out[...])
    results = [
        pltpu.make_async_copy(held, out, result_sems.at[k])
        for k, (held, out) in enumerate(
            (
                (tokens_out, tokens_hbm),
                (outer_out, outer_hbm),
                (inner_out, inner_hbm),
                (mixer_out, mixer_hbm),
            )
        )
    ]
    results[0].start()
    m_one.stage_three()
    for copy in bias_plane:
        copy.wait()
    bias_sum[2] = bias_sum[1] + bias_got[1] + bias_got[2] + bias_got[3]
    start(bias_z)
    j_one.stage_two()
    i_two.stage_four()
    j_two.stage_two()
    m_one.stage_four()
    j_one.stage_three()
    j_two.stage_three()
    o_one.stage_five()
    o_two.stage_five()
    i_one.stage_five()

    def parts_of(j):
        jobs[j].stage_six()
        whole = buffers[7 * j + 6]
        return [whole[low].astype(F32) for low in range(2)]

    def own_lanes(rows):
        width_own = rows.shape[1] // 2
        return jnp.where(p.core == 0, rows[:, :width_own], rows[:, width_own:])

    def put_out(out, pieces):
        out[...] = jnp.concatenate(pieces, axis=0).T

    one, two = parts_of(0), parts_of(1)
    outer_out[...] = jnp.concatenate(
        [jnp.where(p.core == 0, a, b) for a, b in zip(one, two)], axis=0
    )
    results[1].start()
    i_two.stage_five()
    m_one.stage_five()
    one, two = parts_of(2), parts_of(3)
    put_out(inner_out, [own_lanes(r) for r in (one[0], two[0], one[1], two[1])])
    results[2].start()
    put_out(mixer_out, [own_lanes(r) for r in parts_of(4)])
    results[3].start()
    for copy in bias_z:
        copy.wait()
    bias_total = bias_sum[2] + bias_got[4] + bias_got[5] + bias_got[6]
    index = me * 4 + p.shard
    world = 4 * count
    lane = lax.broadcasted_iota(jnp.int32, (D, 128), 0)
    place = lax.broadcasted_iota(jnp.int32, (D, 128), 1)

    def picked(rows, first):
        ones_there = jnp.where(lane == place + first, 1.0, 0.0)
        return jnp.dot(
            rows, ones_there, precision=lax.Precision.HIGHEST, preferred_element_type=F32
        )

    own_hidden = FF // world
    in_row = D // own_hidden
    row = lax.broadcasted_iota(jnp.int32, (8, D), 0)
    hidden = jnp.where(row == index // in_row, bias_total[8:16], 0.0)
    hidden = jnp.broadcast_to(jnp.sum(hidden, axis=0, keepdims=True), (8, D))
    bias_out[0:8, :] = picked(bias_total[0:8], index * (D // world))
    bias_out[8:16, :] = picked(hidden, lax.rem(index, in_row) * own_hidden)

    def sent(unit, carry):
        owner, slot = owner_of(count, unit), unit // count

        @pl.when(owner != me)
        def _():
            unit_copy(flow_put, flow_got, flow_sems, owner, slot).wait_send()

        return carry

    lax.fori_loop(0, total_units, sent, 0)

    def returned(slot, carry):
        def one(step, inner):
            unit_copy(put, home_got, home_sems, lax.rem(me + step, count), slot).wait_send()
            return inner

        lax.fori_loop(1, count, one, 0)
        return carry

    lax.fori_loop(0, mine, returned, 0)
    j_one.stage_five()
    j_two.stage_five()
    one, two = parts_of(5), parts_of(6)
    put_out(joint_out, [own_lanes(r) for r in (one[0], two[0], one[1], two[1])])
    for copy in results:
        copy.wait()


def backward(
    starts, flow, got, wide, lse, source, residual, biases, joint, activations, number
):
    count, units, _, lanes = got.shape
    length = count * lanes
    width = 2 * lanes
    pairs = H // 2
    vm = pl.BlockSpec(memory_space=pltpu.VMEM)
    hbm = pl.BlockSpec(memory_space=pl.ANY)
    dma = pltpu.SemaphoreType.DMA
    small = D // (2 * count)
    half_joint = 3 * D // (2 * count)
    early = first_rows(half_joint, 16)
    plan = (
        (small, FF // 2, small, True),
        (small, FF // 2, small, True),
        (2 * small, D, 2 * small - 16, True),
        (2 * small, D, 2 * small - 16, True),
        (small, D, small, True),
        (early, D, first_rows(early, 16), False),
        (half_joint - early, D, first_rows(half_joint - early, 16), False),
    )
    buffers = []
    for half, full, head, _ in plan:
        buffers += reduction_buffers(half, full // 2, head, BF16)
    outs = [
        jax.ShapeDtypeStruct((2 * small, FF // 4), F32),
        jax.ShapeDtypeStruct((D // 4, FF // count), F32),
        jax.ShapeDtypeStruct((D // 4, 2 * small), F32),
        jax.ShapeDtypeStruct((D // 4, 2 * half_joint), F32),
    ]
    return pl.pallas_call(
        functools.partial(backward_kernel, width, plan),
        out_shape=(
            jax.ShapeDtypeStruct(residual.shape, F32),
            *outs,
            jax.ShapeDtypeStruct((BIAS_ROWS, 128), F32),
        ),
        in_specs=[pl.BlockSpec(memory_space=pltpu.SMEM)] + [hbm] * 14,
        out_specs=(hbm,) * 4 + (vm,) * 2,
        scratch_shapes=[
            pltpu.VMEM(residual.shape, F32),
            *[pltpu.VMEM(o.shape, F32) for o in outs[:3]],
            *[
                pltpu.VMEM(a.shape, a.dtype)
                for a in (flow, got, wide, lse, source, residual, biases, *activations)
            ],
            pltpu.VMEM((count, units, HD, lanes), BF16),
            pltpu.VMEM((count, units, HD, lanes), BF16),
            pltpu.VMEM((count, units, 3 * HD, lanes), BF16),
            pltpu.VMEM((count, units, 3 * HD, lanes), BF16),
            pltpu.VMEM((length, HD), BF16),
            pltpu.VMEM((length, HD), BF16),
            pltpu.VMEM((HD, length), BF16),
            pltpu.VMEM((length, lanes), jnp.int32),
            pltpu.VMEM((length, HD), F32),
            pltpu.VMEM((length, HD), F32),
            pltpu.VMEM((pairs, D, 384), BF16),
            *[pltpu.VMEM((2, 2, 2, 2, half, full), BF16) for half, full, _, _ in plan],
            pltpu.VMEM((pairs, MB * lanes, 384), BF16),
            pltpu.VMEM((3, BIAS_ROWS, D), F32),
            pltpu.VMEM((7, BIAS_ROWS, D), F32),
            dma((2, count, units)),
            dma((2, count, units)),
            dma((3, units)),
            dma((2, len(plan), 7)),
            dma((2, len(plan), 4)),
            dma((2, 7)),
            dma((13,)),
            dma((4,)),
            *buffers,
        ],
        compiler_params=pltpu.CompilerParams(
            collective_id=number, has_side_effects=True, vmem_limit_bytes=67043328
        ),
        name="backward",
    )(starts, flow, got, wide, lse, source, residual, biases, joint, *activations)


def settle_kernel(count, *refs):
    sources, outs, held = refs[:count], refs[count : 2 * count], refs[2 * count : 3 * count]
    sems = refs[3 * count]
    copies_in = [
        pltpu.make_async_copy(sources[i], held[i], sems.at[0, i]) for i in range(count)
    ]
    copies_out = [pltpu.make_async_copy(held[i], outs[i], sems.at[1, i]) for i in range(count)]
    start(copies_in)
    for first, second in zip(copies_in, copies_out):
        first.wait()
        second.start()
    for copy in copies_out:
        copy.wait()


def settle(*arrays):
    count = len(arrays)
    return pl.pallas_call(
        functools.partial(settle_kernel, count),
        out_shape=[jax.ShapeDtypeStruct(a.shape, a.dtype) for a in arrays],
        in_specs=[pl.BlockSpec(memory_space=pl.ANY)] * count,
        out_specs=[pl.BlockSpec(memory_space=pl.ANY)] * count,
        scratch_shapes=[
            *[pltpu.VMEM(a.shape, a.dtype) for a in arrays],
            pltpu.SemaphoreType.DMA((2, count)),
        ],
        name="settle",
    )(*arrays)


def on_device(
    count,
    shards,
    tokens,
    doc_starts,
    joint_weight,
    mixer_weight,
    inner_weight,
    outer_weight,
    query_bias,
    value_bias,
    mixer_bias,
    first_gain,
    first_shift,
    inner_bias,
    outer_bias,
    second_gain,
    second_shift,
    upstream,
):
    rows = tokens.shape[2]
    length = rows * count
    units = -(-MB * H // count)
    me = lax.axis_index("ctx")

    part = D // shards
    vectors = [
        query_bias,
        value_bias,
        mixer_bias,
        first_gain,
        first_shift,
        outer_bias,
        second_gain,
        second_shift,
        inner_bias,
    ]
    source = tokens.reshape(MB * rows, D)
    attended, received, wide, lse, joint, vectors, ibias, mixer, inner, outer = forward(
        count,
        doc_starts,
        source,
        joint_weight,
        mixer_weight,
        inner_weight,
        outer_weight,
        vectors,
        0,
    )
    joint = joint.reshape(H // 2, D, 384)
    mixer, inner, outer = mixer.reshape(D, D), inner.reshape(D, FF), outer.reshape(FF, D)
    _, _, mbias, gain_one, shift_one, obias, gain_two, shift_two = [
        vectors[i : i + 1] for i in range(8)
    ]

    branch = mul_nn(attended, mixer) + mbias
    first, first_normed, first_recip = norm_forward(
        source.astype(F32) + branch, gain_one, shift_one
    )
    first_low = first.astype(BF16)
    inner_pre = mul_nn(first_low, inner) + ibias
    activated, gelu_slope = gelu_parts(inner_pre)
    activated_low = activated.astype(BF16)
    outer_out = mul_nn(activated_low, outer) + obias
    final, second_normed, second_recip = norm_forward(first + outer_out, gain_two, shift_two)
    result = final.astype(BF16).reshape(MB, 1, rows, D)

    incoming = upstream.reshape(MB * rows, D).astype(F32)
    rescale_grad = jnp.sum(incoming * second_normed, axis=0)
    reshift_grad = jnp.sum(incoming, axis=0)
    d_second = norm_backward(incoming, second_normed, second_recip, gain_two)
    d_outer = d_second.astype(BF16)
    return_grad = jnp.sum(d_outer.astype(F32), axis=0)
    d_inner = (mul_nt(d_outer, outer) * gelu_slope).astype(BF16)
    hidden_grad = jnp.sum(d_inner.astype(F32), axis=0)
    d_first = d_second + mul_nt(d_inner, inner)
    scale_grad = jnp.sum(d_first * first_normed, axis=0)
    shift_grad = jnp.sum(d_first, axis=0)
    d_residual = norm_backward(d_first, first_normed, first_recip, gain_one)
    d_branch = d_residual.astype(BF16)
    mixing_grad = jnp.sum(d_branch.astype(F32), axis=0)
    world = count * shards
    index = me * shards + lax.axis_index("fsdp")
    sums = [
        mixing_grad,
        scale_grad,
        shift_grad,
        return_grad,
        rescale_grad,
        reshift_grad,
        *hidden_grad.reshape(FF // D, D),
    ]
    if shards == 4 and count == 8:
        flow = mul_nt(d_branch, mixer).astype(BF16)
        biases = jnp.pad(jnp.stack(sums), ((2, BIAS_ROWS - 2 - len(sums)), (0, 0)))
        tokens_grad, *blocks, biases = backward(
            doc_starts,
            flow,
            received,
            wide,
            lse,
            source,
            d_residual,
            biases,
            joint,
            [d_outer, activated_low, d_inner, first_low, d_branch, attended],
            1,
        )
        *blocks, tokens_grad = settle(*blocks, tokens_grad)
        blocks[0] = blocks[0].T
        own, own_hidden = biases[:8, : D // world], biases[8, : FF // world]
    else:
        natural = joint.reshape(H // 2, D, 3, 128).transpose(1, 2, 0, 3).reshape(D, 3 * D)
        flow = mul_nt(mixer, d_branch).astype(BF16)
        flow_units = exchange(to_units(flow, 1, count, units), 2)
        d_units = attend_back(received, flow_units, doc_starts, wide, lse[:, :1])
        d_joint = from_units(exchange(d_units, 3), 3)
        bias_sums = jnp.sum(d_joint.astype(F32), axis=1)
        turned = [
            mul_tn(d_outer, activated_low),
            mul_tn(d_inner, first_low),
            mul_tn(d_branch, attended),
            mul_nn(d_joint, source),
        ]
        tokens_grad = d_residual + mul_tt(d_joint, natural)

        def reduced(grad):
            over_lanes = lax.psum_scatter(
                grad.astype(BF16), "fsdp", scatter_dimension=1, tiled=True
            )
            over_rows = lax.psum_scatter(over_lanes, "ctx", scatter_dimension=0, tiled=True)
            return over_rows.T.astype(F32)

        blocks = [reduced(g) for g in turned]
        biases = jnp.stack([bias_sums[:D], bias_sums[2 * D :], *sums])
        biases = lax.psum(biases, ("ctx", "fsdp"))
        own = lax.dynamic_slice_in_dim(biases[:8], index * (D // world), D // world, 1)
        hidden_rows = biases[8 : 8 + FF // D].reshape(FF)
        own_hidden = lax.dynamic_slice_in_dim(hidden_rows, index * (FF // world), FF // world, 0)
    tokens_grad = tokens_grad.reshape(MB, 1, rows, D)
    outer_out_grad, inner_out, mixer_out, joint_out = blocks
    sums = [*own[:5], own_hidden, *own[5:]]
    return (result, tokens_grad, joint_out, mixer_out, inner_out, outer_out_grad, *sums)


def solution(mesh):
    in_specs = (
        P(None, "fsdp", "ctx", None),
        P(None, "fsdp", None),
        P("fsdp", None),
        P("fsdp", None),
        P("fsdp", None),
        P("fsdp", None),
        P("fsdp"),
        P("fsdp"),
        P("fsdp"),
        P("fsdp"),
        P("fsdp"),
        P("fsdp"),
        P("fsdp"),
        P("fsdp"),
        P("fsdp"),
        P(None, "fsdp", "ctx", None),
    )
    out_specs = (
        P(None, "fsdp", "ctx", None),
        P(None, "fsdp", "ctx", None),
        P("fsdp", "ctx"),
        P("fsdp", "ctx"),
        P("fsdp", "ctx"),
        P("fsdp", "ctx"),
        P(("ctx", "fsdp")),
        P(("ctx", "fsdp")),
        P(("ctx", "fsdp")),
        P(("ctx", "fsdp")),
        P(("ctx", "fsdp")),
        P(("ctx", "fsdp")),
        P(("ctx", "fsdp")),
        P(("ctx", "fsdp")),
        P(("ctx", "fsdp")),
    )
    return jax.shard_map(
        functools.partial(on_device, mesh.shape["ctx"], mesh.shape["fsdp"]),
        mesh=mesh,
        in_specs=in_specs,
        out_specs=out_specs,
        check_vma=False,
    )
```

```python
import functools
import math

import jax
import jax.numpy as jnp
from jax import lax
from jax.experimental import pallas as pl
from jax.experimental.pallas import tpu as pltpu
from jax.sharding import PartitionSpec as P

D = 768
H = 12
HD = 64
FF = 3072
MB = 3

SCALE = 0.125
EPSILON = 1e-12
MASKED = -1000000000.0
ROOT_HALF = 0.7071067811865476
GAUSS_PEAK = 0.3989422804014327

F32 = jnp.float32
BF16 = jnp.bfloat16


def norm_forward(hidden, gain, shift):
    average = jnp.mean(hidden, axis=-1, keepdims=True)
    centred = hidden - average
    reciprocal = lax.rsqrt(jnp.mean(centred * centred, axis=-1, keepdims=True) + EPSILON)
    normed = centred * reciprocal
    return (normed * gain + shift, normed, reciprocal)


def norm_backward(incoming, normed, reciprocal, gain):
    scaled = incoming * gain
    return reciprocal * (
        scaled
        - jnp.mean(scaled, axis=-1, keepdims=True)
        - normed * jnp.mean(scaled * normed, axis=-1, keepdims=True)
    )


def gelu_parts(inner):
    cumulative = 0.5 * (1.0 + lax.erf(inner * ROOT_HALF))
    return (inner * cumulative, cumulative + inner * jnp.exp(-0.5 * inner * inner) * GAUSS_PEAK)


UNITS = MB * H
BIAS_ROWS = 16
RELAY_PIECES = 3


def spare_owner(count, j):
    stride = count // (UNITS % count)
    return j * stride + (j % 2 if stride > 1 else 0)


def owner_of(count, unit):
    full, rest = UNITS // count, UNITS % count
    if rest == 0:
        return unit % count
    if full == 0:
        return spare_owner(count, unit)
    late = unit // (full * count)
    return (1 - late) * (unit % count) + late * spare_owner(count, unit - full * count)


def spare_index(count, device):
    return device // (count // (UNITS % count))


def owned(count, device):
    full, rest = UNITS // count, UNITS % count
    if rest == 0:
        return full
    j = spare_index(count, device)
    extra = (spare_owner(count, j) == device) & (j < rest)
    return full + extra.astype(jnp.int32)


def batch_of(count, device, slot):
    full, rest = UNITS // count, UNITS % count
    if rest == 0:
        return (slot * count + device) % MB
    if full == 0:
        return jnp.minimum(spare_index(count, device), UNITS - 1) % MB
    late = slot // full
    unit = slot * count + (1 - late) * device + late * spare_index(count, device)
    return unit % MB


def exchange_kernel(count, x_ref, y_ref, held, send_sem, recv_sem, own_sem):
    me = lax.axis_index("ctx")
    barrier = pltpu.get_barrier_semaphore()

    def greet(step, carry):
        peer = lax.rem(me + step, count)
        pl.semaphore_signal(barrier, inc=1, device_id={"ctx": peer})
        return carry

    lax.fori_loop(1, count, greet, 0)
    own_in = pltpu.make_async_copy(x_ref.at[me], held, own_sem)
    own_in.start()
    pl.semaphore_wait(barrier, count - 1)

    def transfer(step):
        peer = lax.rem(me + step, count)
        return pltpu.make_async_remote_copy(
            src_ref=x_ref.at[peer],
            dst_ref=y_ref.at[me],
            send_sem=send_sem.at[step],
            recv_sem=recv_sem.at[step],
            device_id={"ctx": peer},
        )

    def begin(step, carry):
        transfer(step).start()
        return carry

    lax.fori_loop(1, count, begin, 0)
    own_in.wait()
    own_out = pltpu.make_async_copy(held, y_ref.at[me], own_sem)
    own_out.start()
    own_out.wait()

    def finish(step, carry):
        transfer(step).wait()
        return carry

    lax.fori_loop(1, count, finish, 0)


def exchange(x, number):
    count = x.shape[0]
    return pl.pallas_call(
        functools.partial(exchange_kernel, count),
        out_shape=jax.ShapeDtypeStruct(x.shape, x.dtype),
        in_specs=[pl.BlockSpec(memory_space=pl.ANY)],
        out_specs=pl.BlockSpec(memory_space=pl.ANY),
        scratch_shapes=[
            pltpu.VMEM(x.shape[1:], x.dtype),
            pltpu.SemaphoreType.DMA((count,)),
            pltpu.SemaphoreType.DMA((count,)),
            pltpu.SemaphoreType.DMA,
        ],
        compiler_params=pltpu.CompilerParams(collective_id=number, has_side_effects=True),
        name=f"exchange_{number}",
    )(x)


def across(ref, first, rows, width, lanes):
    parts = [ref[first + i, 0, rows, :] for i in range(width // lanes)]
    return parts[0] if len(parts) == 1 else jnp.concatenate(parts, axis=1)


def document(starts_ref, batch, position):
    docs = jnp.zeros(position.shape, jnp.int32) - 1
    for j in range(starts_ref.shape[2]):
        docs = docs + jnp.where(position >= starts_ref[batch, 0, j], 1, 0)
    return docs


def key_documents(starts_ref, batch, key_docs):
    key_docs[...] = document(
        starts_ref, batch, lax.broadcasted_iota(jnp.int32, key_docs.shape, 0)
    )


def query_documents(starts_ref, batch, begin, width):
    return document(
        starts_ref, batch, lax.broadcasted_iota(jnp.int32, (1, width), 1) + begin
    )


def same_document(key_docs, first, width, query_docs):
    keys = key_docs[pl.ds(first, width), :]
    lanes = keys.shape[1]
    parts = [keys == query_docs[:, i : i + lanes] for i in range(0, query_docs.shape[1], lanes)]
    return parts[0] if len(parts) == 1 else jnp.concatenate(parts, axis=1)


def over_chunks(chunks, body, carry):
    if chunks == 1:
        return body(0, carry)
    return lax.fori_loop(0, chunks, body, carry)


def attend_back_kernel(
    width,
    starts_ref,
    x_ref,
    flow_ref,
    wide_ref,
    lse_ref,
    d_ref,
    key_rows,
    value_rows,
    key_t,
    key_docs,
    d_key,
    d_value,
):
    count, _, _, lanes = x_ref.shape
    length = count * lanes
    depth = min(length, 1024)
    unit = pl.program_id(0)
    for i in range(count):
        rows = slice(i * lanes, (i + 1) * lanes)
        key_rows[rows, :] = x_ref[i, 0, HD : 2 * HD, :].T
        value_rows[rows, :] = x_ref[i, 0, 2 * HD : 3 * HD, :].T
        key_t[:, rows] = x_ref[i, 0, HD : 2 * HD, :]
    batch = batch_of(count, lax.axis_index("ctx"), unit)
    key_documents(starts_ref, batch, key_docs)
    d_key[...] = jnp.zeros_like(d_key)
    d_value[...] = jnp.zeros_like(d_value)
    group = width // lanes

    def block(number, carry):
        begin = pl.multiple_of(number * width, width)
        queries = across(x_ref, number * group, slice(0, HD), width, lanes)
        flow = across(flow_ref, number * group, slice(0, HD), width, lanes)
        query_rows = queries.T
        flow_rows = flow.T
        query_docs = query_documents(starts_ref, batch, begin, width)
        log_total = lse_ref[0, :, pl.ds(begin, width)]
        spread = jnp.sum(
            flow.astype(F32) * wide_ref[0, :, pl.ds(begin, width)], axis=0, keepdims=True
        )

        def chunk(index, d_query):
            first = pl.multiple_of(index * depth, depth)
            rows = pl.ds(first, depth)
            scores = jnp.dot(key_rows[rows, :], queries, preferred_element_type=F32)
            same = same_document(key_docs, first, depth, query_docs)
            probs = jnp.exp(jnp.where(same, scores, MASKED) - log_total)
            pressure = jnp.dot(value_rows[rows, :], flow, preferred_element_type=F32)
            d_scores = (probs * (pressure - spread)).astype(BF16)
            d_value[rows, :] += jnp.dot(
                probs.astype(BF16), flow_rows, preferred_element_type=F32
            )
            d_key[rows, :] += jnp.dot(d_scores, query_rows, preferred_element_type=F32)
            return d_query + jnp.dot(key_t[:, rows], d_scores, preferred_element_type=F32)

        d_query = over_chunks(length // depth, chunk, jnp.zeros((HD, width), F32))
        low = (d_query * SCALE).astype(BF16)
        for i in range(group):
            d_ref[number * group + i, 0, 0:HD, :] = low[:, i * lanes : (i + 1) * lanes]
        return carry

    lax.fori_loop(0, length // width, block, 0)
    for i in range(count):
        rows = slice(i * lanes, (i + 1) * lanes)
        d_ref[i, 0, HD : 2 * HD, :] = d_key[rows, :].T.astype(BF16)
        d_ref[i, 0, 2 * HD : 3 * HD, :] = d_value[rows, :].T.astype(BF16)


def unit_block(*dims):
    return pl.BlockSpec(dims, lambda u, starts: (0, u) + (0,) * (len(dims) - 2))


def own_block(*dims):
    return pl.BlockSpec(dims, lambda u, starts: (u,) + (0,) * (len(dims) - 1))


def attend_back(x, flow, starts, wide, lse):
    count, units, _, lanes = x.shape
    length = count * lanes
    width = 2 * lanes if count % 2 == 0 else lanes
    return pl.pallas_call(
        functools.partial(attend_back_kernel, width),
        out_shape=jax.ShapeDtypeStruct(x.shape, BF16),
        grid_spec=pltpu.PrefetchScalarGridSpec(
            num_scalar_prefetch=1,
            grid=(units,),
            in_specs=[
                unit_block(count, 1, 3 * HD, lanes),
                unit_block(count, 1, HD, lanes),
                own_block(1, HD, length),
                own_block(1, 1, length),
            ],
            out_specs=unit_block(count, 1, 3 * HD, lanes),
            scratch_shapes=[
                pltpu.VMEM((length, HD), BF16),
                pltpu.VMEM((length, HD), BF16),
                pltpu.VMEM((HD, length), BF16),
                pltpu.VMEM((length, lanes), jnp.int32),
                pltpu.VMEM((length, HD), F32),
                pltpu.VMEM((length, HD), F32),
            ],
        ),
        compiler_params=pltpu.CompilerParams(dimension_semantics=("arbitrary",)),
        name="attend_back",
    )(starts, x, flow, wide, lse)


def to_units(columns, parts, count, units):
    rows = columns.shape[1] // MB
    x = columns.reshape(parts, H, HD, MB, rows).transpose(1, 3, 0, 2, 4)
    x = x.reshape(UNITS, parts * HD, rows)
    places = [owner_of(count, u) * units + u // count for u in range(UNITS)]
    y = jnp.zeros((count * units, parts * HD, rows), columns.dtype)
    return y.at[jnp.array(places)].set(x).reshape(count, units, parts * HD, rows)


def from_units(x, parts):
    count, units, _, rows = x.shape
    places = [owner_of(count, u) * units + u // count for u in range(UNITS)]
    x = x.reshape(count * units, parts * HD, rows)[jnp.array(places)]
    x = x.reshape(H, MB, parts, HD, rows).transpose(2, 0, 3, 1, 4)
    return x.reshape(parts * D, MB * rows)


def mul_nn(a, b):
    return jnp.dot(a, b, preferred_element_type=F32)


def mul_tn(a, b):
    return lax.dot_general(a, b, (((0,), (0,)), ((), ())), preferred_element_type=F32)


def mul_nt(a, b):
    return lax.dot_general(a, b, (((1,), (1,)), ((), ())), preferred_element_type=F32)


def mul_tt(a, b):
    return lax.dot_general(a, b, (((0,), (1,)), ((), ())), preferred_element_type=F32)


def forward_kernel(
    width,
    starts_ref,
    tok_in,
    joint_ref,
    mixer_ref,
    inner_ref,
    outer_ref,
    *refs,
):
    vec_refs = refs[:9]
    (
    att_out,
    got_out,
    wide_out,
    lse_out,
    joint_out,
    vec_full,
    inner_bias_full,
    mixer_out,
    inner_out,
    outer_out,
    tok_ref,
    att_ref,
    got_ref,
    wide_ref,
    lse_ref,
    joint_all,
    vec_put,
    vec_out,
    bias_rows,
    put,
    back_put,
    back_got,
    key_rows,
    value_t,
    key_docs,
    mixer_own,
    inner_own,
    outer_own,
    put_sem,
    got_sem,
    back_put_sem,
    back_got_sem,
    joint_sems,
    weight_sems,
    relay_sems,
    own_sems,
    out_sems,
    row_sems,
    ) = refs[9:]
    count, units, _, lanes = got_ref.shape
    length = count * lanes
    depth = min(length, 1024)
    group = width // lanes
    pairs = H // 2
    total_units = MB * H
    part = joint_ref.shape[0]
    me, shard = lax.axis_index("ctx"), lax.axis_index("fsdp")
    y, core = shard // 2, lax.rem(shard, 2)
    x = lax.rem(me, 2)
    far = 2 * (1 - y) + core
    other_core = {"fsdp": 2 * y + 1 - core}
    other_y = {"fsdp": far}
    other_x = {"ctx": me + 1 - 2 * x}
    mine = owned(count, me)

    barrier = pltpu.get_barrier_semaphore()

    def greet(step, carry):
        pl.semaphore_signal(barrier, inc=1, device_id={"ctx": lax.rem(me + step, count)})
        return carry

    lax.fori_loop(1, count, greet, 0)
    pl.semaphore_signal(barrier, inc=1, device_id=other_core)
    pl.semaphore_signal(barrier, inc=1, device_id=other_y)

    def remote(src, dst, sems, index, peer):
        return pltpu.make_async_remote_copy(
            src_ref=src,
            dst_ref=dst,
            send_sem=sems.at[(0, *index)],
            recv_sem=sems.at[(1, *index)],
            device_id=peer,
        )

    def own_joint(pair, third):
        columns = pl.ds(pl.multiple_of(third * D + pair * 128, 128), 128)
        return pltpu.make_async_copy(
            joint_ref.at[:, columns],
            joint_all.at[pair, shard, :, pl.ds(third * 128, 128)],
            own_sems.at[0, pair, third],
        )

    def joint_copy(kind, pair, third, which, peer, source=None):
        here = joint_all.at[pair, which, :, pl.ds(third * 128, 128)]
        if source is None:
            source = here
        else:
            source = source.at[:, pl.ds(pl.multiple_of(third * D + pair * 128, 128), 128)]
        return remote(source, here, joint_sems, (kind, pair, third), peer)

    def joint_y(pair, third):
        return joint_copy(0, pair, third, shard, other_y, joint_ref)

    def joint_core(pair, third):
        return joint_copy(1, pair, third, shard, other_core, joint_ref)

    def joint_pass(pair, third):
        return joint_copy(2, pair, third, far, other_core)

    def joint_store(pair):
        return pltpu.make_async_copy(
            joint_all.at[pair], joint_out.at[pair], own_sems.at[0, pair, 0]
        )

    def each_third(pair, make, act):
        for third in range(3):
            getattr(make(pair, third), act)()

    def every_pair(make, act):
        def body(pair, carry):
            each_third(pair, make, act)
            return carry

        lax.fori_loop(0, pairs, body, 0)

    tok_load = pltpu.make_async_copy(tok_in, tok_ref, row_sems.at[MB])
    tok_load.start()
    every_pair(own_joint, "start")
    wholes = ((mixer_ref, mixer_own, mixer_out), (inner_ref, inner_own, inner_out), (outer_ref, outer_own, outer_out))
    own_in = [
        pltpu.make_async_copy(ref, held, own_sems.at[1, i, 0])
        for i, (ref, held, _) in enumerate(wholes)
    ]
    own_out = [
        pltpu.make_async_copy(held, out.at[shard], own_sems.at[1, i, 1])
        for i, (_, held, out) in enumerate(wholes)
    ]
    for copy in own_in:
        copy.start()
    for i, ref in enumerate(vec_refs):
        vec_put[i : i + 1, 0 : ref.shape[0]] = ref[...].astype(F32).reshape(1, ref.shape[0])
    vec_out[shard] = vec_put[...]
    pl.semaphore_wait(barrier, count + 1)

    class Vectors:
        def __init__(self, rows, columns, keys):
            mine, theirs = vec_out.at[shard, rows, columns], vec_out.at[far, rows, columns]
            source = vec_put.at[rows, columns]
            self.over_y = remote(source, mine, weight_sems, keys[0], other_y)
            self.core = remote(source, mine, weight_sems, keys[1], other_core)
            self.all = remote(theirs, theirs, weight_sems, keys[2], other_core)

        def begin(self):
            self.over_y.start()
            self.core.start()

        def hand_on(self):
            self.over_y.wait_recv()
            self.all.start()

        def arrive(self):
            self.core.wait_recv()
            self.all.wait_recv()

        def end(self):
            for copy in (self.over_y, self.core, self.all):
                copy.wait_send()

    narrow = Vectors(pl.ds(0, 8), pl.ds(0, -(-part // 128) * 128), ((0, 0), (0, 1), (0, 2)))
    broad = Vectors(pl.ds(8, 8), pl.ds(0, D), ((0, 3), (1, 3), (2, 3)))
    mixer_y = remote(mixer_ref, mixer_out.at[shard], weight_sems, (1, 0), other_y)
    mixer_core = remote(mixer_ref, mixer_out.at[shard], weight_sems, (1, 1), other_core)
    mixer_pass = remote(mixer_out.at[far], mixer_out.at[far], weight_sems, (1, 2), other_core)
    class Relayed:
        def __init__(self, ref, out, index, pieces):
            size = ref.shape[0] // 2
            piece = size // RELAY_PIECES
            self.over_y, self.over_x, self.rest = [], [], []
            for k in range(pieces):
                rows = pl.ds(pl.multiple_of(x * size + k * piece, piece), piece)
                self.over_y.append(
                    remote(
                        ref.at[rows, :],
                        out.at[shard, rows, :],
                        relay_sems,
                        (index, 0, k),
                        other_y,
                    )
                )
                passed = out.at[far, rows, :]
                self.over_x.append(remote(passed, passed, relay_sems, (index, 1, k), other_x))
            for k in range(2):
                if pieces < RELAY_PIECES:
                    rows = pl.ds(k * size + pieces * piece, size - pieces * piece)
                    self.rest.append(
                        remote(
                            ref.at[rows, :],
                            out.at[shard, rows, :],
                            relay_sems,
                            (index, 2, k),
                            other_y,
                        )
                    )
            self.core = remote(ref, out.at[shard], weight_sems, (2 + index, 0), other_core)
            self.all = remote(out.at[far], out.at[far], weight_sems, (2 + index, 1), other_core)

        def begin(self):
            for copy in self.over_y:
                copy.start()
            self.core.start()

        def begin_rest(self):
            for copy in self.rest:
                copy.start()

        def relay(self, k):
            self.over_y[k].wait_recv()
            self.over_x[k].start()

        def hand_on(self):
            for copy in self.over_x + self.rest:
                copy.wait_recv()
            self.all.start()

        def end(self):
            for copy in self.over_y + self.over_x + self.rest:
                copy.wait_send()
            self.core.wait()
            self.all.wait()

    outer_way = Relayed(outer_ref, outer_out, 0, RELAY_PIECES)
    inner_way = Relayed(inner_ref, inner_out, 1, 1)
    narrow.begin()

    def send_joint(pair, carry):
        each_third(pair, joint_y, "start")
        each_third(pair, joint_core, "start")
        return carry

    lax.fori_loop(0, pairs, send_joint, 0)
    outer_way.begin()
    inner_way.begin()
    inner_way.begin_rest()
    mixer_y.start()
    mixer_core.start()
    broad.begin()
    for first, second in zip(own_in, own_out):
        first.wait()
        second.start()

    narrow.hand_on()
    narrow.arrive()
    tok_load.wait()

    def bias_of(slot):
        pieces = [
            vec_out[f, slot : slot + 1, 0:part] for f in range(4)
        ]
        return jnp.concatenate(pieces, axis=1)

    query_bias, value_bias = bias_of(0), bias_of(1)
    for pair in range(pairs):
        columns = slice(pair * 128, (pair + 1) * 128)
        bias_rows[pair, :, 0:128] = jnp.broadcast_to(query_bias[:, columns], (8, 128))
        bias_rows[pair, :, 128:256] = jnp.zeros((8, 128), F32)
        bias_rows[pair, :, 256:384] = jnp.broadcast_to(value_bias[:, columns], (8, 128))

    def sent_sem(unit):
        return owner_of(count, unit), unit // count

    def send_copy(unit):
        owner, slot = sent_sem(unit)
        return pltpu.make_async_remote_copy(
            src_ref=put.at[owner, slot],
            dst_ref=got_ref.at[me, slot],
            send_sem=put_sem.at[owner, slot],
            recv_sem=got_sem.at[me, slot],
            device_id={"ctx": owner},
        )

    def keep_copy(slot):
        return pltpu.make_async_copy(
            put.at[me, slot], got_ref.at[me, slot], own_sems.at[2, slot, 0]
        )

    def project(pair, carry):
        each_third(pair, own_joint, "wait")
        each_third(pair, joint_y, "wait_recv")
        each_third(pair, joint_pass, "start")
        each_third(pair, joint_core, "wait_recv")
        each_third(pair, joint_pass, "wait_recv")
        joint_store(pair).start()
        weight = joint_all[pair].reshape(4 * part, 384)
        rows = jnp.dot(tok_ref[...], weight, preferred_element_type=F32)
        rows = (rows + bias_rows[pair, 0:1, :]).astype(BF16)
        for third in range(3):
            for batch in range(MB):
                block = rows[batch * lanes : (batch + 1) * lanes, third * 128 : (third + 1) * 128]
                turned = block.T
                if third == 0:
                    turned = turned * SCALE
                for j in range(2):
                    unit = (2 * pair + j) * MB + batch
                    put[owner_of(count, unit), unit // count, third * HD : (third + 1) * HD, :] = (
                        turned[j * HD : (j + 1) * HD]
                    )
        for i in range(2 * MB):
            unit = 2 * pair * MB + i
            owner, slot = owner_of(count, unit), unit // count

            @pl.when(owner != me)
            def _():
                send_copy(unit).start()

            @pl.when(owner == me)
            def _():
                keep_copy(slot).start()

        return carry

    lax.fori_loop(0, pairs, project, 0)

    def arrival(sender, slot):
        return pltpu.make_async_remote_copy(
            src_ref=put.at[sender, slot],
            dst_ref=got_ref.at[sender, slot],
            send_sem=put_sem.at[sender, slot],
            recv_sem=got_sem.at[sender, slot],
            device_id={"ctx": sender},
        )

    def back_copy(peer, slot):
        return pltpu.make_async_remote_copy(
            src_ref=back_put.at[peer, slot],
            dst_ref=back_got.at[me, slot],
            send_sem=back_put_sem.at[peer, slot],
            recv_sem=back_got_sem.at[me, slot],
            device_id={"ctx": peer},
        )

    def back_keep(slot):
        return pltpu.make_async_copy(
            back_put.at[me, slot], back_got.at[me, slot], own_sems.at[2, slot, 1]
        )

    early = total_units // count > 2

    def outputs(slot):
        return (
            pltpu.make_async_copy(got_ref.at[:, slot], got_out.at[:, slot], out_sems.at[slot, 0]),
            pltpu.make_async_copy(wide_ref.at[slot], wide_out.at[slot], out_sems.at[slot, 1]),
            pltpu.make_async_copy(lse_ref.at[slot], lse_out.at[slot], out_sems.at[slot, 2]),
        )

    def unit_step(slot, carry):
        def wait_one(step, inner):
            arrival(lax.rem(me + step, count), slot).wait_recv()
            return inner

        lax.fori_loop(1, count, wait_one, 0)
        keep_copy(slot).wait()
        outputs(slot)[0].start()
        for i in range(count):
            rows = slice(i * lanes, (i + 1) * lanes)
            key_rows[rows, :] = got_ref[i, slot, HD : 2 * HD, :].T
            value_t[:, rows] = got_ref[i, slot, 2 * HD : 3 * HD, :]
        batch = batch_of(count, me, slot)
        key_documents(starts_ref, batch, key_docs)

        def block(number, inner):
            begin = pl.multiple_of(number * width, width)
            parts = [got_ref[number * group + i, slot, 0:HD, :] for i in range(group)]
            queries = parts[0] if group == 1 else jnp.concatenate(parts, axis=1)
            query_docs = query_documents(starts_ref, batch, begin, width)

            def chunk(index, running):
                peak, total, mixed = running
                first = pl.multiple_of(index * depth, depth)
                scores = jnp.dot(
                    key_rows[pl.ds(first, depth), :], queries, preferred_element_type=F32
                )
                same = same_document(key_docs, first, depth, query_docs)
                scores = jnp.where(same, scores, MASKED)
                new_peak = jnp.maximum(peak, jnp.max(scores, axis=0, keepdims=True))
                scaling = jnp.exp(peak - new_peak)
                weights = jnp.exp(scores - new_peak)
                return (
                    new_peak,
                    total * scaling + jnp.sum(weights, axis=0, keepdims=True),
                    mixed * scaling
                    + jnp.dot(
                        value_t[:, pl.ds(first, depth)],
                        weights.astype(BF16),
                        preferred_element_type=F32,
                    ),
                )

            peak, total, mixed = over_chunks(
                length // depth,
                chunk,
                (
                    jnp.full((1, width), -jnp.inf, F32),
                    jnp.zeros((1, width), F32),
                    jnp.zeros((HD, width), F32),
                ),
            )
            mixed = mixed / total
            wide_ref[slot, :, pl.ds(begin, width)] = mixed
            lse_ref[slot, :, pl.ds(begin, width)] = jnp.broadcast_to(
                peak + jnp.log(total), (8, width)
            )
            low = mixed.astype(BF16)
            for i in range(group):
                back_put[number * group + i, slot] = low[:, i * lanes : (i + 1) * lanes]
            return inner

        lax.fori_loop(0, length // width, block, 0)

        def send_one(step, inner):
            back_copy(lax.rem(me + step, count), slot).start()
            return inner

        lax.fori_loop(1, count, send_one, 0)
        back_keep(slot).start()
        start(outputs(slot)[1:])
        if early:

            @pl.when(slot == 0)
            def _():
                outer_way.relay(0)
                outer_way.relay(1)

            @pl.when(slot == 1)
            def _():
                outer_way.relay(2)

            @pl.when(slot == 2)
            def _():
                inner_way.relay(0)

        return carry

    lax.fori_loop(0, mine, unit_step, 0)

    if not early:
        outer_way.relay(0)
        outer_way.relay(1)
        outer_way.relay(2)
        inner_way.relay(0)
    outer_way.hand_on()

    def sent(unit, carry):
        @pl.when(owner_of(count, unit) != me)
        def _():
            send_copy(unit).wait_send()

        return carry

    lax.fori_loop(0, total_units, sent, 0)

    def returned(slot, carry):
        def one(step, inner):
            back_copy(lax.rem(me + step, count), slot).wait_send()
            return inner

        lax.fori_loop(1, count, one, 0)
        for copy in outputs(slot):
            copy.wait()
        return carry

    lax.fori_loop(0, mine, returned, 0)
    inner_way.hand_on()
    mixer_y.wait_recv()
    mixer_pass.start()
    broad.hand_on()

    def home(unit, carry):
        owner, slot = owner_of(count, unit), unit // count

        @pl.when(owner != me)
        def _():
            pltpu.make_async_remote_copy(
                src_ref=back_put.at[owner, slot],
                dst_ref=back_got.at[owner, slot],
                send_sem=back_put_sem.at[owner, slot],
                recv_sem=back_got_sem.at[owner, slot],
                device_id={"ctx": owner},
            ).wait_recv()

        @pl.when(owner == me)
        def _():
            back_keep(slot).wait()

        return carry

    lax.fori_loop(0, total_units, home, 0)
    att_stores = []
    for batch in range(MB):
        rows = slice(batch * lanes, (batch + 1) * lanes)
        for pair in range(pairs):
            tops = []
            for j in range(2):
                unit = (2 * pair + j) * MB + batch
                tops.append(back_got[owner_of(count, unit), unit // count])
            att_ref[rows, pair * 128 : (pair + 1) * 128] = jnp.concatenate(tops, axis=0).T
        att_stores.append(
            pltpu.make_async_copy(att_ref.at[rows, :], att_out.at[rows, :], row_sems.at[batch])
        )
        att_stores[-1].start()

    outer_way.end()
    inner_way.end()
    broad.arrive()
    narrow.end()
    broad.end()
    for i in range(8):
        vec_full[i : i + 1, :] = bias_of(i)
    vec_full[8:16, :] = jnp.zeros((8, D), F32)
    for k in range(4):
        inner_bias_full[:, k * D : (k + 1) * D] = vec_out[k, 8:9, :]
    mixer_y.wait_send()
    mixer_core.wait()
    mixer_pass.wait()
    every_pair(joint_y, "wait_send")
    every_pair(joint_core, "wait_send")
    every_pair(joint_pass, "wait_send")
    for copy in own_out:
        copy.wait()

    for copy in att_stores:
        copy.wait()
    for pair in range(pairs):
        joint_store(pair).wait()


def forward(count, starts, tokens, joint, mixer, inner, outer, vectors, number):
    units = -(-UNITS // count)
    lanes = tokens.shape[0] // MB
    length = count * lanes
    width = 2 * lanes
    part = joint.shape[0]
    pairs = H // 2
    vm = pl.BlockSpec(memory_space=pltpu.VMEM)
    hbm = pl.BlockSpec(memory_space=pl.ANY)
    dma = pltpu.SemaphoreType.DMA
    return pl.pallas_call(
        functools.partial(forward_kernel, width),
        out_shape=(
            jax.ShapeDtypeStruct(tokens.shape, BF16),
            jax.ShapeDtypeStruct((count, units, 3 * HD, lanes), BF16),
            jax.ShapeDtypeStruct((units, HD, length), F32),
            jax.ShapeDtypeStruct((units, 8, length), F32),
            jax.ShapeDtypeStruct((pairs, 4, part, 384), BF16),
            jax.ShapeDtypeStruct((BIAS_ROWS, D), F32),
            jax.ShapeDtypeStruct((1, FF), F32),
            jax.ShapeDtypeStruct((4, *mixer.shape), BF16),
            jax.ShapeDtypeStruct((4, *inner.shape), BF16),
            jax.ShapeDtypeStruct((4, *outer.shape), BF16),
        ),
        in_specs=[pl.BlockSpec(memory_space=pltpu.SMEM)] + [hbm] * 5 + [vm] * 9,
        out_specs=(hbm, hbm, hbm, hbm, hbm, vm, vm, hbm, hbm, hbm),
        scratch_shapes=[
            pltpu.VMEM(tokens.shape, BF16),
            pltpu.VMEM(tokens.shape, BF16),
            pltpu.VMEM((count, units, 3 * HD, lanes), BF16),
            pltpu.VMEM((units, HD, length), F32),
            pltpu.VMEM((units, 8, length), F32),
            pltpu.VMEM((pairs, 4, part, 384), BF16),
            pltpu.VMEM((BIAS_ROWS, D), F32),
            pltpu.VMEM((4, BIAS_ROWS, D), F32),
            pltpu.VMEM((pairs, 8, 384), F32),
            pltpu.VMEM((count, units, 3 * HD, lanes), BF16),
            pltpu.VMEM((count, units, HD, lanes), BF16),
            pltpu.VMEM((count, units, HD, lanes), BF16),
            pltpu.VMEM((length, HD), BF16),
            pltpu.VMEM((HD, length), BF16),
            pltpu.VMEM((length, lanes), jnp.int32),
            pltpu.VMEM(mixer.shape, BF16),
            pltpu.VMEM(inner.shape, BF16),
            pltpu.VMEM(outer.shape, BF16),
            dma((count, units)),
            dma((count, units)),
            dma((count, units)),
            dma((count, units)),
            dma((2, 3, pairs, 3)),
            dma((2, 4, 4)),
            dma((2, 2, 3, RELAY_PIECES)),
            dma((3, max(pairs, units, 4), 3)),
            dma((units, 3)),
            dma((MB + 1,)),
        ],
        compiler_params=pltpu.CompilerParams(
            collective_id=number, has_side_effects=True, vmem_limit_bytes=56 * 1024 * 1024
        ),
        name="forward",
    )(starts, tokens, joint, mixer, inner, outer, *vectors)


def first_rows(half, tile):
    return half if half <= tile else (half // tile + 1) // 2 * tile


class Place:
    def __init__(self, count):
        self.count = count
        self.depth = count // 2
        self.me, self.shard = lax.axis_index("ctx"), lax.axis_index("fsdp")
        self.y, self.core = self.shard // 2, lax.rem(self.shard, 2)
        self.z, self.x = self.me // 2, lax.rem(self.me, 2)
        self.other_core = {"fsdp": 2 * self.y + 1 - self.core}
        self.other_y = {"fsdp": 2 * (1 - self.y) + self.core}
        self.other_x = {"ctx": 2 * self.z + 1 - self.x}

        self.hi, self.lo = self.z // 2, lax.rem(self.z, 2)

    def along_z(self, step):
        return lax.rem(self.z + step, self.depth)

    def peer_z(self, step):
        return {"ctx": 2 * self.along_z(step) + self.x}


def start(copies):
    for copy in copies:
        copy.start()


def added(a, b):
    return (a.astype(F32) + b.astype(F32)).astype(a.dtype)


class Reduction:
    def __init__(self, place, j, grad, out, head, paired, buffers, sems, z_sems):
        got, y_one, x_one, x_two, y_two, z_got = buffers
        self.place, self.grad, self.out, self.head, self.buffers = place, grad, out, head, buffers
        half, lanes = grad.shape[4], grad.shape[5] // 2
        self.half, self.lanes, self.paired = half, lanes, paired
        p = place
        here, there = self.side(p.y), self.side(1 - p.y)

        def remote(src, dst, slot, peer):
            return pltpu.make_async_remote_copy(
                src_ref=src,
                dst_ref=dst,
                send_sem=sems.at[0, j, slot],
                recv_sem=sems.at[1, j, slot],
                device_id=peer,
            )

        def z_copy(z, target, step):
            return pltpu.make_async_remote_copy(
                src_ref=grad.at[z // 2, lax.rem(z, 2), p.x, p.core, :, here],
                dst_ref=z_got.at[target],
                send_sem=z_sems.at[0, j, step],
                recv_sem=z_sems.at[1, j, step],
                device_id={"ctx": 2 * z + p.x},
            )

        self.first = [remote(grad.at[:, :, :, 1 - p.core], got, 0, p.other_core)]
        self.second = [remote(grad.at[:, :, :, p.core, 0:head, there], y_one, 1, p.other_y)]
        self.third = [
            remote(grad.at[:, :, 1 - p.x, p.core, 0:head, here], x_two, 2, p.other_x)
        ]
        if head < half:
            self.second.append(
                remote(grad.at[:, :, 1 - p.x, p.core, head:half, :], x_one, 3, p.other_x)
            )
            self.third.append(
                remote(grad.at[:, :, p.x, p.core, head:half, there], y_two, 4, p.other_y)
            )
        if paired:
            near = {"ctx": 2 * (2 * p.hi + 1 - p.lo) + p.x}
            self.fourth = [
                remote(
                    grad.at[:, 1 - p.lo, p.x, p.core, :, here], z_got.at[pl.ds(0, 2)], 6, near
                )
            ]
            self.fifth = [z_copy(2 * (1 - p.hi) + p.lo, 2, 1)]
        else:
            self.fourth = []
            self.fifth = [z_copy(lax.rem(p.z + step, 4), p.z, step) for step in range(1, 4)]
        self.last = [remote(out.at[p.core], out.at[p.core], 5, p.other_core)]

    def side(self, y):
        return pl.ds(pl.multiple_of(y * self.lanes, 128), self.lanes)

    def each(self, body):
        def step(block, carry):
            body(block // 2, lax.rem(block, 2))
            return carry

        lax.fori_loop(0, 4, step, 0)

    def stage_zero(self):
        start(self.first)

    def stage_one(self):
        p, grad, got = self.place, self.grad, self.buffers[0]
        for copy in self.first:
            copy.wait_recv()

        def body(hi, lo):
            for x in range(2):
                grad[hi, lo, x, p.core] = added(grad[hi, lo, x, p.core], got[hi, lo, x])

        self.each(body)
        start(self.second)

    def stage_two(self):
        p, grad, head, half = self.place, self.grad, self.head, self.half
        y_one, x_one = self.buffers[1], self.buffers[2]
        here = self.side(p.y)
        for copy in self.second:
            copy.wait()

        def body(hi, lo):
            for x in range(2):
                grad[hi, lo, x, p.core, 0:head, here] = added(
                    grad[hi, lo, x, p.core, 0:head, here], y_one[hi, lo, x]
                )
            if head < half:
                grad[hi, lo, p.x, p.core, head:half, :] = added(
                    grad[hi, lo, p.x, p.core, head:half, :], x_one[hi, lo]
                )

        self.each(body)
        start(self.third)

    def stage_three(self):
        p, grad, head, half = self.place, self.grad, self.head, self.half
        x_two, y_two = self.buffers[3], self.buffers[4]
        here = self.side(p.y)
        for copy in self.third:
            copy.wait()

        def body(hi, lo):
            grad[hi, lo, p.x, p.core, 0:head, here] = added(
                grad[hi, lo, p.x, p.core, 0:head, here], x_two[hi, lo]
            )
            if head < half:
                grad[hi, lo, p.x, p.core, head:half, here] = added(
                    grad[hi, lo, p.x, p.core, head:half, here], y_two[hi, lo]
                )

        self.each(body)
        start(self.fourth if self.paired else self.fifth)

    def stage_four(self):
        p, grad, z_got = self.place, self.grad, self.buffers[5]
        here = self.side(p.y)
        for copy in self.fourth:
            copy.wait()
        for hi in range(2):
            grad[hi, p.lo, p.x, p.core, :, here] = added(
                grad[hi, p.lo, p.x, p.core, :, here], z_got[hi]
            )
        start(self.fifth)

    def stage_five(self):
        p, z_got = self.place, self.buffers[5]
        for copy in self.fifth:
            copy.wait()
        total = self.grad[p.hi, p.lo, p.x, p.core, :, self.side(p.y)].astype(F32)
        if self.paired:
            total = total + z_got[2].astype(F32)
        else:
            for step in range(1, 4):
                total = total + z_got[lax.rem(p.z + step, 4)].astype(F32)
        self.out[p.core] = total.astype(self.out.dtype)
        start(self.last)

    def stage_six(self):
        for copy in self.last:
            copy.wait()
        for copy in self.first:
            copy.wait_send()


def reduction_buffers(half, lanes, head, dtype):
    tail = max(half - head, 16)
    shapes = (
        (2, 2, 2, half, 2 * lanes),
        (2, 2, 2, head, lanes),
        (2, 2, tail, 2 * lanes),
        (2, 2, head, lanes),
        (2, 2, tail, lanes),
        (4, half, lanes),
        (2, half, lanes),
    )
    return [pltpu.VMEM(shape, dtype) for shape in shapes]


def backward_kernel(width, plan, *refs):
    (
        starts_ref,
        flow_in,
        got_in,
        wide_in,
        lse_in,
        tok_in,
        residual_in,
        bias_in,
        joint_in,
        d_outer_in,
        act_in,
        d_inner_in,
        first_in,
        d_branch_in,
        att_in,
        tokens_hbm,
        outer_hbm,
        inner_hbm,
        mixer_hbm,
        joint_out,
        bias_out,
        tokens_out,
        outer_out,
        inner_out,
        mixer_out,
        flow_ref,
        got_ref,
        wide_ref,
        lse_ref,
        tok_ref,
        residual_ref,
        bias_ref,
        d_outer_ref,
        act_ref,
        d_inner_ref,
        first_ref,
        d_branch_ref,
        att_ref,
        flow_put,
        flow_got,
        put,
        home_got,
        key_rows,
        value_rows,
        key_t,
        key_docs,
        d_key,
        d_value,
        joint_all,
        outer_one,
        outer_two,
        inner_one,
        inner_two,
        mixer_grad,
        joint_one,
        joint_two,
        d_turned,
        bias_sum,
        bias_got,
        flow_sems,
        home_sems,
        own_sems,
        sems,
        z_sems,
        bias_sems,
        in_sems,
        result_sems,
        *buffers,
    ) = refs
    count, units, _, lanes = got_ref.shape
    length = count * lanes
    depth = min(length, 1024)
    group = width // lanes
    pairs = H // 2
    total_units = MB * H
    p = Place(count)
    me = p.me
    mine = owned(count, me)

    sources = (
        (flow_in, flow_ref),
        (d_outer_in, d_outer_ref),
        (act_in, act_ref),
        (d_inner_in, d_inner_ref),
        (first_in, first_ref),
        (d_branch_in, d_branch_ref),
        (att_in, att_ref),
        (bias_in, bias_ref),
        (got_in, got_ref),
        (wide_in, wide_ref),
        (lse_in, lse_ref),
        (tok_in, tok_ref),
        (residual_in, residual_ref),
    )
    loads = [
        pltpu.make_async_copy(source, held, in_sems.at[k])
        for k, (source, held) in enumerate(sources)
    ]
    start(loads)

    def loaded(first, last):
        for copy in loads[first:last]:
            copy.wait()

    barrier = pltpu.get_barrier_semaphore()

    def greet(step, carry):
        pl.semaphore_signal(barrier, inc=1, device_id={"ctx": lax.rem(me + step, count)})
        return carry

    lax.fori_loop(1, count, greet, 0)
    pl.semaphore_signal(barrier, inc=1, device_id=p.other_core)
    pl.semaphore_signal(barrier, inc=1, device_id=p.other_y)
    pl.semaphore_signal(barrier, inc=1, device_id={**p.other_y, **p.other_x})
    joint_load = pltpu.make_async_copy(joint_in, joint_all, own_sems.at[2, 0])
    joint_load.start()

    grads = (outer_one, outer_two, inner_one, inner_two, mixer_grad, joint_one, joint_two)
    jobs = [
        Reduction(
            p,
            j,
            grads[j],
            buffers[7 * j + 6],
            plan[j][2],
            plan[j][3],
            buffers[7 * j : 7 * j + 6],
            sems,
            z_sems,
        )
        for j in range(len(grads))
    ]
    o_one, o_two, i_one, i_two, m_one, j_one, j_two = jobs

    def store_rows(targets, row, values, columns):
        half = sum(t.shape[4] for t in targets)
        done = 0
        while done < values.shape[0]:
            block, inside = (row + done) // half, (row + done) % half
            k = 0
            while inside >= targets[k].shape[4]:
                inside -= targets[k].shape[4]
                k += 1
            size = min(values.shape[0] - done, targets[k].shape[4] - inside)
            targets[k][
                block // 8,
                block // 4 % 2,
                block // 2 % 2,
                block % 2,
                inside : inside + size,
                columns,
            ] = values[done : done + size]
            done += size

    loaded(0, 3)
    d_outer_turned = d_outer_ref[...].T

    def outer_gradient(which):
        for side in range(2):
            begin = (2 * side + which) * D
            values = jnp.dot(
                d_outer_turned, act_ref[:, begin : begin + D], preferred_element_type=F32
            )
            columns = slice(side * D, (side + 1) * D)
            store_rows(((outer_one, outer_two)[which],), 0, values.astype(BF16), columns)

    def inner_gradient():
        for k in range(FF // D):
            turned = d_inner_ref[:, k * D : (k + 1) * D].T
            values = jnp.dot(turned, first_ref[...], preferred_element_type=F32)
            store_rows((inner_one, inner_two), k * D, values.astype(BF16), slice(0, D))

    def mixer_gradient():
        values = jnp.dot(d_branch_ref[...].T, att_ref[...], preferred_element_type=F32)
        store_rows((mixer_grad,), 0, values.astype(BF16), slice(0, D))

    def unit_copy(source, target, sem, owner, slot):
        return pltpu.make_async_remote_copy(
            src_ref=source.at[owner, slot],
            dst_ref=target.at[me, slot],
            send_sem=sem.at[0, owner, slot],
            recv_sem=sem.at[1, me, slot],
            device_id={"ctx": owner},
        )

    def unit_arrival(source, target, sem, sender, slot):
        return pltpu.make_async_remote_copy(
            src_ref=source.at[sender, slot],
            dst_ref=target.at[sender, slot],
            send_sem=sem.at[0, sender, slot],
            recv_sem=sem.at[1, sender, slot],
            device_id={"ctx": sender},
        )

    def unit_keep(source, target, kind, slot):
        return pltpu.make_async_copy(
            source.at[me, slot], target.at[me, slot], own_sems.at[kind, slot]
        )

    for pair in range(pairs):
        for batch in range(MB):
            block = flow_ref[
                batch * lanes : (batch + 1) * lanes, pair * 128 : (pair + 1) * 128
            ].T
            for j in range(2):
                unit = (2 * pair + j) * MB + batch
                flow_put[owner_of(count, unit), unit // count] = block[j * HD : (j + 1) * HD]

    outer_gradient(0)
    pl.semaphore_wait(barrier, count + 2)
    o_one.stage_zero()

    def send_flow(turn, carry):
        slot, owner = turn // count, lax.rem(me + turn, count)

        @pl.when((owner != me) & (slot < owned(count, owner)))
        def _():
            unit_copy(flow_put, flow_got, flow_sems, owner, slot).start()

        @pl.when((owner == me) & (slot < mine))
        def _():
            unit_keep(flow_put, flow_got, 0, slot).start()

        return carry

    lax.fori_loop(0, units * count, send_flow, 0)
    loaded(3, 8)
    bias_sum[0] = bias_ref[...]
    outer_gradient(1)
    o_two.stage_zero()
    o_one.stage_one()
    inner_gradient()
    i_one.stage_zero()
    i_two.stage_zero()
    mixer_gradient()
    m_one.stage_zero()

    loaded(8, len(loads))

    def unit_step(slot, carry):
        def wait_one(step, inner):
            unit_arrival(flow_put, flow_got, flow_sems, lax.rem(me + step, count), slot).wait_recv()
            return inner

        lax.fori_loop(1, count, wait_one, 0)
        unit_keep(flow_put, flow_got, 0, slot).wait()
        for i in range(count):
            rows = slice(i * lanes, (i + 1) * lanes)
            key_rows[rows, :] = got_ref[i, slot, HD : 2 * HD, :].T
            value_rows[rows, :] = got_ref[i, slot, 2 * HD : 3 * HD, :].T
            key_t[:, rows] = got_ref[i, slot, HD : 2 * HD, :]
        batch = batch_of(count, me, slot)
        key_documents(starts_ref, batch, key_docs)
        d_key[...] = jnp.zeros_like(d_key)
        d_value[...] = jnp.zeros_like(d_value)

        def block(number, inner):
            begin = pl.multiple_of(number * width, width)

            def beside(ref):
                parts = [ref[number * group + i, slot, 0:HD, :] for i in range(group)]
                return parts[0] if group == 1 else jnp.concatenate(parts, axis=1)

            queries, flow = beside(got_ref), beside(flow_got)
            query_rows, flow_rows = queries.T, flow.T
            query_docs = query_documents(starts_ref, batch, begin, width)
            log_total = lse_ref[slot, 0:1, pl.ds(begin, width)]
            spread = jnp.sum(
                flow.astype(F32) * wide_ref[slot, :, pl.ds(begin, width)], axis=0, keepdims=True
            )

            def chunk(index, d_query):
                first = pl.multiple_of(index * depth, depth)
                rows = pl.ds(first, depth)
                scores = jnp.dot(key_rows[rows, :], queries, preferred_element_type=F32)
                same = same_document(key_docs, first, depth, query_docs)
                probs = jnp.exp(jnp.where(same, scores, MASKED) - log_total)
                pressure = jnp.dot(value_rows[rows, :], flow, preferred_element_type=F32)
                d_scores = (probs * (pressure - spread)).astype(BF16)
                d_value[rows, :] += jnp.dot(
                    probs.astype(BF16), flow_rows, preferred_element_type=F32
                )
                d_key[rows, :] += jnp.dot(d_scores, query_rows, preferred_element_type=F32)
                return d_query + jnp.dot(key_t[:, rows], d_scores, preferred_element_type=F32)

            d_query = over_chunks(length // depth, chunk, jnp.zeros((HD, width), F32))
            low = (d_query * SCALE).astype(BF16)
            for i in range(group):
                put[number * group + i, slot, 0:HD, :] = low[:, i * lanes : (i + 1) * lanes]
            return inner

        lax.fori_loop(0, length // width, block, 0)
        for i in range(count):
            rows = slice(i * lanes, (i + 1) * lanes)
            put[i, slot, HD : 2 * HD, :] = d_key[rows, :].T.astype(BF16)
            put[i, slot, 2 * HD : 3 * HD, :] = d_value[rows, :].T.astype(BF16)

        def send_one(step, inner):
            unit_copy(put, home_got, home_sems, lax.rem(me + step, count), slot).start()
            return inner

        lax.fori_loop(1, count, send_one, 0)
        unit_keep(put, home_got, 1, slot).start()

        @pl.when(slot == 0)
        def _():
            o_two.stage_one()

        @pl.when(slot == 1)
        def _():
            i_one.stage_one()

        @pl.when(slot == 2)
        def _():
            o_one.stage_two()

        return carry

    lax.fori_loop(0, mine, unit_step, 0)
    o_two.stage_two()
    i_two.stage_one()
    o_one.stage_three()
    i_one.stage_two()
    m_one.stage_one()

    ones = jnp.ones((8, MB * lanes), BF16)
    for pair in range(pairs):
        columns = []
        for batch in range(MB):
            blocks = []
            for j in range(2):
                unit = (2 * pair + j) * MB + batch
                owner, slot = owner_of(count, unit), unit // count

                @pl.when(owner != me)
                def _():
                    unit_arrival(put, home_got, home_sems, owner, slot).wait_recv()

                @pl.when(owner == me)
                def _():
                    unit_keep(put, home_got, 1, slot).wait()

                blocks.append(home_got[owner, slot])
            rows = [b[third * HD : (third + 1) * HD] for third in range(3) for b in blocks]
            columns.append(jnp.concatenate(rows, axis=0))
        d_pair = jnp.concatenate(columns, axis=1)
        d_turned[pair] = d_pair.T
        grad = jnp.dot(d_pair, tok_ref[...], preferred_element_type=F32).astype(BF16)
        for third in range(3):
            store_rows(
                (joint_one, joint_two),
                third * D + pair * 128,
                grad[third * 128 : (third + 1) * 128],
                slice(0, D),
            )
        sums = lax.dot_general(
            ones, d_pair, (((1,), (1,)), ((), ())), preferred_element_type=F32
        )
        bias_sum[0, 0:1, pair * 128 : (pair + 1) * 128] = sums[0:1, 0:128]
        bias_sum[0, 1:2, pair * 128 : (pair + 1) * 128] = sums[0:1, 256:384]
        if pair == 2:
            o_two.stage_three()
            o_one.stage_four()
            i_two.stage_two()
            i_one.stage_three()

    m_one.stage_two()
    o_two.stage_four()

    plane = (p.other_y, p.other_x, {**p.other_y, **p.other_x})

    def bias_copy(level, number, slot, peer):
        return pltpu.make_async_remote_copy(
            src_ref=bias_sum.at[level],
            dst_ref=bias_got.at[slot],
            send_sem=bias_sems.at[0, number],
            recv_sem=bias_sems.at[1, number],
            device_id=peer,
        )

    bias_core = bias_copy(0, 0, 0, p.other_core)
    bias_plane = [bias_copy(1, 1 + i, 1 + i, peer) for i, peer in enumerate(plane)]
    bias_z = [
        bias_copy(2, 3 + step, 3 + step, {"ctx": 2 * lax.rem(p.z + step, 4) + p.x})
        for step in range(1, 4)
    ]
    bias_core.start()
    j_one.stage_zero()
    j_two.stage_zero()

    joint_load.wait()

    def token_terms(first, last, total):
        for pair in range(first, last):
            total = total + lax.dot_general(
                d_turned[pair],
                joint_all[pair],
                (((1,), (1,)), ((), ())),
                preferred_element_type=F32,
            )
        tokens_out[...] = total

    token_terms(0, pairs // 2, residual_ref[...])
    bias_core.wait()
    bias_sum[1] = bias_sum[0] + bias_got[0]
    start(bias_plane)
    j_one.stage_one()
    j_two.stage_one()
    i_two.stage_three()
    i_one.stage_four()
    token_terms(pairs // 2, pairs, tokens_out[...])
    results = [
        pltpu.make_async_copy(held, out, result_sems.at[k])
        for k, (held, out) in enumerate(
            (
                (tokens_out, tokens_hbm),
                (outer_out, outer_hbm),
                (inner_out, inner_hbm),
                (mixer_out, mixer_hbm),
            )
        )
    ]
    results[0].start()
    m_one.stage_three()
    for copy in bias_plane:
        copy.wait()
    bias_sum[2] = bias_sum[1] + bias_got[1] + bias_got[2] + bias_got[3]
    start(bias_z)
    j_one.stage_two()
    i_two.stage_four()
    j_two.stage_two()
    m_one.stage_four()
    j_one.stage_three()
    j_two.stage_three()
    o_one.stage_five()
    o_two.stage_five()
    i_one.stage_five()

    def parts_of(j):
        jobs[j].stage_six()
        whole = buffers[7 * j + 6]
        return [whole[low].astype(F32) for low in range(2)]

    def own_lanes(rows):
        width_own = rows.shape[1] // 2
        return jnp.where(p.core == 0, rows[:, :width_own], rows[:, width_own:])

    def put_out(out, pieces):
        out[...] = jnp.concatenate(pieces, axis=0).T

    one, two = parts_of(0), parts_of(1)
    outer_out[...] = jnp.concatenate(
        [jnp.where(p.core == 0, a, b) for a, b in zip(one, two)], axis=0
    )
    results[1].start()
    i_two.stage_five()
    m_one.stage_five()
    one, two = parts_of(2), parts_of(3)
    put_out(inner_out, [own_lanes(r) for r in (one[0], two[0], one[1], two[1])])
    results[2].start()
    put_out(mixer_out, [own_lanes(r) for r in parts_of(4)])
    results[3].start()
    for copy in bias_z:
        copy.wait()
    bias_total = bias_sum[2] + bias_got[4] + bias_got[5] + bias_got[6]
    index = me * 4 + p.shard
    world = 4 * count
    lane = lax.broadcasted_iota(jnp.int32, (D, 128), 0)
    place = lax.broadcasted_iota(jnp.int32, (D, 128), 1)

    def picked(rows, first):
        ones_there = jnp.where(lane == place + first, 1.0, 0.0)
        return jnp.dot(
            rows, ones_there, precision=lax.Precision.HIGHEST, preferred_element_type=F32
        )

    own_hidden = FF // world
    in_row = D // own_hidden
    row = lax.broadcasted_iota(jnp.int32, (8, D), 0)
    hidden = jnp.where(row == index // in_row, bias_total[8:16], 0.0)
    hidden = jnp.broadcast_to(jnp.sum(hidden, axis=0, keepdims=True), (8, D))
    bias_out[0:8, :] = picked(bias_total[0:8], index * (D // world))
    bias_out[8:16, :] = picked(hidden, lax.rem(index, in_row) * own_hidden)

    def sent(unit, carry):
        owner, slot = owner_of(count, unit), unit // count

        @pl.when(owner != me)
        def _():
            unit_copy(flow_put, flow_got, flow_sems, owner, slot).wait_send()

        return carry

    lax.fori_loop(0, total_units, sent, 0)

    def returned(slot, carry):
        def one(step, inner):
            unit_copy(put, home_got, home_sems, lax.rem(me + step, count), slot).wait_send()
            return inner

        lax.fori_loop(1, count, one, 0)
        return carry

    lax.fori_loop(0, mine, returned, 0)
    j_one.stage_five()
    j_two.stage_five()
    one, two = parts_of(5), parts_of(6)
    put_out(joint_out, [own_lanes(r) for r in (one[0], two[0], one[1], two[1])])
    for copy in results:
        copy.wait()


def backward(
    starts, flow, got, wide, lse, source, residual, biases, joint, activations, number
):
    count, units, _, lanes = got.shape
    length = count * lanes
    width = 2 * lanes
    pairs = H // 2
    vm = pl.BlockSpec(memory_space=pltpu.VMEM)
    hbm = pl.BlockSpec(memory_space=pl.ANY)
    dma = pltpu.SemaphoreType.DMA
    small = D // (2 * count)
    half_joint = 3 * D // (2 * count)
    early = first_rows(half_joint, 16)
    plan = (
        (small, FF // 2, small, True),
        (small, FF // 2, small, True),
        (2 * small, D, 2 * small - 16, True),
        (2 * small, D, 2 * small - 16, True),
        (small, D, small, True),
        (early, D, first_rows(early, 16), False),
        (half_joint - early, D, first_rows(half_joint - early, 16), False),
    )
    buffers = []
    for half, full, head, _ in plan:
        buffers += reduction_buffers(half, full // 2, head, BF16)
    outs = [
        jax.ShapeDtypeStruct((2 * small, FF // 4), F32),
        jax.ShapeDtypeStruct((D // 4, FF // count), F32),
        jax.ShapeDtypeStruct((D // 4, 2 * small), F32),
        jax.ShapeDtypeStruct((D // 4, 2 * half_joint), F32),
    ]
    return pl.pallas_call(
        functools.partial(backward_kernel, width, plan),
        out_shape=(
            jax.ShapeDtypeStruct(residual.shape, F32),
            *outs,
            jax.ShapeDtypeStruct((BIAS_ROWS, 128), F32),
        ),
        in_specs=[pl.BlockSpec(memory_space=pltpu.SMEM)] + [hbm] * 14,
        out_specs=(hbm,) * 4 + (vm,) * 2,
        scratch_shapes=[
            pltpu.VMEM(residual.shape, F32),
            *[pltpu.VMEM(o.shape, F32) for o in outs[:3]],
            *[
                pltpu.VMEM(a.shape, a.dtype)
                for a in (flow, got, wide, lse, source, residual, biases, *activations)
            ],
            pltpu.VMEM((count, units, HD, lanes), BF16),
            pltpu.VMEM((count, units, HD, lanes), BF16),
            pltpu.VMEM((count, units, 3 * HD, lanes), BF16),
            pltpu.VMEM((count, units, 3 * HD, lanes), BF16),
            pltpu.VMEM((length, HD), BF16),
            pltpu.VMEM((length, HD), BF16),
            pltpu.VMEM((HD, length), BF16),
            pltpu.VMEM((length, lanes), jnp.int32),
            pltpu.VMEM((length, HD), F32),
            pltpu.VMEM((length, HD), F32),
            pltpu.VMEM((pairs, D, 384), BF16),
            *[pltpu.VMEM((2, 2, 2, 2, half, full), BF16) for half, full, _, _ in plan],
            pltpu.VMEM((pairs, MB * lanes, 384), BF16),
            pltpu.VMEM((3, BIAS_ROWS, D), F32),
            pltpu.VMEM((7, BIAS_ROWS, D), F32),
            dma((2, count, units)),
            dma((2, count, units)),
            dma((3, units)),
            dma((2, len(plan), 7)),
            dma((2, len(plan), 4)),
            dma((2, 7)),
            dma((13,)),
            dma((4,)),
            *buffers,
        ],
        compiler_params=pltpu.CompilerParams(
            collective_id=number, has_side_effects=True, vmem_limit_bytes=67043328
        ),
        name="backward",
    )(starts, flow, got, wide, lse, source, residual, biases, joint, *activations)


def settle_kernel(count, *refs):
    sources, outs, held = refs[:count], refs[count : 2 * count], refs[2 * count : 3 * count]
    sems = refs[3 * count]
    copies_in = [
        pltpu.make_async_copy(sources[i], held[i], sems.at[0, i]) for i in range(count)
    ]
    copies_out = [pltpu.make_async_copy(held[i], outs[i], sems.at[1, i]) for i in range(count)]
    start(copies_in)
    for first, second in zip(copies_in, copies_out):
        first.wait()
        second.start()
    for copy in copies_out:
        copy.wait()


def settle(*arrays):
    count = len(arrays)
    return pl.pallas_call(
        functools.partial(settle_kernel, count),
        out_shape=[jax.ShapeDtypeStruct(a.shape, a.dtype) for a in arrays],
        in_specs=[pl.BlockSpec(memory_space=pl.ANY)] * count,
        out_specs=[pl.BlockSpec(memory_space=pl.ANY)] * count,
        scratch_shapes=[
            *[pltpu.VMEM(a.shape, a.dtype) for a in arrays],
            pltpu.SemaphoreType.DMA((2, count)),
        ],
        name="settle",
    )(*arrays)


def on_device(
    count,
    shards,
    tokens,
    doc_starts,
    joint_weight,
    mixer_weight,
    inner_weight,
    outer_weight,
    query_bias,
    value_bias,
    mixer_bias,
    first_gain,
    first_shift,
    inner_bias,
    outer_bias,
    second_gain,
    second_shift,
    upstream,
):
    rows = tokens.shape[2]
    length = rows * count
    units = -(-MB * H // count)
    me = lax.axis_index("ctx")

    part = D // shards
    vectors = [
        query_bias,
        value_bias,
        mixer_bias,
        first_gain,
        first_shift,
        outer_bias,
        second_gain,
        second_shift,
        inner_bias,
    ]
    source = tokens.reshape(MB * rows, D)
    attended, received, wide, lse, joint, vectors, ibias, mixer, inner, outer = forward(
        count,
        doc_starts,
        source,
        joint_weight,
        mixer_weight,
        inner_weight,
        outer_weight,
        vectors,
        0,
    )
    joint = joint.reshape(H // 2, D, 384)
    mixer, inner, outer = mixer.reshape(D, D), inner.reshape(D, FF), outer.reshape(FF, D)
    _, _, mbias, gain_one, shift_one, obias, gain_two, shift_two = [
        vectors[i : i + 1] for i in range(8)
    ]

    branch = mul_nn(attended, mixer) + mbias
    first, first_normed, first_recip = norm_forward(
        source.astype(F32) + branch, gain_one, shift_one
    )
    first_low = first.astype(BF16)
    inner_pre = mul_nn(first_low, inner) + ibias
    activated, gelu_slope = gelu_parts(inner_pre)
    activated_low = activated.astype(BF16)
    outer_out = mul_nn(activated_low, outer) + obias
    final, second_normed, second_recip = norm_forward(first + outer_out, gain_two, shift_two)
    result = final.astype(BF16).reshape(MB, 1, rows, D)

    incoming = upstream.reshape(MB * rows, D).astype(F32)
    rescale_grad = jnp.sum(incoming * second_normed, axis=0)
    reshift_grad = jnp.sum(incoming, axis=0)
    d_second = norm_backward(incoming, second_normed, second_recip, gain_two)
    d_outer = d_second.astype(BF16)
    return_grad = jnp.sum(d_outer.astype(F32), axis=0)
    d_inner = (mul_nt(d_outer, outer) * gelu_slope).astype(BF16)
    hidden_grad = jnp.sum(d_inner.astype(F32), axis=0)
    d_first = d_second + mul_nt(d_inner, inner)
    scale_grad = jnp.sum(d_first * first_normed, axis=0)
    shift_grad = jnp.sum(d_first, axis=0)
    d_residual = norm_backward(d_first, first_normed, first_recip, gain_one)
    d_branch = d_residual.astype(BF16)
    mixing_grad = jnp.sum(d_branch.astype(F32), axis=0)
    world = count * shards
    index = me * shards + lax.axis_index("fsdp")
    sums = [
        mixing_grad,
        scale_grad,
        shift_grad,
        return_grad,
        rescale_grad,
        reshift_grad,
        *hidden_grad.reshape(FF // D, D),
    ]
    if shards == 4 and count == 8:
        flow = mul_nt(d_branch, mixer).astype(BF16)
        biases = jnp.pad(jnp.stack(sums), ((2, BIAS_ROWS - 2 - len(sums)), (0, 0)))
        tokens_grad, *blocks, biases = backward(
            doc_starts,
            flow,
            received,
            wide,
            lse,
            source,
            d_residual,
            biases,
            joint,
            [d_outer, activated_low, d_inner, first_low, d_branch, attended],
            1,
        )
        *blocks, tokens_grad = settle(*blocks, tokens_grad)
        blocks[0] = blocks[0].T
        own, own_hidden = biases[:8, : D // world], biases[8, : FF // world]
    else:
        natural = joint.reshape(H // 2, D, 3, 128).transpose(1, 2, 0, 3).reshape(D, 3 * D)
        flow = mul_nt(mixer, d_branch).astype(BF16)
        flow_units = exchange(to_units(flow, 1, count, units), 2)
        d_units = attend_back(received, flow_units, doc_starts, wide, lse[:, :1])
        d_joint = from_units(exchange(d_units, 3), 3)
        bias_sums = jnp.sum(d_joint.astype(F32), axis=1)
        turned = [
            mul_tn(d_outer, activated_low),
            mul_tn(d_inner, first_low),
            mul_tn(d_branch, attended),
            mul_nn(d_joint, source),
        ]
        tokens_grad = d_residual + mul_tt(d_joint, natural)

        def reduced(grad):
            over_lanes = lax.psum_scatter(
                grad.astype(BF16), "fsdp", scatter_dimension=1, tiled=True
            )
            over_rows = lax.psum_scatter(over_lanes, "ctx", scatter_dimension=0, tiled=True)
            return over_rows.T.astype(F32)

        blocks = [reduced(g) for g in turned]
        biases = jnp.stack([bias_sums[:D], bias_sums[2 * D :], *sums])
        biases = lax.psum(biases, ("ctx", "fsdp"))
        own = lax.dynamic_slice_in_dim(biases[:8], index * (D // world), D // world, 1)
        hidden_rows = biases[8 : 8 + FF // D].reshape(FF)
        own_hidden = lax.dynamic_slice_in_dim(hidden_rows, index * (FF // world), FF // world, 0)
    tokens_grad = tokens_grad.reshape(MB, 1, rows, D)
    outer_out_grad, inner_out, mixer_out, joint_out = blocks
    sums = [*own[:5], own_hidden, *own[5:]]
    return (result, tokens_grad, joint_out, mixer_out, inner_out, outer_out_grad, *sums)


def solution(mesh):
    in_specs = (
        P(None, "fsdp", "ctx", None),
        P(None, "fsdp", None),
        P("fsdp", None),
        P("fsdp", None),
        P("fsdp", None),
        P("fsdp", None),
        P("fsdp"),
        P("fsdp"),
        P("fsdp"),
        P("fsdp"),
        P("fsdp"),
        P("fsdp"),
        P("fsdp"),
        P("fsdp"),
        P("fsdp"),
        P(None, "fsdp", "ctx", None),
    )
    out_specs = (
        P(None, "fsdp", "ctx", None),
        P(None, "fsdp", "ctx", None),
        P("fsdp", "ctx"),
        P("fsdp", "ctx"),
        P("fsdp", "ctx"),
        P("fsdp", "ctx"),
        P(("ctx", "fsdp")),
        P(("ctx", "fsdp")),
        P(("ctx", "fsdp")),
        P(("ctx", "fsdp")),
        P(("ctx", "fsdp")),
        P(("ctx", "fsdp")),
        P(("ctx", "fsdp")),
        P(("ctx", "fsdp")),
        P(("ctx", "fsdp")),
    )
    return jax.shard_map(
        functools.partial(on_device, mesh.shape["ctx"], mesh.shape["fsdp"]),
        mesh=mesh,
        in_specs=in_specs,
        out_specs=out_specs,
        check_vma=False,
    )
```

```python
import functools
import math

import jax
import jax.numpy as jnp
from jax import lax
from jax.experimental import pallas as pl
from jax.experimental.pallas import tpu as pltpu
from jax.sharding import PartitionSpec as P

D = 768
H = 12
HD = 64
FF = 3072
MB = 3

SCALE = 0.125
EPSILON = 1e-12
MASKED = -1000000000.0
ROOT_HALF = 0.7071067811865476
GAUSS_PEAK = 0.3989422804014327

F32 = jnp.float32
BF16 = jnp.bfloat16


def norm_forward(hidden, gain, shift):
    average = jnp.mean(hidden, axis=-1, keepdims=True)
    centred = hidden - average
    reciprocal = lax.rsqrt(jnp.mean(centred * centred, axis=-1, keepdims=True) + EPSILON)
    normed = centred * reciprocal
    return (normed * gain + shift, normed, reciprocal)


def norm_backward(incoming, normed, reciprocal, gain):
    scaled = incoming * gain
    return reciprocal * (
        scaled
        - jnp.mean(scaled, axis=-1, keepdims=True)
        - normed * jnp.mean(scaled * normed, axis=-1, keepdims=True)
    )


def gelu_parts(inner):
    cumulative = 0.5 * (1.0 + lax.erf(inner * ROOT_HALF))
    return (inner * cumulative, cumulative + inner * jnp.exp(-0.5 * inner * inner) * GAUSS_PEAK)


UNITS = MB * H
BIAS_ROWS = 16
RELAY_PIECES = 3


def spare_owner(count, j):
    stride = count // (UNITS % count)
    return j * stride + (j % 2 if stride > 1 else 0)


def owner_of(count, unit):
    full, rest = UNITS // count, UNITS % count
    if rest == 0:
        return unit % count
    if full == 0:
        return spare_owner(count, unit)
    late = unit // (full * count)
    return (1 - late) * (unit % count) + late * spare_owner(count, unit - full * count)


def spare_index(count, device):
    return device // (count // (UNITS % count))


def owned(count, device):
    full, rest = UNITS // count, UNITS % count
    if rest == 0:
        return full
    j = spare_index(count, device)
    extra = (spare_owner(count, j) == device) & (j < rest)
    return full + extra.astype(jnp.int32)


def batch_of(count, device, slot):
    full, rest = UNITS // count, UNITS % count
    if rest == 0:
        return (slot * count + device) % MB
    if full == 0:
        return jnp.minimum(spare_index(count, device), UNITS - 1) % MB
    late = slot // full
    unit = slot * count + (1 - late) * device + late * spare_index(count, device)
    return unit % MB


def exchange_kernel(count, x_ref, y_ref, held, send_sem, recv_sem, own_sem):
    me = lax.axis_index("ctx")
    barrier = pltpu.get_barrier_semaphore()

    def greet(step, carry):
        peer = lax.rem(me + step, count)
        pl.semaphore_signal(barrier, inc=1, device_id={"ctx": peer})
        return carry

    lax.fori_loop(1, count, greet, 0)
    own_in = pltpu.make_async_copy(x_ref.at[me], held, own_sem)
    own_in.start()
    pl.semaphore_wait(barrier, count - 1)

    def transfer(step):
        peer = lax.rem(me + step, count)
        return pltpu.make_async_remote_copy(
            src_ref=x_ref.at[peer],
            dst_ref=y_ref.at[me],
            send_sem=send_sem.at[step],
            recv_sem=recv_sem.at[step],
            device_id={"ctx": peer},
        )

    def begin(step, carry):
        transfer(step).start()
        return carry

    lax.fori_loop(1, count, begin, 0)
    own_in.wait()
    own_out = pltpu.make_async_copy(held, y_ref.at[me], own_sem)
    own_out.start()
    own_out.wait()

    def finish(step, carry):
        transfer(step).wait()
        return carry

    lax.fori_loop(1, count, finish, 0)


def exchange(x, number):
    count = x.shape[0]
    return pl.pallas_call(
        functools.partial(exchange_kernel, count),
        out_shape=jax.ShapeDtypeStruct(x.shape, x.dtype),
        in_specs=[pl.BlockSpec(memory_space=pl.ANY)],
        out_specs=pl.BlockSpec(memory_space=pl.ANY),
        scratch_shapes=[
            pltpu.VMEM(x.shape[1:], x.dtype),
            pltpu.SemaphoreType.DMA((count,)),
            pltpu.SemaphoreType.DMA((count,)),
            pltpu.SemaphoreType.DMA,
        ],
        compiler_params=pltpu.CompilerParams(collective_id=number, has_side_effects=True),
        name=f"exchange_{number}",
    )(x)


def across(ref, first, rows, width, lanes):
    parts = [ref[first + i, 0, rows, :] for i in range(width // lanes)]
    return parts[0] if len(parts) == 1 else jnp.concatenate(parts, axis=1)


def document(starts_ref, batch, position):
    docs = jnp.zeros(position.shape, jnp.int32) - 1
    for j in range(starts_ref.shape[2]):
        docs = docs + jnp.where(position >= starts_ref[batch, 0, j], 1, 0)
    return docs


def key_documents(starts_ref, batch, key_docs):
    key_docs[...] = document(
        starts_ref, batch, lax.broadcasted_iota(jnp.int32, key_docs.shape, 0)
    )


def query_documents(starts_ref, batch, begin, width):
    return document(
        starts_ref, batch, lax.broadcasted_iota(jnp.int32, (1, width), 1) + begin
    )


def same_document(key_docs, first, width, query_docs):
    keys = key_docs[pl.ds(first, width), :]
    lanes = keys.shape[1]
    parts = [keys == query_docs[:, i : i + lanes] for i in range(0, query_docs.shape[1], lanes)]
    return parts[0] if len(parts) == 1 else jnp.concatenate(parts, axis=1)


def over_chunks(chunks, body, carry):
    if chunks == 1:
        return body(0, carry)
    return lax.fori_loop(0, chunks, body, carry)


def attend_back_kernel(
    width,
    starts_ref,
    x_ref,
    flow_ref,
    wide_ref,
    lse_ref,
    d_ref,
    key_rows,
    value_rows,
    key_t,
    key_docs,
    d_key,
    d_value,
):
    count, _, _, lanes = x_ref.shape
    length = count * lanes
    depth = min(length, 1024)
    unit = pl.program_id(0)
    for i in range(count):
        rows = slice(i * lanes, (i + 1) * lanes)
        key_rows[rows, :] = x_ref[i, 0, HD : 2 * HD, :].T
        value_rows[rows, :] = x_ref[i, 0, 2 * HD : 3 * HD, :].T
        key_t[:, rows] = x_ref[i, 0, HD : 2 * HD, :]
    batch = batch_of(count, lax.axis_index("ctx"), unit)
    key_documents(starts_ref, batch, key_docs)
    d_key[...] = jnp.zeros_like(d_key)
    d_value[...] = jnp.zeros_like(d_value)
    group = width // lanes

    def block(number, carry):
        begin = pl.multiple_of(number * width, width)
        queries = across(x_ref, number * group, slice(0, HD), width, lanes)
        flow = across(flow_ref, number * group, slice(0, HD), width, lanes)
        query_rows = queries.T
        flow_rows = flow.T
        query_docs = query_documents(starts_ref, batch, begin, width)
        log_total = lse_ref[0, :, pl.ds(begin, width)]
        spread = jnp.sum(
            flow.astype(F32) * wide_ref[0, :, pl.ds(begin, width)], axis=0, keepdims=True
        )

        def chunk(index, d_query):
            first = pl.multiple_of(index * depth, depth)
            rows = pl.ds(first, depth)
            scores = jnp.dot(key_rows[rows, :], queries, preferred_element_type=F32)
            same = same_document(key_docs, first, depth, query_docs)
            probs = jnp.exp(jnp.where(same, scores, MASKED) - log_total)
            pressure = jnp.dot(value_rows[rows, :], flow, preferred_element_type=F32)
            d_scores = (probs * (pressure - spread)).astype(BF16)
            d_value[rows, :] += jnp.dot(
                probs.astype(BF16), flow_rows, preferred_element_type=F32
            )
            d_key[rows, :] += jnp.dot(d_scores, query_rows, preferred_element_type=F32)
            return d_query + jnp.dot(key_t[:, rows], d_scores, preferred_element_type=F32)

        d_query = over_chunks(length // depth, chunk, jnp.zeros((HD, width), F32))
        low = (d_query * SCALE).astype(BF16)
        for i in range(group):
            d_ref[number * group + i, 0, 0:HD, :] = low[:, i * lanes : (i + 1) * lanes]
        return carry

    lax.fori_loop(0, length // width, block, 0)
    for i in range(count):
        rows = slice(i * lanes, (i + 1) * lanes)
        d_ref[i, 0, HD : 2 * HD, :] = d_key[rows, :].T.astype(BF16)
        d_ref[i, 0, 2 * HD : 3 * HD, :] = d_value[rows, :].T.astype(BF16)


def unit_block(*dims):
    return pl.BlockSpec(dims, lambda u, starts: (0, u) + (0,) * (len(dims) - 2))


def own_block(*dims):
    return pl.BlockSpec(dims, lambda u, starts: (u,) + (0,) * (len(dims) - 1))


def attend_back(x, flow, starts, wide, lse):
    count, units, _, lanes = x.shape
    length = count * lanes
    width = 2 * lanes if count % 2 == 0 else lanes
    return pl.pallas_call(
        functools.partial(attend_back_kernel, width),
        out_shape=jax.ShapeDtypeStruct(x.shape, BF16),
        grid_spec=pltpu.PrefetchScalarGridSpec(
            num_scalar_prefetch=1,
            grid=(units,),
            in_specs=[
                unit_block(count, 1, 3 * HD, lanes),
                unit_block(count, 1, HD, lanes),
                own_block(1, HD, length),
                own_block(1, 1, length),
            ],
            out_specs=unit_block(count, 1, 3 * HD, lanes),
            scratch_shapes=[
                pltpu.VMEM((length, HD), BF16),
                pltpu.VMEM((length, HD), BF16),
                pltpu.VMEM((HD, length), BF16),
                pltpu.VMEM((length, lanes), jnp.int32),
                pltpu.VMEM((length, HD), F32),
                pltpu.VMEM((length, HD), F32),
            ],
        ),
        compiler_params=pltpu.CompilerParams(dimension_semantics=("arbitrary",)),
        name="attend_back",
    )(starts, x, flow, wide, lse)


def to_units(columns, parts, count, units):
    rows = columns.shape[1] // MB
    x = columns.reshape(parts, H, HD, MB, rows).transpose(1, 3, 0, 2, 4)
    x = x.reshape(UNITS, parts * HD, rows)
    places = [owner_of(count, u) * units + u // count for u in range(UNITS)]
    y = jnp.zeros((count * units, parts * HD, rows), columns.dtype)
    return y.at[jnp.array(places)].set(x).reshape(count, units, parts * HD, rows)


def from_units(x, parts):
    count, units, _, rows = x.shape
    places = [owner_of(count, u) * units + u // count for u in range(UNITS)]
    x = x.reshape(count * units, parts * HD, rows)[jnp.array(places)]
    x = x.reshape(H, MB, parts, HD, rows).transpose(2, 0, 3, 1, 4)
    return x.reshape(parts * D, MB * rows)


def mul_nn(a, b):
    return jnp.dot(a, b, preferred_element_type=F32)


def mul_tn(a, b):
    return lax.dot_general(a, b, (((0,), (0,)), ((), ())), preferred_element_type=F32)


def mul_nt(a, b):
    return lax.dot_general(a, b, (((1,), (1,)), ((), ())), preferred_element_type=F32)


def mul_tt(a, b):
    return lax.dot_general(a, b, (((0,), (1,)), ((), ())), preferred_element_type=F32)


def forward_kernel(
    width,
    starts_ref,
    tok_in,
    joint_ref,
    mixer_ref,
    inner_ref,
    outer_ref,
    *refs,
):
    vec_refs = refs[:9]
    (
    att_out,
    got_out,
    wide_out,
    lse_out,
    joint_out,
    vec_full,
    inner_bias_full,
    mixer_out,
    inner_out,
    outer_out,
    tok_ref,
    att_ref,
    got_ref,
    wide_ref,
    lse_ref,
    joint_all,
    vec_put,
    vec_out,
    bias_rows,
    put,
    back_put,
    back_got,
    key_rows,
    value_t,
    key_docs,
    mixer_own,
    inner_own,
    outer_own,
    put_sem,
    got_sem,
    back_put_sem,
    back_got_sem,
    joint_sems,
    weight_sems,
    relay_sems,
    own_sems,
    out_sems,
    row_sems,
    ) = refs[9:]
    count, units, _, lanes = got_ref.shape
    length = count * lanes
    depth = min(length, 1024)
    group = width // lanes
    pairs = H // 2
    total_units = MB * H
    part = joint_ref.shape[0]
    me, shard = lax.axis_index("ctx"), lax.axis_index("fsdp")
    y, core = shard // 2, lax.rem(shard, 2)
    x = lax.rem(me, 2)
    far = 2 * (1 - y) + core
    other_core = {"fsdp": 2 * y + 1 - core}
    other_y = {"fsdp": far}
    other_x = {"ctx": me + 1 - 2 * x}
    mine = owned(count, me)

    barrier = pltpu.get_barrier_semaphore()

    def greet(step, carry):
        pl.semaphore_signal(barrier, inc=1, device_id={"ctx": lax.rem(me + step, count)})
        return carry

    lax.fori_loop(1, count, greet, 0)
    pl.semaphore_signal(barrier, inc=1, device_id=other_core)
    pl.semaphore_signal(barrier, inc=1, device_id=other_y)

    def remote(src, dst, sems, index, peer):
        return pltpu.make_async_remote_copy(
            src_ref=src,
            dst_ref=dst,
            send_sem=sems.at[(0, *index)],
            recv_sem=sems.at[(1, *index)],
            device_id=peer,
        )

    def own_joint(pair, third):
        columns = pl.ds(pl.multiple_of(third * D + pair * 128, 128), 128)
        return pltpu.make_async_copy(
            joint_ref.at[:, columns],
            joint_all.at[pair, shard, :, pl.ds(third * 128, 128)],
            own_sems.at[0, pair, third],
        )

    def joint_copy(kind, pair, third, which, peer, source=None):
        here = joint_all.at[pair, which, :, pl.ds(third * 128, 128)]
        if source is None:
            source = here
        else:
            source = source.at[:, pl.ds(pl.multiple_of(third * D + pair * 128, 128), 128)]
        return remote(source, here, joint_sems, (kind, pair, third), peer)

    def joint_y(pair, third):
        return joint_copy(0, pair, third, shard, other_y, joint_ref)

    def joint_core(pair, third):
        return joint_copy(1, pair, third, shard, other_core, joint_ref)

    def joint_pass(pair, third):
        return joint_copy(2, pair, third, far, other_core)

    def joint_store(pair):
        return pltpu.make_async_copy(
            joint_all.at[pair], joint_out.at[pair], own_sems.at[0, pair, 0]
        )

    def each_third(pair, make, act):
        for third in range(3):
            getattr(make(pair, third), act)()

    def every_pair(make, act):
        def body(pair, carry):
            each_third(pair, make, act)
            return carry

        lax.fori_loop(0, pairs, body, 0)

    tok_load = pltpu.make_async_copy(tok_in, tok_ref, row_sems.at[MB])
    tok_load.start()
    every_pair(own_joint, "start")
    wholes = ((mixer_ref, mixer_own, mixer_out), (inner_ref, inner_own, inner_out), (outer_ref, outer_own, outer_out))
    own_in = [
        pltpu.make_async_copy(ref, held, own_sems.at[1, i, 0])
        for i, (ref, held, _) in enumerate(wholes)
    ]
    own_out = [
        pltpu.make_async_copy(held, out.at[shard], own_sems.at[1, i, 1])
        for i, (_, held, out) in enumerate(wholes)
    ]
    for copy in own_in:
        copy.start()
    for i, ref in enumerate(vec_refs):
        vec_put[i : i + 1, 0 : ref.shape[0]] = ref[...].astype(F32).reshape(1, ref.shape[0])
    vec_out[shard] = vec_put[...]
    pl.semaphore_wait(barrier, count + 1)

    class Vectors:
        def __init__(self, rows, columns, keys):
            mine, theirs = vec_out.at[shard, rows, columns], vec_out.at[far, rows, columns]
            source = vec_put.at[rows, columns]
            self.over_y = remote(source, mine, weight_sems, keys[0], other_y)
            self.core = remote(source, mine, weight_sems, keys[1], other_core)
            self.all = remote(theirs, theirs, weight_sems, keys[2], other_core)

        def begin(self):
            self.over_y.start()
            self.core.start()

        def hand_on(self):
            self.over_y.wait_recv()
            self.all.start()

        def arrive(self):
            self.core.wait_recv()
            self.all.wait_recv()

        def end(self):
            for copy in (self.over_y, self.core, self.all):
                copy.wait_send()

    narrow = Vectors(pl.ds(0, 8), pl.ds(0, -(-part // 128) * 128), ((0, 0), (0, 1), (0, 2)))
    broad = Vectors(pl.ds(8, 8), pl.ds(0, D), ((0, 3), (1, 3), (2, 3)))
    mixer_y = remote(mixer_ref, mixer_out.at[shard], weight_sems, (1, 0), other_y)
    mixer_core = remote(mixer_ref, mixer_out.at[shard], weight_sems, (1, 1), other_core)
    mixer_pass = remote(mixer_out.at[far], mixer_out.at[far], weight_sems, (1, 2), other_core)
    class Relayed:
        def __init__(self, ref, out, index, pieces):
            size = ref.shape[0] // 2
            piece = size // RELAY_PIECES
            self.over_y, self.over_x, self.rest = [], [], []
            for k in range(pieces):
                rows = pl.ds(pl.multiple_of(x * size + k * piece, piece), piece)
                self.over_y.append(
                    remote(
                        ref.at[rows, :],
                        out.at[shard, rows, :],
                        relay_sems,
                        (index, 0, k),
                        other_y,
                    )
                )
                passed = out.at[far, rows, :]
                self.over_x.append(remote(passed, passed, relay_sems, (index, 1, k), other_x))
            for k in range(2):
                if pieces < RELAY_PIECES:
                    rows = pl.ds(k * size + pieces * piece, size - pieces * piece)
                    self.rest.append(
                        remote(
                            ref.at[rows, :],
                            out.at[shard, rows, :],
                            relay_sems,
                            (index, 2, k),
                            other_y,
                        )
                    )
            self.core = remote(ref, out.at[shard], weight_sems, (2 + index, 0), other_core)
            self.all = remote(out.at[far], out.at[far], weight_sems, (2 + index, 1), other_core)

        def begin(self):
            for copy in self.over_y:
                copy.start()
            self.core.start()

        def begin_rest(self):
            for copy in self.rest:
                copy.start()

        def relay(self, k):
            self.over_y[k].wait_recv()
            self.over_x[k].start()

        def hand_on(self):
            for copy in self.over_x + self.rest:
                copy.wait_recv()
            self.all.start()

        def end(self):
            for copy in self.over_y + self.over_x + self.rest:
                copy.wait_send()
            self.core.wait()
            self.all.wait()

    outer_way = Relayed(outer_ref, outer_out, 0, RELAY_PIECES)
    inner_way = Relayed(inner_ref, inner_out, 1, 1)
    narrow.begin()

    def send_joint(pair, carry):
        each_third(pair, joint_y, "start")
        each_third(pair, joint_core, "start")
        return carry

    lax.fori_loop(0, pairs, send_joint, 0)
    outer_way.begin()
    inner_way.begin()
    mixer_y.start()
    mixer_core.start()
    inner_way.begin_rest()
    broad.begin()
    for first, second in zip(own_in, own_out):
        first.wait()
        second.start()

    for batch in range(MB):
        key_documents(starts_ref, batch, key_docs.at[batch])
    narrow.hand_on()
    narrow.arrive()
    tok_load.wait()

    def bias_of(slot):
        pieces = [
            vec_out[f, slot : slot + 1, 0:part] for f in range(4)
        ]
        return jnp.concatenate(pieces, axis=1)

    query_bias, value_bias = bias_of(0), bias_of(1)
    for pair in range(pairs):
        columns = slice(pair * 128, (pair + 1) * 128)
        bias_rows[pair, :, 0:128] = jnp.broadcast_to(query_bias[:, columns], (8, 128))
        bias_rows[pair, :, 128:256] = jnp.zeros((8, 128), F32)
        bias_rows[pair, :, 256:384] = jnp.broadcast_to(value_bias[:, columns], (8, 128))

    def sent_sem(unit):
        return owner_of(count, unit), unit // count

    def send_copy(unit):
        owner, slot = sent_sem(unit)
        return pltpu.make_async_remote_copy(
            src_ref=put.at[owner, slot],
            dst_ref=got_ref.at[me, slot],
            send_sem=put_sem.at[owner, slot],
            recv_sem=got_sem.at[me, slot],
            device_id={"ctx": owner},
        )

    def keep_copy(slot):
        return pltpu.make_async_copy(
            put.at[me, slot], got_ref.at[me, slot], own_sems.at[2, slot, 0]
        )

    def project(pair, carry):
        each_third(pair, own_joint, "wait")
        each_third(pair, joint_y, "wait_recv")
        each_third(pair, joint_pass, "start")
        each_third(pair, joint_core, "wait_recv")
        each_third(pair, joint_pass, "wait_recv")
        joint_store(pair).start()
        weight = joint_all[pair].reshape(4 * part, 384)
        rows = jnp.dot(tok_ref[...], weight, preferred_element_type=F32)
        rows = (rows + bias_rows[pair, 0:1, :]).astype(BF16)
        for third in range(3):
            for batch in range(MB):
                block = rows[batch * lanes : (batch + 1) * lanes, third * 128 : (third + 1) * 128]
                turned = block.T
                if third == 0:
                    turned = turned * SCALE
                for j in range(2):
                    unit = (2 * pair + j) * MB + batch
                    put[owner_of(count, unit), unit // count, third * HD : (third + 1) * HD, :] = (
                        turned[j * HD : (j + 1) * HD]
                    )
        for i in range(2 * MB):
            unit = 2 * pair * MB + i
            owner, slot = owner_of(count, unit), unit // count

            @pl.when(owner != me)
            def _():
                send_copy(unit).start()

            @pl.when(owner == me)
            def _():
                keep_copy(slot).start()

        return carry

    lax.fori_loop(0, pairs, project, 0)

    def arrival(sender, slot):
        return pltpu.make_async_remote_copy(
            src_ref=put.at[sender, slot],
            dst_ref=got_ref.at[sender, slot],
            send_sem=put_sem.at[sender, slot],
            recv_sem=got_sem.at[sender, slot],
            device_id={"ctx": sender},
        )

    def back_copy(peer, slot):
        return pltpu.make_async_remote_copy(
            src_ref=back_put.at[peer, slot],
            dst_ref=back_got.at[me, slot],
            send_sem=back_put_sem.at[peer, slot],
            recv_sem=back_got_sem.at[me, slot],
            device_id={"ctx": peer},
        )

    def back_keep(slot):
        return pltpu.make_async_copy(
            back_put.at[me, slot], back_got.at[me, slot], own_sems.at[2, slot, 1]
        )

    early = total_units // count > 2

    def outputs(slot):
        return (
            pltpu.make_async_copy(got_ref.at[:, slot], got_out.at[:, slot], out_sems.at[slot, 0]),
            pltpu.make_async_copy(wide_ref.at[slot], wide_out.at[slot], out_sems.at[slot, 1]),
            pltpu.make_async_copy(lse_ref.at[slot], lse_out.at[slot], out_sems.at[slot, 2]),
        )

    def unit_step(slot, carry):
        def wait_one(step, inner):
            arrival(lax.rem(me + step, count), slot).wait_recv()
            return inner

        lax.fori_loop(1, count, wait_one, 0)
        keep_copy(slot).wait()
        outputs(slot)[0].start()
        for i in range(count):
            rows = slice(i * lanes, (i + 1) * lanes)
            key_rows[rows, :] = got_ref[i, slot, HD : 2 * HD, :].T
            value_t[:, rows] = got_ref[i, slot, 2 * HD : 3 * HD, :]
        batch = batch_of(count, me, slot)

        def block(number, inner):
            begin = pl.multiple_of(number * width, width)
            parts = [got_ref[number * group + i, slot, 0:HD, :] for i in range(group)]
            queries = parts[0] if group == 1 else jnp.concatenate(parts, axis=1)
            query_docs = query_documents(starts_ref, batch, begin, width)

            def chunk(index, running):
                peak, total, mixed = running
                first = pl.multiple_of(index * depth, depth)
                scores = jnp.dot(
                    key_rows[pl.ds(first, depth), :], queries, preferred_element_type=F32
                )
                same = same_document(key_docs.at[batch], first, depth, query_docs)
                scores = jnp.where(same, scores, MASKED)
                new_peak = jnp.maximum(peak, jnp.max(scores, axis=0, keepdims=True))
                scaling = jnp.exp(peak - new_peak)
                weights = jnp.exp(scores - new_peak)
                return (
                    new_peak,
                    total * scaling + jnp.sum(weights, axis=0, keepdims=True),
                    mixed * scaling
                    + jnp.dot(
                        value_t[:, pl.ds(first, depth)],
                        weights.astype(BF16),
                        preferred_element_type=F32,
                    ),
                )

            peak, total, mixed = over_chunks(
                length // depth,
                chunk,
                (
                    jnp.full((1, width), -jnp.inf, F32),
                    jnp.zeros((1, width), F32),
                    jnp.zeros((HD, width), F32),
                ),
            )
            mixed = mixed / total
            wide_ref[slot, :, pl.ds(begin, width)] = mixed
            lse_ref[slot, :, pl.ds(begin, width)] = jnp.broadcast_to(
                peak + jnp.log(total), (8, width)
            )
            low = mixed.astype(BF16)
            for i in range(group):
                back_put[number * group + i, slot] = low[:, i * lanes : (i + 1) * lanes]
            return inner

        lax.fori_loop(0, length // width, block, 0)

        def send_one(step, inner):
            back_copy(lax.rem(me + step, count), slot).start()
            return inner

        lax.fori_loop(1, count, send_one, 0)
        back_keep(slot).start()
        start(outputs(slot)[1:])
        if early:

            @pl.when(slot == 0)
            def _():
                outer_way.relay(0)
                outer_way.relay(1)

            @pl.when(slot == 1)
            def _():
                outer_way.relay(2)

            @pl.when(slot == 2)
            def _():
                inner_way.relay(0)

        return carry

    lax.fori_loop(0, mine, unit_step, 0)

    if not early:
        outer_way.relay(0)
        outer_way.relay(1)
        outer_way.relay(2)
        inner_way.relay(0)
    mixer_y.wait_recv()
    mixer_pass.start()
    outer_way.hand_on()

    def sent(unit, carry):
        @pl.when(owner_of(count, unit) != me)
        def _():
            send_copy(unit).wait_send()

        return carry

    lax.fori_loop(0, total_units, sent, 0)

    def returned(slot, carry):
        def one(step, inner):
            back_copy(lax.rem(me + step, count), slot).wait_send()
            return inner

        lax.fori_loop(1, count, one, 0)
        for copy in outputs(slot):
            copy.wait()
        return carry

    lax.fori_loop(0, mine, returned, 0)
    inner_way.hand_on()
    broad.hand_on()

    def home(unit, carry):
        owner, slot = owner_of(count, unit), unit // count

        @pl.when(owner != me)
        def _():
            pltpu.make_async_remote_copy(
                src_ref=back_put.at[owner, slot],
                dst_ref=back_got.at[owner, slot],
                send_sem=back_put_sem.at[owner, slot],
                recv_sem=back_got_sem.at[owner, slot],
                device_id={"ctx": owner},
            ).wait_recv()

        @pl.when(owner == me)
        def _():
            back_keep(slot).wait()

        return carry

    lax.fori_loop(0, total_units, home, 0)
    att_stores = []
    for batch in range(MB):
        rows = slice(batch * lanes, (batch + 1) * lanes)
        for pair in range(pairs):
            tops = []
            for j in range(2):
                unit = (2 * pair + j) * MB + batch
                tops.append(back_got[owner_of(count, unit), unit // count])
            att_ref[rows, pair * 128 : (pair + 1) * 128] = jnp.concatenate(tops, axis=0).T
        att_stores.append(
            pltpu.make_async_copy(att_ref.at[rows, :], att_out.at[rows, :], row_sems.at[batch])
        )
        att_stores[-1].start()

    outer_way.end()
    inner_way.end()
    broad.arrive()
    narrow.end()
    broad.end()
    for i in range(8):
        vec_full[i : i + 1, :] = bias_of(i)
    vec_full[8:16, :] = jnp.zeros((8, D), F32)
    for k in range(4):
        inner_bias_full[:, k * D : (k + 1) * D] = vec_out[k, 8:9, :]
    mixer_y.wait_send()
    mixer_core.wait()
    mixer_pass.wait()
    every_pair(joint_y, "wait_send")
    every_pair(joint_core, "wait_send")
    every_pair(joint_pass, "wait_send")
    for copy in own_out:
        copy.wait()

    for copy in att_stores:
        copy.wait()
    for pair in range(pairs):
        joint_store(pair).wait()


def forward(count, starts, tokens, joint, mixer, inner, outer, vectors, number):
    units = -(-UNITS // count)
    lanes = tokens.shape[0] // MB
    length = count * lanes
    width = 2 * lanes
    part = joint.shape[0]
    pairs = H // 2
    vm = pl.BlockSpec(memory_space=pltpu.VMEM)
    hbm = pl.BlockSpec(memory_space=pl.ANY)
    dma = pltpu.SemaphoreType.DMA
    return pl.pallas_call(
        functools.partial(forward_kernel, width),
        out_shape=(
            jax.ShapeDtypeStruct(tokens.shape, BF16),
            jax.ShapeDtypeStruct((count, units, 3 * HD, lanes), BF16),
            jax.ShapeDtypeStruct((units, HD, length), F32),
            jax.ShapeDtypeStruct((units, 8, length), F32),
            jax.ShapeDtypeStruct((pairs, 4, part, 384), BF16),
            jax.ShapeDtypeStruct((BIAS_ROWS, D), F32),
            jax.ShapeDtypeStruct((1, FF), F32),
            jax.ShapeDtypeStruct((4, *mixer.shape), BF16),
            jax.ShapeDtypeStruct((4, *inner.shape), BF16),
            jax.ShapeDtypeStruct((4, *outer.shape), BF16),
        ),
        in_specs=[pl.BlockSpec(memory_space=pltpu.SMEM)] + [hbm] * 5 + [vm] * 9,
        out_specs=(hbm, hbm, hbm, hbm, hbm, vm, vm, hbm, hbm, hbm),
        scratch_shapes=[
            pltpu.VMEM(tokens.shape, BF16),
            pltpu.VMEM(tokens.shape, BF16),
            pltpu.VMEM((count, units, 3 * HD, lanes), BF16),
            pltpu.VMEM((units, HD, length), F32),
            pltpu.VMEM((units, 8, length), F32),
            pltpu.VMEM((pairs, 4, part, 384), BF16),
            pltpu.VMEM((BIAS_ROWS, D), F32),
            pltpu.VMEM((4, BIAS_ROWS, D), F32),
            pltpu.VMEM((pairs, 8, 384), F32),
            pltpu.VMEM((count, units, 3 * HD, lanes), BF16),
            pltpu.VMEM((count, units, HD, lanes), BF16),
            pltpu.VMEM((count, units, HD, lanes), BF16),
            pltpu.VMEM((length, HD), BF16),
            pltpu.VMEM((HD, length), BF16),
            pltpu.VMEM((MB, length, lanes), jnp.int32),
            pltpu.VMEM(mixer.shape, BF16),
            pltpu.VMEM(inner.shape, BF16),
            pltpu.VMEM(outer.shape, BF16),
            dma((count, units)),
            dma((count, units)),
            dma((count, units)),
            dma((count, units)),
            dma((2, 3, pairs, 3)),
            dma((2, 4, 4)),
            dma((2, 2, 3, RELAY_PIECES)),
            dma((3, max(pairs, units, 4), 3)),
            dma((units, 3)),
            dma((MB + 1,)),
        ],
        compiler_params=pltpu.CompilerParams(
            collective_id=number, has_side_effects=True, vmem_limit_bytes=56 * 1024 * 1024
        ),
        name="forward",
    )(starts, tokens, joint, mixer, inner, outer, *vectors)


def first_rows(half, tile):
    return half if half <= tile else (half // tile + 1) // 2 * tile


class Place:
    def __init__(self, count):
        self.count = count
        self.depth = count // 2
        self.me, self.shard = lax.axis_index("ctx"), lax.axis_index("fsdp")
        self.y, self.core = self.shard // 2, lax.rem(self.shard, 2)
        self.z, self.x = self.me // 2, lax.rem(self.me, 2)
        self.other_core = {"fsdp": 2 * self.y + 1 - self.core}
        self.other_y = {"fsdp": 2 * (1 - self.y) + self.core}
        self.other_x = {"ctx": 2 * self.z + 1 - self.x}

        self.hi, self.lo = self.z // 2, lax.rem(self.z, 2)

    def along_z(self, step):
        return lax.rem(self.z + step, self.depth)

    def peer_z(self, step):
        return {"ctx": 2 * self.along_z(step) + self.x}


def start(copies):
    for copy in copies:
        copy.start()


def added(a, b):
    return (a.astype(F32) + b.astype(F32)).astype(a.dtype)


class Reduction:
    def __init__(self, place, j, grad, out, head, paired, buffers, sems, z_sems):
        got, y_one, x_one, x_two, y_two, z_got = buffers
        self.place, self.grad, self.out, self.head, self.buffers = place, grad, out, head, buffers
        half, lanes = grad.shape[4], grad.shape[5] // 2
        self.half, self.lanes, self.paired = half, lanes, paired
        p = place
        here, there = self.side(p.y), self.side(1 - p.y)

        def remote(src, dst, slot, peer):
            return pltpu.make_async_remote_copy(
                src_ref=src,
                dst_ref=dst,
                send_sem=sems.at[0, j, slot],
                recv_sem=sems.at[1, j, slot],
                device_id=peer,
            )

        def z_copy(z, target, step):
            return pltpu.make_async_remote_copy(
                src_ref=grad.at[z // 2, lax.rem(z, 2), p.x, p.core, :, here],
                dst_ref=z_got.at[target],
                send_sem=z_sems.at[0, j, step],
                recv_sem=z_sems.at[1, j, step],
                device_id={"ctx": 2 * z + p.x},
            )

        self.first = [remote(grad.at[:, :, :, 1 - p.core], got, 0, p.other_core)]
        self.second = [remote(grad.at[:, :, :, p.core, 0:head, there], y_one, 1, p.other_y)]
        self.third = [
            remote(grad.at[:, :, 1 - p.x, p.core, 0:head, here], x_two, 2, p.other_x)
        ]
        if head < half:
            self.second.append(
                remote(grad.at[:, :, 1 - p.x, p.core, head:half, :], x_one, 3, p.other_x)
            )
            self.third.append(
                remote(grad.at[:, :, p.x, p.core, head:half, there], y_two, 4, p.other_y)
            )
        if paired:
            near = {"ctx": 2 * (2 * p.hi + 1 - p.lo) + p.x}
            self.fourth = [
                remote(
                    grad.at[:, 1 - p.lo, p.x, p.core, :, here], z_got.at[pl.ds(0, 2)], 6, near
                )
            ]
            self.fifth = [z_copy(2 * (1 - p.hi) + p.lo, 2, 1)]
        else:
            self.fourth = []
            self.fifth = [z_copy(lax.rem(p.z + step, 4), p.z, step) for step in range(1, 4)]
        self.last = [remote(out.at[p.core], out.at[p.core], 5, p.other_core)]

    def side(self, y):
        return pl.ds(pl.multiple_of(y * self.lanes, 128), self.lanes)

    def each(self, body):
        def step(block, carry):
            body(block // 2, lax.rem(block, 2))
            return carry

        lax.fori_loop(0, 4, step, 0)

    def stage_zero(self):
        start(self.first)

    def stage_one(self):
        p, grad, got = self.place, self.grad, self.buffers[0]
        for copy in self.first:
            copy.wait_recv()

        def body(hi, lo):
            for x in range(2):
                grad[hi, lo, x, p.core] = added(grad[hi, lo, x, p.core], got[hi, lo, x])

        self.each(body)
        start(self.second)

    def stage_two(self):
        p, grad, head, half = self.place, self.grad, self.head, self.half
        y_one, x_one = self.buffers[1], self.buffers[2]
        here = self.side(p.y)
        for copy in self.second:
            copy.wait()

        def body(hi, lo):
            for x in range(2):
                grad[hi, lo, x, p.core, 0:head, here] = added(
                    grad[hi, lo, x, p.core, 0:head, here], y_one[hi, lo, x]
                )
            if head < half:
                grad[hi, lo, p.x, p.core, head:half, :] = added(
                    grad[hi, lo, p.x, p.core, head:half, :], x_one[hi, lo]
                )

        self.each(body)
        start(self.third)

    def stage_three(self):
        p, grad, head, half = self.place, self.grad, self.head, self.half
        x_two, y_two = self.buffers[3], self.buffers[4]
        here = self.side(p.y)
        for copy in self.third:
            copy.wait()

        def body(hi, lo):
            grad[hi, lo, p.x, p.core, 0:head, here] = added(
                grad[hi, lo, p.x, p.core, 0:head, here], x_two[hi, lo]
            )
            if head < half:
                grad[hi, lo, p.x, p.core, head:half, here] = added(
                    grad[hi, lo, p.x, p.core, head:half, here], y_two[hi, lo]
                )

        self.each(body)
        start(self.fourth if self.paired else self.fifth)

    def stage_four(self):
        p, grad, z_got = self.place, self.grad, self.buffers[5]
        here = self.side(p.y)
        for copy in self.fourth:
            copy.wait()
        for hi in range(2):
            grad[hi, p.lo, p.x, p.core, :, here] = added(
                grad[hi, p.lo, p.x, p.core, :, here], z_got[hi]
            )
        start(self.fifth)

    def stage_five(self):
        p, z_got = self.place, self.buffers[5]
        for copy in self.fifth:
            copy.wait()
        total = self.grad[p.hi, p.lo, p.x, p.core, :, self.side(p.y)].astype(F32)
        if self.paired:
            total = total + z_got[2].astype(F32)
        else:
            for step in range(1, 4):
                total = total + z_got[lax.rem(p.z + step, 4)].astype(F32)
        self.out[p.core] = total.astype(self.out.dtype)
        start(self.last)

    def stage_six(self):
        for copy in self.last:
            copy.wait()
        for copy in self.first:
            copy.wait_send()


def reduction_buffers(half, lanes, head, dtype):
    tail = max(half - head, 16)
    shapes = (
        (2, 2, 2, half, 2 * lanes),
        (2, 2, 2, head, lanes),
        (2, 2, tail, 2 * lanes),
        (2, 2, head, lanes),
        (2, 2, tail, lanes),
        (4, half, lanes),
        (2, half, lanes),
    )
    return [pltpu.VMEM(shape, dtype) for shape in shapes]


def backward_kernel(width, plan, *refs):
    (
        starts_ref,
        flow_in,
        got_in,
        wide_in,
        lse_in,
        tok_in,
        residual_in,
        bias_in,
        joint_in,
        d_outer_in,
        act_in,
        d_inner_in,
        first_in,
        d_branch_in,
        att_in,
        tokens_hbm,
        outer_hbm,
        inner_hbm,
        mixer_hbm,
        joint_out,
        bias_out,
        tokens_out,
        outer_out,
        inner_out,
        mixer_out,
        flow_ref,
        got_ref,
        wide_ref,
        lse_ref,
        tok_ref,
        residual_ref,
        bias_ref,
        d_outer_ref,
        act_ref,
        d_inner_ref,
        first_ref,
        d_branch_ref,
        att_ref,
        flow_put,
        flow_got,
        put,
        home_got,
        key_rows,
        value_rows,
        key_t,
        key_docs,
        d_key,
        d_value,
        joint_all,
        outer_one,
        outer_two,
        inner_one,
        inner_two,
        mixer_grad,
        joint_one,
        joint_two,
        d_turned,
        bias_sum,
        bias_got,
        flow_sems,
        home_sems,
        own_sems,
        sems,
        z_sems,
        bias_sems,
        in_sems,
        result_sems,
        *buffers,
    ) = refs
    count, units, _, lanes = got_ref.shape
    length = count * lanes
    depth = min(length, 1024)
    group = width // lanes
    pairs = H // 2
    total_units = MB * H
    p = Place(count)
    me = p.me
    mine = owned(count, me)

    sources = (
        (flow_in, flow_ref),
        (d_outer_in, d_outer_ref),
        (act_in, act_ref),
        (d_inner_in, d_inner_ref),
        (first_in, first_ref),
        (d_branch_in, d_branch_ref),
        (att_in, att_ref),
        (bias_in, bias_ref),
        (got_in, got_ref),
        (wide_in, wide_ref),
        (lse_in, lse_ref),
        (tok_in, tok_ref),
        (residual_in, residual_ref),
    )
    loads = [
        pltpu.make_async_copy(source, held, in_sems.at[k])
        for k, (source, held) in enumerate(sources)
    ]
    start(loads)

    def loaded(first, last):
        for copy in loads[first:last]:
            copy.wait()

    barrier = pltpu.get_barrier_semaphore()

    def greet(step, carry):
        pl.semaphore_signal(barrier, inc=1, device_id={"ctx": lax.rem(me + step, count)})
        return carry

    lax.fori_loop(1, count, greet, 0)
    pl.semaphore_signal(barrier, inc=1, device_id=p.other_core)
    pl.semaphore_signal(barrier, inc=1, device_id=p.other_y)
    pl.semaphore_signal(barrier, inc=1, device_id={**p.other_y, **p.other_x})
    joint_load = pltpu.make_async_copy(joint_in, joint_all, own_sems.at[2, 0])
    joint_load.start()

    grads = (outer_one, outer_two, inner_one, inner_two, mixer_grad, joint_one, joint_two)
    jobs = [
        Reduction(
            p,
            j,
            grads[j],
            buffers[7 * j + 6],
            plan[j][2],
            plan[j][3],
            buffers[7 * j : 7 * j + 6],
            sems,
            z_sems,
        )
        for j in range(len(grads))
    ]
    o_one, o_two, i_one, i_two, m_one, j_one, j_two = jobs

    def store_rows(targets, row, values, columns):
        half = sum(t.shape[4] for t in targets)
        done = 0
        while done < values.shape[0]:
            block, inside = (row + done) // half, (row + done) % half
            k = 0
            while inside >= targets[k].shape[4]:
                inside -= targets[k].shape[4]
                k += 1
            size = min(values.shape[0] - done, targets[k].shape[4] - inside)
            targets[k][
                block // 8,
                block // 4 % 2,
                block // 2 % 2,
                block % 2,
                inside : inside + size,
                columns,
            ] = values[done : done + size]
            done += size

    loaded(0, 3)
    d_outer_turned = d_outer_ref[...].T

    def outer_gradient(which):
        for side in range(2):
            begin = (2 * side + which) * D
            values = jnp.dot(
                d_outer_turned, act_ref[:, begin : begin + D], preferred_element_type=F32
            )
            columns = slice(side * D, (side + 1) * D)
            store_rows(((outer_one, outer_two)[which],), 0, values.astype(BF16), columns)

    def inner_gradient():
        for k in range(FF // D):
            turned = d_inner_ref[:, k * D : (k + 1) * D].T
            values = jnp.dot(turned, first_ref[...], preferred_element_type=F32)
            store_rows((inner_one, inner_two), k * D, values.astype(BF16), slice(0, D))

    def mixer_gradient():
        values = jnp.dot(d_branch_ref[...].T, att_ref[...], preferred_element_type=F32)
        store_rows((mixer_grad,), 0, values.astype(BF16), slice(0, D))

    def unit_copy(source, target, sem, owner, slot):
        return pltpu.make_async_remote_copy(
            src_ref=source.at[owner, slot],
            dst_ref=target.at[me, slot],
            send_sem=sem.at[0, owner, slot],
            recv_sem=sem.at[1, me, slot],
            device_id={"ctx": owner},
        )

    def unit_arrival(source, target, sem, sender, slot):
        return pltpu.make_async_remote_copy(
            src_ref=source.at[sender, slot],
            dst_ref=target.at[sender, slot],
            send_sem=sem.at[0, sender, slot],
            recv_sem=sem.at[1, sender, slot],
            device_id={"ctx": sender},
        )

    def unit_keep(source, target, kind, slot):
        return pltpu.make_async_copy(
            source.at[me, slot], target.at[me, slot], own_sems.at[kind, slot]
        )

    for pair in range(pairs):
        for batch in range(MB):
            block = flow_ref[
                batch * lanes : (batch + 1) * lanes, pair * 128 : (pair + 1) * 128
            ].T
            for j in range(2):
                unit = (2 * pair + j) * MB + batch
                flow_put[owner_of(count, unit), unit // count] = block[j * HD : (j + 1) * HD]

    outer_gradient(0)
    pl.semaphore_wait(barrier, count + 2)
    o_one.stage_zero()

    def send_flow(turn, carry):
        slot, owner = turn // count, lax.rem(me + turn, count)

        @pl.when((owner != me) & (slot < owned(count, owner)))
        def _():
            unit_copy(flow_put, flow_got, flow_sems, owner, slot).start()

        @pl.when((owner == me) & (slot < mine))
        def _():
            unit_keep(flow_put, flow_got, 0, slot).start()

        return carry

    lax.fori_loop(0, units * count, send_flow, 0)
    loaded(3, 8)
    bias_sum[0] = bias_ref[...]
    outer_gradient(1)
    o_two.stage_zero()
    o_one.stage_one()
    inner_gradient()
    i_one.stage_zero()
    i_two.stage_zero()
    mixer_gradient()
    m_one.stage_zero()

    loaded(8, len(loads))

    def unit_step(slot, carry):
        def wait_one(step, inner):
            unit_arrival(flow_put, flow_got, flow_sems, lax.rem(me + step, count), slot).wait_recv()
            return inner

        lax.fori_loop(1, count, wait_one, 0)
        unit_keep(flow_put, flow_got, 0, slot).wait()
        for i in range(count):
            rows = slice(i * lanes, (i + 1) * lanes)
            key_rows[rows, :] = got_ref[i, slot, HD : 2 * HD, :].T
            value_rows[rows, :] = got_ref[i, slot, 2 * HD : 3 * HD, :].T
            key_t[:, rows] = got_ref[i, slot, HD : 2 * HD, :]
        batch = batch_of(count, me, slot)
        key_documents(starts_ref, batch, key_docs)
        d_key[...] = jnp.zeros_like(d_key)
        d_value[...] = jnp.zeros_like(d_value)

        def block(number, inner):
            begin = pl.multiple_of(number * width, width)

            def beside(ref):
                parts = [ref[number * group + i, slot, 0:HD, :] for i in range(group)]
                return parts[0] if group == 1 else jnp.concatenate(parts, axis=1)

            queries, flow = beside(got_ref), beside(flow_got)
            query_rows, flow_rows = queries.T, flow.T
            query_docs = query_documents(starts_ref, batch, begin, width)
            log_total = lse_ref[slot, 0:1, pl.ds(begin, width)]
            spread = jnp.sum(
                flow.astype(F32) * wide_ref[slot, :, pl.ds(begin, width)], axis=0, keepdims=True
            )

            def chunk(index, d_query):
                first = pl.multiple_of(index * depth, depth)
                rows = pl.ds(first, depth)
                scores = jnp.dot(key_rows[rows, :], queries, preferred_element_type=F32)
                same = same_document(key_docs, first, depth, query_docs)
                probs = jnp.exp(jnp.where(same, scores, MASKED) - log_total)
                pressure = jnp.dot(value_rows[rows, :], flow, preferred_element_type=F32)
                d_scores = (probs * (pressure - spread)).astype(BF16)
                d_value[rows, :] += jnp.dot(
                    probs.astype(BF16), flow_rows, preferred_element_type=F32
                )
                d_key[rows, :] += jnp.dot(d_scores, query_rows, preferred_element_type=F32)
                return d_query + jnp.dot(key_t[:, rows], d_scores, preferred_element_type=F32)

            d_query = over_chunks(length // depth, chunk, jnp.zeros((HD, width), F32))
            low = (d_query * SCALE).astype(BF16)
            for i in range(group):
                put[number * group + i, slot, 0:HD, :] = low[:, i * lanes : (i + 1) * lanes]
            return inner

        lax.fori_loop(0, length // width, block, 0)
        for i in range(count):
            rows = slice(i * lanes, (i + 1) * lanes)
            put[i, slot, HD : 2 * HD, :] = d_key[rows, :].T.astype(BF16)
            put[i, slot, 2 * HD : 3 * HD, :] = d_value[rows, :].T.astype(BF16)

        def send_one(step, inner):
            unit_copy(put, home_got, home_sems, lax.rem(me + step, count), slot).start()
            return inner

        lax.fori_loop(1, count, send_one, 0)
        unit_keep(put, home_got, 1, slot).start()

        @pl.when(slot == 0)
        def _():
            o_two.stage_one()

        @pl.when(slot == 1)
        def _():
            i_one.stage_one()

        @pl.when(slot == 2)
        def _():
            o_one.stage_two()

        return carry

    lax.fori_loop(0, mine, unit_step, 0)
    o_two.stage_two()
    i_two.stage_one()
    o_one.stage_three()
    i_one.stage_two()
    m_one.stage_one()

    ones = jnp.ones((8, MB * lanes), BF16)
    for pair in range(pairs):
        columns = []
        for batch in range(MB):
            blocks = []
            for j in range(2):
                unit = (2 * pair + j) * MB + batch
                owner, slot = owner_of(count, unit), unit // count

                @pl.when(owner != me)
                def _():
                    unit_arrival(put, home_got, home_sems, owner, slot).wait_recv()

                @pl.when(owner == me)
                def _():
                    unit_keep(put, home_got, 1, slot).wait()

                blocks.append(home_got[owner, slot])
            rows = [b[third * HD : (third + 1) * HD] for third in range(3) for b in blocks]
            columns.append(jnp.concatenate(rows, axis=0))
        d_pair = jnp.concatenate(columns, axis=1)
        d_turned[pair] = d_pair.T
        grad = jnp.dot(d_pair, tok_ref[...], preferred_element_type=F32).astype(BF16)
        for third in range(3):
            store_rows(
                (joint_one, joint_two),
                third * D + pair * 128,
                grad[third * 128 : (third + 1) * 128],
                slice(0, D),
            )
        sums = lax.dot_general(
            ones, d_pair, (((1,), (1,)), ((), ())), preferred_element_type=F32
        )
        bias_sum[0, 0:1, pair * 128 : (pair + 1) * 128] = sums[0:1, 0:128]
        bias_sum[0, 1:2, pair * 128 : (pair + 1) * 128] = sums[0:1, 256:384]
        if pair == 2:
            o_two.stage_three()
            o_one.stage_four()
            i_two.stage_two()
            i_one.stage_three()

    m_one.stage_two()
    o_two.stage_four()

    plane = (p.other_y, p.other_x, {**p.other_y, **p.other_x})

    def bias_copy(level, number, slot, peer):
        return pltpu.make_async_remote_copy(
            src_ref=bias_sum.at[level],
            dst_ref=bias_got.at[slot],
            send_sem=bias_sems.at[0, number],
            recv_sem=bias_sems.at[1, number],
            device_id=peer,
        )

    bias_core = bias_copy(0, 0, 0, p.other_core)
    bias_plane = [bias_copy(1, 1 + i, 1 + i, peer) for i, peer in enumerate(plane)]
    bias_z = [
        bias_copy(2, 3 + step, 3 + step, {"ctx": 2 * lax.rem(p.z + step, 4) + p.x})
        for step in range(1, 4)
    ]
    bias_core.start()
    j_one.stage_zero()
    j_two.stage_zero()

    joint_load.wait()

    def token_terms(first, last, total):
        for pair in range(first, last):
            total = total + lax.dot_general(
                d_turned[pair],
                joint_all[pair],
                (((1,), (1,)), ((), ())),
                preferred_element_type=F32,
            )
        tokens_out[...] = total

    token_terms(0, pairs // 2, residual_ref[...])
    bias_core.wait()
    bias_sum[1] = bias_sum[0] + bias_got[0]
    start(bias_plane)
    j_one.stage_one()
    j_two.stage_one()
    i_two.stage_three()
    i_one.stage_four()
    token_terms(pairs // 2, pairs, tokens_out[...])
    results = [
        pltpu.make_async_copy(held, out, result_sems.at[k])
        for k, (held, out) in enumerate(
            (
                (tokens_out, tokens_hbm),
                (outer_out, outer_hbm),
                (inner_out, inner_hbm),
                (mixer_out, mixer_hbm),
            )
        )
    ]
    results[0].start()
    m_one.stage_three()
    for copy in bias_plane:
        copy.wait()
    bias_sum[2] = bias_sum[1] + bias_got[1] + bias_got[2] + bias_got[3]
    start(bias_z)
    j_one.stage_two()
    i_two.stage_four()
    j_two.stage_two()
    m_one.stage_four()
    j_one.stage_three()
    j_two.stage_three()
    o_one.stage_five()
    o_two.stage_five()
    i_one.stage_five()

    def parts_of(j):
        jobs[j].stage_six()
        whole = buffers[7 * j + 6]
        return [whole[low].astype(F32) for low in range(2)]

    def own_lanes(rows):
        width_own = rows.shape[1] // 2
        return jnp.where(p.core == 0, rows[:, :width_own], rows[:, width_own:])

    def put_out(out, pieces):
        out[...] = jnp.concatenate(pieces, axis=0).T

    one, two = parts_of(0), parts_of(1)
    outer_out[...] = jnp.concatenate(
        [jnp.where(p.core == 0, a, b) for a, b in zip(one, two)], axis=0
    )
    results[1].start()
    i_two.stage_five()
    m_one.stage_five()
    one, two = parts_of(2), parts_of(3)
    put_out(inner_out, [own_lanes(r) for r in (one[0], two[0], one[1], two[1])])
    results[2].start()
    put_out(mixer_out, [own_lanes(r) for r in parts_of(4)])
    results[3].start()
    for copy in bias_z:
        copy.wait()
    bias_total = bias_sum[2] + bias_got[4] + bias_got[5] + bias_got[6]
    index = me * 4 + p.shard
    world = 4 * count
    lane = lax.broadcasted_iota(jnp.int32, (D, 128), 0)
    place = lax.broadcasted_iota(jnp.int32, (D, 128), 1)

    def picked(rows, first):
        ones_there = jnp.where(lane == place + first, 1.0, 0.0)
        return jnp.dot(
            rows, ones_there, precision=lax.Precision.HIGHEST, preferred_element_type=F32
        )

    own_hidden = FF // world
    in_row = D // own_hidden
    row = lax.broadcasted_iota(jnp.int32, (8, D), 0)
    hidden = jnp.where(row == index // in_row, bias_total[8:16], 0.0)
    hidden = jnp.broadcast_to(jnp.sum(hidden, axis=0, keepdims=True), (8, D))
    bias_out[0:8, :] = picked(bias_total[0:8], index * (D // world))
    bias_out[8:16, :] = picked(hidden, lax.rem(index, in_row) * own_hidden)

    def sent(unit, carry):
        owner, slot = owner_of(count, unit), unit // count

        @pl.when(owner != me)
        def _():
            unit_copy(flow_put, flow_got, flow_sems, owner, slot).wait_send()

        return carry

    lax.fori_loop(0, total_units, sent, 0)

    def returned(slot, carry):
        def one(step, inner):
            unit_copy(put, home_got, home_sems, lax.rem(me + step, count), slot).wait_send()
            return inner

        lax.fori_loop(1, count, one, 0)
        return carry

    lax.fori_loop(0, mine, returned, 0)
    j_one.stage_five()
    j_two.stage_five()
    one, two = parts_of(5), parts_of(6)
    put_out(joint_out, [own_lanes(r) for r in (one[0], two[0], one[1], two[1])])
    for copy in results:
        copy.wait()


def backward(
    starts, flow, got, wide, lse, source, residual, biases, joint, activations, number
):
    count, units, _, lanes = got.shape
    length = count * lanes
    width = 2 * lanes
    pairs = H // 2
    vm = pl.BlockSpec(memory_space=pltpu.VMEM)
    hbm = pl.BlockSpec(memory_space=pl.ANY)
    dma = pltpu.SemaphoreType.DMA
    small = D // (2 * count)
    half_joint = 3 * D // (2 * count)
    early = first_rows(half_joint, 16)
    plan = (
        (small, FF // 2, small, True),
        (small, FF // 2, small, True),
        (2 * small, D, 2 * small - 16, True),
        (2 * small, D, 2 * small - 16, True),
        (small, D, small, True),
        (early, D, first_rows(early, 16), False),
        (half_joint - early, D, first_rows(half_joint - early, 16), False),
    )
    buffers = []
    for half, full, head, _ in plan:
        buffers += reduction_buffers(half, full // 2, head, BF16)
    outs = [
        jax.ShapeDtypeStruct((2 * small, FF // 4), F32),
        jax.ShapeDtypeStruct((D // 4, FF // count), F32),
        jax.ShapeDtypeStruct((D // 4, 2 * small), F32),
        jax.ShapeDtypeStruct((D // 4, 2 * half_joint), F32),
    ]
    return pl.pallas_call(
        functools.partial(backward_kernel, width, plan),
        out_shape=(
            jax.ShapeDtypeStruct(residual.shape, F32),
            *outs,
            jax.ShapeDtypeStruct((BIAS_ROWS, 128), F32),
        ),
        in_specs=[pl.BlockSpec(memory_space=pltpu.SMEM)] + [hbm] * 14,
        out_specs=(hbm,) * 4 + (vm,) * 2,
        scratch_shapes=[
            pltpu.VMEM(residual.shape, F32),
            *[pltpu.VMEM(o.shape, F32) for o in outs[:3]],
            *[
                pltpu.VMEM(a.shape, a.dtype)
                for a in (flow, got, wide, lse, source, residual, biases, *activations)
            ],
            pltpu.VMEM((count, units, HD, lanes), BF16),
            pltpu.VMEM((count, units, HD, lanes), BF16),
            pltpu.VMEM((count, units, 3 * HD, lanes), BF16),
            pltpu.VMEM((count, units, 3 * HD, lanes), BF16),
            pltpu.VMEM((length, HD), BF16),
            pltpu.VMEM((length, HD), BF16),
            pltpu.VMEM((HD, length), BF16),
            pltpu.VMEM((length, lanes), jnp.int32),
            pltpu.VMEM((length, HD), F32),
            pltpu.VMEM((length, HD), F32),
            pltpu.VMEM((pairs, D, 384), BF16),
            *[pltpu.VMEM((2, 2, 2, 2, half, full), BF16) for half, full, _, _ in plan],
            pltpu.VMEM((pairs, MB * lanes, 384), BF16),
            pltpu.VMEM((3, BIAS_ROWS, D), F32),
            pltpu.VMEM((7, BIAS_ROWS, D), F32),
            dma((2, count, units)),
            dma((2, count, units)),
            dma((3, units)),
            dma((2, len(plan), 7)),
            dma((2, len(plan), 4)),
            dma((2, 7)),
            dma((13,)),
            dma((4,)),
            *buffers,
        ],
        compiler_params=pltpu.CompilerParams(
            collective_id=number, has_side_effects=True, vmem_limit_bytes=67043328
        ),
        name="backward",
    )(starts, flow, got, wide, lse, source, residual, biases, joint, *activations)


def settle_kernel(count, *refs):
    sources, outs, held = refs[:count], refs[count : 2 * count], refs[2 * count : 3 * count]
    sems = refs[3 * count]
    copies_in = [
        pltpu.make_async_copy(sources[i], held[i], sems.at[0, i]) for i in range(count)
    ]
    copies_out = [pltpu.make_async_copy(held[i], outs[i], sems.at[1, i]) for i in range(count)]
    start(copies_in)
    for first, second in zip(copies_in, copies_out):
        first.wait()
        second.start()
    for copy in copies_out:
        copy.wait()


def settle(*arrays):
    count = len(arrays)
    return pl.pallas_call(
        functools.partial(settle_kernel, count),
        out_shape=[jax.ShapeDtypeStruct(a.shape, a.dtype) for a in arrays],
        in_specs=[pl.BlockSpec(memory_space=pl.ANY)] * count,
        out_specs=[pl.BlockSpec(memory_space=pl.ANY)] * count,
        scratch_shapes=[
            *[pltpu.VMEM(a.shape, a.dtype) for a in arrays],
            pltpu.SemaphoreType.DMA((2, count)),
        ],
        name="settle",
    )(*arrays)


def on_device(
    count,
    shards,
    tokens,
    doc_starts,
    joint_weight,
    mixer_weight,
    inner_weight,
    outer_weight,
    query_bias,
    value_bias,
    mixer_bias,
    first_gain,
    first_shift,
    inner_bias,
    outer_bias,
    second_gain,
    second_shift,
    upstream,
):
    rows = tokens.shape[2]
    length = rows * count
    units = -(-MB * H // count)
    me = lax.axis_index("ctx")

    part = D // shards
    vectors = [
        query_bias,
        value_bias,
        mixer_bias,
        first_gain,
        first_shift,
        outer_bias,
        second_gain,
        second_shift,
        inner_bias,
    ]
    source = tokens.reshape(MB * rows, D)
    attended, received, wide, lse, joint, vectors, ibias, mixer, inner, outer = forward(
        count,
        doc_starts,
        source,
        joint_weight,
        mixer_weight,
        inner_weight,
        outer_weight,
        vectors,
        0,
    )
    joint = joint.reshape(H // 2, D, 384)
    mixer, inner, outer = mixer.reshape(D, D), inner.reshape(D, FF), outer.reshape(FF, D)
    _, _, mbias, gain_one, shift_one, obias, gain_two, shift_two = [
        vectors[i : i + 1] for i in range(8)
    ]

    branch = mul_nn(attended, mixer) + mbias
    first, first_normed, first_recip = norm_forward(
        source.astype(F32) + branch, gain_one, shift_one
    )
    first_low = first.astype(BF16)
    inner_pre = mul_nn(first_low, inner) + ibias
    activated, gelu_slope = gelu_parts(inner_pre)
    activated_low = activated.astype(BF16)
    outer_out = mul_nn(activated_low, outer) + obias
    final, second_normed, second_recip = norm_forward(first + outer_out, gain_two, shift_two)
    result = final.astype(BF16).reshape(MB, 1, rows, D)

    incoming = upstream.reshape(MB * rows, D).astype(F32)
    rescale_grad = jnp.sum(incoming * second_normed, axis=0)
    reshift_grad = jnp.sum(incoming, axis=0)
    d_second = norm_backward(incoming, second_normed, second_recip, gain_two)
    d_outer = d_second.astype(BF16)
    return_grad = jnp.sum(d_outer.astype(F32), axis=0)
    d_inner = (mul_nt(d_outer, outer) * gelu_slope).astype(BF16)
    hidden_grad = jnp.sum(d_inner.astype(F32), axis=0)
    d_first = d_second + mul_nt(d_inner, inner)
    scale_grad = jnp.sum(d_first * first_normed, axis=0)
    shift_grad = jnp.sum(d_first, axis=0)
    d_residual = norm_backward(d_first, first_normed, first_recip, gain_one)
    d_branch = d_residual.astype(BF16)
    mixing_grad = jnp.sum(d_branch.astype(F32), axis=0)
    world = count * shards
    index = me * shards + lax.axis_index("fsdp")
    sums = [
        mixing_grad,
        scale_grad,
        shift_grad,
        return_grad,
        rescale_grad,
        reshift_grad,
        *hidden_grad.reshape(FF // D, D),
    ]
    if shards == 4 and count == 8:
        flow = mul_nt(d_branch, mixer).astype(BF16)
        biases = jnp.pad(jnp.stack(sums), ((2, BIAS_ROWS - 2 - len(sums)), (0, 0)))
        tokens_grad, *blocks, biases = backward(
            doc_starts,
            flow,
            received,
            wide,
            lse,
            source,
            d_residual,
            biases,
            joint,
            [d_outer, activated_low, d_inner, first_low, d_branch, attended],
            1,
        )
        *blocks, tokens_grad = settle(*blocks, tokens_grad)
        blocks[0] = blocks[0].T
        own, own_hidden = biases[:8, : D // world], biases[8, : FF // world]
    else:
        natural = joint.reshape(H // 2, D, 3, 128).transpose(1, 2, 0, 3).reshape(D, 3 * D)
        flow = mul_nt(mixer, d_branch).astype(BF16)
        flow_units = exchange(to_units(flow, 1, count, units), 2)
        d_units = attend_back(received, flow_units, doc_starts, wide, lse[:, :1])
        d_joint = from_units(exchange(d_units, 3), 3)
        bias_sums = jnp.sum(d_joint.astype(F32), axis=1)
        turned = [
            mul_tn(d_outer, activated_low),
            mul_tn(d_inner, first_low),
            mul_tn(d_branch, attended),
            mul_nn(d_joint, source),
        ]
        tokens_grad = d_residual + mul_tt(d_joint, natural)

        def reduced(grad):
            over_lanes = lax.psum_scatter(
                grad.astype(BF16), "fsdp", scatter_dimension=1, tiled=True
            )
            over_rows = lax.psum_scatter(over_lanes, "ctx", scatter_dimension=0, tiled=True)
            return over_rows.T.astype(F32)

        blocks = [reduced(g) for g in turned]
        biases = jnp.stack([bias_sums[:D], bias_sums[2 * D :], *sums])
        biases = lax.psum(biases, ("ctx", "fsdp"))
        own = lax.dynamic_slice_in_dim(biases[:8], index * (D // world), D // world, 1)
        hidden_rows = biases[8 : 8 + FF // D].reshape(FF)
        own_hidden = lax.dynamic_slice_in_dim(hidden_rows, index * (FF // world), FF // world, 0)
    tokens_grad = tokens_grad.reshape(MB, 1, rows, D)
    outer_out_grad, inner_out, mixer_out, joint_out = blocks
    sums = [*own[:5], own_hidden, *own[5:]]
    return (result, tokens_grad, joint_out, mixer_out, inner_out, outer_out_grad, *sums)


def solution(mesh):
    in_specs = (
        P(None, "fsdp", "ctx", None),
        P(None, "fsdp", None),
        P("fsdp", None),
        P("fsdp", None),
        P("fsdp", None),
        P("fsdp", None),
        P("fsdp"),
        P("fsdp"),
        P("fsdp"),
        P("fsdp"),
        P("fsdp"),
        P("fsdp"),
        P("fsdp"),
        P("fsdp"),
        P("fsdp"),
        P(None, "fsdp", "ctx", None),
    )
    out_specs = (
        P(None, "fsdp", "ctx", None),
        P(None, "fsdp", "ctx", None),
        P("fsdp", "ctx"),
        P("fsdp", "ctx"),
        P("fsdp", "ctx"),
        P("fsdp", "ctx"),
        P(("ctx", "fsdp")),
        P(("ctx", "fsdp")),
        P(("ctx", "fsdp")),
        P(("ctx", "fsdp")),
        P(("ctx", "fsdp")),
        P(("ctx", "fsdp")),
        P(("ctx", "fsdp")),
        P(("ctx", "fsdp")),
        P(("ctx", "fsdp")),
    )
    return jax.shard_map(
        functools.partial(on_device, mesh.shape["ctx"], mesh.shape["fsdp"]),
        mesh=mesh,
        in_specs=in_specs,
        out_specs=out_specs,
        check_vma=False,
    )
```
